32 devices in a mesh: row: 8 (over y, x, core), seq: 4 (over z).
Axes of the slice: x: 2, y: 2, z: 4, core: 2. Of those that a mesh axis runs over, the one named last changes fastest.
Arguments:
- tokens: bfloat16 [8, 2048, 768], P('row', 'seq'), may hold values from -6 to 6
- cotangent: bfloat16 [8, 2048, 768], P('row', 'seq'), may hold values from -6 to 6
- seg_ids: int32 [8, 2048], P('row', 'seq'), may hold values from 0 to 15, as said below
- seg_lengths: int32 [8, 16], P('row'), may hold values from 0 to 2048, as said below
- weights: float32 [123, 65536], P(None, ('row', 'seq'))
- vectors: float32 [9, 768], replicated
- vec_moments: float32 [2, 9, 768], replicated, as said below
- moments: float32 [128, 2, 256, 256], P(('row', 'seq')), as said below
- stats: float32 [128, 2, 256, 256], P(('row', 'seq')), as said below
- bases: float32 [128, 2, 256, 256], P(('row', 'seq')), as said below
- owners: int32 [123], replicated, may hold values from 0 to 31, as said below
- step_count: int32 [1], replicated, may hold values from 2 to 20
Outputs:
- layer_out: bfloat16 [8, 2048, 768], P('row', 'seq')
- x_grad: float32 [8, 2048, 768], P('row', 'seq')
- new_weights: float32 [123, 65536], P(None, ('row', 'seq'))
- new_moments: float32 [128, 2, 256, 256], P(('row', 'seq'))
- new_stats: float32 [128, 2, 256, 256], P(('row', 'seq'))
- new_bases: float32 [128, 2, 256, 256], P(('row', 'seq'))
- new_vectors: float32 [9, 768], replicated
- new_vec_moments: float32 [2, 9, 768], replicated
- grad_norm: float32 [1], replicated
The draws below stay inside these ranges and needn't reach their ends.
Inputs may be any that keep to these rules, and one draw needn't show every extreme that they name: `seg_ids`: numbers never fall along a row and start at 0; segment s of row r covers exactly seg_lengths[r, s] positions. A row holds 1, 2, 4, ... or up to 16 segments; some row holds 16. `seg_lengths`: A row's lengths sum to 2048; slots beyond its segments hold 0; some row is one segment of 2048 positions. owners[m] is a device index in the order of row+seq (row slowest); no device owns more than 4 blocks, and some device owns exactly 4. `bases`: each of a slot's two matrices is orthogonal. `stats`: each of a slot's two matrices is symmetric, with a positive diagonal larger than the sum of magnitudes of its row's other entries. Second moments are positive. `vec_moments`: second moments are positive.
All inputs are finite; a program needn't handle non-finite values.
Results may differ from the reference program's by a relative error of at most 0.013.
Values may be sent and summed in bfloat16 or wider, within the bound.
A program may use at most 576 MiB of HBM per device.

```python
import math
import jax
import jax.numpy as jnp
from jax import lax

D = 768
HEADS = 12
HD = 64
FF = 3072
LEN = 2048
BS = 256
NSEG = 16
ROWS = 8
OWNERS = 32
BLOCKS = 123
OWN_MAX = 4
SLOTS = 128
VROWS = 9


def block_bounds_drawn():
    model_blocks = D // BS
    first_end = model_blocks * model_blocks
    synth_end = first_end + model_blocks * (LEN // BS)
    value_end = synth_end + first_end
    output_end = value_end + first_end
    expand_end = output_end + model_blocks * (FF // BS)
    return (first_end, synth_end, value_end, output_end, expand_end)


def block_scales_drawn():
    first_end, synth_end, value_end, output_end, expand_end = block_bounds_drawn()
    spots = jnp.arange(BLOCKS)
    scales = jnp.where(spots < first_end, D ** (-0.5), jnp.where(spots < synth_end, 3.0 * HD ** (-0.5), jnp.where(spots < value_end, D ** (-0.5), jnp.where(spots < output_end, 4.0 * D ** (-0.5), jnp.where(spots < expand_end, D ** (-0.5), FF ** (-0.5))))))
    return scales.astype(jnp.float32)


def unit_noise(key, shape):
    return jax.random.normal(key, shape, jnp.float32)


def draw_weights(key, part):
    return unit_noise(key, (BLOCKS, BS * BS)) * block_scales_drawn()[:, None]


def draw_vectors(key, part):
    noise = unit_noise(key, (VROWS, D))
    row_index = jnp.arange(VROWS)[:, None]
    gain_rows = (row_index == 0) | (row_index == 2)
    return jnp.where(gain_rows, 1.0 + 0.1 * noise, 0.3 * noise)


def draw_vec_moments(key, part):
    key_first, key_level, key_spread = jax.random.split(key, 3)
    first_moment = 0.16 * jax.random.normal(key_first, (VROWS, D), jnp.float32)
    level = jax.random.uniform(key_level, (VROWS, 1), jnp.float32, 1.0, 4.0)
    spread = jax.random.uniform(key_spread, (VROWS, D), jnp.float32, 0.5, 2.0)
    return jnp.stack([first_moment, 0.48 * level * spread])


def draw_moments(key, part):
    key_first, key_level, key_spread = jax.random.split(key, 3)
    first_moment = 0.053 * jax.random.normal(key_first, (SLOTS, BS, BS), jnp.float32)
    level = jax.random.uniform(key_level, (SLOTS, 1, 1), jnp.float32, 1.0, 4.0)
    spread = jax.random.uniform(key_spread, (SLOTS, BS, BS), jnp.float32, 0.5, 2.0)
    return jnp.stack([first_moment, 0.053 * level * spread], axis=1)


def draw_stats(key, part):
    key_level, key_raw = jax.random.split(key, 2)
    level = 0.2 * BS * jax.random.uniform(key_level, (SLOTS, 2, 1, 1), jnp.float32, 1.0, 4.0)
    raw_part = jax.random.uniform(key_raw, (SLOTS, 2, BS, BS), jnp.float32, -1.0, 1.0)
    symmetric = (raw_part + jnp.swapaxes(raw_part, 2, 3)) * (0.4 / BS)
    diagonal = jnp.arange(BS)[:, None] == jnp.arange(BS)[None, :]
    return level * jnp.where(diagonal, 1.0, symmetric)


def cosine_basis(basis_key):
    key_perm, key_sign = jax.random.split(basis_key, 2)
    sample = jnp.arange(BS, dtype=jnp.float32)[:, None]
    frequency = jax.random.permutation(key_perm, BS).astype(jnp.float32)[None, :]
    table = math.sqrt(2.0 / BS) * jnp.cos(math.pi * (sample + 0.5) * frequency / BS)
    table = jnp.where(frequency == 0, table * math.sqrt(0.5), table)
    signs = (2 * jax.random.randint(key_sign, (BS, 1), 0, 2) - 1).astype(jnp.float32)
    basis = signs * table
    return basis


def draw_bases(key, part):
    basis_keys = jax.random.split(key, SLOTS * 2)
    return jax.vmap(cosine_basis)(basis_keys).reshape(SLOTS, 2, BS, BS)


def segment_layout(key):
    base_key = jax.random.fold_in(key, 11)
    key_count, key_full, key_cuts = jax.random.split(base_key, 3)
    levels = NSEG.bit_length()
    power = jax.random.randint(key_count, (ROWS,), 0, levels)
    cuts = jnp.left_shift(jnp.ones((ROWS,), jnp.int32), power.astype(jnp.int32)) - 1
    full_row = jax.random.randint(key_full, (), 0, ROWS)
    row_index = jnp.arange(ROWS, dtype=jnp.int32)
    cuts = jnp.where(row_index == full_row, 0, cuts)
    cuts = jnp.where(row_index == (full_row + 1) % ROWS, NSEG - 1, cuts)
    row_keys = jax.random.split(key_cuts, ROWS)
    orders = jax.vmap(lambda row_key: jax.random.permutation(row_key, LEN - 1))(row_keys) + 1
    picked = (jnp.arange(LEN - 1)[None, :] < cuts[:, None]).astype(jnp.int32)
    marks = jnp.zeros((ROWS, LEN), jnp.int32).at[row_index[:, None], orders].set(picked)
    seg_ids = jnp.cumsum(marks, axis=1).astype(jnp.int32)
    seg_lengths = jnp.sum((seg_ids[:, :, None] == jnp.arange(NSEG)[None, None, :]).astype(jnp.int32), axis=1)
    return (seg_ids, seg_lengths.astype(jnp.int32))


def draw_seg_ids(key, part):
    return segment_layout(key)[0]


def draw_seg_lengths(key, part):
    return segment_layout(key)[1]


def draw_owners(key, part):
    base_key = jax.random.fold_in(key, 23)
    key_full, key_spread, key_order = jax.random.split(base_key, 3)
    full_owner = jax.random.randint(key_full, (), 0, OWNERS)
    other_slots = jax.random.permutation(key_spread, (OWNERS - 1) * OWN_MAX)[:BLOCKS - OWN_MAX]
    others = other_slots // OWN_MAX
    others = others + (others >= full_owner).astype(jnp.int32)
    listed = jnp.concatenate([jnp.full((OWN_MAX,), full_owner, jnp.int32), others.astype(jnp.int32)])
    block_order = jax.random.permutation(key_order, BLOCKS)
    return jnp.zeros((BLOCKS,), jnp.int32).at[block_order].set(listed)


def level_of(key, dims, shards, low, high):
    factor_of, own = 1.0, jax.random.fold_in(key, 6)
    for axis_at, shards_of in shards:
        draws = jnp.exp(jax.random.uniform(jax.random.fold_in(own, axis_at), (shards_of,), jnp.float32, low / len(shards), high / len(shards)))
        factor_of = factor_of * jnp.repeat(draws, dims[axis_at] // shards_of).reshape([-1 if axis == axis_at else 1 for axis in range(len(dims))])
    return factor_of


def scatter_about(rng, dims, scale, most, cuts=(), held_as=jnp.bfloat16):
    entries = jax.random.normal(rng, dims, jnp.float32) * scale
    if len(cuts) > 0:
        entries = level_of(rng, dims, cuts, -0.22, 0.18) * entries
    return jnp.clip(entries, min=-most, max=most).astype(held_as)


def setup_inputs(seed: int = 0) -> dict:
    key_of = jax.random.split(jax.random.key(seed), 13)
    tokens = scatter_about(key_of[0], (ROWS, LEN, D), 1.0, 6.0, ((0, 8), (1, 4)))
    cotangent = scatter_about(key_of[1], (ROWS, LEN, D), 1.0, 6.0, ((0, 8), (1, 4)))
    seg_ids = draw_seg_ids(jax.random.fold_in(key_of[12], 71), 0)
    seg_lengths = draw_seg_lengths(jax.random.fold_in(key_of[12], 71), 0)
    weights = draw_weights(jax.random.fold_in(key_of[12], 71), 0)
    vectors = draw_vectors(jax.random.fold_in(key_of[12], 71), 0)
    vec_moments = draw_vec_moments(jax.random.fold_in(key_of[12], 71), 0)
    moments = draw_moments(jax.random.fold_in(key_of[12], 71), 0)
    stats = draw_stats(jax.random.fold_in(key_of[12], 71), 0)
    bases = draw_bases(jax.random.fold_in(key_of[12], 71), 0)
    owners = draw_owners(jax.random.fold_in(key_of[12], 71), 0)
    step_count = jax.random.randint(key_of[11], (1,), 2, 21).astype(jnp.int32)
    return {"tokens": tokens, "cotangent": cotangent, "seg_ids": seg_ids, "seg_lengths": seg_lengths, "weights": weights, "vectors": vectors, "vec_moments": vec_moments, "moments": moments, "stats": stats, "bases": bases, "owners": owners, "step_count": step_count}


BETA_MOM = 0.95
BETA_SEC = 0.95
EPSILON = 1e-08
DECAY = 0.01
VECTOR_RATE = 0.3
RATE_FACTOR = 2.0
NORM_EPS = 1e-05
HIGHEST = lax.Precision.HIGHEST

@jax.custom_vjp
def low(v):
    return lax.optimization_barrier(v.astype(jnp.bfloat16)).astype(jnp.float32)

@jax.custom_vjp
def low_back(v):
    return v

def low_keep(v):
    return (low(v), None)

def low_pass(kept, grad):
    return (grad,)

def back_keep(v):
    return (v, None)

def back_low(kept, grad):
    return (low(grad),)
low.defvjp(low_keep, low_pass)
low_back.defvjp(back_keep, back_low)

def block_bounds():
    model_blocks = D // BS
    first_end = model_blocks * model_blocks
    synth_end = first_end + model_blocks * (LEN // BS)
    value_end = synth_end + first_end
    output_end = value_end + first_end
    expand_end = output_end + model_blocks * (FF // BS)
    return (first_end, synth_end, value_end, output_end, expand_end)

def block_scales():
    first_end, synth_end, value_end, output_end, expand_end = block_bounds()
    spots = jnp.arange(BLOCKS)
    scales = jnp.where(spots < first_end, D ** (-0.5), jnp.where(spots < synth_end, 3.0 * HD ** (-0.5), jnp.where(spots < value_end, D ** (-0.5), jnp.where(spots < output_end, 4.0 * D ** (-0.5), jnp.where(spots < expand_end, D ** (-0.5), FF ** (-0.5))))))
    return scales.astype(jnp.float32)

def dense(left, right):
    return jnp.matmul(left, right, precision=HIGHEST)

def matrix_of(blocks, start_block, row_blocks, col_blocks):
    tiles = blocks[start_block:start_block + row_blocks * col_blocks].reshape(row_blocks, col_blocks, BS, BS)
    return tiles.transpose(0, 2, 1, 3).reshape(row_blocks * BS, col_blocks * BS)

def layer_norm(values, gain_row, shift_row):
    centered = values - lax.optimization_barrier(jnp.mean(values, axis=-1, keepdims=True))
    inverse = lax.rsqrt(lax.optimization_barrier(jnp.mean(centered * centered, axis=-1, keepdims=True)) + NORM_EPS)
    return centered * inverse * gain_row + shift_row

def row_forward(row_tokens, row_ids, row_lengths, matrices, vectors):
    first_w, synth_w, value_w, output_w, expand_w, contract_w = matrices
    starts = jnp.cumsum(row_lengths) - row_lengths
    onehot = row_ids[:, None] == jnp.arange(NSEG, dtype=jnp.int32)[None, :]
    query_start = lax.optimization_barrier(jnp.sum(jnp.where(onehot, starts[None, :], 0), axis=1)).astype(jnp.int32)
    query_length = lax.optimization_barrier(jnp.sum(jnp.where(onehot, row_lengths[None, :], 0), axis=1)).astype(jnp.int32)
    first_in = low(layer_norm(row_tokens, vectors[0], vectors[1]))
    first_pre = low_back(dense(first_in, first_w) + vectors[4])
    hidden = low_back(low(jax.nn.silu(first_pre)))
    logits = low_back(jnp.einsum('qhc,hcj->qhj', hidden.reshape(LEN, HEADS, HD), synth_w.reshape(HEADS, HD, LEN), precision=HIGHEST))
    spots = jnp.arange(LEN, dtype=jnp.int32)
    in_segment = (spots[None, :] < query_length[:, None])[:, None, :]
    masked = jnp.where(in_segment, logits, -1e+30)
    row_top = lax.optimization_barrier(jnp.max(masked, axis=2, keepdims=True))
    exp_terms = jnp.where(in_segment, jnp.exp(masked - row_top), 0.0)
    attention = low(exp_terms / lax.optimization_barrier(jnp.sum(exp_terms, axis=2, keepdims=True)))
    values_row = low_back(low(dense(first_in, value_w)))
    gather_index = jnp.clip(spots[None, :] - query_start[:, None], 0, LEN - 1).astype(jnp.int32)[:, None, :]
    after_start = (spots[None, :] >= query_start[:, None])[:, None, :]
    key_weights = jnp.where(after_start, jnp.take_along_axis(attention, gather_index, axis=2), 0.0)
    mixed = jnp.einsum('qhk,khd->qhd', key_weights, values_row.reshape(LEN, HEADS, HD), precision=HIGHEST).reshape(LEN, D)
    mixed = low_back(low(mixed))
    middle = row_tokens + low_back(dense(mixed, output_w))
    second_in = low(layer_norm(middle, vectors[2], vectors[3]))
    expand_pre = low_back(dense(second_in, expand_w) + vectors[5:].reshape(FF))
    expanded = low_back(low(jax.nn.silu(expand_pre)))
    return middle + low_back(dense(expanded, contract_w))

def forward(tokens_f, blocks, vectors, seg_ids, seg_lengths):
    low_blocks = low(blocks)
    first_end, synth_end, value_end, output_end, expand_end = block_bounds()
    model_blocks = D // BS
    matrices = (matrix_of(low_blocks, 0, model_blocks, model_blocks), matrix_of(low_blocks, first_end, model_blocks, LEN // BS), matrix_of(low_blocks, synth_end, model_blocks, model_blocks), matrix_of(low_blocks, value_end, model_blocks, model_blocks), matrix_of(low_blocks, output_end, model_blocks, FF // BS), matrix_of(low_blocks, expand_end, FF // BS, model_blocks))

    def one_row(row_pack):
        return row_forward(row_pack[0], row_pack[1], row_pack[2], matrices, vectors)
    return lax.map(jax.checkpoint(one_row), (tokens_f, seg_ids, seg_lengths))

def orthonormal(matrix):
    gram_matrix = dense(matrix.T, matrix)
    factor = jnp.linalg.cholesky(gram_matrix)
    return jax.scipy.linalg.solve_triangular(factor, matrix.T, lower=True).T

def soap_block(grad_tile, master_tile, moment_pair, stat_pair, basis_pair, rate_value, mom_fix, sec_fix):
    left_basis = basis_pair[0]
    right_basis = basis_pair[1]
    left_stat = BETA_SEC * stat_pair[0] + (1 - BETA_SEC) * dense(grad_tile, grad_tile.T)
    right_stat = BETA_SEC * stat_pair[1] + (1 - BETA_SEC) * dense(grad_tile.T, grad_tile)
    momentum = BETA_MOM * moment_pair[0] + (1 - BETA_MOM) * grad_tile
    turned_grad = dense(dense(left_basis.T, grad_tile), right_basis)
    turned_mom = dense(dense(left_basis.T, momentum), right_basis)
    second = BETA_SEC * moment_pair[1] + (1 - BETA_SEC) * turned_grad * turned_grad
    turned_step = turned_mom / mom_fix / (jnp.sqrt(second / sec_fix) + EPSILON)
    update = dense(dense(left_basis, turned_step), right_basis.T)
    new_master = master_tile - rate_value * (update + DECAY * master_tile)
    new_left = orthonormal(dense(left_stat, left_basis))
    new_right = orthonormal(dense(right_stat, right_basis))
    return (new_master, jnp.stack([momentum, second]), jnp.stack([left_stat, right_stat]), jnp.stack([new_left, new_right]))

def slot_table(owners, own_most, slot_total):
    block_count = owners.shape[0]
    block_index = jnp.arange(block_count, dtype=jnp.int32)
    same_owner = owners[:, None] == owners[None, :]
    earlier = block_index[None, :] < block_index[:, None]
    rank_within = lax.optimization_barrier(jnp.sum(jnp.where(same_owner & earlier, 1, 0), axis=1)).astype(jnp.int32)
    slot_id = (owners * own_most + rank_within).astype(jnp.int32)
    slot_hit = slot_id[:, None] == jnp.arange(slot_total, dtype=jnp.int32)[None, :]
    used = jnp.any(slot_hit, axis=0)
    block_of = lax.optimization_barrier(jnp.sum(jnp.where(slot_hit, block_index[:, None], 0), axis=0)).astype(jnp.int32)
    return (slot_id, used, block_of)

def vector_adam(vectors, vec_moments, grad_rows, mom_fix, sec_fix):
    first_moment = BETA_MOM * vec_moments[0] + (1 - BETA_MOM) * grad_rows
    second = BETA_SEC * vec_moments[1] + (1 - BETA_SEC) * grad_rows * grad_rows
    step_rows = first_moment / mom_fix / (jnp.sqrt(second / sec_fix) + EPSILON)
    return (vectors - VECTOR_RATE * step_rows, jnp.stack([first_moment, second]))

def reference(tokens, cotangent, seg_ids, seg_lengths, weights, vectors, vec_moments, moments, stats, bases, owners, step_count):
    tokens_f = tokens.astype(jnp.float32)

    def wrapped(token_in, block_in, vector_in):
        return forward(token_in, block_in, vector_in, seg_ids, seg_lengths)
    result, pullback = jax.vjp(wrapped, tokens_f, weights, vectors)
    x_grad, block_grad, vector_grad = pullback(cotangent.astype(jnp.float32))
    grad_norm = jnp.sqrt(jnp.sum(block_grad * block_grad) + jnp.sum(vector_grad * vector_grad))
    clip_max = math.sqrt(BLOCKS * BS * BS + VROWS * D)
    scale = jnp.minimum(1.0, clip_max / grad_norm)
    step_value = step_count[0].astype(jnp.float32)
    mom_fix = 1.0 - jnp.power(BETA_MOM, step_value)
    sec_fix = 1.0 - jnp.power(BETA_SEC, step_value)
    new_vectors, new_vec_moments = vector_adam(vectors, vec_moments, vector_grad * scale, mom_fix, sec_fix)
    slot_id, used, block_of = slot_table(owners, OWN_MAX, SLOTS)
    clipped = (block_grad * scale).reshape(BLOCKS, BS, BS)
    masters = weights.reshape(BLOCKS, BS, BS)
    rates = RATE_FACTOR * block_scales()
    slot_grads = jnp.where(used[:, None, None], clipped[block_of], 0.0)
    slot_masters = jnp.where(used[:, None, None], masters[block_of], 0.0)
    slot_rates = rates[block_of]

    def one_slot(slot_pack):
        return soap_block(slot_pack[0], slot_pack[1], slot_pack[2], slot_pack[3], slot_pack[4], slot_pack[5], mom_fix, sec_fix)
    new_master, new_moment, new_stat, new_basis = lax.map(one_slot, (slot_grads, slot_masters, moments, stats, bases, slot_rates))
    keep_slot = used[:, None, None, None]
    new_moments = jnp.where(keep_slot, new_moment, moments)
    new_stats = jnp.where(keep_slot, new_stat, stats)
    new_bases = jnp.where(keep_slot, new_basis, bases)
    new_weights = new_master[slot_id].reshape(BLOCKS, BS * BS)
    return (result.astype(jnp.bfloat16), x_grad, new_weights, new_moments, new_stats, new_bases, new_vectors, new_vec_moments, grad_norm.reshape(1))
```

```python
import math

import jax
import jax.numpy as jnp
from jax import lax
from jax.sharding import PartitionSpec as P

D = 768
HEADS = 12
HD = 64
FF = 3072
LEN = 2048
BS = 256
BLOCKS = 123


BETA_MOM = 0.95
BETA_SEC = 0.95
EPSILON = 1e-08
DECAY = 0.01
VECTOR_RATE = 0.3
RATE_FACTOR = 2.0
NORM_EPS = 1e-05
HIGHEST = lax.Precision.HIGHEST


def block_bounds():
    model_blocks = D // BS
    first_end = model_blocks * model_blocks
    synth_end = first_end + model_blocks * (LEN // BS)
    value_end = synth_end + first_end
    output_end = value_end + first_end
    expand_end = output_end + model_blocks * (FF // BS)
    return (first_end, synth_end, value_end, output_end, expand_end)


def block_scales():
    first_end, synth_end, value_end, output_end, expand_end = block_bounds()
    spots = jnp.arange(BLOCKS)
    scales = jnp.where(
        spots < first_end,
        D ** (-0.5),
        jnp.where(
            spots < synth_end,
            3.0 * HD ** (-0.5),
            jnp.where(
                spots < value_end,
                D ** (-0.5),
                jnp.where(
                    spots < output_end,
                    4.0 * D ** (-0.5),
                    jnp.where(spots < expand_end, D ** (-0.5), FF ** (-0.5)),
                ),
            ),
        ),
    )
    return scales.astype(jnp.float32)


def dense(left, right):
    return jnp.matmul(left, right, precision=HIGHEST)


def silu_slope(values):
    sigma = jax.nn.sigmoid(values)
    return sigma * (1.0 + values * (1.0 - sigma))


def layer_norm(values, gain_row, shift_row):
    centered = values - jnp.mean(values, axis=-1, keepdims=True)
    inverse = lax.rsqrt(jnp.mean(centered * centered, axis=-1, keepdims=True) + NORM_EPS)
    normed = centered * inverse
    return (normed * gain_row + shift_row, normed, inverse)


def norm_back(grad_out, normed, inverse, gain_row):
    scaled = grad_out * gain_row
    return inverse * (
        scaled
        - jnp.mean(scaled, axis=-1, keepdims=True)
        - normed * jnp.mean(scaled * normed, axis=-1, keepdims=True)
    )


def apply_blocks(inputs, matrix):
    token_count = inputs.shape[0]
    row_blocks, col_blocks = (matrix.shape[0], matrix.shape[1])
    result = jnp.einsum(
        "nri,rcij->ncj",
        inputs.reshape(token_count, row_blocks, BS),
        matrix,
        preferred_element_type=jnp.float32,
    )
    return result.reshape(token_count, col_blocks * BS)


def back_blocks(grad_rows, matrix):
    token_count = grad_rows.shape[0]
    row_blocks, col_blocks = (matrix.shape[0], matrix.shape[1])
    result = jnp.einsum(
        "ncj,rcij->nri",
        grad_rows.reshape(token_count, col_blocks, BS),
        matrix,
        preferred_element_type=jnp.float32,
    )
    return result.reshape(token_count, row_blocks * BS)


def grad_blocks(inputs, grad_rows, row_blocks, col_blocks):
    token_count = inputs.shape[0]
    result = jnp.einsum(
        "nri,ncj->rcij",
        inputs.reshape(token_count, row_blocks, BS),
        grad_rows.reshape(token_count, col_blocks, BS),
        preferred_element_type=jnp.float32,
    )
    return result.reshape(row_blocks * col_blocks, BS * BS)


def synth_logits(hidden_group, synth_w):
    group_rows, positions = (hidden_group.shape[0], hidden_group.shape[1])
    model_blocks, length_blocks, per_block = (synth_w.shape[0], synth_w.shape[1], synth_w.shape[2])
    result = jnp.einsum(
        "nrhc,rkhcj->nrhkj",
        hidden_group.reshape(group_rows * positions, model_blocks, per_block, HD),
        synth_w,
        preferred_element_type=jnp.float32,
    )
    return result.reshape(group_rows, positions, HEADS, LEN)


def shift_rows(values, offsets, zeros_first):
    zeros = jnp.zeros(values.shape, values.dtype)
    if zeros_first:
        padded = jnp.concatenate([zeros, values], axis=3)
    else:
        padded = jnp.concatenate([values, zeros], axis=3)

    def take_one(query_row, offset):
        return lax.dynamic_slice_in_dim(query_row, offset, LEN, 1)

    return jax.vmap(jax.vmap(take_one))(padded, offsets)


def to_keys(rel_weights, query_start):
    return shift_rows(rel_weights, LEN - query_start, True)


def to_relative(key_values, query_start, query_length):
    spots = jnp.arange(LEN, dtype=jnp.int32)
    inside = (spots[None, None, :] < query_length[:, :, None])[:, :, None, :]
    return jnp.where(inside, shift_rows(key_values, query_start, False), 0.0)


def softmax_parts(hidden_group, length_group, synth_w):
    logits = synth_logits(hidden_group, synth_w)
    spots = jnp.arange(LEN, dtype=jnp.int32)
    in_segment = (spots[None, None, :] < length_group[:, :, None])[:, :, None, :]
    masked = jnp.where(in_segment, logits, -1e30)
    return (masked, in_segment)


def log_totals(masked, in_segment):
    row_top = jnp.max(masked, axis=3, keepdims=True)
    exp_total = jnp.sum(
        jnp.where(in_segment, jnp.exp(masked - row_top), 0.0), axis=3, keepdims=True
    )
    return row_top + jnp.log(exp_total)


def orthonormal(matrix):
    gram_matrix = dense(matrix.T, matrix)
    factor = jnp.linalg.cholesky(gram_matrix)
    return jax.scipy.linalg.solve_triangular(factor, matrix.T, lower=True).T


def soap_block(
    grad_tile, master_tile, moment_pair, stat_pair, basis_pair, rate_value, mom_fix, sec_fix
):
    left_basis = basis_pair[0]
    right_basis = basis_pair[1]
    left_stat = BETA_SEC * stat_pair[0] + (1 - BETA_SEC) * dense(grad_tile, grad_tile.T)
    right_stat = BETA_SEC * stat_pair[1] + (1 - BETA_SEC) * dense(grad_tile.T, grad_tile)
    momentum = BETA_MOM * moment_pair[0] + (1 - BETA_MOM) * grad_tile
    turned_grad = dense(dense(left_basis.T, grad_tile), right_basis)
    turned_mom = dense(dense(left_basis.T, momentum), right_basis)
    second = BETA_SEC * moment_pair[1] + (1 - BETA_SEC) * turned_grad * turned_grad
    turned_step = turned_mom / mom_fix / (jnp.sqrt(second / sec_fix) + EPSILON)
    update = dense(dense(left_basis, turned_step), right_basis.T)
    new_master = master_tile - rate_value * (update + DECAY * master_tile)
    new_left = orthonormal(dense(left_stat, left_basis))
    new_right = orthonormal(dense(right_stat, right_basis))
    return (
        new_master,
        jnp.stack([momentum, second]),
        jnp.stack([left_stat, right_stat]),
        jnp.stack([new_left, new_right]),
    )


def slot_table(owners, own_most, slot_total):
    block_count = owners.shape[0]
    block_index = jnp.arange(block_count, dtype=jnp.int32)
    same_owner = owners[:, None] == owners[None, :]
    earlier = block_index[None, :] < block_index[:, None]
    rank_within = jnp.sum(jnp.where(same_owner & earlier, 1, 0), axis=1).astype(jnp.int32)
    slot_id = owners * own_most + rank_within
    slot_hit = slot_id[:, None] == jnp.arange(slot_total, dtype=jnp.int32)[None, :]
    used = jnp.any(slot_hit, axis=0)
    block_of = jnp.sum(jnp.where(slot_hit, block_index[:, None], 0), axis=0)
    return (slot_id, used, block_of)


def vector_adam(vectors, vec_moments, grad_rows, mom_fix, sec_fix):
    first_moment = BETA_MOM * vec_moments[0] + (1 - BETA_MOM) * grad_rows
    second = BETA_SEC * vec_moments[1] + (1 - BETA_SEC) * grad_rows * grad_rows
    step_rows = first_moment / mom_fix / (jnp.sqrt(second / sec_fix) + EPSILON)
    return (vectors - VECTOR_RATE * step_rows, jnp.stack([first_moment, second]))


def local(
    tokens,
    cotangent,
    seg_ids,
    seg_lengths,
    weights,
    vectors,
    vec_moments,
    moments,
    stats,
    bases,
    owners,
    step_count,
):
    rows_here, positions, width = tokens.shape
    token_count = rows_here * positions
    owner_count = lax.axis_size("row") * lax.axis_size("seq")
    own_most = moments.shape[0]
    slot_count = owner_count * own_most
    block_count = weights.shape[0]
    piece_size = weights.shape[1]
    model_blocks = D // BS
    hidden_blocks = FF // BS
    length_blocks = LEN // BS
    per_block = BS // HD
    first_end, synth_end, value_end, output_end, expand_end = block_bounds()
    gathered = lax.all_gather(weights.astype(jnp.bfloat16), ("row", "seq"), axis=1, tiled=True)

    def tiles_at(start_block, row_blocks, col_blocks):
        return gathered[start_block : start_block + row_blocks * col_blocks].reshape(
            row_blocks, col_blocks, BS, BS
        )

    first_w = tiles_at(0, model_blocks, model_blocks)
    synth_w = tiles_at(first_end, model_blocks, length_blocks).reshape(
        model_blocks, length_blocks, per_block, HD, BS
    )
    value_w = tiles_at(synth_end, model_blocks, model_blocks)
    output_w = tiles_at(value_end, model_blocks, model_blocks)
    expand_w = tiles_at(output_end, model_blocks, hidden_blocks)
    contract_w = tiles_at(expand_end, hidden_blocks, model_blocks)
    ffn_bias = vectors[5:].reshape(FF)
    slot_range = jnp.arange(seg_lengths.shape[1], dtype=jnp.int32)
    before = slot_range[None, :] < slot_range[:, None]
    starts = jnp.sum(jnp.where(before[None, :, :], seg_lengths[:, None, :], 0), axis=2)
    onehot = seg_ids[:, :, None] == slot_range[None, None, :]
    query_start = jnp.sum(jnp.where(onehot, starts[:, None, :], 0), axis=2)
    query_length = jnp.sum(jnp.where(onehot, seg_lengths[:, None, :], 0), axis=2)
    inputs = tokens.reshape(token_count, width).astype(jnp.float32)
    normed_one, hat_one, inv_one = layer_norm(inputs, vectors[0], vectors[1])
    first_in = normed_one.astype(jnp.bfloat16)
    first_pre = apply_blocks(first_in, first_w) + vectors[4]
    hidden = jax.nn.silu(first_pre).astype(jnp.bfloat16)
    values_local = (
        apply_blocks(first_in, value_w).astype(jnp.bfloat16).reshape(rows_here, positions, width)
    )
    value_rows = lax.all_gather(values_local, "seq", axis=1, tiled=True)
    group_rows = min(rows_here, max(1, 512 // positions))
    group_count = rows_here // group_rows

    def grouped(array):
        return array.reshape((group_count, group_rows) + array.shape[1:])

    hidden_groups = grouped(hidden.reshape(rows_here, positions, width))
    start_groups = grouped(query_start)
    length_groups = grouped(query_length)

    def forward_group(carry_in, group_pack):
        hidden_g, start_g, length_g, values_g = group_pack
        masked, in_segment = softmax_parts(hidden_g, length_g, synth_w)
        log_total = log_totals(masked, in_segment)
        rel_weights = jnp.where(in_segment, jnp.exp(masked - log_total), 0.0).astype(jnp.bfloat16)
        key_weights = to_keys(rel_weights, start_g)
        mixed = jnp.einsum(
            "rqhk,rkhd->rqhd",
            key_weights,
            values_g.reshape(group_rows, LEN, HEADS, HD),
            preferred_element_type=jnp.float32,
        )
        return (carry_in, (mixed.astype(jnp.bfloat16), log_total))

    unused_carry, (mixed_groups, log_groups) = lax.scan(
        forward_group,
        jnp.zeros((), jnp.float32),
        (hidden_groups, start_groups, length_groups, grouped(value_rows)),
    )
    mixed_all = mixed_groups.reshape(token_count, width)
    middle = inputs + apply_blocks(mixed_all, output_w)
    normed_two, hat_two, inv_two = layer_norm(middle, vectors[2], vectors[3])
    second_in = normed_two.astype(jnp.bfloat16)
    expand_pre = apply_blocks(second_in, expand_w) + ffn_bias
    expanded = jax.nn.silu(expand_pre).astype(jnp.bfloat16)
    result = middle + apply_blocks(expanded, contract_w)
    layer_out = result.astype(jnp.bfloat16).reshape(rows_here, positions, width)
    back_out = cotangent.reshape(token_count, width)
    grad_contract = grad_blocks(expanded, back_out, hidden_blocks, model_blocks)
    back_expanded = back_blocks(back_out, contract_w).astype(jnp.bfloat16)
    back_pre = (back_expanded.astype(jnp.float32) * silu_slope(expand_pre)).astype(jnp.bfloat16)
    grad_expand = grad_blocks(second_in, back_pre, model_blocks, hidden_blocks)
    grad_ffn_bias = jnp.sum(back_pre.astype(jnp.float32), axis=0)
    back_normed_two = back_blocks(back_pre, expand_w)
    grad_gain_two = jnp.sum(back_normed_two * hat_two, axis=0)
    grad_shift_two = jnp.sum(back_normed_two, axis=0)
    back_middle = back_out.astype(jnp.float32) + norm_back(
        back_normed_two, hat_two, inv_two, vectors[2]
    )
    back_attn = back_middle.astype(jnp.bfloat16)
    grad_output = grad_blocks(mixed_all, back_attn, model_blocks, model_blocks)
    back_mixed = back_blocks(back_attn, output_w).astype(jnp.bfloat16)

    def backward_group(synth_grad, group_pack):
        hidden_g, start_g, length_g, log_g, back_g, values_g = group_pack
        masked, in_segment = softmax_parts(hidden_g, length_g, synth_w)
        prob_full = jnp.where(in_segment, jnp.exp(masked - log_g), 0.0)
        back_heads = back_g.reshape(group_rows, positions, HEADS, HD)
        back_key = jnp.einsum(
            "rqhd,rkhd->rqhk",
            back_heads,
            values_g.reshape(group_rows, LEN, HEADS, HD),
            preferred_element_type=jnp.float32,
        )
        back_rel = to_relative(back_key, start_g, length_g)
        back_logits = (
            prob_full * (back_rel - jnp.sum(prob_full * back_rel, axis=3, keepdims=True))
        ).astype(jnp.bfloat16)
        flat_hidden = hidden_g.reshape(group_rows * positions, model_blocks, per_block, HD)
        flat_back = back_logits.reshape(
            group_rows * positions, model_blocks, per_block, length_blocks, BS
        )
        synth_grad = synth_grad + jnp.einsum(
            "nrhc,nrhkj->rkhcj", flat_hidden, flat_back, preferred_element_type=jnp.float32
        )
        back_hidden = jnp.einsum(
            "nrhkj,rkhcj->nrhc", flat_back, synth_w, preferred_element_type=jnp.float32
        ).reshape(group_rows, positions, width)
        key_weights = to_keys(prob_full.astype(jnp.bfloat16), start_g)
        value_term = jnp.einsum(
            "rqhk,rqhd->rkhd", key_weights, back_heads, preferred_element_type=jnp.float32
        ).reshape(group_rows, LEN, width)
        return (synth_grad, (back_hidden, value_term))

    synth_start = jnp.zeros((model_blocks, length_blocks, per_block, HD, BS), jnp.float32)
    synth_grad, group_outs = lax.scan(
        backward_group,
        synth_start,
        (
            hidden_groups,
            start_groups,
            length_groups,
            log_groups,
            grouped(back_mixed.reshape(rows_here, positions, width)),
            grouped(value_rows),
        ),
    )
    back_hidden_groups = group_outs[0]
    value_terms = group_outs[1]
    value_sums = lax.psum_scatter(
        value_terms.reshape(rows_here, LEN, width).astype(jnp.bfloat16),
        "seq",
        scatter_dimension=1,
        tiled=True,
    ).astype(jnp.float32)
    back_values = value_sums.reshape(token_count, width).astype(jnp.bfloat16)
    back_hidden = back_hidden_groups.reshape(token_count, width).astype(jnp.bfloat16)
    back_first = (back_hidden.astype(jnp.float32) * silu_slope(first_pre)).astype(jnp.bfloat16)
    grad_first = grad_blocks(first_in, back_first, model_blocks, model_blocks)
    grad_first_bias = jnp.sum(back_first.astype(jnp.float32), axis=0)
    grad_value = grad_blocks(first_in, back_values, model_blocks, model_blocks)
    back_normed_one = back_blocks(back_first, first_w) + back_blocks(back_values, value_w)
    grad_gain_one = jnp.sum(back_normed_one * hat_one, axis=0)
    grad_shift_one = jnp.sum(back_normed_one, axis=0)
    back_inputs = back_middle + norm_back(back_normed_one, hat_one, inv_one, vectors[0])
    x_grad = back_inputs.reshape(rows_here, positions, width)
    local_grads = jnp.concatenate(
        [
            grad_first,
            synth_grad.reshape(model_blocks * length_blocks, BS * BS),
            grad_value,
            grad_output,
            grad_expand,
            grad_contract,
        ],
        axis=0,
    )
    vector_local = jnp.concatenate(
        [
            jnp.stack(
                [grad_gain_one, grad_shift_one, grad_gain_two, grad_shift_two, grad_first_bias]
            ),
            grad_ffn_bias.reshape(FF // D, D),
        ],
        axis=0,
    )
    slot_id, used, block_of = slot_table(owners, own_most, slot_count)
    device_index = lax.axis_index(("row", "seq"))
    mine_used = lax.dynamic_slice_in_dim(used, device_index * own_most, own_most)
    mine_block = lax.dynamic_slice_in_dim(block_of, device_index * own_most, own_most)
    send_master = jnp.where(used[:, None], weights[block_of], 0.0).reshape(
        owner_count, own_most, piece_size
    )
    arranged = jnp.where(used[:, None], local_grads[block_of], 0.0)
    owned_flat = lax.psum_scatter(arranged, ("row", "seq"), scatter_dimension=0, tiled=True)
    squares = jnp.sum(owned_flat * owned_flat)
    owned_grad = owned_flat.reshape(own_most, BS, BS)
    got_master = lax.all_to_all(
        send_master.astype(jnp.bfloat16), ("row", "seq"), split_axis=0, concat_axis=2, tiled=True
    ).astype(send_master.dtype)
    owned_master = got_master.reshape(own_most, BS, BS)
    vector_total, square_total = lax.psum((vector_local, squares), ("row", "seq"))
    grad_norm = jnp.sqrt(square_total + jnp.sum(vector_total * vector_total))
    clip_max = math.sqrt(block_count * BS * BS + vectors.shape[0] * vectors.shape[1])
    scale = jnp.minimum(1.0, clip_max / grad_norm)
    step_value = step_count[0].astype(jnp.float32)
    mom_fix = 1.0 - jnp.power(BETA_MOM, step_value)
    sec_fix = 1.0 - jnp.power(BETA_SEC, step_value)
    new_vectors, new_vec_moments = vector_adam(
        vectors, vec_moments, vector_total * scale, mom_fix, sec_fix
    )
    rate_table = RATE_FACTOR * block_scales()
    slot_rates = jnp.sum(
        jnp.where(
            mine_block[:, None] == jnp.arange(block_count, dtype=jnp.int32)[None, :],
            rate_table[None, :],
            0.0,
        ),
        axis=1,
    )
    new_master, new_moment, new_stat, new_basis = jax.vmap(
        soap_block, in_axes=(0, 0, 0, 0, 0, 0, None, None)
    )(owned_grad * scale, owned_master, moments, stats, bases, slot_rates, mom_fix, sec_fix)
    keep_slot = mine_used[:, None, None, None]
    new_moments = jnp.where(keep_slot, new_moment, moments)
    new_stats = jnp.where(keep_slot, new_stat, stats)
    new_bases = jnp.where(keep_slot, new_basis, bases)
    returned = lax.all_to_all(
        new_master.reshape(1, own_most, BS * BS).astype(jnp.bfloat16),
        ("row", "seq"),
        split_axis=2,
        concat_axis=0,
        tiled=True,
    ).astype(jnp.float32)
    new_weights = returned.reshape(slot_count, piece_size)[slot_id]
    return (
        layer_out,
        x_grad,
        new_weights,
        new_moments,
        new_stats,
        new_bases,
        new_vectors,
        new_vec_moments,
        grad_norm.reshape(1),
    )


def solution(mesh):
    placed = (
        P("row", "seq", None),
        P("row", "seq", None),
        P("row", "seq"),
        P("row", None),
        P(None, ("row", "seq")),
        P(),
        P(),
        P(("row", "seq"), None, None, None),
        P(("row", "seq"), None, None, None),
        P(("row", "seq"), None, None, None),
        P(),
        P(),
    )
    return jax.shard_map(
        local,
        mesh=mesh,
        in_specs=placed,
        out_specs=(
            P("row", "seq", None),
            P("row", "seq", None),
            P(None, ("row", "seq")),
            P(("row", "seq"), None, None, None),
            P(("row", "seq"), None, None, None),
            P(("row", "seq"), None, None, None),
            P(),
            P(),
            P(),
        ),
        check_vma=False,
    )
```

```python
import functools
import math

import jax
import jax.numpy as jnp
from jax import lax
from jax.experimental import pallas as pl
from jax.experimental.pallas import tpu as pltpu
from jax.sharding import PartitionSpec as P

D = 768
HEADS = 12
HD = 64
FF = 3072
LEN = 2048
BS = 256
BLOCKS = 123

BETA_MOM = 0.95
BETA_SEC = 0.95
EPSILON = 1e-08
DECAY = 0.01
VECTOR_RATE = 0.3
RATE_FACTOR = 2.0
NORM_EPS = 1e-05
NEG = -1e30
PANEL = 32
HIGHEST = lax.Precision.HIGHEST
VMEM = pltpu.VMEM
AXES = ("row", "seq")


def dot_nn(a,b): return lax.dot_general(a,b,(((1,),(0,)),((),())),preferred_element_type=jnp.float32)
def dot_nt(a,b): return lax.dot_general(a,b,(((1,),(1,)),((),())),preferred_element_type=jnp.float32)

def tile_rows(positions): return min(positions,256)

def attn_forward_body(tq, tables, hid_ref, synth_ref, value_ref, mixed_ref, lse_ref, f2m, v32, lbuf):
    length = value_ref.shape[0]
    tiles = hid_ref.shape[0] // tq
    blocks = synth_ref.shape[1]
    segs = (tables.shape[0] - 2 * tiles - 1) // 2
    low_rows = lax.broadcasted_iota(jnp.int32, (2 * HD, BS), 0) < HD
    for j in range(blocks):
        tile = synth_ref[0, j]
        zero = jnp.zeros_like(tile)
        f2m[0, j] = jnp.where(low_rows, tile, zero)
        f2m[1, j] = jnp.where(low_rows, zero, tile)
    v32[0:length] = value_ref[...].astype(jnp.float32)
    v32[length:] = jnp.zeros((BS, 2 * HD), jnp.float32)
    left = lax.broadcasted_iota(jnp.int32, (tq, 2 * HD), 1) < HD
    lane = lax.broadcasted_iota(jnp.int32, (1, BS), 1)
    row = lax.broadcasted_iota(jnp.int32, (tq, 1), 0)
    for t in range(tiles):
        hid = hid_ref[t * tq:(t + 1) * tq]
        base = tables[2 * segs + 2 * tiles] + t * tq

        def segment(s, carry):
            start, count = tables[s], tables[segs + s]
            used = (count + BS - 1) // BS

            def scores(j, tops):
                keep = lane < count - j * BS
                out = []
                for h in range(2):
                    part = jnp.where(keep, dot_nn(hid, f2m[h, j]), NEG)
                    lbuf[h, j] = part
                    out.append(jnp.maximum(tops[h], jnp.maximum(part[:, :128], part[:, 128:])))
                return tuple(out)

            none = jnp.full((tq, 128), NEG, jnp.float32)
            tops = lax.fori_loop(0, used, scores, (none, none))
            tops = [jnp.max(top, axis=1, keepdims=True) for top in tops]

            def weigh(j, carried):
                value = v32[pl.ds(start + j * BS, BS), :].astype(jnp.bfloat16)
                out = []
                for h in range(2):
                    total, mix = carried[h]
                    part = jnp.exp(lbuf[h, j] - tops[h])
                    total = total + part[:, :128] + part[:, 128:]
                    mix = mix + dot_nn(part.astype(jnp.bfloat16), value)
                    out.append((total, mix))
                return tuple(out)

            blank = jnp.zeros((tq, 128), jnp.float32)
            pair = lax.fori_loop(0, used, weigh, ((blank, blank), (blank, blank)))
            sums = [jnp.sum(total, axis=1, keepdims=True) for total, _ in pair]
            mix = jnp.where(left, pair[0][1] / sums[0], pair[1][1] / sums[1])
            log = jnp.where(left, tops[0] + jnp.log(sums[0]), tops[1] + jnp.log(sums[1]))
            here = (row + base >= start) & (row + base < start + count)
            rows = pl.ds(t * tq, tq)
            mixed_ref[rows] = jnp.where(here, mix, mixed_ref[rows])
            lse_ref[rows] = jnp.where(here, log, lse_ref[rows])
            return carry

        lax.fori_loop(tables[2 * segs + t], tables[2 * segs + tiles + t], segment, 0)

def attn_forward(tables, hidden, synth, values):
    positions, width = hidden.shape
    length = values.shape[0]
    tq = tile_rows(positions)
    pairs = width // (2 * HD)
    blocks = synth.shape[1]
    per = BS // (2 * HD)
    return pl.pallas_call(
        functools.partial(attn_forward_body, tq),
        name="attn_forward",
        out_shape=(jax.ShapeDtypeStruct((positions, width), jnp.float32),) * 2,
        grid_spec=pltpu.PrefetchScalarGridSpec(
            num_scalar_prefetch=1,
            grid=(pairs,),
            in_specs=[
                pl.BlockSpec((positions, 2 * HD), lambda p, t: (0, p)),
                pl.BlockSpec((1, blocks, 2 * HD, BS), lambda p, t: (p // per, 0, p % per, 0)),
                pl.BlockSpec((length, 2 * HD), lambda p, t: (0, p)),
            ],
            out_specs=[pl.BlockSpec((positions, 2 * HD), lambda p, t: (0, p))] * 2,
            scratch_shapes=[
                pltpu.VMEM((2, blocks, 2 * HD, BS), jnp.bfloat16),
                pltpu.VMEM((length + BS, 2 * HD), jnp.float32),
                pltpu.VMEM((2, blocks, tq, BS), jnp.float32),
            ],
        ),
        compiler_params=pltpu.CompilerParams(vmem_limit_bytes=40 << 20, dimension_semantics=("arbitrary",)),
        cost_estimate=pl.CostEstimate(flops=4 * positions * length * width * 2, bytes_accessed=12 << 20, transcendentals=positions * length * 12),
    )(tables, hidden, synth, values)

def attn_backward_body(tq, tables, hid_ref, synth_ref, value_ref, dmix_ref, mixed_ref, lse_ref,
                       dsynth_ref, dhid_ref, dvalue_ref, f2m, v32, dv32, dmm, dacc):
    length = value_ref.shape[0]
    tiles = hid_ref.shape[0] // tq
    blocks = synth_ref.shape[1]
    segs = (tables.shape[0] - 2 * tiles - 1) // 2
    low_rows = lax.broadcasted_iota(jnp.int32, (2 * HD, BS), 0) < HD
    for j in range(blocks):
        tile = synth_ref[0, j]
        zero = jnp.zeros_like(tile)
        f2m[0, j] = jnp.where(low_rows, tile, zero)
        f2m[1, j] = jnp.where(low_rows, zero, tile)
    v32[0:length] = value_ref[...].astype(jnp.float32)
    v32[length:] = jnp.zeros((BS, 2 * HD), jnp.float32)
    dv32[...] = jnp.zeros_like(dv32)
    dsynth_ref[...] = jnp.zeros_like(dsynth_ref)
    left = lax.broadcasted_iota(jnp.int32, (tq, 2 * HD), 1) < HD
    lane = lax.broadcasted_iota(jnp.int32, (1, BS), 1)
    row = lax.broadcasted_iota(jnp.int32, (tq, 1), 0)
    for t in range(tiles):
        rows = pl.ds(t * tq, tq)
        hid = hid_ref[rows]
        hid_t = hid.astype(jnp.float32).T.astype(jnp.bfloat16)
        dmix32 = dmix_ref[rows].astype(jnp.float32)
        dmix_t = dmix32.T.astype(jnp.bfloat16)
        dot_pair = dmix32 * mixed_ref[rows]
        nil = jnp.zeros_like(dmix32)
        deltas = (
            jnp.sum(jnp.where(left, dot_pair, nil), axis=1, keepdims=True),
            jnp.sum(jnp.where(left, nil, dot_pair), axis=1, keepdims=True),
        )
        dmm[0] = jnp.where(left, dmix32, nil).astype(jnp.bfloat16)
        dmm[1] = jnp.where(left, nil, dmix32).astype(jnp.bfloat16)
        base = tables[2 * segs + 2 * tiles] + t * tq
        logs = lse_ref[rows]
        dacc[...] = jnp.zeros_like(dacc)

        def segment(s, carry):
            start, count = tables[s], tables[segs + s]
            used = (count + BS - 1) // BS
            here = (row + base >= start) & (row + base < start + count)
            lse = [jnp.where(here, logs[:, h * HD:h * HD + 1], -NEG) for h in range(2)]

            def block(j, carry):
                keep = lane < count - j * BS
                value = v32[pl.ds(start + j * BS, BS), :].astype(jnp.bfloat16)
                parts = []
                total = None
                for h in range(2):
                    synth = f2m[h, j]
                    prob = jnp.where(keep, jnp.exp(dot_nn(hid, synth) - lse[h]), 0.0)
                    dprob = dot_nt(dmm[h], value)
                    dlog = (prob * (dprob - deltas[h])).astype(jnp.bfloat16)
                    head = slice(h * HD, (h + 1) * HD)
                    dsynth_ref[0, j, head, :] += dot_nn(hid_t[head], dlog)
                    back = dot_nt(dlog, synth)
                    total = back if total is None else total + back
                    parts.append(dot_nn(dmix_t[head], prob.astype(jnp.bfloat16)))
                dacc[...] += total
                dv32[pl.ds(start + j * BS, BS), :] += jnp.concatenate(parts, axis=0).T
                return carry

            lax.fori_loop(0, used, block, 0)
            return carry

        lax.fori_loop(tables[2 * segs + t], tables[2 * segs + tiles + t], segment, 0)
        dhid_ref[rows] = dacc[...]
    dvalue_ref[...] = dv32[0:length].astype(jnp.bfloat16)

def attn_backward(tables, hidden, synth, values, dmix, mixed, lse):
    positions, width = hidden.shape
    length = values.shape[0]
    tq = tile_rows(positions)
    pairs = width // (2 * HD)
    blocks = synth.shape[1]
    per = BS // (2 * HD)
    tok = pl.BlockSpec((positions, 2 * HD), lambda p, t: (0, p))
    f2 = pl.BlockSpec((1, blocks, 2 * HD, BS), lambda p, t: (p // per, 0, p % per, 0))
    val = pl.BlockSpec((length, 2 * HD), lambda p, t: (0, p))
    return pl.pallas_call(
        functools.partial(attn_backward_body, tq),
        name="attn_backward",
        out_shape=(
            jax.ShapeDtypeStruct(synth.shape, jnp.float32),
            jax.ShapeDtypeStruct((positions, width), jnp.float32),
            jax.ShapeDtypeStruct((length, width), jnp.bfloat16),
        ),
        grid_spec=pltpu.PrefetchScalarGridSpec(
            num_scalar_prefetch=1,
            grid=(pairs,),
            in_specs=[tok, f2, val, tok, tok, tok],
            out_specs=[f2, tok, val],
            scratch_shapes=[
                pltpu.VMEM((2, blocks, 2 * HD, BS), jnp.bfloat16),
                pltpu.VMEM((length + BS, 2 * HD), jnp.float32),
                pltpu.VMEM((length + BS, 2 * HD), jnp.float32),
                pltpu.VMEM((2, tq, 2 * HD), jnp.bfloat16),
                pltpu.VMEM((tq, 2 * HD), jnp.float32),
            ],
        ),
        compiler_params=pltpu.CompilerParams(vmem_limit_bytes=40 << 20, dimension_semantics=("arbitrary",)),
        cost_estimate=pl.CostEstimate(flops=10 * positions * length * width * 2, bytes_accessed=24 << 20, transcendentals=positions * length * 12),
    )(tables, hidden, synth, values, dmix, mixed, lse)


def exact(a, b, da=1, db=0):
    return lax.dot_general(a, b, (((da,), (db,)), ((), ())), precision=HIGHEST, preferred_element_type=jnp.float32)

def soap_body(ints, floats, grad_ref, one_ref, two_ref, moment_ref, stat_ref, basis_ref,
              new_master_ref, new_moment_ref, new_stat_ref, new_basis_ref, wide, master_ref, sems):
    slots = grad_ref.shape[0]
    split = one_ref.shape[0]

    def master_copy(k, source):
        return pltpu.make_async_copy(source, master_ref.at[k], sems.at[k])

    for k in range(slots):
        block = ints[slots + k]

        @pl.when(block < split)
        def _():
            master_copy(k, one_ref.at[block]).start()

        @pl.when(block >= split)
        def _():
            master_copy(k, two_ref.at[block - split]).start()

    for k in range(slots):
        master_copy(k, one_ref.at[0]).wait()
    scale, mom_fix, sec_fix = floats[0], floats[1], floats[2]

    def prepare(k, carry):
        used = ints[k] > 0
        grad = jnp.where(used, grad_ref[k].astype(jnp.float32) * scale, 0.0)
        left, right = basis_ref[k, 0], basis_ref[k, 1]
        old_left, old_right = stat_ref[k, 0], stat_ref[k, 1]
        left_stat = BETA_SEC * old_left + (1 - BETA_SEC) * exact(grad, grad, 1, 1)
        right_stat = BETA_SEC * old_right + (1 - BETA_SEC) * exact(grad, grad, 0, 0)
        new_stat_ref[k, 0] = jnp.where(used, left_stat, old_left)
        new_stat_ref[k, 1] = jnp.where(used, right_stat, old_right)
        left_t = left.T
        for side, (turn, stat) in enumerate(((left_t, left_stat), (right.T, right_stat))):
            cross = exact(turn, stat)
            wide[2 * k + side, :, 0:BS] = exact(cross, cross, 1, 1)
            wide[2 * k + side, :, BS:] = cross
        momentum = BETA_MOM * moment_ref[k, 0] + (1 - BETA_MOM) * grad
        turned_grad = exact(exact(left_t, grad), right)
        turned_mom = exact(exact(left_t, momentum), right)
        old_second = moment_ref[k, 1]
        second = BETA_SEC * old_second + (1 - BETA_SEC) * turned_grad * turned_grad
        step = turned_mom / mom_fix / (jnp.sqrt(second / sec_fix) + EPSILON)
        update = exact(exact(left, step), right, 1, 1)
        master = master_ref[k].astype(jnp.float32)
        new_master_ref[k] = (master - floats[3 + k] * (update + DECAY * master)).astype(jnp.bfloat16)
        new_moment_ref[k, 0] = jnp.where(used, momentum, moment_ref[k, 0])
        new_moment_ref[k, 1] = jnp.where(used, second, old_second)
        return carry

    lax.fori_loop(0, slots, prepare, 0)

    count = 2 * slots
    group = 128 // PANEL
    groups = count // group
    row = lax.broadcasted_iota(jnp.int32, (PANEL, 128), 0)
    lane = lax.broadcasted_iota(jnp.int32, (PANEL, 128), 1)
    unit = jnp.where(row == lane % PANEL, 1.0, 0.0)
    spot = lane // PANEL * PANEL
    for p in range(BS // PANEL):
        low = p * PANEL
        rows = slice(low, low + PANEL)
        schur, inverse, pivots = [], [], []
        for q in range(groups):
            schur.append(jnp.concatenate([wide[q * group + i, rows, low:low + PANEL] for i in range(group)], axis=1))
            inverse.append(unit)
            pivots.append(unit)

        for k in range(PANEL):
            below = row > k
            for q in range(groups):
                a, b = schur[q], inverse[q]
                column = jnp.take_along_axis(a, spot + k, axis=1)
                pivot = jnp.take_along_axis(jnp.broadcast_to(a[k:k + 1], (8, 128)), spot[:8] + k, axis=1)[0:1]
                factor = jnp.where(below, column * (1.0 / pivot), 0.0)
                schur[q] = a - factor * a[k:k + 1]
                inverse[q] = b - factor * b[k:k + 1]
                pivots[q] = jnp.where(row == k, pivot, pivots[q])
        for q in range(groups):
            whole = inverse[q] * lax.rsqrt(pivots[q])
            for i in range(group):
                m = q * group + i
                part = exact(whole[:, i * PANEL:(i + 1) * PANEL], wide[m, rows, :])
                wide[m, rows, :] = part
                if low + PANEL < BS:
                    wide[m, low + PANEL:, :] -= exact(part[:, low + PANEL:BS], part, 0, 0)

    def finish(k, carry):
        used = ints[k] > 0
        for side in range(2):
            new_basis_ref[k, side] = jnp.where(used, wide[2 * k + side, :, BS:].T, basis_ref[k, side])
        return carry

    lax.fori_loop(0, slots, finish, 0)

def soap_step(ints, floats, grads, one, two, moments, stats, bases):
    slots = grads.shape[0]
    whole = pl.BlockSpec(memory_space=VMEM)
    scalar = pl.BlockSpec(memory_space=pltpu.SMEM)
    anywhere = pl.BlockSpec(memory_space=pl.ANY)
    pair = jax.ShapeDtypeStruct(moments.shape, jnp.float32)
    return pl.pallas_call(
        soap_body,
        name="soap_step",
        out_shape=(jax.ShapeDtypeStruct(grads.shape, jnp.bfloat16), pair, pair, pair),
        in_specs=[scalar, scalar, whole, anywhere, anywhere] + [whole] * 3,
        out_specs=[whole] * 4,
        scratch_shapes=[
            VMEM((2 * slots, BS, 2 * BS), jnp.float32),
            VMEM((slots, BS, BS), jnp.bfloat16),
            pltpu.SemaphoreType.DMA((slots,)),
        ],
        compiler_params=pltpu.CompilerParams(vmem_limit_bytes=48 << 20),
        cost_estimate=pl.CostEstimate(flops=slots * 16 * 6 * 2 * BS ** 3, bytes_accessed=slots * 14 * 4 * BS * BS, transcendentals=slots * BS * BS),
    )(ints, floats, grads, one, two, moments, stats, bases)


def spread_pieces_body(split, weight_ref, one_ref, two_ref, lay):
    for i in range(one_ref.shape[1]):
        lay[:, i, :] = weight_ref[:, i * BS:(i + 1) * BS]
    one_ref[...] = lay[:split].astype(jnp.bfloat16)
    two_ref[...] = lay[split:].astype(jnp.bfloat16)


def spread_pieces(weights, split):
    count, rows = weights.shape[0], weights.shape[1] // BS
    whole = pl.BlockSpec(memory_space=VMEM)
    return pl.pallas_call(
        functools.partial(spread_pieces_body, split),
        name="spread_pieces",
        out_shape=(
            jax.ShapeDtypeStruct((split, rows, BS), jnp.bfloat16),
            jax.ShapeDtypeStruct((count - split, rows, BS), jnp.bfloat16),
        ),
        in_specs=[whole],
        out_specs=[whole] * 2,
        scratch_shapes=[VMEM((count, rows, BS), jnp.float32)],
        compiler_params=pltpu.CompilerParams(vmem_limit_bytes=32 << 20),
    )(weights)


def arrange_body(block_of, late_ref, early_ref, out_ref, square_ref):
    split, rows = late_ref.shape[0], late_ref.shape[1]

    def place(s, carry):
        block = block_of[s]
        low = late_ref[jnp.minimum(block, split - 1)]
        high = early_ref[jnp.maximum(block - split, 0)]
        out_ref[s] = jnp.where(block < split, low, high)
        return carry

    lax.fori_loop(0, out_ref.shape[0], place, 0)

    def add(ref):
        def step(m, total):
            part = ref[m].astype(jnp.float32)
            return total + part * part

        return lambda total: lax.fori_loop(0, ref.shape[0], step, total)

    total = add(early_ref)(add(late_ref)(jnp.zeros((rows, BS), jnp.float32)))
    square_ref[...] = total


def arrange(block_of, late, early):
    rows = late.shape[1]
    whole = pl.BlockSpec(memory_space=VMEM)
    return pl.pallas_call(
        arrange_body,
        name="arrange",
        out_shape=(
            jax.ShapeDtypeStruct((block_of.shape[0], rows, BS), jnp.bfloat16),
            jax.ShapeDtypeStruct((rows, BS), jnp.float32),
        ),
        in_specs=[pl.BlockSpec(memory_space=pltpu.SMEM), whole, whole],
        out_specs=[whole] * 2,
        compiler_params=pltpu.CompilerParams(vmem_limit_bytes=32 << 20),
    )(block_of, late, early)


def collect_body(slot_id, piece_ref, out_ref):
    rows = piece_ref.shape[1]

    def place(m, carry):
        piece = piece_ref[slot_id[m]].astype(jnp.float32)
        for i in range(rows):
            out_ref[pl.ds(m, 1), i * BS:(i + 1) * BS] = piece[i:i + 1]
        return carry

    lax.fori_loop(0, out_ref.shape[0], place, 0)


def collect(slot_id, pieces):
    count, rows = slot_id.shape[0], pieces.shape[1]
    whole = pl.BlockSpec(memory_space=VMEM)
    return pl.pallas_call(
        collect_body,
        name="collect",
        out_shape=jax.ShapeDtypeStruct((count, rows * BS), jnp.float32),
        in_specs=[pl.BlockSpec(memory_space=pltpu.SMEM), whole],
        out_specs=whole,
        compiler_params=pltpu.CompilerParams(vmem_limit_bytes=32 << 20),
    )(slot_id, pieces)


def block_bounds():
    model_blocks = D // BS
    first_end = model_blocks * model_blocks
    synth_end = first_end + model_blocks * (LEN // BS)
    value_end = synth_end + first_end
    output_end = value_end + first_end
    expand_end = output_end + model_blocks * (FF // BS)
    return (first_end, synth_end, value_end, output_end, expand_end)


def block_scales():
    first_end, synth_end, value_end, output_end, expand_end = block_bounds()
    spots = jnp.arange(BLOCKS)
    scales = jnp.where(
        spots < first_end,
        D ** (-0.5),
        jnp.where(
            spots < synth_end,
            3.0 * HD ** (-0.5),
            jnp.where(
                spots < value_end,
                D ** (-0.5),
                jnp.where(
                    spots < output_end,
                    4.0 * D ** (-0.5),
                    jnp.where(spots < expand_end, D ** (-0.5), FF ** (-0.5)),
                ),
            ),
        ),
    )
    return scales.astype(jnp.float32)


def silu_slope(values):
    sigma = jax.nn.sigmoid(values)
    return sigma * (1.0 + values * (1.0 - sigma))


def layer_norm(values, gain_row, shift_row):
    centered = values - jnp.mean(values, axis=-1, keepdims=True)
    inverse = lax.rsqrt(jnp.mean(centered * centered, axis=-1, keepdims=True) + NORM_EPS)
    normed = centered * inverse
    return (normed * gain_row + shift_row, normed, inverse)


def norm_back(grad_out, normed, inverse, gain_row):
    scaled = grad_out * gain_row
    return inverse * (
        scaled
        - jnp.mean(scaled, axis=-1, keepdims=True)
        - normed * jnp.mean(scaled * normed, axis=-1, keepdims=True)
    )


def apply_blocks(inputs, matrix):
    token_count = inputs.shape[0]
    row_blocks, col_blocks = (matrix.shape[0], matrix.shape[1])
    result = jnp.einsum(
        "nri,rcij->ncj",
        inputs.reshape(token_count, row_blocks, BS),
        matrix,
        preferred_element_type=jnp.float32,
    )
    return result.reshape(token_count, col_blocks * BS)


def back_blocks(grad_rows, matrix):
    token_count = grad_rows.shape[0]
    row_blocks, col_blocks = (matrix.shape[0], matrix.shape[1])
    result = jnp.einsum(
        "ncj,rcij->nri",
        grad_rows.reshape(token_count, col_blocks, BS),
        matrix,
        preferred_element_type=jnp.float32,
    )
    return result.reshape(token_count, row_blocks * BS)


def grad_blocks(inputs, grad_rows, row_blocks, col_blocks):
    token_count = inputs.shape[0]
    result = jnp.einsum(
        "nri,ncj->rcij",
        inputs.reshape(token_count, row_blocks, BS),
        grad_rows.reshape(token_count, col_blocks, BS),
        preferred_element_type=jnp.float32,
    )
    return result.reshape(row_blocks * col_blocks, BS, BS).astype(jnp.bfloat16)


def slot_table(owners, own_most, slot_total):
    block_count = owners.shape[0]
    block_index = jnp.arange(block_count, dtype=jnp.int32)
    same_owner = owners[:, None] == owners[None, :]
    earlier = block_index[None, :] < block_index[:, None]
    rank_within = jnp.sum(jnp.where(same_owner & earlier, 1, 0), axis=1).astype(jnp.int32)
    slot_id = owners * own_most + rank_within
    slot_hit = slot_id[:, None] == jnp.arange(slot_total, dtype=jnp.int32)[None, :]
    used = jnp.any(slot_hit, axis=0)
    block_of = jnp.sum(jnp.where(slot_hit, block_index[:, None], 0), axis=0)
    return (slot_id, used, block_of)


def vector_adam(vectors, vec_moments, grad_rows, mom_fix, sec_fix):
    first_moment = BETA_MOM * vec_moments[0] + (1 - BETA_MOM) * grad_rows
    second = BETA_SEC * vec_moments[1] + (1 - BETA_SEC) * grad_rows * grad_rows
    step_rows = first_moment / mom_fix / (jnp.sqrt(second / sec_fix) + EPSILON)
    return (vectors - VECTOR_RATE * step_rows, jnp.stack([first_moment, second]))


def scatter_sum(terms):
    part = lax.psum_scatter(terms, "row", scatter_dimension=1, tiled=True)
    return lax.psum_scatter(part, "seq", scatter_dimension=1, tiled=True)


def local(
    tokens,
    cotangent,
    seg_ids,
    seg_lengths,
    weights,
    vectors,
    vec_moments,
    moments,
    stats,
    bases,
    owners,
    step_count,
):
    rows_here, positions, width = tokens.shape
    owner_count = lax.axis_size("row") * lax.axis_size("seq")
    own_most = moments.shape[0]
    slot_count = owner_count * own_most
    block_count = weights.shape[0]
    piece_rows = weights.shape[1] // BS
    model_blocks = D // BS
    hidden_blocks = FF // BS
    length_blocks = LEN // BS
    first_end, synth_end, value_end, output_end, expand_end = block_bounds()
    pieces_one, pieces_two = spread_pieces(weights, value_end)
    gathered_one = lax.all_gather(pieces_one, AXES, axis=1, tiled=True)
    gathered_two = lax.all_gather(pieces_two, AXES, axis=1, tiled=True)
    token_row = lax.all_gather(tokens, "seq", axis=1, tiled=True).reshape(LEN, width)

    def tiles_at(start_block, row_blocks, col_blocks):
        if start_block < value_end:
            part = gathered_one[start_block : start_block + row_blocks * col_blocks]
        else:
            start_block = start_block - value_end
            part = gathered_two[start_block : start_block + row_blocks * col_blocks]
        return part.reshape(row_blocks, col_blocks, BS, BS)

    first_w = tiles_at(0, model_blocks, model_blocks)
    synth_w = tiles_at(first_end, model_blocks, length_blocks)
    value_w = tiles_at(synth_end, model_blocks, model_blocks)
    output_w = tiles_at(value_end, model_blocks, model_blocks)
    expand_w = tiles_at(output_end, model_blocks, hidden_blocks)
    contract_w = tiles_at(expand_end, hidden_blocks, model_blocks)
    ffn_bias = vectors[5:].reshape(FF)

    slot_range = jnp.arange(seg_lengths.shape[1], dtype=jnp.int32)
    before = slot_range[None, :] < slot_range[:, None]
    starts = jnp.sum(jnp.where(before, seg_lengths[0][None, :], 0), axis=1)
    tq = tile_rows(positions)
    tile_ids = seg_ids[0].reshape(positions // tq, tq)
    offset = lax.axis_index("seq") * positions
    tables = jnp.concatenate(
        [
            starts,
            seg_lengths[0],
            tile_ids[:, 0],
            tile_ids[:, tq - 1] + 1,
            jnp.full((1,), offset, jnp.int32),
        ]
    ).astype(jnp.int32)

    inputs = tokens.reshape(positions, width).astype(jnp.float32)
    normed_one, hat_one, inv_one = layer_norm(inputs, vectors[0], vectors[1])
    first_in = normed_one.astype(jnp.bfloat16)
    first_pre = apply_blocks(first_in, first_w) + vectors[4]
    hidden = jax.nn.silu(first_pre).astype(jnp.bfloat16)
    normed_row, hat_row, _ = layer_norm(token_row.astype(jnp.float32), vectors[0], vectors[1])
    row_in = normed_row.astype(jnp.bfloat16)
    values = apply_blocks(row_in, value_w).astype(jnp.bfloat16)

    mixed_wide, log_total = attn_forward(tables, hidden, synth_w, values)
    mixed = mixed_wide.astype(jnp.bfloat16)
    middle = inputs + apply_blocks(mixed, output_w)
    normed_two, hat_two, inv_two = layer_norm(middle, vectors[2], vectors[3])
    second_in = normed_two.astype(jnp.bfloat16)
    expand_pre = apply_blocks(second_in, expand_w) + ffn_bias
    expanded = jax.nn.silu(expand_pre).astype(jnp.bfloat16)
    result = middle + apply_blocks(expanded, contract_w)
    layer_out = result.astype(jnp.bfloat16).reshape(rows_here, positions, width)
    back_out = cotangent.reshape(positions, width)
    grad_contract = grad_blocks(expanded, back_out, hidden_blocks, model_blocks)
    back_expanded = back_blocks(back_out, contract_w).astype(jnp.bfloat16)
    back_pre = (back_expanded.astype(jnp.float32) * silu_slope(expand_pre)).astype(jnp.bfloat16)
    grad_expand = grad_blocks(second_in, back_pre, model_blocks, hidden_blocks)
    grad_ffn_bias = jnp.sum(back_pre.astype(jnp.float32), axis=0)
    back_normed_two = back_blocks(back_pre, expand_w)
    grad_gain_two = jnp.sum(back_normed_two * hat_two, axis=0)
    grad_shift_two = jnp.sum(back_normed_two, axis=0)
    back_middle = back_out.astype(jnp.float32) + norm_back(
        back_normed_two, hat_two, inv_two, vectors[2]
    )
    back_attn = back_middle.astype(jnp.bfloat16)
    grad_output = grad_blocks(mixed, back_attn, model_blocks, model_blocks)
    back_mixed = back_blocks(back_attn, output_w).astype(jnp.bfloat16)
    early = scatter_sum(jnp.concatenate([grad_output, grad_expand, grad_contract], axis=0))

    synth_grad, back_hidden, value_terms = attn_backward(
        tables, hidden, synth_w, values, back_mixed, mixed_wide, log_total
    )
    back_hidden = back_hidden.astype(jnp.bfloat16)
    back_first = (back_hidden.astype(jnp.float32) * silu_slope(first_pre)).astype(jnp.bfloat16)
    grad_first = grad_blocks(first_in, back_first, model_blocks, model_blocks)
    grad_first_bias = jnp.sum(back_first.astype(jnp.float32), axis=0)
    grad_value = grad_blocks(row_in, value_terms, model_blocks, model_blocks)
    synth_grad = synth_grad.reshape(model_blocks * length_blocks, BS, BS).astype(jnp.bfloat16)
    late = scatter_sum(jnp.concatenate([grad_first, synth_grad, grad_value], axis=0))
    back_from_first = back_blocks(back_first, first_w)
    back_from_value = back_blocks(value_terms, value_w)
    grad_gain_one = jnp.sum(back_from_first * hat_one, axis=0) + jnp.sum(
        back_from_value * hat_row, axis=0
    )
    grad_shift_one = jnp.sum(back_from_first, axis=0) + jnp.sum(back_from_value, axis=0)
    value_sums = lax.psum_scatter(value_terms, "seq", scatter_dimension=0, tiled=True)
    back_normed_one = back_from_first + back_blocks(value_sums, value_w)
    back_inputs = back_middle + norm_back(back_normed_one, hat_one, inv_one, vectors[0])
    x_grad = back_inputs.reshape(rows_here, positions, width)

    vector_local = jnp.concatenate(
        [
            jnp.stack(
                [grad_gain_one, grad_shift_one, grad_gain_two, grad_shift_two, grad_first_bias]
            ),
            grad_ffn_bias.reshape(FF // D, D),
        ],
        axis=0,
    )
    slot_id, used, block_of = slot_table(owners, own_most, slot_count)
    device_index = lax.axis_index(AXES)
    mine_used = lax.dynamic_slice_in_dim(used, device_index * own_most, own_most)
    mine_block = lax.dynamic_slice_in_dim(block_of, device_index * own_most, own_most)
    arranged, square_rows = arrange(block_of, late, early)
    squares = jnp.sum(square_rows)
    arranged = arranged.reshape(owner_count, own_most, piece_rows, BS)
    owned_grad = lax.all_to_all(arranged, AXES, split_axis=0, concat_axis=2, tiled=True)
    owned_grad = owned_grad.reshape(own_most, BS, BS)
    vector_total, square_total = lax.psum((vector_local, squares), AXES)
    grad_norm = jnp.sqrt(square_total + jnp.sum(vector_total * vector_total))
    clip_max = math.sqrt(block_count * BS * BS + vectors.shape[0] * vectors.shape[1])
    scale = jnp.minimum(1.0, clip_max / grad_norm)
    step_value = step_count[0].astype(jnp.float32)
    mom_fix = 1.0 - jnp.power(BETA_MOM, step_value)
    sec_fix = 1.0 - jnp.power(BETA_SEC, step_value)
    new_vectors, new_vec_moments = vector_adam(
        vectors, vec_moments, vector_total * scale, mom_fix, sec_fix
    )
    rate_table = RATE_FACTOR * block_scales()
    slot_rates = jnp.sum(
        jnp.where(
            mine_block[:, None] == jnp.arange(block_count, dtype=jnp.int32)[None, :],
            rate_table[None, :],
            0.0,
        ),
        axis=1,
    )
    floats = jnp.concatenate([jnp.stack([scale, mom_fix, sec_fix]), slot_rates])
    ints = jnp.concatenate([mine_used.astype(jnp.int32), mine_block])
    new_master, new_moments, new_stats, new_bases = soap_step(
        ints, floats, owned_grad, gathered_one, gathered_two, moments, stats, bases
    )
    returned = lax.all_to_all(
        new_master.reshape(1, own_most, BS, BS), AXES, split_axis=2, concat_axis=0, tiled=True
    )
    new_weights = collect(slot_id, returned.reshape(slot_count, piece_rows, BS))
    return (
        layer_out,
        x_grad,
        new_weights,
        new_moments,
        new_stats,
        new_bases,
        new_vectors,
        new_vec_moments,
        grad_norm.reshape(1),
    )


def solution(mesh):
    placed = (
        P("row", "seq", None),
        P("row", "seq", None),
        P("row", "seq"),
        P("row", None),
        P(None, ("row", "seq")),
        P(),
        P(),
        P(("row", "seq"), None, None, None),
        P(("row", "seq"), None, None, None),
        P(("row", "seq"), None, None, None),
        P(),
        P(),
    )
    return jax.shard_map(
        local,
        mesh=mesh,
        in_specs=placed,
        out_specs=(
            P("row", "seq", None),
            P("row", "seq", None),
            P(None, ("row", "seq")),
            P(("row", "seq"), None, None, None),
            P(("row", "seq"), None, None, None),
            P(("row", "seq"), None, None, None),
            P(),
            P(),
            P(),
        ),
        check_vma=False,
    )
```

```python
import functools
import math

import jax
import jax.numpy as jnp
from jax import lax
from jax.experimental import pallas as pl
from jax.experimental.pallas import tpu as pltpu
from jax.sharding import PartitionSpec as P

D = 768
HEADS = 12
HD = 64
FF = 3072
LEN = 2048
BS = 256
BLOCKS = 123

BETA_MOM = 0.95
BETA_SEC = 0.95
EPSILON = 1e-08
DECAY = 0.01
VECTOR_RATE = 0.3
RATE_FACTOR = 2.0
NORM_EPS = 1e-05
NEG = -1e30
PANEL = 32
HIGHEST = lax.Precision.HIGHEST
VMEM = pltpu.VMEM
AXES = ("row", "seq")
MESH = pl.DeviceIdType.MESH


def dot_nn(a,b): return lax.dot_general(a,b,(((1,),(0,)),((),())),preferred_element_type=jnp.float32)
def dot_nt(a,b): return lax.dot_general(a,b,(((1,),(1,)),((),())),preferred_element_type=jnp.float32)

def tile_rows(positions): return min(positions,256)

def attn_forward_body(tq, tables, hid_ref, synth_ref, value_ref, mixed_ref, lse_ref, f2m, v32, lbuf):
    length = value_ref.shape[0]
    tiles = hid_ref.shape[0] // tq
    blocks = synth_ref.shape[1]
    segs = (tables.shape[0] - 2 * tiles - 1) // 2
    low_rows = lax.broadcasted_iota(jnp.int32, (2 * HD, BS), 0) < HD
    for j in range(blocks):
        tile = synth_ref[0, j]
        zero = jnp.zeros_like(tile)
        f2m[0, j] = jnp.where(low_rows, tile, zero)
        f2m[1, j] = jnp.where(low_rows, zero, tile)
    v32[0:length] = value_ref[...].astype(jnp.float32)
    v32[length:] = jnp.zeros((BS, 2 * HD), jnp.float32)
    left = lax.broadcasted_iota(jnp.int32, (tq, 2 * HD), 1) < HD
    lane = lax.broadcasted_iota(jnp.int32, (1, BS), 1)
    row = lax.broadcasted_iota(jnp.int32, (tq, 1), 0)
    for t in range(tiles):
        hid = hid_ref[t * tq:(t + 1) * tq]
        base = tables[2 * segs + 2 * tiles] + t * tq

        def segment(s, carry):
            start, count = tables[s], tables[segs + s]
            used = (count + BS - 1) // BS

            def scores(j, tops):
                keep = lane < count - j * BS
                out = []
                for h in range(2):
                    part = jnp.where(keep, dot_nn(hid, f2m[h, j]), NEG)
                    lbuf[h, j] = part
                    out.append(jnp.maximum(tops[h], jnp.maximum(part[:, :128], part[:, 128:])))
                return tuple(out)

            none = jnp.full((tq, 128), NEG, jnp.float32)
            tops = lax.fori_loop(0, used, scores, (none, none))
            tops = [jnp.max(top, axis=1, keepdims=True) for top in tops]

            def weigh(j, carried):
                value = v32[pl.ds(start + j * BS, BS), :].astype(jnp.bfloat16)
                out = []
                for h in range(2):
                    total, mix = carried[h]
                    part = jnp.exp(lbuf[h, j] - tops[h])
                    total = total + part[:, :128] + part[:, 128:]
                    mix = mix + dot_nn(part.astype(jnp.bfloat16), value)
                    out.append((total, mix))
                return tuple(out)

            blank = jnp.zeros((tq, 128), jnp.float32)
            pair = lax.fori_loop(0, used, weigh, ((blank, blank), (blank, blank)))
            sums = [jnp.sum(total, axis=1, keepdims=True) for total, _ in pair]
            mix = jnp.where(left, pair[0][1] / sums[0], pair[1][1] / sums[1])
            log = jnp.where(left, tops[0] + jnp.log(sums[0]), tops[1] + jnp.log(sums[1]))
            here = (row + base >= start) & (row + base < start + count)
            rows = pl.ds(t * tq, tq)
            mixed_ref[rows] = jnp.where(here, mix, mixed_ref[rows])
            lse_ref[rows] = jnp.where(here, log, lse_ref[rows])
            return carry

        lax.fori_loop(tables[2 * segs + t], tables[2 * segs + tiles + t], segment, 0)

def attn_forward(tables, hidden, synth, values):
    positions, width = hidden.shape
    length = values.shape[0]
    tq = tile_rows(positions)
    pairs = width // (2 * HD)
    blocks = synth.shape[1]
    per = BS // (2 * HD)
    return pl.pallas_call(
        functools.partial(attn_forward_body, tq),
        name="attn_forward",
        out_shape=(jax.ShapeDtypeStruct((positions, width), jnp.float32),) * 2,
        grid_spec=pltpu.PrefetchScalarGridSpec(
            num_scalar_prefetch=1,
            grid=(pairs,),
            in_specs=[
                pl.BlockSpec((positions, 2 * HD), lambda p, t: (0, p)),
                pl.BlockSpec((1, blocks, 2 * HD, BS), lambda p, t: (p // per, 0, p % per, 0)),
                pl.BlockSpec((length, 2 * HD), lambda p, t: (0, p)),
            ],
            out_specs=[pl.BlockSpec((positions, 2 * HD), lambda p, t: (0, p))] * 2,
            scratch_shapes=[
                pltpu.VMEM((2, blocks, 2 * HD, BS), jnp.bfloat16),
                pltpu.VMEM((length + BS, 2 * HD), jnp.float32),
                pltpu.VMEM((2, blocks, tq, BS), jnp.float32),
            ],
        ),
        compiler_params=pltpu.CompilerParams(vmem_limit_bytes=40 << 20, dimension_semantics=("arbitrary",)),
        cost_estimate=pl.CostEstimate(flops=4 * positions * length * width * 2, bytes_accessed=12 << 20, transcendentals=positions * length * 12),
    )(tables, hidden, synth, values)

def attn_backward_body(tq, tables, hid_ref, synth_ref, value_ref, dmix_ref, mixed_ref, lse_ref,
                       dsynth_ref, dhid_ref, dvalue_ref, f2m, v32, dv32, dmm, dacc, df2):
    length = value_ref.shape[0]
    tiles = hid_ref.shape[0] // tq
    blocks = synth_ref.shape[1]
    segs = (tables.shape[0] - 2 * tiles - 1) // 2
    low_rows = lax.broadcasted_iota(jnp.int32, (2 * HD, BS), 0) < HD
    for j in range(blocks):
        tile = synth_ref[0, j]
        zero = jnp.zeros_like(tile)
        f2m[0, j] = jnp.where(low_rows, tile, zero)
        f2m[1, j] = jnp.where(low_rows, zero, tile)
    v32[0:length] = value_ref[...].astype(jnp.float32)
    v32[length:] = jnp.zeros((BS, 2 * HD), jnp.float32)
    dv32[...] = jnp.zeros_like(dv32)
    df2[...] = jnp.zeros_like(df2)
    left = lax.broadcasted_iota(jnp.int32, (tq, 2 * HD), 1) < HD
    lane = lax.broadcasted_iota(jnp.int32, (1, BS), 1)
    row = lax.broadcasted_iota(jnp.int32, (tq, 1), 0)
    for t in range(tiles):
        rows = pl.ds(t * tq, tq)
        hid = hid_ref[rows]
        hid_t = hid.astype(jnp.float32).T.astype(jnp.bfloat16)
        dmix32 = dmix_ref[rows].astype(jnp.float32)
        dmix_t = dmix32.T.astype(jnp.bfloat16)
        dot_pair = dmix32 * mixed_ref[rows]
        nil = jnp.zeros_like(dmix32)
        deltas = (
            jnp.sum(jnp.where(left, dot_pair, nil), axis=1, keepdims=True),
            jnp.sum(jnp.where(left, nil, dot_pair), axis=1, keepdims=True),
        )
        dmm[0] = jnp.where(left, dmix32, nil).astype(jnp.bfloat16)
        dmm[1] = jnp.where(left, nil, dmix32).astype(jnp.bfloat16)
        base = tables[2 * segs + 2 * tiles] + t * tq
        logs = lse_ref[rows]
        dacc[...] = jnp.zeros_like(dacc)

        def segment(s, carry):
            start, count = tables[s], tables[segs + s]
            used = (count + BS - 1) // BS
            here = (row + base >= start) & (row + base < start + count)
            lse = [jnp.where(here, logs[:, h * HD:h * HD + 1], -NEG) for h in range(2)]

            def block(j, carry):
                keep = lane < count - j * BS
                value = v32[pl.ds(start + j * BS, BS), :].astype(jnp.bfloat16)
                parts = []
                total = None
                for h in range(2):
                    synth = f2m[h, j]
                    prob = jnp.where(keep, jnp.exp(dot_nn(hid, synth) - lse[h]), 0.0)
                    dprob = dot_nt(dmm[h], value)
                    dlog = (prob * (dprob - deltas[h])).astype(jnp.bfloat16)
                    head = slice(h * HD, (h + 1) * HD)
                    df2[j, head, :] += dot_nn(hid_t[head], dlog)
                    back = dot_nt(dlog, synth)
                    total = back if total is None else total + back
                    parts.append(dot_nn(dmix_t[head], prob.astype(jnp.bfloat16)))
                dacc[...] += total
                dv32[pl.ds(start + j * BS, BS), :] += jnp.concatenate(parts, axis=0).T
                return carry

            lax.fori_loop(0, used, block, 0)
            return carry

        lax.fori_loop(tables[2 * segs + t], tables[2 * segs + tiles + t], segment, 0)
        dhid_ref[rows] = dacc[...].astype(jnp.bfloat16)
    dvalue_ref[...] = dv32[0:length].astype(jnp.bfloat16)
    dsynth_ref[0] = df2[...].astype(jnp.bfloat16)

def attn_backward(tables, hidden, synth, values, dmix, mixed, lse):
    positions, width = hidden.shape
    length = values.shape[0]
    tq = tile_rows(positions)
    pairs = width // (2 * HD)
    blocks = synth.shape[1]
    per = BS // (2 * HD)
    tok = pl.BlockSpec((positions, 2 * HD), lambda p, t: (0, p))
    f2 = pl.BlockSpec((1, blocks, 2 * HD, BS), lambda p, t: (p // per, 0, p % per, 0))
    val = pl.BlockSpec((length, 2 * HD), lambda p, t: (0, p))
    return pl.pallas_call(
        functools.partial(attn_backward_body, tq),
        name="attn_backward",
        out_shape=(
            jax.ShapeDtypeStruct(synth.shape, jnp.bfloat16),
            jax.ShapeDtypeStruct((positions, width), jnp.bfloat16),
            jax.ShapeDtypeStruct((length, width), jnp.bfloat16),
        ),
        grid_spec=pltpu.PrefetchScalarGridSpec(
            num_scalar_prefetch=1,
            grid=(pairs,),
            in_specs=[tok, f2, val, tok, tok, tok],
            out_specs=[f2, tok, val],
            scratch_shapes=[
                pltpu.VMEM((2, blocks, 2 * HD, BS), jnp.bfloat16),
                pltpu.VMEM((length + BS, 2 * HD), jnp.float32),
                pltpu.VMEM((length + BS, 2 * HD), jnp.float32),
                pltpu.VMEM((2, tq, 2 * HD), jnp.bfloat16),
                pltpu.VMEM((tq, 2 * HD), jnp.float32),
                pltpu.VMEM((blocks, 2 * HD, BS), jnp.float32),
            ],
        ),
        compiler_params=pltpu.CompilerParams(vmem_limit_bytes=40 << 20, dimension_semantics=("arbitrary",)),
        cost_estimate=pl.CostEstimate(flops=10 * positions * length * width * 2, bytes_accessed=24 << 20, transcendentals=positions * length * 12),
    )(tables, hidden, synth, values, dmix, mixed, lse)


def exact(a, b, da=1, db=0):
    return lax.dot_general(a, b, (((da,), (db,)), ((), ())), precision=HIGHEST, preferred_element_type=jnp.float32)

def soap_update_body(ints, floats, got_ref, one_ref, two_ref, moment_ref, stat_ref, basis_ref,
                     new_master_ref, new_moment_ref, new_stat_ref, wide_ref, grad_ref, master_ref, sems):
    devices, slots, part = got_ref.shape[0], got_ref.shape[1], got_ref.shape[2]
    split = one_ref.shape[0]

    def master_copy(k, source):
        return pltpu.make_async_copy(source, master_ref.at[k], sems.at[k])

    for k in range(slots):
        block = ints[slots + k]

        @pl.when(block < split)
        def _():
            master_copy(k, one_ref.at[block]).start()

        @pl.when(block >= split)
        def _():
            master_copy(k, two_ref.at[block - split]).start()

    scale, mom_fix, sec_fix = floats[0], floats[1], floats[2]

    per = max(1, 8 // part)

    def join(d, carry):
        rows = pl.ds(pl.multiple_of(d * (per * part), per * part), per * part)
        for k in range(slots):
            pieces = [got_ref[d * per + i, k].astype(jnp.float32) for i in range(per)]
            grad_ref[k, rows, :] = pieces[0] if per == 1 else jnp.concatenate(pieces, axis=0)
        return carry

    lax.fori_loop(0, devices // per, join, 0)
    for k in range(slots):
        master_copy(k, one_ref.at[0]).wait()

    def prepare(k, carry):
        used = ints[k] > 0
        grad = jnp.where(used, grad_ref[k] * scale, 0.0)
        left, right = basis_ref[k, 0], basis_ref[k, 1]
        old_left, old_right = stat_ref[k, 0], stat_ref[k, 1]
        left_stat = BETA_SEC * old_left + (1 - BETA_SEC) * exact(grad, grad, 1, 1)
        right_stat = BETA_SEC * old_right + (1 - BETA_SEC) * exact(grad, grad, 0, 0)
        new_stat_ref[k, 0] = jnp.where(used, left_stat, old_left)
        new_stat_ref[k, 1] = jnp.where(used, right_stat, old_right)
        left_t = left.T
        for side, (turn, stat) in enumerate(((left_t, left_stat), (right.T, right_stat))):
            cross = exact(turn, stat)
            wide_ref[2 * k + side, :, 0:BS] = exact(cross, cross, 1, 1)
            wide_ref[2 * k + side, :, BS:] = cross
        momentum = BETA_MOM * moment_ref[k, 0] + (1 - BETA_MOM) * grad
        turned_grad = exact(exact(left_t, grad), right)
        turned_mom = exact(exact(left_t, momentum), right)
        old_second = moment_ref[k, 1]
        second = BETA_SEC * old_second + (1 - BETA_SEC) * turned_grad * turned_grad
        step = turned_mom / mom_fix / (jnp.sqrt(second / sec_fix) + EPSILON)
        update = exact(exact(left, step), right, 1, 1)
        master = master_ref[k].astype(jnp.float32)
        new_master_ref[k] = (master - floats[3 + k] * (update + DECAY * master)).astype(jnp.bfloat16)
        new_moment_ref[k, 0] = jnp.where(used, momentum, moment_ref[k, 0])
        new_moment_ref[k, 1] = jnp.where(used, second, old_second)
        return carry

    lax.fori_loop(0, slots, prepare, 0)


def soap_update(ints, floats, got, one, two, moments, stats, bases):
    slots = got.shape[1]
    whole = pl.BlockSpec(memory_space=VMEM)
    scalar = pl.BlockSpec(memory_space=pltpu.SMEM)
    anywhere = pl.BlockSpec(memory_space=pl.ANY)
    pair = jax.ShapeDtypeStruct(moments.shape, jnp.float32)
    return pl.pallas_call(
        soap_update_body,
        name="soap_update",
        out_shape=(
            jax.ShapeDtypeStruct((slots, BS, BS), jnp.bfloat16),
            pair,
            pair,
            jax.ShapeDtypeStruct((2 * slots, BS, 2 * BS), jnp.float32),
        ),
        in_specs=[scalar, scalar, whole, anywhere, anywhere] + [whole] * 3,
        out_specs=[whole] * 4,
        scratch_shapes=[
            VMEM((slots, BS, BS), jnp.float32),
            VMEM((slots, BS, BS), jnp.bfloat16),
            pltpu.SemaphoreType.DMA((slots,)),
        ],
        compiler_params=pltpu.CompilerParams(vmem_limit_bytes=48 << 20),
        cost_estimate=pl.CostEstimate(flops=slots * 12 * 6 * 2 * BS ** 3, bytes_accessed=slots * 14 * 4 * BS * BS, transcendentals=slots * BS * BS),
    )(ints, floats, got, one, two, moments, stats, bases)


def soap_bases_body(ints, given_ref, basis_ref, new_basis_ref, wide):
    slots = basis_ref.shape[0]
    count = 2 * slots
    wide[...] = given_ref[...]
    group = 128 // PANEL
    groups = count // group
    row = lax.broadcasted_iota(jnp.int32, (PANEL, 128), 0)
    lane = lax.broadcasted_iota(jnp.int32, (PANEL, 128), 1)
    unit = jnp.where(row == lane % PANEL, 1.0, 0.0)
    spot = lane // PANEL * PANEL
    for p in range(BS // PANEL):
        low = p * PANEL
        rows = slice(low, low + PANEL)
        schur, inverse, pivots = [], [], []
        for q in range(groups):
            schur.append(jnp.concatenate([wide[q * group + i, rows, low:low + PANEL] for i in range(group)], axis=1))
            inverse.append(unit)
            pivots.append(unit)

        for k in range(PANEL):
            below = row > k
            for q in range(groups):
                a, b = schur[q], inverse[q]
                column = jnp.take_along_axis(a, spot + k, axis=1)
                pivot = jnp.take_along_axis(jnp.broadcast_to(a[k:k + 1], (8, 128)), spot[:8] + k, axis=1)[0:1]
                factor = jnp.where(below, column * (1.0 / pivot), 0.0)
                schur[q] = a - factor * a[k:k + 1]
                inverse[q] = b - factor * b[k:k + 1]
                pivots[q] = jnp.where(row == k, pivot, pivots[q])
        for q in range(groups):
            whole = inverse[q] * lax.rsqrt(pivots[q])
            for i in range(group):
                m = q * group + i
                part = exact(whole[:, i * PANEL:(i + 1) * PANEL], wide[m, rows, :])
                wide[m, rows, :] = part
                if low + PANEL < BS:
                    wide[m, low + PANEL:, :] -= exact(part[:, low + PANEL:BS], part, 0, 0)

    def finish(k, carry):
        used = ints[k] > 0
        for side in range(2):
            new_basis_ref[k, side] = jnp.where(used, wide[2 * k + side, :, BS:].T, basis_ref[k, side])
        return carry

    lax.fori_loop(0, slots, finish, 0)


def soap_bases(ints, wide, bases):
    slots = bases.shape[0]
    whole = pl.BlockSpec(memory_space=VMEM)
    return pl.pallas_call(
        soap_bases_body,
        name="soap_bases",
        out_shape=jax.ShapeDtypeStruct(bases.shape, jnp.float32),
        in_specs=[pl.BlockSpec(memory_space=pltpu.SMEM), whole, whole],
        out_specs=whole,
        scratch_shapes=[VMEM(wide.shape, jnp.float32)],
        compiler_params=pltpu.CompilerParams(vmem_limit_bytes=48 << 20),
        cost_estimate=pl.CostEstimate(flops=slots * 4 * 6 * 2 * BS ** 3, bytes_accessed=slots * 8 * 4 * BS * BS, transcendentals=slots * BS * BS),
    )(ints, wide, bases)


def spread_pieces_body(split, weight_ref, one_ref, two_ref, lay):
    for i in range(one_ref.shape[1]):
        lay[:, i, :] = weight_ref[:, i * BS:(i + 1) * BS]
    one_ref[...] = lay[:split].astype(jnp.bfloat16)
    two_ref[...] = lay[split:].astype(jnp.bfloat16)


def spread_pieces(weights, split):
    count, rows = weights.shape[0], weights.shape[1] // BS
    whole = pl.BlockSpec(memory_space=VMEM)
    return pl.pallas_call(
        functools.partial(spread_pieces_body, split),
        name="spread_pieces",
        out_shape=(
            jax.ShapeDtypeStruct((split, rows, BS), jnp.bfloat16),
            jax.ShapeDtypeStruct((count - split, rows, BS), jnp.bfloat16),
        ),
        in_specs=[whole],
        out_specs=[whole] * 2,
        scratch_shapes=[VMEM((count, rows, BS), jnp.float32)],
        compiler_params=pltpu.CompilerParams(vmem_limit_bytes=32 << 20),
    )(weights)


def collect_body(slot_id, piece_ref, out_ref):
    rows = piece_ref.shape[1]

    def place(m, carry):
        piece = piece_ref[slot_id[m]].astype(jnp.float32)
        for i in range(rows):
            out_ref[pl.ds(m, 1), i * BS:(i + 1) * BS] = piece[i:i + 1]
        return carry

    lax.fori_loop(0, out_ref.shape[0], place, 0)


def collect(slot_id, pieces):
    count, rows = slot_id.shape[0], pieces.shape[1]
    whole = pl.BlockSpec(memory_space=VMEM)
    return pl.pallas_call(
        collect_body,
        name="collect",
        out_shape=jax.ShapeDtypeStruct((count, rows * BS), jnp.float32),
        in_specs=[pl.BlockSpec(memory_space=pltpu.SMEM), whole],
        out_specs=whole,
        compiler_params=pltpu.CompilerParams(vmem_limit_bytes=32 << 20),
    )(slot_id, pieces)


def partners(bits):
    row, seq = lax.axis_index("row"), lax.axis_index("seq")
    core, flags, peers = row % 2, [], []
    for k in range(bits):
        flag = row // 2 ** (k + 1) % 2
        flags.append(flag)
        peers.append((row + (1 - 2 * flag) * 2 ** (k + 1), seq))
    return core, (row + 1 - 2 * core, seq), flags, peers


def greet(devices):
    barrier = pltpu.get_barrier_semaphore()
    for device in devices:
        pl.semaphore_signal(barrier, inc=1, device_id=device, device_id_type=MESH)
    pl.semaphore_wait(barrier, len(devices))


def reduce_rows_body(bits, seqs, cut, given, *refs):
    in_refs, (out_ref, near, near_sum, *rest) = refs[:given], refs[given:]
    levels = 2 * bits
    halves = ((0, cut), (cut, out_ref.shape[0]))
    far, far_sum = rest[:levels], rest[levels:2 * levels - 2]
    spread, arrived, send, recv = rest[2 * levels - 2:]
    part = out_ref.shape[1]
    core, sibling, flags, peers = partners(bits)
    row, seq = lax.axis_index("row"), lax.axis_index("seq")
    beside = [(row, (seq + k) % seqs) for k in range(1, seqs)]
    greet([sibling, *peers, *beside])

    def copy(source, target, at, device):
        return pltpu.make_async_remote_copy(
            src_ref=source, dst_ref=target, send_sem=send.at[at], recv_sem=recv.at[at],
            device_id=device, device_id_type=MESH,
        )

    some = slice(None)
    every = (some,) * bits
    spans, at = ([], []), 0
    for ref in in_refs:
        for h, (low, high) in enumerate(halves):
            begin, end = max(low, at), min(high, at + ref.shape[0])
            if begin < end:
                spans[h].append((ref, begin - at, begin, end - begin))
        at += ref.shape[0]
    first = ([], [])
    for h in range(2):
        for ref, source, target, count in spans[h]:
            move = copy(
                ref.at[(pl.ds(source, count), *every, 1 - core)], near.at[pl.ds(target, count)],
                2 * bits + seqs - 1 + len(first[0]) + len(first[1]), sibling,
            )
            move.start()
            first[h].append(move)

    pending = [None, None]
    held = [None, None]
    dims = [list(range(bits - 1, -1, -1)) for _ in range(2)]
    orders = [list(range(bits)), list(range(bits - 1, -1, -1))]
    for step in range(bits + 1):
        for h, (low, high) in enumerate(halves):
            count = high - low
            last = step == bits
            if step == 0:
                for move, (ref, source, target, count_here) in zip(first[h], spans[h]):
                    move.wait()

                    def add(n, carry):
                        mine = ref[(n + source, *every, core)].astype(jnp.float32)
                        total = mine + near[n + target].astype(jnp.float32)
                        near_sum[n + target] = total.astype(jnp.bfloat16)
                        return carry

                    lax.fori_loop(0, count_here, add, 0)
                held[h] = near_sum.at[pl.ds(low, count)]
            else:
                bit = orders[h][step - 1]
                place = dims[h].index(bit)
                keep = (some,) * place + (flags[bit],)
                pending[h].wait()
                mine, other = held[h], far[(step - 1) * 2 + h]
                dims[h].pop(place)
                target = None if last else far_sum[(step - 1) * 2 + h]

                def add(n, carry):
                    total = mine[(n, *keep)].astype(jnp.float32) + other[n].astype(jnp.float32)
                    if target is None:
                        for s in range(seqs):
                            spread[s, low + n] = total[s * part:(s + 1) * part].astype(jnp.bfloat16)
                    else:
                        target[n] = total.astype(jnp.bfloat16)
                    return carry

                lax.fori_loop(0, count, add, 0)
                held[h] = target
            if not last:
                bit = orders[h][step]
                place = dims[h].index(bit)
                pending[h] = copy(
                    held[h].at[(slice(None),) * (place + 1) + (1 - flags[bit],)],
                    far[step * 2 + h], step * 2 + h, peers[bit],
                )
                pending[h].start()

    final = []
    for k, device in enumerate(beside):
        final.append(copy(spread.at[device[1]], arrived.at[k], levels + k, device))
        final[k].start()
    for move in final:
        move.wait()

    def finish(n, carry):
        total = spread[seq, n].astype(jnp.float32)
        for k in range(seqs - 1):
            total = total + arrived[k, n].astype(jnp.float32)
        out_ref[n] = total
        return carry

    lax.fori_loop(0, out_ref.shape[0], finish, 0)


def reduce_rows(terms, rows, seqs, collective):
    count = sum(term.shape[0] for term in terms)
    cut = (count + 1) // 2
    bits = (rows // 2).bit_length() - 1
    slab = BS // rows
    part = slab // seqs
    twos = (2,) * bits
    low = jnp.bfloat16
    whole = pl.BlockSpec(memory_space=VMEM)
    halves = (cut, count - cut)
    far = [VMEM((halves[h], *twos[k + 1:], slab, BS), low) for k in range(bits) for h in range(2)]
    far_sum = [VMEM((halves[h], *twos[k + 1:], slab, BS), low) for k in range(bits - 1) for h in range(2)]
    sems = 2 * bits + seqs - 1 + len(terms) + 1
    return pl.pallas_call(
        functools.partial(reduce_rows_body, bits, seqs, cut, len(terms)),
        name="reduce_rows",
        out_shape=jax.ShapeDtypeStruct((count, part, BS), jnp.float32),
        in_specs=[whole] * len(terms),
        out_specs=whole,
        scratch_shapes=[
            VMEM((count, *twos, slab, BS), low),
            VMEM((count, *twos, slab, BS), low),
            *far,
            *far_sum,
            VMEM((seqs, count, part, BS), low),
            VMEM((seqs - 1, count, part, BS), low),
            pltpu.SemaphoreType.DMA((sems,)),
            pltpu.SemaphoreType.DMA((sems,)),
        ],
        compiler_params=pltpu.CompilerParams(
            collective_id=collective, has_side_effects=True, vmem_limit_bytes=56 << 20
        ),
        cost_estimate=pl.CostEstimate(flops=count * BS * BS, bytes_accessed=4 * count * BS * BS, transcendentals=0),
    )(*[term.reshape(-1, *twos, 2, slab, BS) for term in terms])


def exchange_body(seqs, sources, spot_of, late_ref, early_ref, got_ref, square_ref, vector_ref, out, mine, send, recv):
    devices, own = got_ref.shape[0], got_ref.shape[1]
    split, part = late_ref.shape[0], late_ref.shape[1]
    me = lax.axis_index("row") * seqs + lax.axis_index("seq")
    barrier = pltpu.get_barrier_semaphore()

    def peer(k):
        to = (me + k) % devices
        return to, (to // seqs, to % seqs)

    def hello(k, carry):
        pl.semaphore_signal(barrier, inc=1, device_id=peer(k)[1], device_id_type=MESH)
        return carry

    lax.fori_loop(1, devices, hello, 0)

    def place(d, carry):
        for s in range(own):
            spot = spot_of[d * own + s]
            low = late_ref[jnp.minimum(spot, split - 1)].astype(jnp.bfloat16)
            high = early_ref[jnp.maximum(spot - split, 0)]
            out[d, s] = jnp.where(spot < split, low, high)
        return carry

    lax.fori_loop(0, devices, place, 0)

    def add(ref, total):
        def step(m, total):
            value = ref[m].astype(jnp.float32)
            return total + value * value

        return lax.fori_loop(0, ref.shape[0], step, total)

    total = add(early_ref, add(late_ref, jnp.zeros((part, BS), jnp.float32)))
    mine[...] = total[:, :128] + total[:, 128:]
    pl.semaphore_wait(barrier, devices - 1)

    def move(source, target, kind, k, device):
        return pltpu.make_async_remote_copy(
            src_ref=source, dst_ref=target, send_sem=send.at[kind, k], recv_sem=recv.at[kind, k],
            device_id=device, device_id_type=MESH,
        )

    def moves(k):
        to, device = peer(k)
        return (
            move(out.at[to], got_ref.at[me], 0, k, device),
            move(mine, square_ref.at[me], 1, k, device),
        )

    def launch(k, carry):
        for one in moves(k):
            one.start()
        return carry

    lax.fori_loop(1, devices, launch, 0)

    @pl.when(me < sources[0])
    def _():
        def tell(k, carry):
            move(late_ref.at[sources[1]], vector_ref.at[me], 2, k, peer(k)[1]).start()
            return carry

        lax.fori_loop(1, devices, tell, 0)
        vector_ref[me] = late_ref[sources[1]]

    got_ref[me] = out[me]
    square_ref[me] = mine[...]

    def finish(k, carry):
        for one in moves(k):
            one.wait()
        return carry

    lax.fori_loop(1, devices, finish, 0)

    @pl.when(me < sources[0])
    def _():
        def told(k, carry):
            move(late_ref.at[sources[1]], vector_ref.at[me], 2, k, peer(k)[1]).wait_send()
            return carry

        lax.fori_loop(1, devices, told, 0)

    for d in range(sources[0]):
        @pl.when(me != d)
        def _():
            k = (me - d + devices) % devices
            move(late_ref.at[sources[1]], vector_ref.at[d], 2, k, peer(k)[1]).wait_recv()


def exchange(spot_of, late, early, rows, seqs, vector_spot, vector_rows, collective):
    devices = rows * seqs
    part = late.shape[1]
    own = spot_of.shape[0] // devices
    told = -(-vector_rows // part)
    whole = pl.BlockSpec(memory_space=VMEM)
    return pl.pallas_call(
        functools.partial(exchange_body, seqs, (told, vector_spot)),
        name="exchange",
        out_shape=(
            jax.ShapeDtypeStruct((devices, own, part, BS), jnp.bfloat16),
            jax.ShapeDtypeStruct((devices, part, 128), jnp.float32),
            jax.ShapeDtypeStruct((told, part, BS), jnp.float32),
        ),
        in_specs=[pl.BlockSpec(memory_space=pltpu.SMEM), whole, whole],
        out_specs=[whole] * 3,
        scratch_shapes=[
            VMEM((devices, own, part, BS), jnp.bfloat16),
            VMEM((part, 128), jnp.float32),
            pltpu.SemaphoreType.DMA((3, devices)),
            pltpu.SemaphoreType.DMA((3, devices)),
        ],
        compiler_params=pltpu.CompilerParams(
            collective_id=collective, has_side_effects=True, vmem_limit_bytes=32 << 20
        ),
    )(spot_of, late, early)


def block_bounds():
    model_blocks = D // BS
    first_end = model_blocks * model_blocks
    synth_end = first_end + model_blocks * (LEN // BS)
    value_end = synth_end + first_end
    output_end = value_end + first_end
    expand_end = output_end + model_blocks * (FF // BS)
    return (first_end, synth_end, value_end, output_end, expand_end)


def block_scales():
    first_end, synth_end, value_end, output_end, expand_end = block_bounds()
    spots = jnp.arange(BLOCKS)
    scales = jnp.where(
        spots < first_end,
        D ** (-0.5),
        jnp.where(
            spots < synth_end,
            3.0 * HD ** (-0.5),
            jnp.where(
                spots < value_end,
                D ** (-0.5),
                jnp.where(
                    spots < output_end,
                    4.0 * D ** (-0.5),
                    jnp.where(spots < expand_end, D ** (-0.5), FF ** (-0.5)),
                ),
            ),
        ),
    )
    return scales.astype(jnp.float32)


def silu_slope(values):
    sigma = jax.nn.sigmoid(values)
    return sigma * (1.0 + values * (1.0 - sigma))


def layer_norm(values, gain_row, shift_row):
    centered = values - jnp.mean(values, axis=-1, keepdims=True)
    inverse = lax.rsqrt(jnp.mean(centered * centered, axis=-1, keepdims=True) + NORM_EPS)
    normed = centered * inverse
    return (normed * gain_row + shift_row, normed, inverse)


def norm_back(grad_out, normed, inverse, gain_row):
    scaled = grad_out * gain_row
    return inverse * (
        scaled
        - jnp.mean(scaled, axis=-1, keepdims=True)
        - normed * jnp.mean(scaled * normed, axis=-1, keepdims=True)
    )


def apply_blocks(inputs, matrix):
    token_count = inputs.shape[0]
    row_blocks, col_blocks = (matrix.shape[0], matrix.shape[1])
    result = jnp.einsum(
        "nri,rcij->ncj",
        inputs.reshape(token_count, row_blocks, BS),
        matrix,
        preferred_element_type=jnp.float32,
    )
    return result.reshape(token_count, col_blocks * BS)


def back_blocks(grad_rows, matrix):
    token_count = grad_rows.shape[0]
    row_blocks, col_blocks = (matrix.shape[0], matrix.shape[1])
    result = jnp.einsum(
        "ncj,rcij->nri",
        grad_rows.reshape(token_count, col_blocks, BS),
        matrix,
        preferred_element_type=jnp.float32,
    )
    return result.reshape(token_count, row_blocks * BS)


def grad_blocks(inputs, grad_rows, row_blocks, col_blocks):
    token_count = inputs.shape[0]
    result = jnp.einsum(
        "nri,ncj->rcij",
        inputs.reshape(token_count, row_blocks, BS),
        grad_rows.reshape(token_count, col_blocks, BS),
        preferred_element_type=jnp.float32,
    )
    return result.reshape(row_blocks * col_blocks, BS, BS).astype(jnp.bfloat16)


def slot_table(owners, own_most, slot_total):
    block_count = owners.shape[0]
    block_index = jnp.arange(block_count, dtype=jnp.int32)
    same_owner = owners[:, None] == owners[None, :]
    earlier = block_index[None, :] < block_index[:, None]
    rank_within = jnp.sum(jnp.where(same_owner & earlier, 1, 0), axis=1).astype(jnp.int32)
    slot_id = owners * own_most + rank_within
    slot_hit = slot_id[:, None] == jnp.arange(slot_total, dtype=jnp.int32)[None, :]
    used = jnp.any(slot_hit, axis=0)
    block_of = jnp.sum(jnp.where(slot_hit, block_index[:, None], 0), axis=0)
    return (slot_id, used, block_of)


def vector_adam(vectors, vec_moments, grad_rows, mom_fix, sec_fix):
    first_moment = BETA_MOM * vec_moments[0] + (1 - BETA_MOM) * grad_rows
    second = BETA_SEC * vec_moments[1] + (1 - BETA_SEC) * grad_rows * grad_rows
    step_rows = first_moment / mom_fix / (jnp.sqrt(second / sec_fix) + EPSILON)
    return (vectors - VECTOR_RATE * step_rows, jnp.stack([first_moment, second]))


def scatter_sum(terms):
    part = lax.psum_scatter(terms, "row", scatter_dimension=1, tiled=True)
    return lax.psum_scatter(part, "seq", scatter_dimension=1, tiled=True)


def local(
    tokens,
    cotangent,
    seg_ids,
    seg_lengths,
    weights,
    vectors,
    vec_moments,
    moments,
    stats,
    bases,
    owners,
    step_count,
):
    rows_here, positions, width = tokens.shape
    owner_count = lax.axis_size("row") * lax.axis_size("seq")
    own_most = moments.shape[0]
    slot_count = owner_count * own_most
    block_count = weights.shape[0]
    piece_rows = weights.shape[1] // BS
    model_blocks = D // BS
    hidden_blocks = FF // BS
    length_blocks = LEN // BS
    first_end, synth_end, value_end, output_end, expand_end = block_bounds()
    pieces_one, pieces_two = spread_pieces(weights, value_end)
    gathered_one = lax.all_gather(pieces_one, AXES, axis=1, tiled=True)
    gathered_two = lax.all_gather(pieces_two, AXES, axis=1, tiled=True)
    token_row = lax.all_gather(tokens, "seq", axis=1, tiled=True).reshape(LEN, width)

    def tiles_at(start_block, row_blocks, col_blocks):
        if start_block < value_end:
            part = gathered_one[start_block : start_block + row_blocks * col_blocks]
        else:
            start_block = start_block - value_end
            part = gathered_two[start_block : start_block + row_blocks * col_blocks]
        return part.reshape(row_blocks, col_blocks, BS, BS)

    first_w = tiles_at(0, model_blocks, model_blocks)
    synth_w = tiles_at(first_end, model_blocks, length_blocks)
    value_w = tiles_at(synth_end, model_blocks, model_blocks)
    output_w = tiles_at(value_end, model_blocks, model_blocks)
    expand_w = tiles_at(output_end, model_blocks, hidden_blocks)
    contract_w = tiles_at(expand_end, hidden_blocks, model_blocks)
    ffn_bias = vectors[5:].reshape(FF)

    slot_range = jnp.arange(seg_lengths.shape[1], dtype=jnp.int32)
    before = slot_range[None, :] < slot_range[:, None]
    starts = jnp.sum(jnp.where(before, seg_lengths[0][None, :], 0), axis=1)
    tq = tile_rows(positions)
    tile_ids = seg_ids[0].reshape(positions // tq, tq)
    offset = lax.axis_index("seq") * positions
    tables = jnp.concatenate(
        [
            starts,
            seg_lengths[0],
            tile_ids[:, 0],
            tile_ids[:, tq - 1] + 1,
            jnp.full((1,), offset, jnp.int32),
        ]
    ).astype(jnp.int32)

    inputs = tokens.reshape(positions, width).astype(jnp.float32)
    normed_one, hat_one, inv_one = layer_norm(inputs, vectors[0], vectors[1])
    first_in = normed_one.astype(jnp.bfloat16)
    first_pre = apply_blocks(first_in, first_w) + vectors[4]
    hidden = jax.nn.silu(first_pre).astype(jnp.bfloat16)
    normed_row, hat_row, _ = layer_norm(token_row.astype(jnp.float32), vectors[0], vectors[1])
    row_in = normed_row.astype(jnp.bfloat16)
    values = apply_blocks(row_in, value_w).astype(jnp.bfloat16)

    mixed_wide, log_total = attn_forward(tables, hidden, synth_w, values)
    mixed = mixed_wide.astype(jnp.bfloat16)
    middle = inputs + apply_blocks(mixed, output_w)
    normed_two, hat_two, inv_two = layer_norm(middle, vectors[2], vectors[3])
    second_in = normed_two.astype(jnp.bfloat16)
    expand_pre = apply_blocks(second_in, expand_w) + ffn_bias
    expanded = jax.nn.silu(expand_pre).astype(jnp.bfloat16)
    result = middle + apply_blocks(expanded, contract_w)
    layer_out = result.astype(jnp.bfloat16).reshape(rows_here, positions, width)
    back_out = cotangent.reshape(positions, width)
    grad_contract = grad_blocks(expanded, back_out, hidden_blocks, model_blocks)
    back_expanded = back_blocks(back_out, contract_w).astype(jnp.bfloat16)
    back_pre = (back_expanded.astype(jnp.float32) * silu_slope(expand_pre)).astype(jnp.bfloat16)
    grad_expand = grad_blocks(second_in, back_pre, model_blocks, hidden_blocks)
    grad_ffn_bias = jnp.sum(back_pre.astype(jnp.float32), axis=0)
    back_normed_two = back_blocks(back_pre, expand_w)
    grad_gain_two = jnp.sum(back_normed_two * hat_two, axis=0)
    grad_shift_two = jnp.sum(back_normed_two, axis=0)
    back_middle = back_out.astype(jnp.float32) + norm_back(
        back_normed_two, hat_two, inv_two, vectors[2]
    )
    back_attn = back_middle.astype(jnp.bfloat16)
    grad_output = grad_blocks(mixed, back_attn, model_blocks, model_blocks)
    back_mixed = back_blocks(back_attn, output_w).astype(jnp.bfloat16)
    early_terms = jnp.concatenate([grad_output, grad_expand, grad_contract], axis=0)
    early_terms, back_mixed = lax.optimization_barrier((early_terms, back_mixed))
    early = scatter_sum(early_terms)

    synth_grad, back_hidden, value_terms = attn_backward(
        tables, hidden, synth_w, values, back_mixed, mixed_wide, log_total
    )
    back_first = (back_hidden.astype(jnp.float32) * silu_slope(first_pre)).astype(jnp.bfloat16)
    grad_first = grad_blocks(first_in, back_first, model_blocks, model_blocks)
    grad_first_bias = jnp.sum(back_first.astype(jnp.float32), axis=0)
    grad_value = grad_blocks(row_in, value_terms, model_blocks, model_blocks)
    synth_grad = synth_grad.reshape(model_blocks * length_blocks, BS, BS)
    back_from_first = back_blocks(back_first, first_w)
    back_from_value = back_blocks(value_terms, value_w)
    grad_gain_one = jnp.sum(back_from_first * hat_one, axis=0) + jnp.sum(
        back_from_value * hat_row, axis=0
    )
    grad_shift_one = jnp.sum(back_from_first, axis=0) + jnp.sum(back_from_value, axis=0)
    vector_local = jnp.concatenate(
        [
            jnp.stack(
                [grad_gain_one, grad_shift_one, grad_gain_two, grad_shift_two, grad_first_bias]
            ),
            grad_ffn_bias.reshape(FF // D, D),
        ],
        axis=0,
    )
    vector_count = vectors.shape[0] * vectors.shape[1]
    vector_rows = vector_count // BS
    vector_block = jnp.pad(vector_local.reshape(vector_rows, BS), ((0, BS - vector_rows), (0, 0)))
    rows_total, seqs_total = lax.axis_size("row"), lax.axis_size("seq")
    late = reduce_rows(
        [grad_first, grad_value, vector_block[None].astype(jnp.bfloat16), synth_grad],
        rows_total,
        seqs_total,
        1,
    )
    late, value_late = lax.optimization_barrier((late, value_terms))
    value_sums = lax.psum_scatter(value_late, "seq", scatter_dimension=0, tiled=True)
    back_normed_one = back_from_first + back_blocks(value_sums, value_w)
    back_inputs = back_middle + norm_back(back_normed_one, hat_one, inv_one, vectors[0])
    x_grad = back_inputs.reshape(rows_here, positions, width)

    slot_id, used, block_of = slot_table(owners, own_most, slot_count)
    device_index = lax.axis_index(AXES)
    mine_used = lax.dynamic_slice_in_dim(used, device_index * own_most, own_most)
    mine_block = lax.dynamic_slice_in_dim(block_of, device_index * own_most, own_most)
    vector_spot = 2 * first_end
    spot_of = jnp.where(
        block_of < first_end,
        block_of,
        jnp.where(
            block_of < synth_end,
            block_of + first_end + 1,
            jnp.where(block_of < value_end, block_of - synth_end + first_end, block_of + 1),
        ),
    )
    got, square_parts, vector_parts = exchange(
        spot_of, late, early, rows_total, seqs_total, vector_spot, vector_rows, 2
    )
    vector_total = vector_parts.reshape(-1, BS)[:vector_rows].reshape(vectors.shape)
    grad_norm = jnp.sqrt(jnp.sum(square_parts))
    clip_max = math.sqrt(block_count * BS * BS + vectors.shape[0] * vectors.shape[1])
    scale = jnp.minimum(1.0, clip_max / grad_norm)
    step_value = step_count[0].astype(jnp.float32)
    mom_fix = 1.0 - jnp.power(BETA_MOM, step_value)
    sec_fix = 1.0 - jnp.power(BETA_SEC, step_value)
    new_vectors, new_vec_moments = vector_adam(
        vectors, vec_moments, vector_total * scale, mom_fix, sec_fix
    )
    rate_table = RATE_FACTOR * block_scales()
    slot_rates = jnp.sum(
        jnp.where(
            mine_block[:, None] == jnp.arange(block_count, dtype=jnp.int32)[None, :],
            rate_table[None, :],
            0.0,
        ),
        axis=1,
    )
    floats = jnp.concatenate([jnp.stack([scale, mom_fix, sec_fix]), slot_rates])
    ints = jnp.concatenate([mine_used.astype(jnp.int32), mine_block])
    new_master, new_moments, new_stats, wide = soap_update(
        ints, floats, got, gathered_one, gathered_two, moments, stats, bases
    )
    new_bases = soap_bases(ints, wide, bases)
    returned = lax.all_to_all(
        new_master.reshape(1, own_most, BS, BS), AXES, split_axis=2, concat_axis=0, tiled=True
    )
    new_weights = collect(slot_id, returned.reshape(slot_count, piece_rows, BS))
    return (
        layer_out,
        x_grad,
        new_weights,
        new_moments,
        new_stats,
        new_bases,
        new_vectors,
        new_vec_moments,
        grad_norm.reshape(1),
    )


def solution(mesh):
    placed = (
        P("row", "seq", None),
        P("row", "seq", None),
        P("row", "seq"),
        P("row", None),
        P(None, ("row", "seq")),
        P(),
        P(),
        P(("row", "seq"), None, None, None),
        P(("row", "seq"), None, None, None),
        P(("row", "seq"), None, None, None),
        P(),
        P(),
    )
    return jax.shard_map(
        local,
        mesh=mesh,
        in_specs=placed,
        out_specs=(
            P("row", "seq", None),
            P("row", "seq", None),
            P(None, ("row", "seq")),
            P(("row", "seq"), None, None, None),
            P(("row", "seq"), None, None, None),
            P(("row", "seq"), None, None, None),
            P(),
            P(),
            P(),
        ),
        check_vma=False,
    )
```

```python
import functools
import math

import jax
import jax.numpy as jnp
from jax import lax
from jax.experimental import pallas as pl
from jax.experimental.pallas import tpu as pltpu
from jax.sharding import PartitionSpec as P

D = 768
HEADS = 12
HD = 64
FF = 3072
LEN = 2048
BS = 256
BLOCKS = 123

BETA_MOM = 0.95
BETA_SEC = 0.95
EPSILON = 1e-08
DECAY = 0.01
VECTOR_RATE = 0.3
RATE_FACTOR = 2.0
NORM_EPS = 1e-05
NEG = -1e30
PANEL = 32
HIGHEST = lax.Precision.HIGHEST
VMEM = pltpu.VMEM
AXES = ("row", "seq")
MESH = pl.DeviceIdType.MESH


def dot_nn(a,b): return lax.dot_general(a,b,(((1,),(0,)),((),())),preferred_element_type=jnp.float32)
def dot_nt(a,b): return lax.dot_general(a,b,(((1,),(1,)),((),())),preferred_element_type=jnp.float32)

def tile_rows(positions): return min(positions,256)

def attn_forward_body(tq, tables, hid_ref, synth_ref, value_ref, mixed_ref, lse_ref, f2m, v32, lbuf):
    length = value_ref.shape[0]
    tiles = hid_ref.shape[0] // tq
    blocks = synth_ref.shape[1]
    segs = (tables.shape[0] - 2 * tiles - 1) // 2
    low_rows = lax.broadcasted_iota(jnp.int32, (2 * HD, BS), 0) < HD
    for j in range(blocks):
        tile = synth_ref[0, j]
        zero = jnp.zeros_like(tile)
        f2m[0, j] = jnp.where(low_rows, tile, zero)
        f2m[1, j] = jnp.where(low_rows, zero, tile)
    v32[0:length] = value_ref[...].astype(jnp.float32)
    v32[length:] = jnp.zeros((BS, 2 * HD), jnp.float32)
    left = lax.broadcasted_iota(jnp.int32, (tq, 2 * HD), 1) < HD
    lane = lax.broadcasted_iota(jnp.int32, (1, BS), 1)
    row = lax.broadcasted_iota(jnp.int32, (tq, 1), 0)
    for t in range(tiles):
        hid = hid_ref[t * tq:(t + 1) * tq]
        base = tables[2 * segs + 2 * tiles] + t * tq

        def segment(s, carry):
            start, count = tables[s], tables[segs + s]
            used = (count + BS - 1) // BS

            def scores(j, tops):
                keep = lane < count - j * BS
                out = []
                for h in range(2):
                    part = jnp.where(keep, dot_nn(hid, f2m[h, j]), NEG)
                    lbuf[h, j] = part
                    out.append(jnp.maximum(tops[h], jnp.maximum(part[:, :128], part[:, 128:])))
                return tuple(out)

            none = jnp.full((tq, 128), NEG, jnp.float32)
            tops = lax.fori_loop(0, used, scores, (none, none))
            tops = [jnp.max(top, axis=1, keepdims=True) for top in tops]

            def weigh(j, carried):
                value = v32[pl.ds(start + j * BS, BS), :].astype(jnp.bfloat16)
                out = []
                for h in range(2):
                    total, mix = carried[h]
                    part = jnp.exp(lbuf[h, j] - tops[h])
                    total = total + part[:, :128] + part[:, 128:]
                    mix = mix + dot_nn(part.astype(jnp.bfloat16), value)
                    out.append((total, mix))
                return tuple(out)

            blank = jnp.zeros((tq, 128), jnp.float32)
            pair = lax.fori_loop(0, used, weigh, ((blank, blank), (blank, blank)))
            sums = [jnp.sum(total, axis=1, keepdims=True) for total, _ in pair]
            mix = jnp.where(left, pair[0][1] / sums[0], pair[1][1] / sums[1])
            log = jnp.where(left, tops[0] + jnp.log(sums[0]), tops[1] + jnp.log(sums[1]))
            here = (row + base >= start) & (row + base < start + count)
            rows = pl.ds(t * tq, tq)
            mixed_ref[rows] = jnp.where(here, mix, mixed_ref[rows])
            lse_ref[rows] = jnp.where(here, log, lse_ref[rows])
            return carry

        lax.fori_loop(tables[2 * segs + t], tables[2 * segs + tiles + t], segment, 0)

def attn_forward(tables, hidden, synth, values):
    positions, width = hidden.shape
    length = values.shape[0]
    tq = tile_rows(positions)
    pairs = width // (2 * HD)
    blocks = synth.shape[1]
    per = BS // (2 * HD)
    return pl.pallas_call(
        functools.partial(attn_forward_body, tq),
        name="attn_forward",
        out_shape=(jax.ShapeDtypeStruct((positions, width), jnp.float32),) * 2,
        grid_spec=pltpu.PrefetchScalarGridSpec(
            num_scalar_prefetch=1,
            grid=(pairs,),
            in_specs=[
                pl.BlockSpec((positions, 2 * HD), lambda p, t: (0, p)),
                pl.BlockSpec((1, blocks, 2 * HD, BS), lambda p, t: (p // per, 0, p % per, 0)),
                pl.BlockSpec((length, 2 * HD), lambda p, t: (0, p)),
            ],
            out_specs=[pl.BlockSpec((positions, 2 * HD), lambda p, t: (0, p))] * 2,
            scratch_shapes=[
                pltpu.VMEM((2, blocks, 2 * HD, BS), jnp.bfloat16),
                pltpu.VMEM((length + BS, 2 * HD), jnp.float32),
                pltpu.VMEM((2, blocks, tq, BS), jnp.float32),
            ],
        ),
        compiler_params=pltpu.CompilerParams(vmem_limit_bytes=40 << 20, dimension_semantics=("arbitrary",)),
        cost_estimate=pl.CostEstimate(flops=4 * positions * length * width * 2, bytes_accessed=12 << 20, transcendentals=positions * length * 12),
    )(tables, hidden, synth, values)

def attn_backward_body(tq, tables, hid_ref, synth_ref, value_ref, dmix_ref, mixed_ref, lse_ref,
                       dsynth_ref, dhid_ref, dvalue_ref, f2m, v32, dv32, dmm, dacc, df2):
    length = value_ref.shape[0]
    tiles = hid_ref.shape[0] // tq
    blocks = synth_ref.shape[1]
    segs = (tables.shape[0] - 2 * tiles - 1) // 2
    low_rows = lax.broadcasted_iota(jnp.int32, (2 * HD, BS), 0) < HD
    for j in range(blocks):
        tile = synth_ref[0, j]
        zero = jnp.zeros_like(tile)
        f2m[0, j] = jnp.where(low_rows, tile, zero)
        f2m[1, j] = jnp.where(low_rows, zero, tile)
    v32[0:length] = value_ref[...].astype(jnp.float32)
    v32[length:] = jnp.zeros((BS, 2 * HD), jnp.float32)
    dv32[...] = jnp.zeros_like(dv32)
    df2[...] = jnp.zeros_like(df2)
    left = lax.broadcasted_iota(jnp.int32, (tq, 2 * HD), 1) < HD
    lane = lax.broadcasted_iota(jnp.int32, (1, BS), 1)
    row = lax.broadcasted_iota(jnp.int32, (tq, 1), 0)
    for t in range(tiles):
        rows = pl.ds(t * tq, tq)
        hid = hid_ref[rows]
        hid_t = hid.astype(jnp.float32).T.astype(jnp.bfloat16)
        dmix32 = dmix_ref[rows].astype(jnp.float32)
        dmix_t = dmix32.T.astype(jnp.bfloat16)
        dot_pair = dmix32 * mixed_ref[rows]
        nil = jnp.zeros_like(dmix32)
        deltas = (
            jnp.sum(jnp.where(left, dot_pair, nil), axis=1, keepdims=True),
            jnp.sum(jnp.where(left, nil, dot_pair), axis=1, keepdims=True),
        )
        dmm[0] = jnp.where(left, dmix32, nil).astype(jnp.bfloat16)
        dmm[1] = jnp.where(left, nil, dmix32).astype(jnp.bfloat16)
        base = tables[2 * segs + 2 * tiles] + t * tq
        logs = lse_ref[rows]
        dacc[...] = jnp.zeros_like(dacc)

        def segment(s, carry):
            start, count = tables[s], tables[segs + s]
            used = (count + BS - 1) // BS
            here = (row + base >= start) & (row + base < start + count)
            lse = [jnp.where(here, logs[:, h * HD:h * HD + 1], -NEG) for h in range(2)]

            def block(j, carry):
                keep = lane < count - j * BS
                value = v32[pl.ds(start + j * BS, BS), :].astype(jnp.bfloat16)
                parts = []
                total = None
                for h in range(2):
                    synth = f2m[h, j]
                    prob = jnp.where(keep, jnp.exp(dot_nn(hid, synth) - lse[h]), 0.0)
                    dprob = dot_nt(dmm[h], value)
                    dlog = (prob * (dprob - deltas[h])).astype(jnp.bfloat16)
                    head = slice(h * HD, (h + 1) * HD)
                    df2[j, head, :] += dot_nn(hid_t[head], dlog)
                    back = dot_nt(dlog, synth)
                    total = back if total is None else total + back
                    parts.append(dot_nn(dmix_t[head], prob.astype(jnp.bfloat16)))
                dacc[...] += total
                dv32[pl.ds(start + j * BS, BS), :] += jnp.concatenate(parts, axis=0).T
                return carry

            lax.fori_loop(0, used, block, 0)
            return carry

        lax.fori_loop(tables[2 * segs + t], tables[2 * segs + tiles + t], segment, 0)
        dhid_ref[rows] = dacc[...].astype(jnp.bfloat16)
    dvalue_ref[...] = dv32[0:length].astype(jnp.bfloat16)
    dsynth_ref[0] = df2[...].astype(jnp.bfloat16)

def attn_backward(tables, hidden, synth, values, dmix, mixed, lse):
    positions, width = hidden.shape
    length = values.shape[0]
    tq = tile_rows(positions)
    pairs = width // (2 * HD)
    blocks = synth.shape[1]
    per = BS // (2 * HD)
    tok = pl.BlockSpec((positions, 2 * HD), lambda p, t: (0, p))
    f2 = pl.BlockSpec((1, blocks, 2 * HD, BS), lambda p, t: (p // per, 0, p % per, 0))
    val = pl.BlockSpec((length, 2 * HD), lambda p, t: (0, p))
    return pl.pallas_call(
        functools.partial(attn_backward_body, tq),
        name="attn_backward",
        out_shape=(
            jax.ShapeDtypeStruct(synth.shape, jnp.bfloat16),
            jax.ShapeDtypeStruct((positions, width), jnp.bfloat16),
            jax.ShapeDtypeStruct((length, width), jnp.bfloat16),
        ),
        grid_spec=pltpu.PrefetchScalarGridSpec(
            num_scalar_prefetch=1,
            grid=(pairs,),
            in_specs=[tok, f2, val, tok, tok, tok],
            out_specs=[f2, tok, val],
            scratch_shapes=[
                pltpu.VMEM((2, blocks, 2 * HD, BS), jnp.bfloat16),
                pltpu.VMEM((length + BS, 2 * HD), jnp.float32),
                pltpu.VMEM((length + BS, 2 * HD), jnp.float32),
                pltpu.VMEM((2, tq, 2 * HD), jnp.bfloat16),
                pltpu.VMEM((tq, 2 * HD), jnp.float32),
                pltpu.VMEM((blocks, 2 * HD, BS), jnp.float32),
            ],
        ),
        compiler_params=pltpu.CompilerParams(vmem_limit_bytes=40 << 20, dimension_semantics=("arbitrary",)),
        cost_estimate=pl.CostEstimate(flops=10 * positions * length * width * 2, bytes_accessed=24 << 20, transcendentals=positions * length * 12),
    )(tables, hidden, synth, values, dmix, mixed, lse)


def exact(a, b, da=1, db=0):
    return lax.dot_general(a, b, (((da,), (db,)), ((), ())), precision=HIGHEST, preferred_element_type=jnp.float32)

def soap_update_body(ints, floats, got_ref, one_ref, two_ref, moment_ref, stat_ref, basis_ref,
                     new_master_ref, new_moment_ref, new_stat_ref, wide_ref, grad_ref, master_ref, sems):
    devices, slots, part = got_ref.shape[0], got_ref.shape[1], got_ref.shape[2]
    split = one_ref.shape[0]

    def master_copy(k, source):
        return pltpu.make_async_copy(source, master_ref.at[k], sems.at[k])

    for k in range(slots):
        block = ints[slots + k]

        @pl.when(block < split)
        def _():
            master_copy(k, one_ref.at[block]).start()

        @pl.when(block >= split)
        def _():
            master_copy(k, two_ref.at[block - split]).start()

    scale, mom_fix, sec_fix = floats[0], floats[1], floats[2]

    per = max(1, 8 // part)

    def join(d, carry):
        rows = pl.ds(pl.multiple_of(d * (per * part), per * part), per * part)
        for k in range(slots):
            pieces = [got_ref[d * per + i, k].astype(jnp.float32) for i in range(per)]
            grad_ref[k, rows, :] = pieces[0] if per == 1 else jnp.concatenate(pieces, axis=0)
        return carry

    lax.fori_loop(0, devices // per, join, 0)
    for k in range(slots):
        master_copy(k, one_ref.at[0]).wait()

    def prepare(k, carry):
        used = ints[k] > 0
        grad = jnp.where(used, grad_ref[k] * scale, 0.0)
        left, right = basis_ref[k, 0], basis_ref[k, 1]
        old_left, old_right = stat_ref[k, 0], stat_ref[k, 1]
        left_stat = BETA_SEC * old_left + (1 - BETA_SEC) * exact(grad, grad, 1, 1)
        right_stat = BETA_SEC * old_right + (1 - BETA_SEC) * exact(grad, grad, 0, 0)
        new_stat_ref[k, 0] = jnp.where(used, left_stat, old_left)
        new_stat_ref[k, 1] = jnp.where(used, right_stat, old_right)
        left_t = left.T
        for side, (turn, stat) in enumerate(((left_t, left_stat), (right.T, right_stat))):
            cross = exact(turn, stat)
            wide_ref[2 * k + side, :, 0:BS] = exact(cross, cross, 1, 1)
            wide_ref[2 * k + side, :, BS:] = cross
        momentum = BETA_MOM * moment_ref[k, 0] + (1 - BETA_MOM) * grad
        turned_grad = exact(exact(left_t, grad), right)
        turned_mom = exact(exact(left_t, momentum), right)
        old_second = moment_ref[k, 1]
        second = BETA_SEC * old_second + (1 - BETA_SEC) * turned_grad * turned_grad
        step = turned_mom / mom_fix / (jnp.sqrt(second / sec_fix) + EPSILON)
        update = exact(exact(left, step), right, 1, 1)
        master = master_ref[k].astype(jnp.float32)
        new_master_ref[k] = (master - floats[3 + k] * (update + DECAY * master)).astype(jnp.bfloat16)
        new_moment_ref[k, 0] = jnp.where(used, momentum, moment_ref[k, 0])
        new_moment_ref[k, 1] = jnp.where(used, second, old_second)
        return carry

    lax.fori_loop(0, slots, prepare, 0)


def soap_update(ints, floats, got, one, two, moments, stats, bases):
    slots = got.shape[1]
    whole = pl.BlockSpec(memory_space=VMEM)
    scalar = pl.BlockSpec(memory_space=pltpu.SMEM)
    anywhere = pl.BlockSpec(memory_space=pl.ANY)
    pair = jax.ShapeDtypeStruct(moments.shape, jnp.float32)
    return pl.pallas_call(
        soap_update_body,
        name="soap_update",
        out_shape=(
            jax.ShapeDtypeStruct((slots, BS, BS), jnp.bfloat16),
            pair,
            pair,
            jax.ShapeDtypeStruct((2 * slots, BS, 2 * BS), jnp.float32),
        ),
        in_specs=[scalar, scalar, whole, anywhere, anywhere] + [whole] * 3,
        out_specs=[whole] * 4,
        scratch_shapes=[
            VMEM((slots, BS, BS), jnp.float32),
            VMEM((slots, BS, BS), jnp.bfloat16),
            pltpu.SemaphoreType.DMA((slots,)),
        ],
        compiler_params=pltpu.CompilerParams(vmem_limit_bytes=48 << 20),
        cost_estimate=pl.CostEstimate(flops=slots * 12 * 6 * 2 * BS ** 3, bytes_accessed=slots * 14 * 4 * BS * BS, transcendentals=slots * BS * BS),
    )(ints, floats, got, one, two, moments, stats, bases)


def soap_bases_body(ints, given_ref, basis_ref, new_basis_ref, wide):
    slots = basis_ref.shape[0]
    count = 2 * slots
    wide[...] = given_ref[...]
    group = 128 // PANEL
    groups = count // group
    row = lax.broadcasted_iota(jnp.int32, (PANEL, 128), 0)
    lane = lax.broadcasted_iota(jnp.int32, (PANEL, 128), 1)
    unit = jnp.where(row == lane % PANEL, 1.0, 0.0)
    spot = lane // PANEL * PANEL
    for p in range(BS // PANEL):
        low = p * PANEL
        rows = slice(low, low + PANEL)
        schur, inverse, pivots = [], [], []
        for q in range(groups):
            schur.append(jnp.concatenate([wide[q * group + i, rows, low:low + PANEL] for i in range(group)], axis=1))
            inverse.append(unit)
            pivots.append(unit)

        for k in range(PANEL):
            below = row > k
            for q in range(groups):
                a, b = schur[q], inverse[q]
                column = jnp.take_along_axis(a, spot + k, axis=1)
                pivot = jnp.take_along_axis(jnp.broadcast_to(a[k:k + 1], (8, 128)), spot[:8] + k, axis=1)[0:1]
                factor = jnp.where(below, column * (1.0 / pivot), 0.0)
                schur[q] = a - factor * a[k:k + 1]
                inverse[q] = b - factor * b[k:k + 1]
                pivots[q] = jnp.where(row == k, pivot, pivots[q])
        for q in range(groups):
            whole = inverse[q] * lax.rsqrt(pivots[q])
            for i in range(group):
                m = q * group + i
                part = exact(whole[:, i * PANEL:(i + 1) * PANEL], wide[m, rows, :])
                wide[m, rows, :] = part
                if low + PANEL < BS:
                    wide[m, low + PANEL:, :] -= exact(part[:, low + PANEL:BS], part, 0, 0)

    def finish(k, carry):
        used = ints[k] > 0
        for side in range(2):
            new_basis_ref[k, side] = jnp.where(used, wide[2 * k + side, :, BS:].T, basis_ref[k, side])
        return carry

    lax.fori_loop(0, slots, finish, 0)


def soap_bases(ints, wide, bases):
    slots = bases.shape[0]
    whole = pl.BlockSpec(memory_space=VMEM)
    return pl.pallas_call(
        soap_bases_body,
        name="soap_bases",
        out_shape=jax.ShapeDtypeStruct(bases.shape, jnp.float32),
        in_specs=[pl.BlockSpec(memory_space=pltpu.SMEM), whole, whole],
        out_specs=whole,
        scratch_shapes=[VMEM(wide.shape, jnp.float32)],
        compiler_params=pltpu.CompilerParams(vmem_limit_bytes=48 << 20),
        cost_estimate=pl.CostEstimate(flops=slots * 4 * 6 * 2 * BS ** 3, bytes_accessed=slots * 8 * 4 * BS * BS, transcendentals=slots * BS * BS),
    )(ints, wide, bases)


def spread_pieces_body(split, weight_ref, one_ref, two_ref, lay):
    for i in range(one_ref.shape[1]):
        lay[:, i, :] = weight_ref[:, i * BS:(i + 1) * BS]
    one_ref[...] = lay[:split].astype(jnp.bfloat16)
    two_ref[...] = lay[split:].astype(jnp.bfloat16)


def spread_pieces(weights, split):
    count, rows = weights.shape[0], weights.shape[1] // BS
    whole = pl.BlockSpec(memory_space=VMEM)
    return pl.pallas_call(
        functools.partial(spread_pieces_body, split),
        name="spread_pieces",
        out_shape=(
            jax.ShapeDtypeStruct((split, rows, BS), jnp.bfloat16),
            jax.ShapeDtypeStruct((count - split, rows, BS), jnp.bfloat16),
        ),
        in_specs=[whole],
        out_specs=[whole] * 2,
        scratch_shapes=[VMEM((count, rows, BS), jnp.float32)],
        compiler_params=pltpu.CompilerParams(vmem_limit_bytes=32 << 20),
    )(weights)


def collect_body(slot_id, piece_ref, out_ref):
    rows = piece_ref.shape[1]

    def place(m, carry):
        piece = piece_ref[slot_id[m]].astype(jnp.float32)
        for i in range(rows):
            out_ref[pl.ds(m, 1), i * BS:(i + 1) * BS] = piece[i:i + 1]
        return carry

    lax.fori_loop(0, out_ref.shape[0], place, 0)


def collect(slot_id, pieces):
    count, rows = slot_id.shape[0], pieces.shape[1]
    whole = pl.BlockSpec(memory_space=VMEM)
    return pl.pallas_call(
        collect_body,
        name="collect",
        out_shape=jax.ShapeDtypeStruct((count, rows * BS), jnp.float32),
        in_specs=[pl.BlockSpec(memory_space=pltpu.SMEM), whole],
        out_specs=whole,
        compiler_params=pltpu.CompilerParams(vmem_limit_bytes=32 << 20),
    )(slot_id, pieces)


def partners(bits):
    row, seq = lax.axis_index("row"), lax.axis_index("seq")
    core, flags, peers = row % 2, [], []
    for k in range(bits):
        flag = row // 2 ** (k + 1) % 2
        flags.append(flag)
        peers.append((row + (1 - 2 * flag) * 2 ** (k + 1), seq))
    return core, (row + 1 - 2 * core, seq), flags, peers


def greet(devices):
    barrier = pltpu.get_barrier_semaphore()
    for device in devices:
        pl.semaphore_signal(barrier, inc=1, device_id=device, device_id_type=MESH)
    pl.semaphore_wait(barrier, len(devices))


def reduce_rows_body(bits, seqs, cut, given, *refs):
    in_refs, (out_ref, near, near_sum, *rest) = refs[:given], refs[given:]
    levels = 2 * bits
    halves = ((0, cut), (cut, out_ref.shape[0]))
    far, far_sum = rest[:levels], rest[levels:2 * levels - 2]
    spread, arrived, send, recv = rest[2 * levels - 2:]
    part = out_ref.shape[1]
    core, sibling, flags, peers = partners(bits)
    row, seq = lax.axis_index("row"), lax.axis_index("seq")
    beside = [(row, (seq + k) % seqs) for k in range(1, seqs)]
    greet([sibling, *peers, *beside])

    def copy(source, target, at, device):
        return pltpu.make_async_remote_copy(
            src_ref=source, dst_ref=target, send_sem=send.at[at], recv_sem=recv.at[at],
            device_id=device, device_id_type=MESH,
        )

    some = slice(None)
    every = (some,) * bits
    spans, at = ([], []), 0
    for ref in in_refs:
        for h, (low, high) in enumerate(halves):
            begin, end = max(low, at), min(high, at + ref.shape[0])
            if begin < end:
                spans[h].append((ref, begin - at, begin, end - begin))
        at += ref.shape[0]
    first = ([], [])
    for h in range(2):
        for ref, source, target, count in spans[h]:
            move = copy(
                ref.at[(pl.ds(source, count), *every, 1 - core)], near.at[pl.ds(target, count)],
                2 * bits + seqs - 1 + len(first[0]) + len(first[1]), sibling,
            )
            move.start()
            first[h].append(move)

    pending = [None, None]
    held = [None, None]
    dims = [list(range(bits - 1, -1, -1)) for _ in range(2)]
    orders = [list(range(bits)), list(range(bits - 1, -1, -1))]
    for step in range(bits + 1):
        for h, (low, high) in enumerate(halves):
            count = high - low
            last = step == bits
            if step == 0:
                for move, (ref, source, target, count_here) in zip(first[h], spans[h]):
                    move.wait()

                    def add(n, carry):
                        mine = ref[(n + source, *every, core)].astype(jnp.float32)
                        total = mine + near[n + target].astype(jnp.float32)
                        near_sum[n + target] = total.astype(jnp.bfloat16)
                        return carry

                    lax.fori_loop(0, count_here, add, 0)
                held[h] = near_sum.at[pl.ds(low, count)]
            else:
                bit = orders[h][step - 1]
                place = dims[h].index(bit)
                keep = (some,) * place + (flags[bit],)
                pending[h].wait()
                mine, other = held[h], far[(step - 1) * 2 + h]
                dims[h].pop(place)
                target = None if last else far_sum[(step - 1) * 2 + h]

                def add(n, carry):
                    total = mine[(n, *keep)].astype(jnp.float32) + other[n].astype(jnp.float32)
                    if target is None:
                        for s in range(seqs):
                            spread[s, low + n] = total[s * part:(s + 1) * part].astype(jnp.bfloat16)
                    else:
                        target[n] = total.astype(jnp.bfloat16)
                    return carry

                lax.fori_loop(0, count, add, 0)
                held[h] = target
            if not last:
                bit = orders[h][step]
                place = dims[h].index(bit)
                pending[h] = copy(
                    held[h].at[(slice(None),) * (place + 1) + (1 - flags[bit],)],
                    far[step * 2 + h], step * 2 + h, peers[bit],
                )
                pending[h].start()

    final = []
    for k, device in enumerate(beside):
        final.append(copy(spread.at[device[1]], arrived.at[k], levels + k, device))
        final[k].start()
    for move in final:
        move.wait()

    def finish(n, carry):
        total = spread[seq, n].astype(jnp.float32)
        for k in range(seqs - 1):
            total = total + arrived[k, n].astype(jnp.float32)
        out_ref[n] = total
        return carry

    lax.fori_loop(0, out_ref.shape[0], finish, 0)


def reduce_rows(terms, rows, seqs, collective):
    count = sum(term.shape[0] for term in terms)
    cut = (count + 1) // 2
    bits = (rows // 2).bit_length() - 1
    slab = BS // rows
    part = slab // seqs
    twos = (2,) * bits
    low = jnp.bfloat16
    whole = pl.BlockSpec(memory_space=VMEM)
    halves = (cut, count - cut)
    far = [VMEM((halves[h], *twos[k + 1:], slab, BS), low) for k in range(bits) for h in range(2)]
    far_sum = [VMEM((halves[h], *twos[k + 1:], slab, BS), low) for k in range(bits - 1) for h in range(2)]
    sems = 2 * bits + seqs - 1 + len(terms) + 1
    return pl.pallas_call(
        functools.partial(reduce_rows_body, bits, seqs, cut, len(terms)),
        name="reduce_rows",
        out_shape=jax.ShapeDtypeStruct((count, part, BS), jnp.float32),
        in_specs=[whole] * len(terms),
        out_specs=whole,
        scratch_shapes=[
            VMEM((count, *twos, slab, BS), low),
            VMEM((count, *twos, slab, BS), low),
            *far,
            *far_sum,
            VMEM((seqs, count, part, BS), low),
            VMEM((seqs - 1, count, part, BS), low),
            pltpu.SemaphoreType.DMA((sems,)),
            pltpu.SemaphoreType.DMA((sems,)),
        ],
        compiler_params=pltpu.CompilerParams(
            collective_id=collective, has_side_effects=True, vmem_limit_bytes=56 << 20
        ),
        cost_estimate=pl.CostEstimate(flops=count * BS * BS, bytes_accessed=4 * count * BS * BS, transcendentals=0),
    )(*[term.reshape(-1, *twos, 2, slab, BS) for term in terms])


def exchange_body(seqs, sources, spot_of, late_ref, early_ref, got_ref, square_ref, vector_ref, out, mine, send, recv):
    devices, own = got_ref.shape[0], got_ref.shape[1]
    split, part = late_ref.shape[0], late_ref.shape[1]
    me = lax.axis_index("row") * seqs + lax.axis_index("seq")
    barrier = pltpu.get_barrier_semaphore()

    def peer(k):
        to = (me + k) % devices
        return to, (to // seqs, to % seqs)

    def hello(k, carry):
        pl.semaphore_signal(barrier, inc=1, device_id=peer(k)[1], device_id_type=MESH)
        return carry

    lax.fori_loop(1, devices, hello, 0)

    def place(d, carry):
        for s in range(own):
            spot = spot_of[d * own + s]
            low = late_ref[jnp.minimum(spot, split - 1)].astype(jnp.bfloat16)
            high = early_ref[jnp.maximum(spot - split, 0)]
            out[d, s] = jnp.where(spot < split, low, high)
        return carry

    lax.fori_loop(0, devices, place, 0)

    def add(ref, total):
        def step(m, total):
            value = ref[m].astype(jnp.float32)
            return total + value * value

        return lax.fori_loop(0, ref.shape[0], step, total)

    total = add(early_ref, add(late_ref, jnp.zeros((part, BS), jnp.float32)))
    mine[...] = total[:, :128] + total[:, 128:]
    pl.semaphore_wait(barrier, devices - 1)

    def move(source, target, kind, k, device):
        return pltpu.make_async_remote_copy(
            src_ref=source, dst_ref=target, send_sem=send.at[kind, k], recv_sem=recv.at[kind, k],
            device_id=device, device_id_type=MESH,
        )

    def moves(k):
        to, device = peer(k)
        return (
            move(out.at[to], got_ref.at[me], 0, k, device),
            move(mine, square_ref.at[me], 1, k, device),
        )

    def launch(k, carry):
        for one in moves(k):
            one.start()
        return carry

    lax.fori_loop(1, devices, launch, 0)

    @pl.when(me < sources[0])
    def _():
        def tell(k, carry):
            move(late_ref.at[sources[1]], vector_ref.at[me], 2, k, peer(k)[1]).start()
            return carry

        lax.fori_loop(1, devices, tell, 0)
        vector_ref[me] = late_ref[sources[1]]

    got_ref[me] = out[me]
    square_ref[me] = mine[...]

    def finish(k, carry):
        for one in moves(k):
            one.wait()
        return carry

    lax.fori_loop(1, devices, finish, 0)

    @pl.when(me < sources[0])
    def _():
        def told(k, carry):
            move(late_ref.at[sources[1]], vector_ref.at[me], 2, k, peer(k)[1]).wait_send()
            return carry

        lax.fori_loop(1, devices, told, 0)

    for d in range(sources[0]):
        @pl.when(me != d)
        def _():
            k = (me - d + devices) % devices
            move(late_ref.at[sources[1]], vector_ref.at[d], 2, k, peer(k)[1]).wait_recv()


def exchange(spot_of, late, early, rows, seqs, vector_spot, vector_rows, collective):
    devices = rows * seqs
    part = late.shape[1]
    own = spot_of.shape[0] // devices
    told = -(-vector_rows // part)
    whole = pl.BlockSpec(memory_space=VMEM)
    return pl.pallas_call(
        functools.partial(exchange_body, seqs, (told, vector_spot)),
        name="exchange",
        out_shape=(
            jax.ShapeDtypeStruct((devices, own, part, BS), jnp.bfloat16),
            jax.ShapeDtypeStruct((devices, part, 128), jnp.float32),
            jax.ShapeDtypeStruct((told, part, BS), jnp.float32),
        ),
        in_specs=[pl.BlockSpec(memory_space=pltpu.SMEM), whole, whole],
        out_specs=[whole] * 3,
        scratch_shapes=[
            VMEM((devices, own, part, BS), jnp.bfloat16),
            VMEM((part, 128), jnp.float32),
            pltpu.SemaphoreType.DMA((3, devices)),
            pltpu.SemaphoreType.DMA((3, devices)),
        ],
        compiler_params=pltpu.CompilerParams(
            collective_id=collective, has_side_effects=True, vmem_limit_bytes=32 << 20
        ),
    )(spot_of, late, early)


def gather_rows_body(bits, seqs, cut, piece_ref, token_ref, full_ref, row_ref, *rest):
    near, send, recv, chain_send, chain_recv, own_sem = rest
    count, part = piece_ref.shape[0], piece_ref.shape[1]
    halves = ((0, cut), (cut, count))
    core, sibling, flags, peers = partners(bits)
    row, seq = lax.axis_index("row"), lax.axis_index("seq")
    beside = [(row, (seq + k) % seqs) for k in range(1, seqs)]
    greet([sibling, *peers, *beside])
    used = [0]

    def copy(source, target, device):
        at = used[0]
        used[0] += 1
        return pltpu.make_async_remote_copy(
            src_ref=source, dst_ref=target, send_sem=send.at[at], recv_sem=recv.at[at],
            device_id=device, device_id_type=MESH,
        )

    first = [copy(piece_ref, near.at[seq], device) for device in beside]
    for move in first:
        move.start()
    keep_tokens = pltpu.make_async_copy(token_ref, row_ref.at[seq], own_sem)
    keep_tokens.start()
    near[seq] = piece_ref[...]

    def hop(to_right, step):
        spot = seq - step if to_right else seq + step
        source = token_ref if step == 0 else row_ref.at[spot]
        side = 0 if to_right else 1
        return spot, pltpu.make_async_remote_copy(
            src_ref=source, dst_ref=row_ref.at[spot], send_sem=chain_send.at[side, step],
            recv_sem=chain_recv.at[spot], device_id=(row, seq + (1 if to_right else -1)), device_id_type=MESH,
        )

    def ends(to_right, step):
        there = seq - step >= 0 if to_right else seq + step < seqs
        onward = seq + 1 < seqs if to_right else seq - 1 >= 0
        return there, onward

    def chain(step):
        for to_right in (True, False):
            there, onward = ends(to_right, step)
            if step > 0:

                @pl.when(there)
                def _():
                    hop(to_right, step)[1].wait_recv()

            @pl.when(there & onward)
            def _():
                hop(to_right, step)[1].start()

    chain(0)
    for move in first:
        move.wait()

    def join(n, carry):
        pieces = [near[s, n] for s in range(seqs)]
        slab = jnp.concatenate([piece.astype(jnp.float32) for piece in pieces], axis=0)
        full_ref[(n, *flags[::-1], core)] = slab.astype(jnp.bfloat16)
        return carry

    lax.fori_loop(0, count, join, 0)

    orders = [list(range(bits)), list(range(bits - 1, -1, -1))]
    onward, across = [], []
    held = [[tuple(flags)] for _ in range(2)]

    def slab_at(h, place, at_core):
        low, high = halves[h]
        return full_ref.at[(pl.ds(low, high - low), *place[::-1], at_core)]

    def pass_on(h, place):
        spot = slab_at(h, place, core)
        move = copy(spot, spot, sibling)
        move.start()
        across.append(move)

    for h in range(2):
        pass_on(h, held[h][0])
    for level in range(bits):
        for h in range(2):
            bit = orders[h][level]
            moves = []
            for place in held[h]:
                spot = slab_at(h, place, core)
                move = copy(spot, spot, peers[bit])
                moves.append((place, move))
            for place, move in moves:
                move.start()
            onward.append((h, bit, moves))
        if level + 1 < seqs:
            chain(level + 1)
        for h, bit, moves in onward[-2:]:
            for place, move in moves:
                move.wait_recv()
                other = list(place)
                other[bit] = 1 - flags[bit]
                held[h].append(tuple(other))
                pass_on(h, tuple(other))
    for step in range(bits + 1, seqs):
        chain(step)
    for _, _, moves in onward:
        for _, move in moves:
            move.wait_send()
    for move in across:
        move.wait()
    keep_tokens.wait()
    for step in range(seqs):
        for to_right in (True, False):
            there, more = ends(to_right, step)

            @pl.when(there & more)
            def _():
                hop(to_right, step)[1].wait_send()


def gather_rows(pieces, tokens, rows, seqs, collective):
    count, part, _ = pieces.shape
    bits = (rows // 2).bit_length() - 1
    slab = BS // rows
    twos = (2,) * bits
    low = jnp.bfloat16
    whole = pl.BlockSpec(memory_space=VMEM)
    sems = seqs - 1 + 2 * (2 ** bits - 1) + 2 * 2 ** bits
    full, token_row = pl.pallas_call(
        functools.partial(gather_rows_body, bits, seqs, (count + 1) // 2),
        name="gather_rows",
        out_shape=(
            jax.ShapeDtypeStruct((count, *twos, 2, slab, BS), low),
            jax.ShapeDtypeStruct((seqs, *tokens.shape), low),
        ),
        in_specs=[whole] * 2,
        out_specs=[whole] * 2,
        scratch_shapes=[
            VMEM((seqs, count, part, BS), low),
            pltpu.SemaphoreType.DMA((sems,)),
            pltpu.SemaphoreType.DMA((sems,)),
            pltpu.SemaphoreType.DMA((2, seqs)),
            pltpu.SemaphoreType.DMA((seqs,)),
            pltpu.SemaphoreType.DMA,
        ],
        compiler_params=pltpu.CompilerParams(
            collective_id=collective, has_side_effects=True, vmem_limit_bytes=40 << 20
        ),
        cost_estimate=pl.CostEstimate(flops=0, bytes_accessed=4 * count * BS * BS, transcendentals=0),
    )(pieces, tokens)
    return full.reshape(count, BS, BS), token_row.reshape(-1, tokens.shape[1])


def block_bounds():
    model_blocks = D // BS
    first_end = model_blocks * model_blocks
    synth_end = first_end + model_blocks * (LEN // BS)
    value_end = synth_end + first_end
    output_end = value_end + first_end
    expand_end = output_end + model_blocks * (FF // BS)
    return (first_end, synth_end, value_end, output_end, expand_end)


def block_scales():
    first_end, synth_end, value_end, output_end, expand_end = block_bounds()
    spots = jnp.arange(BLOCKS)
    scales = jnp.where(
        spots < first_end,
        D ** (-0.5),
        jnp.where(
            spots < synth_end,
            3.0 * HD ** (-0.5),
            jnp.where(
                spots < value_end,
                D ** (-0.5),
                jnp.where(
                    spots < output_end,
                    4.0 * D ** (-0.5),
                    jnp.where(spots < expand_end, D ** (-0.5), FF ** (-0.5)),
                ),
            ),
        ),
    )
    return scales.astype(jnp.float32)


def silu_slope(values):
    sigma = jax.nn.sigmoid(values)
    return sigma * (1.0 + values * (1.0 - sigma))


def layer_norm(values, gain_row, shift_row):
    centered = values - jnp.mean(values, axis=-1, keepdims=True)
    inverse = lax.rsqrt(jnp.mean(centered * centered, axis=-1, keepdims=True) + NORM_EPS)
    normed = centered * inverse
    return (normed * gain_row + shift_row, normed, inverse)


def norm_back(grad_out, normed, inverse, gain_row):
    scaled = grad_out * gain_row
    return inverse * (
        scaled
        - jnp.mean(scaled, axis=-1, keepdims=True)
        - normed * jnp.mean(scaled * normed, axis=-1, keepdims=True)
    )


def apply_blocks(inputs, matrix):
    token_count = inputs.shape[0]
    row_blocks, col_blocks = (matrix.shape[0], matrix.shape[1])
    result = jnp.einsum(
        "nri,rcij->ncj",
        inputs.reshape(token_count, row_blocks, BS),
        matrix,
        preferred_element_type=jnp.float32,
    )
    return result.reshape(token_count, col_blocks * BS)


def back_blocks(grad_rows, matrix):
    token_count = grad_rows.shape[0]
    row_blocks, col_blocks = (matrix.shape[0], matrix.shape[1])
    result = jnp.einsum(
        "ncj,rcij->nri",
        grad_rows.reshape(token_count, col_blocks, BS),
        matrix,
        preferred_element_type=jnp.float32,
    )
    return result.reshape(token_count, row_blocks * BS)


def grad_blocks(inputs, grad_rows, row_blocks, col_blocks):
    token_count = inputs.shape[0]
    result = jnp.einsum(
        "nri,ncj->rcij",
        inputs.reshape(token_count, row_blocks, BS),
        grad_rows.reshape(token_count, col_blocks, BS),
        preferred_element_type=jnp.float32,
    )
    return result.reshape(row_blocks * col_blocks, BS, BS).astype(jnp.bfloat16)


def slot_table(owners, own_most, slot_total):
    block_count = owners.shape[0]
    block_index = jnp.arange(block_count, dtype=jnp.int32)
    same_owner = owners[:, None] == owners[None, :]
    earlier = block_index[None, :] < block_index[:, None]
    rank_within = jnp.sum(jnp.where(same_owner & earlier, 1, 0), axis=1).astype(jnp.int32)
    slot_id = owners * own_most + rank_within
    slot_hit = slot_id[:, None] == jnp.arange(slot_total, dtype=jnp.int32)[None, :]
    used = jnp.any(slot_hit, axis=0)
    block_of = jnp.sum(jnp.where(slot_hit, block_index[:, None], 0), axis=0)
    return (slot_id, used, block_of)


def vector_adam(vectors, vec_moments, grad_rows, mom_fix, sec_fix):
    first_moment = BETA_MOM * vec_moments[0] + (1 - BETA_MOM) * grad_rows
    second = BETA_SEC * vec_moments[1] + (1 - BETA_SEC) * grad_rows * grad_rows
    step_rows = first_moment / mom_fix / (jnp.sqrt(second / sec_fix) + EPSILON)
    return (vectors - VECTOR_RATE * step_rows, jnp.stack([first_moment, second]))


def local(
    tokens,
    cotangent,
    seg_ids,
    seg_lengths,
    weights,
    vectors,
    vec_moments,
    moments,
    stats,
    bases,
    owners,
    step_count,
):
    rows_here, positions, width = tokens.shape
    owner_count = lax.axis_size("row") * lax.axis_size("seq")
    own_most = moments.shape[0]
    slot_count = owner_count * own_most
    block_count = weights.shape[0]
    piece_rows = weights.shape[1] // BS
    model_blocks = D // BS
    hidden_blocks = FF // BS
    length_blocks = LEN // BS
    first_end, synth_end, value_end, output_end, expand_end = block_bounds()
    pieces_one, pieces_two = spread_pieces(weights, value_end)
    rows_total, seqs_total = lax.axis_size("row"), lax.axis_size("seq")
    gathered_two = lax.all_gather(pieces_two, AXES, axis=1, tiled=True)
    gathered_one, token_row = gather_rows(
        pieces_one, tokens.reshape(positions, width), rows_total, seqs_total, 3
    )

    def tiles_at(start_block, row_blocks, col_blocks):
        if start_block < value_end:
            part = gathered_one[start_block : start_block + row_blocks * col_blocks]
        else:
            start_block = start_block - value_end
            part = gathered_two[start_block : start_block + row_blocks * col_blocks]
        return part.reshape(row_blocks, col_blocks, BS, BS)

    first_w = tiles_at(0, model_blocks, model_blocks)
    synth_w = tiles_at(first_end, model_blocks, length_blocks)
    value_w = tiles_at(synth_end, model_blocks, model_blocks)
    output_w = tiles_at(value_end, model_blocks, model_blocks)
    expand_w = tiles_at(output_end, model_blocks, hidden_blocks)
    contract_w = tiles_at(expand_end, hidden_blocks, model_blocks)
    ffn_bias = vectors[5:].reshape(FF)

    slot_range = jnp.arange(seg_lengths.shape[1], dtype=jnp.int32)
    before = slot_range[None, :] < slot_range[:, None]
    starts = jnp.sum(jnp.where(before, seg_lengths[0][None, :], 0), axis=1)
    tq = tile_rows(positions)
    tile_ids = seg_ids[0].reshape(positions // tq, tq)
    offset = lax.axis_index("seq") * positions
    tables = jnp.concatenate(
        [
            starts,
            seg_lengths[0],
            tile_ids[:, 0],
            tile_ids[:, tq - 1] + 1,
            jnp.full((1,), offset, jnp.int32),
        ]
    ).astype(jnp.int32)

    inputs = tokens.reshape(positions, width).astype(jnp.float32)
    normed_one, hat_one, inv_one = layer_norm(inputs, vectors[0], vectors[1])
    first_in = normed_one.astype(jnp.bfloat16)
    first_pre = apply_blocks(first_in, first_w) + vectors[4]
    hidden = jax.nn.silu(first_pre).astype(jnp.bfloat16)
    normed_row, hat_row, _ = layer_norm(token_row.astype(jnp.float32), vectors[0], vectors[1])
    row_in = normed_row.astype(jnp.bfloat16)
    values = apply_blocks(row_in, value_w).astype(jnp.bfloat16)

    mixed_wide, log_total = attn_forward(tables, hidden, synth_w, values)
    mixed = mixed_wide.astype(jnp.bfloat16)
    middle = inputs + apply_blocks(mixed, output_w)
    normed_two, hat_two, inv_two = layer_norm(middle, vectors[2], vectors[3])
    second_in = normed_two.astype(jnp.bfloat16)
    expand_pre = apply_blocks(second_in, expand_w) + ffn_bias
    expanded = jax.nn.silu(expand_pre).astype(jnp.bfloat16)
    result = middle + apply_blocks(expanded, contract_w)
    layer_out = result.astype(jnp.bfloat16).reshape(rows_here, positions, width)
    back_out = cotangent.reshape(positions, width)
    grad_contract = grad_blocks(expanded, back_out, hidden_blocks, model_blocks)
    back_expanded = back_blocks(back_out, contract_w).astype(jnp.bfloat16)
    back_pre = (back_expanded.astype(jnp.float32) * silu_slope(expand_pre)).astype(jnp.bfloat16)
    grad_expand = grad_blocks(second_in, back_pre, model_blocks, hidden_blocks)
    grad_ffn_bias = jnp.sum(back_pre.astype(jnp.float32), axis=0)
    back_normed_two = back_blocks(back_pre, expand_w)
    grad_gain_two = jnp.sum(back_normed_two * hat_two, axis=0)
    grad_shift_two = jnp.sum(back_normed_two, axis=0)
    back_middle = back_out.astype(jnp.float32) + norm_back(
        back_normed_two, hat_two, inv_two, vectors[2]
    )
    back_attn = back_middle.astype(jnp.bfloat16)
    grad_output = grad_blocks(mixed, back_attn, model_blocks, model_blocks)
    back_mixed = back_blocks(back_attn, output_w).astype(jnp.bfloat16)
    early_terms = jnp.concatenate([grad_output, grad_expand, grad_contract], axis=0)
    early_terms, back_mixed = lax.optimization_barrier((early_terms, back_mixed))
    early_part = lax.psum_scatter(early_terms, "row", scatter_dimension=1, tiled=True)

    synth_grad, back_hidden, value_terms = attn_backward(
        tables, hidden, synth_w, values, back_mixed, mixed_wide, log_total
    )
    back_first = (back_hidden.astype(jnp.float32) * silu_slope(first_pre)).astype(jnp.bfloat16)
    grad_first = grad_blocks(first_in, back_first, model_blocks, model_blocks)
    grad_first_bias = jnp.sum(back_first.astype(jnp.float32), axis=0)
    grad_value = grad_blocks(row_in, value_terms, model_blocks, model_blocks)
    synth_grad = synth_grad.reshape(model_blocks * length_blocks, BS, BS)
    back_from_first = back_blocks(back_first, first_w)
    back_from_value = back_blocks(value_terms, value_w)
    grad_gain_one = jnp.sum(back_from_first * hat_one, axis=0) + jnp.sum(
        back_from_value * hat_row, axis=0
    )
    grad_shift_one = jnp.sum(back_from_first, axis=0) + jnp.sum(back_from_value, axis=0)
    vector_local = jnp.concatenate(
        [
            jnp.stack(
                [grad_gain_one, grad_shift_one, grad_gain_two, grad_shift_two, grad_first_bias]
            ),
            grad_ffn_bias.reshape(FF // D, D),
        ],
        axis=0,
    )
    vector_count = vectors.shape[0] * vectors.shape[1]
    vector_rows = vector_count // BS
    vector_block = jnp.pad(vector_local.reshape(vector_rows, BS), ((0, BS - vector_rows), (0, 0)))
    late_terms = [grad_first, grad_value, vector_block[None].astype(jnp.bfloat16), synth_grad]
    late_terms, early_part = lax.optimization_barrier((late_terms, early_part))
    early = lax.psum_scatter(early_part, "seq", scatter_dimension=1, tiled=True)
    late = reduce_rows(late_terms, rows_total, seqs_total, 1)
    slot_id, used, block_of = slot_table(owners, own_most, slot_count)
    device_index = lax.axis_index(AXES)
    mine_used = lax.dynamic_slice_in_dim(used, device_index * own_most, own_most)
    mine_block = lax.dynamic_slice_in_dim(block_of, device_index * own_most, own_most)
    vector_spot = 2 * first_end
    spot_of = jnp.where(
        block_of < first_end,
        block_of,
        jnp.where(
            block_of < synth_end,
            block_of + first_end + 1,
            jnp.where(block_of < value_end, block_of - synth_end + first_end, block_of + 1),
        ),
    )
    got, square_parts, vector_parts = exchange(
        spot_of, late, early, rows_total, seqs_total, vector_spot, vector_rows, 2
    )
    got, value_late = lax.optimization_barrier((got, value_terms))
    value_sums = lax.psum_scatter(value_late, "seq", scatter_dimension=0, tiled=True)
    back_normed_one = back_from_first + back_blocks(value_sums, value_w)
    back_inputs = back_middle + norm_back(back_normed_one, hat_one, inv_one, vectors[0])
    x_grad = back_inputs.reshape(rows_here, positions, width)

    vector_total = vector_parts.reshape(-1, BS)[:vector_rows].reshape(vectors.shape)
    grad_norm = jnp.sqrt(jnp.sum(square_parts))
    clip_max = math.sqrt(block_count * BS * BS + vectors.shape[0] * vectors.shape[1])
    scale = jnp.minimum(1.0, clip_max / grad_norm)
    step_value = step_count[0].astype(jnp.float32)
    mom_fix = 1.0 - jnp.power(BETA_MOM, step_value)
    sec_fix = 1.0 - jnp.power(BETA_SEC, step_value)
    new_vectors, new_vec_moments = vector_adam(
        vectors, vec_moments, vector_total * scale, mom_fix, sec_fix
    )
    rate_table = RATE_FACTOR * block_scales()
    slot_rates = jnp.sum(
        jnp.where(
            mine_block[:, None] == jnp.arange(block_count, dtype=jnp.int32)[None, :],
            rate_table[None, :],
            0.0,
        ),
        axis=1,
    )
    floats = jnp.concatenate([jnp.stack([scale, mom_fix, sec_fix]), slot_rates])
    ints = jnp.concatenate([mine_used.astype(jnp.int32), mine_block])
    new_master, new_moments, new_stats, wide = soap_update(
        ints, floats, got, gathered_one, gathered_two, moments, stats, bases
    )
    new_bases = soap_bases(ints, wide, bases)
    returned = lax.all_to_all(
        new_master.reshape(1, own_most, BS, BS), AXES, split_axis=2, concat_axis=0, tiled=True
    )
    new_weights = collect(slot_id, returned.reshape(slot_count, piece_rows, BS))
    return (
        layer_out,
        x_grad,
        new_weights,
        new_moments,
        new_stats,
        new_bases,
        new_vectors,
        new_vec_moments,
        grad_norm.reshape(1),
    )


def solution(mesh):
    placed = (
        P("row", "seq", None),
        P("row", "seq", None),
        P("row", "seq"),
        P("row", None),
        P(None, ("row", "seq")),
        P(),
        P(),
        P(("row", "seq"), None, None, None),
        P(("row", "seq"), None, None, None),
        P(("row", "seq"), None, None, None),
        P(),
        P(),
    )
    return jax.shard_map(
        local,
        mesh=mesh,
        in_specs=placed,
        out_specs=(
            P("row", "seq", None),
            P("row", "seq", None),
            P(None, ("row", "seq")),
            P(("row", "seq"), None, None, None),
            P(("row", "seq"), None, None, None),
            P(("row", "seq"), None, None, None),
            P(),
            P(),
            P(),
        ),
        check_vma=False,
    )
```

```python
import functools
import math

import jax
import jax.numpy as jnp
from jax import lax
from jax.experimental import pallas as pl
from jax.experimental.pallas import tpu as pltpu
from jax.sharding import PartitionSpec as P

D = 768
HEADS = 12
HD = 64
FF = 3072
LEN = 2048
BS = 256
BLOCKS = 123

BETA_MOM = 0.95
BETA_SEC = 0.95
EPSILON = 1e-08
DECAY = 0.01
VECTOR_RATE = 0.3
RATE_FACTOR = 2.0
NORM_EPS = 1e-05
NEG = -1e30
PANEL = 32
HIGHEST = lax.Precision.HIGHEST
VMEM = pltpu.VMEM
AXES = ("row", "seq")
MESH = pl.DeviceIdType.MESH


def dot_nn(a,b): return lax.dot_general(a,b,(((1,),(0,)),((),())),preferred_element_type=jnp.float32)
def dot_nt(a,b): return lax.dot_general(a,b,(((1,),(1,)),((),())),preferred_element_type=jnp.float32)

def tile_rows(positions): return min(positions,256)

def attn_forward_body(tq, tables, hid_ref, synth_ref, value_ref, mixed_ref, lse_ref, f2m, v32, lbuf):
    length = value_ref.shape[0]
    tiles = hid_ref.shape[0] // tq
    blocks = synth_ref.shape[0]
    segs = (tables.shape[0] - 2 * tiles - 1) // 2
    low_rows = lax.broadcasted_iota(jnp.int32, (2 * HD, BS), 0) < HD
    for j in range(blocks):
        tile = synth_ref[j]
        zero = jnp.zeros_like(tile)
        f2m[0, j] = jnp.where(low_rows, tile, zero)
        f2m[1, j] = jnp.where(low_rows, zero, tile)
    v32[0:length] = value_ref[...].astype(jnp.float32)
    v32[length:] = jnp.zeros((BS, 2 * HD), jnp.float32)
    left = lax.broadcasted_iota(jnp.int32, (tq, 2 * HD), 1) < HD
    lane = lax.broadcasted_iota(jnp.int32, (1, BS), 1)
    row = lax.broadcasted_iota(jnp.int32, (tq, 1), 0)
    for t in range(tiles):
        hid = hid_ref[t * tq:(t + 1) * tq]
        base = tables[2 * segs + 2 * tiles] + t * tq

        def segment(s, carry):
            start, count = tables[s], tables[segs + s]
            used = (count + BS - 1) // BS

            def scores(j, tops):
                keep = lane < count - j * BS
                out = []
                for h in range(2):
                    part = jnp.where(keep, dot_nn(hid, f2m[h, j]), NEG)
                    lbuf[h, j] = part
                    out.append(jnp.maximum(tops[h], jnp.maximum(part[:, :128], part[:, 128:])))
                return tuple(out)

            none = jnp.full((tq, 128), NEG, jnp.float32)
            tops = lax.fori_loop(0, used, scores, (none, none))
            tops = [jnp.max(top, axis=1, keepdims=True) for top in tops]

            def weigh(j, carried):
                value = v32[pl.ds(start + j * BS, BS), :].astype(jnp.bfloat16)
                out = []
                for h in range(2):
                    total, mix = carried[h]
                    part = jnp.exp(lbuf[h, j] - tops[h])
                    total = total + part[:, :128] + part[:, 128:]
                    mix = mix + dot_nn(part.astype(jnp.bfloat16), value)
                    out.append((total, mix))
                return tuple(out)

            blank = jnp.zeros((tq, 128), jnp.float32)
            pair = lax.fori_loop(0, used, weigh, ((blank, blank), (blank, blank)))
            sums = [jnp.sum(total, axis=1, keepdims=True) for total, _ in pair]
            mix = jnp.where(left, pair[0][1] / sums[0], pair[1][1] / sums[1])
            log = jnp.where(left, tops[0] + jnp.log(sums[0]), tops[1] + jnp.log(sums[1]))
            here = (row + base >= start) & (row + base < start + count)
            rows = pl.ds(t * tq, tq)
            mixed_ref[rows] = jnp.where(here, mix, mixed_ref[rows])
            lse_ref[rows] = jnp.where(here, log, lse_ref[rows])
            return carry

        lax.fori_loop(tables[2 * segs + t], tables[2 * segs + tiles + t], segment, 0)

def attn_forward(tables, hidden, synth, values):
    positions, width = hidden.shape
    length = values.shape[0]
    tq = tile_rows(positions)
    pairs = width // (2 * HD)
    blocks = length // BS
    per = BS // (2 * HD)
    return pl.pallas_call(
        functools.partial(attn_forward_body, tq),
        name="attn_forward",
        out_shape=(jax.ShapeDtypeStruct((positions, width), jnp.float32),) * 2,
        grid_spec=pltpu.PrefetchScalarGridSpec(
            num_scalar_prefetch=1,
            grid=(pairs,),
            in_specs=[
                pl.BlockSpec((positions, 2 * HD), lambda p, t: (0, p)),
                pl.BlockSpec((blocks, 2 * HD, BS), lambda p, t: (p // per, p % per, 0)),
                pl.BlockSpec((length, 2 * HD), lambda p, t: (0, p)),
            ],
            out_specs=[pl.BlockSpec((positions, 2 * HD), lambda p, t: (0, p))] * 2,
            scratch_shapes=[
                pltpu.VMEM((2, blocks, 2 * HD, BS), jnp.bfloat16),
                pltpu.VMEM((length + BS, 2 * HD), jnp.float32),
                pltpu.VMEM((2, blocks, tq, BS), jnp.float32),
            ],
        ),
        compiler_params=pltpu.CompilerParams(vmem_limit_bytes=40 << 20, dimension_semantics=("arbitrary",)),
        cost_estimate=pl.CostEstimate(flops=4 * positions * length * width * 2, bytes_accessed=12 << 20, transcendentals=positions * length * 12),
    )(tables, hidden, synth, values)

def attn_backward_body(tq, tables, hid_ref, synth_ref, value_ref, dmix_ref, mixed_ref, lse_ref,
                       dsynth_ref, dhid_ref, dvalue_ref, f2m, v32, dv32, dmm, dacc, df2):
    length = value_ref.shape[0]
    tiles = hid_ref.shape[0] // tq
    blocks = synth_ref.shape[0]
    segs = (tables.shape[0] - 2 * tiles - 1) // 2
    low_rows = lax.broadcasted_iota(jnp.int32, (2 * HD, BS), 0) < HD
    for j in range(blocks):
        tile = synth_ref[j]
        zero = jnp.zeros_like(tile)
        f2m[0, j] = jnp.where(low_rows, tile, zero)
        f2m[1, j] = jnp.where(low_rows, zero, tile)
    v32[0:length] = value_ref[...].astype(jnp.float32)
    v32[length:] = jnp.zeros((BS, 2 * HD), jnp.float32)
    dv32[...] = jnp.zeros_like(dv32)
    df2[...] = jnp.zeros_like(df2)
    left = lax.broadcasted_iota(jnp.int32, (tq, 2 * HD), 1) < HD
    lane = lax.broadcasted_iota(jnp.int32, (1, BS), 1)
    row = lax.broadcasted_iota(jnp.int32, (tq, 1), 0)
    for t in range(tiles):
        rows = pl.ds(t * tq, tq)
        hid = hid_ref[rows]
        hid_t = hid.astype(jnp.float32).T.astype(jnp.bfloat16)
        dmix32 = dmix_ref[rows].astype(jnp.float32)
        dmix_t = dmix32.T.astype(jnp.bfloat16)
        dot_pair = dmix32 * mixed_ref[rows]
        nil = jnp.zeros_like(dmix32)
        deltas = (
            jnp.sum(jnp.where(left, dot_pair, nil), axis=1, keepdims=True),
            jnp.sum(jnp.where(left, nil, dot_pair), axis=1, keepdims=True),
        )
        dmm[0] = jnp.where(left, dmix32, nil).astype(jnp.bfloat16)
        dmm[1] = jnp.where(left, nil, dmix32).astype(jnp.bfloat16)
        base = tables[2 * segs + 2 * tiles] + t * tq
        logs = lse_ref[rows]
        dacc[...] = jnp.zeros_like(dacc)

        def segment(s, carry):
            start, count = tables[s], tables[segs + s]
            used = (count + BS - 1) // BS
            here = (row + base >= start) & (row + base < start + count)
            lse = [jnp.where(here, logs[:, h * HD:h * HD + 1], -NEG) for h in range(2)]

            def block(j, carry):
                keep = lane < count - j * BS
                value = v32[pl.ds(start + j * BS, BS), :].astype(jnp.bfloat16)
                parts = []
                total = None
                for h in range(2):
                    synth = f2m[h, j]
                    prob = jnp.where(keep, jnp.exp(dot_nn(hid, synth) - lse[h]), 0.0)
                    dprob = dot_nt(dmm[h], value)
                    dlog = (prob * (dprob - deltas[h])).astype(jnp.bfloat16)
                    head = slice(h * HD, (h + 1) * HD)
                    df2[j, head, :] += dot_nn(hid_t[head], dlog)
                    back = dot_nt(dlog, synth)
                    total = back if total is None else total + back
                    parts.append(dot_nn(dmix_t[head], prob.astype(jnp.bfloat16)))
                dacc[...] += total
                dv32[pl.ds(start + j * BS, BS), :] += jnp.concatenate(parts, axis=0).T
                return carry

            lax.fori_loop(0, used, block, 0)
            return carry

        lax.fori_loop(tables[2 * segs + t], tables[2 * segs + tiles + t], segment, 0)
        dhid_ref[rows] = dacc[...].astype(jnp.bfloat16)
    dvalue_ref[...] = dv32[0:length].astype(jnp.bfloat16)
    dsynth_ref[...] = df2[...].astype(jnp.bfloat16)

def attn_backward(tables, hidden, synth, values, dmix, mixed, lse):
    positions, width = hidden.shape
    length = values.shape[0]
    tq = tile_rows(positions)
    pairs = width // (2 * HD)
    blocks = length // BS
    per = BS // (2 * HD)
    tok = pl.BlockSpec((positions, 2 * HD), lambda p, t: (0, p))
    f2 = pl.BlockSpec((blocks, 2 * HD, BS), lambda p, t: (p // per, p % per, 0))
    val = pl.BlockSpec((length, 2 * HD), lambda p, t: (0, p))
    return pl.pallas_call(
        functools.partial(attn_backward_body, tq),
        name="attn_backward",
        out_shape=(
            jax.ShapeDtypeStruct((pairs // per * blocks, BS, BS), jnp.bfloat16),
            jax.ShapeDtypeStruct((positions, width), jnp.bfloat16),
            jax.ShapeDtypeStruct((length, width), jnp.bfloat16),
        ),
        grid_spec=pltpu.PrefetchScalarGridSpec(
            num_scalar_prefetch=1,
            grid=(pairs,),
            in_specs=[tok, f2, val, tok, tok, tok],
            out_specs=[f2, tok, val],
            scratch_shapes=[
                pltpu.VMEM((2, blocks, 2 * HD, BS), jnp.bfloat16),
                pltpu.VMEM((length + BS, 2 * HD), jnp.float32),
                pltpu.VMEM((length + BS, 2 * HD), jnp.float32),
                pltpu.VMEM((2, tq, 2 * HD), jnp.bfloat16),
                pltpu.VMEM((tq, 2 * HD), jnp.float32),
                pltpu.VMEM((blocks, 2 * HD, BS), jnp.float32),
            ],
        ),
        compiler_params=pltpu.CompilerParams(vmem_limit_bytes=40 << 20, dimension_semantics=("arbitrary",)),
        cost_estimate=pl.CostEstimate(flops=10 * positions * length * width * 2, bytes_accessed=24 << 20, transcendentals=positions * length * 12),
    )(tables, hidden, synth, values, dmix, mixed, lse)


def exact(a, b, da=1, db=0):
    return lax.dot_general(a, b, (((da,), (db,)), ((), ())), precision=HIGHEST, preferred_element_type=jnp.float32)

def soap_update_body(ints, floats, got_ref, one_ref, two_ref, moment_ref, stat_ref, basis_ref,
                     new_master_ref, new_moment_ref, new_stat_ref, wide_ref, grad_ref, master_ref, sems):
    devices, slots, part = got_ref.shape[0], got_ref.shape[1], got_ref.shape[2]
    split = one_ref.shape[0]

    def master_copy(k, source):
        return pltpu.make_async_copy(source, master_ref.at[k], sems.at[k])

    for k in range(slots):
        block = ints[slots + k]

        @pl.when(block < split)
        def _():
            master_copy(k, one_ref.at[block]).start()

        @pl.when(block >= split)
        def _():
            master_copy(k, two_ref.at[block - split]).start()

    scale, mom_fix, sec_fix = floats[0], floats[1], floats[2]

    per = max(1, 8 // part)

    def join(d, carry):
        rows = pl.ds(pl.multiple_of(d * (per * part), per * part), per * part)
        for k in range(slots):
            pieces = [got_ref[d * per + i, k].astype(jnp.float32) for i in range(per)]
            grad_ref[k, rows, :] = pieces[0] if per == 1 else jnp.concatenate(pieces, axis=0)
        return carry

    lax.fori_loop(0, devices // per, join, 0)
    for k in range(slots):
        master_copy(k, one_ref.at[0]).wait()

    def prepare(k, carry):
        used = ints[k] > 0
        grad = jnp.where(used, grad_ref[k] * scale, 0.0)
        left, right = basis_ref[k, 0], basis_ref[k, 1]
        old_left, old_right = stat_ref[k, 0], stat_ref[k, 1]
        left_stat = BETA_SEC * old_left + (1 - BETA_SEC) * exact(grad, grad, 1, 1)
        right_stat = BETA_SEC * old_right + (1 - BETA_SEC) * exact(grad, grad, 0, 0)
        new_stat_ref[k, 0] = jnp.where(used, left_stat, old_left)
        new_stat_ref[k, 1] = jnp.where(used, right_stat, old_right)
        left_t = left.T
        for side, (turn, stat) in enumerate(((left_t, left_stat), (right.T, right_stat))):
            cross = exact(turn, stat)
            wide_ref[2 * k + side, :, 0:BS] = exact(cross, cross, 1, 1)
            wide_ref[2 * k + side, :, BS:] = cross
        momentum = BETA_MOM * moment_ref[k, 0] + (1 - BETA_MOM) * grad
        turned_grad = exact(exact(left_t, grad), right)
        turned_mom = exact(exact(left_t, momentum), right)
        old_second = moment_ref[k, 1]
        second = BETA_SEC * old_second + (1 - BETA_SEC) * turned_grad * turned_grad
        step = turned_mom / mom_fix / (jnp.sqrt(second / sec_fix) + EPSILON)
        update = exact(exact(left, step), right, 1, 1)
        master = master_ref[k].astype(jnp.float32)
        new_master_ref[k] = (master - floats[3 + k] * (update + DECAY * master)).astype(jnp.bfloat16)
        new_moment_ref[k, 0] = jnp.where(used, momentum, moment_ref[k, 0])
        new_moment_ref[k, 1] = jnp.where(used, second, old_second)
        return carry

    lax.fori_loop(0, slots, prepare, 0)


def soap_update(ints, floats, got, one, two, moments, stats, bases):
    slots = got.shape[1]
    whole = pl.BlockSpec(memory_space=VMEM)
    scalar = pl.BlockSpec(memory_space=pltpu.SMEM)
    anywhere = pl.BlockSpec(memory_space=pl.ANY)
    pair = jax.ShapeDtypeStruct(moments.shape, jnp.float32)
    return pl.pallas_call(
        soap_update_body,
        name="soap_update",
        out_shape=(
            jax.ShapeDtypeStruct((slots, BS, BS), jnp.bfloat16),
            pair,
            pair,
            jax.ShapeDtypeStruct((2 * slots, BS, 2 * BS), jnp.float32),
        ),
        in_specs=[scalar, scalar, whole, anywhere, anywhere] + [whole] * 3,
        out_specs=[whole] * 4,
        scratch_shapes=[
            VMEM((slots, BS, BS), jnp.float32),
            VMEM((slots, BS, BS), jnp.bfloat16),
            pltpu.SemaphoreType.DMA((slots,)),
        ],
        compiler_params=pltpu.CompilerParams(vmem_limit_bytes=48 << 20),
        cost_estimate=pl.CostEstimate(flops=slots * 12 * 6 * 2 * BS ** 3, bytes_accessed=slots * 14 * 4 * BS * BS, transcendentals=slots * BS * BS),
    )(ints, floats, got, one, two, moments, stats, bases)


def soap_bases_body(ints, given_ref, basis_ref, new_basis_ref, wide):
    slots = basis_ref.shape[0]
    count = 2 * slots
    wide[...] = given_ref[...]
    group = 128 // PANEL
    groups = count // group
    row = lax.broadcasted_iota(jnp.int32, (PANEL, 128), 0)
    lane = lax.broadcasted_iota(jnp.int32, (PANEL, 128), 1)
    unit = jnp.where(row == lane % PANEL, 1.0, 0.0)
    spot = lane // PANEL * PANEL
    for p in range(BS // PANEL):
        low = p * PANEL
        rows = slice(low, low + PANEL)
        schur, inverse, pivots = [], [], []
        for q in range(groups):
            schur.append(jnp.concatenate([wide[q * group + i, rows, low:low + PANEL] for i in range(group)], axis=1))
            inverse.append(unit)
            pivots.append(unit)

        for k in range(PANEL):
            below = row > k
            for q in range(groups):
                a, b = schur[q], inverse[q]
                column = jnp.take_along_axis(a, spot + k, axis=1)
                pivot = jnp.take_along_axis(jnp.broadcast_to(a[k:k + 1], (8, 128)), spot[:8] + k, axis=1)[0:1]
                factor = jnp.where(below, column * (1.0 / pivot), 0.0)
                schur[q] = a - factor * a[k:k + 1]
                inverse[q] = b - factor * b[k:k + 1]
                pivots[q] = jnp.where(row == k, pivot, pivots[q])
        for q in range(groups):
            whole = inverse[q] * lax.rsqrt(pivots[q])
            for i in range(group):
                m = q * group + i
                part = exact(whole[:, i * PANEL:(i + 1) * PANEL], wide[m, rows, :])
                wide[m, rows, :] = part
                if low + PANEL < BS:
                    wide[m, low + PANEL:, :] -= exact(part[:, low + PANEL:BS], part, 0, 0)

    def finish(k, carry):
        used = ints[k] > 0
        for side in range(2):
            new_basis_ref[k, side] = jnp.where(used, wide[2 * k + side, :, BS:].T, basis_ref[k, side])
        return carry

    lax.fori_loop(0, slots, finish, 0)


def soap_bases(ints, wide, bases):
    slots = bases.shape[0]
    whole = pl.BlockSpec(memory_space=VMEM)
    return pl.pallas_call(
        soap_bases_body,
        name="soap_bases",
        out_shape=jax.ShapeDtypeStruct(bases.shape, jnp.float32),
        in_specs=[pl.BlockSpec(memory_space=pltpu.SMEM), whole, whole],
        out_specs=whole,
        scratch_shapes=[VMEM(wide.shape, jnp.float32)],
        compiler_params=pltpu.CompilerParams(vmem_limit_bytes=48 << 20),
        cost_estimate=pl.CostEstimate(flops=slots * 4 * 6 * 2 * BS ** 3, bytes_accessed=slots * 8 * 4 * BS * BS, transcendentals=slots * BS * BS),
    )(ints, wide, bases)


def spread_pieces_body(order, weight_ref, one_ref, two_ref, lay):
    for i in range(one_ref.shape[1]):
        lay[:, i, :] = weight_ref[:, i * BS:(i + 1) * BS]
    at = 0
    for low, high in order:
        one_ref[at:at + high - low] = lay[low:high].astype(jnp.bfloat16)
        at += high - low
    two_ref[...] = lay[at:].astype(jnp.bfloat16)


def spread_pieces(weights, order):
    count, rows = weights.shape[0], weights.shape[1] // BS
    split = sum(high - low for low, high in order)
    whole = pl.BlockSpec(memory_space=VMEM)
    return pl.pallas_call(
        functools.partial(spread_pieces_body, order),
        name="spread_pieces",
        out_shape=(
            jax.ShapeDtypeStruct((split, rows, BS), jnp.bfloat16),
            jax.ShapeDtypeStruct((count - split, rows, BS), jnp.bfloat16),
        ),
        in_specs=[whole],
        out_specs=[whole] * 2,
        scratch_shapes=[VMEM((count, rows, BS), jnp.float32)],
        compiler_params=pltpu.CompilerParams(vmem_limit_bytes=32 << 20),
    )(weights)


def collect_body(slot_id, piece_ref, out_ref):
    rows = piece_ref.shape[1]

    def place(m, carry):
        piece = piece_ref[slot_id[m]].astype(jnp.float32)
        for i in range(rows):
            out_ref[pl.ds(m, 1), i * BS:(i + 1) * BS] = piece[i:i + 1]
        return carry

    lax.fori_loop(0, out_ref.shape[0], place, 0)


def collect(slot_id, pieces):
    count, rows = slot_id.shape[0], pieces.shape[1]
    whole = pl.BlockSpec(memory_space=VMEM)
    return pl.pallas_call(
        collect_body,
        name="collect",
        out_shape=jax.ShapeDtypeStruct((count, rows * BS), jnp.float32),
        in_specs=[pl.BlockSpec(memory_space=pltpu.SMEM), whole],
        out_specs=whole,
        compiler_params=pltpu.CompilerParams(vmem_limit_bytes=32 << 20),
    )(slot_id, pieces)


def partners(bits):
    row, seq = lax.axis_index("row"), lax.axis_index("seq")
    core, flags, peers = row % 2, [], []
    for k in range(bits):
        flag = row // 2 ** (k + 1) % 2
        flags.append(flag)
        peers.append((row + (1 - 2 * flag) * 2 ** (k + 1), seq))
    return core, (row + 1 - 2 * core, seq), flags, peers


def greet(devices):
    barrier = pltpu.get_barrier_semaphore()
    for device in devices:
        pl.semaphore_signal(barrier, inc=1, device_id=device, device_id_type=MESH)
    pl.semaphore_wait(barrier, len(devices))


def reduce_rows_body(bits, seqs, cut, given, *refs):
    in_refs, (out_ref, near, near_sum, *rest) = refs[:given], refs[given:]
    levels = 2 * bits
    halves = ((0, cut), (cut, out_ref.shape[0]))
    far, far_sum = rest[:levels], rest[levels:2 * levels - 2]
    spread, arrived, send, recv = rest[2 * levels - 2:]
    part = out_ref.shape[1]
    core, sibling, flags, peers = partners(bits)
    row, seq = lax.axis_index("row"), lax.axis_index("seq")
    beside = [(row, (seq + k) % seqs) for k in range(1, seqs)]
    greet([sibling, *peers, *beside])

    def copy(source, target, at, device):
        return pltpu.make_async_remote_copy(
            src_ref=source, dst_ref=target, send_sem=send.at[at], recv_sem=recv.at[at],
            device_id=device, device_id_type=MESH,
        )

    some = slice(None)
    every = (some,) * bits
    spans, at = ([], []), 0
    for ref in in_refs:
        for h, (low, high) in enumerate(halves):
            begin, end = max(low, at), min(high, at + ref.shape[0])
            if begin < end:
                spans[h].append((ref, begin - at, begin, end - begin))
        at += ref.shape[0]
    first = ([], [])
    for h in range(2):
        for ref, source, target, count in spans[h]:
            move = copy(
                ref.at[(pl.ds(source, count), *every, 1 - core)], near.at[pl.ds(target, count)],
                2 * bits + seqs - 1 + len(first[0]) + len(first[1]), sibling,
            )
            move.start()
            first[h].append(move)

    pending = [None, None]
    held = [None, None]
    dims = [list(range(bits - 1, -1, -1)) for _ in range(2)]
    orders = [list(range(bits)), list(range(bits - 1, -1, -1))]
    for step in range(bits + 1):
        for h, (low, high) in enumerate(halves):
            count = high - low
            last = step == bits
            if step == 0:
                for move, (ref, source, target, count_here) in zip(first[h], spans[h]):
                    move.wait()

                    def add(n, carry):
                        mine = ref[(n + source, *every, core)].astype(jnp.float32)
                        total = mine + near[n + target].astype(jnp.float32)
                        near_sum[n + target] = total.astype(jnp.bfloat16)
                        return carry

                    lax.fori_loop(0, count_here, add, 0)
                held[h] = near_sum.at[pl.ds(low, count)]
            else:
                bit = orders[h][step - 1]
                place = dims[h].index(bit)
                keep = (some,) * place + (flags[bit],)
                pending[h].wait()
                mine, other = held[h], far[(step - 1) * 2 + h]
                dims[h].pop(place)
                target = None if last else far_sum[(step - 1) * 2 + h]

                def add(n, carry):
                    total = mine[(n, *keep)].astype(jnp.float32) + other[n].astype(jnp.float32)
                    if target is None:
                        for s in range(seqs):
                            spread[s, low + n] = total[s * part:(s + 1) * part].astype(jnp.bfloat16)
                    else:
                        target[n] = total.astype(jnp.bfloat16)
                    return carry

                lax.fori_loop(0, count, add, 0)
                held[h] = target
            if not last:
                bit = orders[h][step]
                place = dims[h].index(bit)
                pending[h] = copy(
                    held[h].at[(slice(None),) * (place + 1) + (1 - flags[bit],)],
                    far[step * 2 + h], step * 2 + h, peers[bit],
                )
                pending[h].start()

    final = []
    for k, device in enumerate(beside):
        final.append(copy(spread.at[device[1]], arrived.at[k], levels + k, device))
        final[k].start()
    for move in final:
        move.wait()

    def finish(n, carry):
        total = spread[seq, n].astype(jnp.float32)
        for k in range(seqs - 1):
            total = total + arrived[k, n].astype(jnp.float32)
        out_ref[n] = total
        return carry

    lax.fori_loop(0, out_ref.shape[0], finish, 0)


def reduce_rows(terms, rows, seqs, collective):
    count = sum(term.shape[0] for term in terms)
    cut = (count + 1) // 2
    bits = (rows // 2).bit_length() - 1
    slab = BS // rows
    part = slab // seqs
    twos = (2,) * bits
    low = jnp.bfloat16
    whole = pl.BlockSpec(memory_space=VMEM)
    halves = (cut, count - cut)
    far = [VMEM((halves[h], *twos[k + 1:], slab, BS), low) for k in range(bits) for h in range(2)]
    far_sum = [VMEM((halves[h], *twos[k + 1:], slab, BS), low) for k in range(bits - 1) for h in range(2)]
    sems = 2 * bits + seqs - 1 + len(terms) + 1
    return pl.pallas_call(
        functools.partial(reduce_rows_body, bits, seqs, cut, len(terms)),
        name="reduce_rows",
        out_shape=jax.ShapeDtypeStruct((count, part, BS), jnp.float32),
        in_specs=[whole] * len(terms),
        out_specs=whole,
        scratch_shapes=[
            VMEM((count, *twos, slab, BS), low),
            VMEM((count, *twos, slab, BS), low),
            *far,
            *far_sum,
            VMEM((seqs, count, part, BS), low),
            VMEM((seqs - 1, count, part, BS), low),
            pltpu.SemaphoreType.DMA((sems,)),
            pltpu.SemaphoreType.DMA((sems,)),
        ],
        compiler_params=pltpu.CompilerParams(
            collective_id=collective, has_side_effects=True, vmem_limit_bytes=56 << 20
        ),
        cost_estimate=pl.CostEstimate(flops=count * BS * BS, bytes_accessed=4 * count * BS * BS, transcendentals=0),
    )(*[term.reshape(-1, *twos, 2, slab, BS) for term in terms])


def exchange_body(seqs, sources, spot_of, late_ref, early_ref, got_ref, square_ref, vector_ref, out, mine, send, recv):
    devices, own = got_ref.shape[0], got_ref.shape[1]
    split, part = late_ref.shape[0], late_ref.shape[1]
    me = lax.axis_index("row") * seqs + lax.axis_index("seq")
    barrier = pltpu.get_barrier_semaphore()

    def peer(k):
        to = (me + k) % devices
        return to, (to // seqs, to % seqs)

    def hello(k, carry):
        pl.semaphore_signal(barrier, inc=1, device_id=peer(k)[1], device_id_type=MESH)
        return carry

    lax.fori_loop(1, devices, hello, 0)

    def place(d, carry):
        for s in range(own):
            spot = spot_of[d * own + s]
            low = late_ref[jnp.minimum(spot, split - 1)].astype(jnp.bfloat16)
            high = early_ref[jnp.maximum(spot - split, 0)]
            out[d, s] = jnp.where(spot < split, low, high)
        return carry

    lax.fori_loop(0, devices, place, 0)

    def add(ref, total):
        def step(m, total):
            value = ref[m].astype(jnp.float32)
            return total + value * value

        return lax.fori_loop(0, ref.shape[0], step, total)

    total = add(early_ref, add(late_ref, jnp.zeros((part, BS), jnp.float32)))
    mine[...] = total[:, :128] + total[:, 128:]
    pl.semaphore_wait(barrier, devices - 1)

    def move(source, target, kind, k, device):
        return pltpu.make_async_remote_copy(
            src_ref=source, dst_ref=target, send_sem=send.at[kind, k], recv_sem=recv.at[kind, k],
            device_id=device, device_id_type=MESH,
        )

    def moves(k):
        to, device = peer(k)
        return (
            move(out.at[to], got_ref.at[me], 0, k, device),
            move(mine, square_ref.at[me], 1, k, device),
        )

    def launch(k, carry):
        for one in moves(k):
            one.start()
        return carry

    lax.fori_loop(1, devices, launch, 0)

    @pl.when(me < sources[0])
    def _():
        def tell(k, carry):
            move(late_ref.at[sources[1]], vector_ref.at[me], 2, k, peer(k)[1]).start()
            return carry

        lax.fori_loop(1, devices, tell, 0)
        vector_ref[me] = late_ref[sources[1]]

    got_ref[me] = out[me]
    square_ref[me] = mine[...]

    def finish(k, carry):
        for one in moves(k):
            one.wait()
        return carry

    lax.fori_loop(1, devices, finish, 0)

    @pl.when(me < sources[0])
    def _():
        def told(k, carry):
            move(late_ref.at[sources[1]], vector_ref.at[me], 2, k, peer(k)[1]).wait_send()
            return carry

        lax.fori_loop(1, devices, told, 0)

    for d in range(sources[0]):
        @pl.when(me != d)
        def _():
            k = (me - d + devices) % devices
            move(late_ref.at[sources[1]], vector_ref.at[d], 2, k, peer(k)[1]).wait_recv()


def exchange(spot_of, late, early, rows, seqs, vector_spot, vector_rows, collective):
    devices = rows * seqs
    part = late.shape[1]
    own = spot_of.shape[0] // devices
    told = -(-vector_rows // part)
    whole = pl.BlockSpec(memory_space=VMEM)
    return pl.pallas_call(
        functools.partial(exchange_body, seqs, (told, vector_spot)),
        name="exchange",
        out_shape=(
            jax.ShapeDtypeStruct((devices, own, part, BS), jnp.bfloat16),
            jax.ShapeDtypeStruct((devices, part, 128), jnp.float32),
            jax.ShapeDtypeStruct((told, part, BS), jnp.float32),
        ),
        in_specs=[pl.BlockSpec(memory_space=pltpu.SMEM), whole, whole],
        out_specs=[whole] * 3,
        scratch_shapes=[
            VMEM((devices, own, part, BS), jnp.bfloat16),
            VMEM((part, 128), jnp.float32),
            pltpu.SemaphoreType.DMA((3, devices)),
            pltpu.SemaphoreType.DMA((3, devices)),
        ],
        compiler_params=pltpu.CompilerParams(
            collective_id=collective, has_side_effects=True, vmem_limit_bytes=32 << 20
        ),
    )(spot_of, late, early)


def gather_rows_body(bits, seqs, cut, piece_ref, token_ref, full_ref, row_ref, *rest):
    near, send, recv, chain_send, chain_recv, own_sem = rest
    count, part = piece_ref.shape[0], piece_ref.shape[1]
    halves = ((0, cut), (cut, count))
    core, sibling, flags, peers = partners(bits)
    row, seq = lax.axis_index("row"), lax.axis_index("seq")
    beside = [(row, (seq + k) % seqs) for k in range(1, seqs)]
    greet([sibling, *peers, *beside])
    used = [0]

    def copy(source, target, device):
        at = used[0]
        used[0] += 1
        return pltpu.make_async_remote_copy(
            src_ref=source, dst_ref=target, send_sem=send.at[at], recv_sem=recv.at[at],
            device_id=device, device_id_type=MESH,
        )

    first = [copy(piece_ref, near.at[seq], device) for device in beside]
    for move in first:
        move.start()
    keep_tokens = pltpu.make_async_copy(token_ref, row_ref.at[seq], own_sem)
    keep_tokens.start()
    near[seq] = piece_ref[...]

    def hop(to_right, step):
        spot = seq - step if to_right else seq + step
        source = token_ref if step == 0 else row_ref.at[spot]
        side = 0 if to_right else 1
        return spot, pltpu.make_async_remote_copy(
            src_ref=source, dst_ref=row_ref.at[spot], send_sem=chain_send.at[side, step],
            recv_sem=chain_recv.at[spot], device_id=(row, seq + (1 if to_right else -1)), device_id_type=MESH,
        )

    def ends(to_right, step):
        there = seq - step >= 0 if to_right else seq + step < seqs
        onward = seq + 1 < seqs if to_right else seq - 1 >= 0
        return there, onward

    def chain(step):
        for to_right in (True, False):
            there, onward = ends(to_right, step)
            if step > 0:

                @pl.when(there)
                def _():
                    hop(to_right, step)[1].wait_recv()

            @pl.when(there & onward)
            def _():
                hop(to_right, step)[1].start()

    chain(0)
    for move in first:
        move.wait()

    def join(n, carry):
        pieces = [near[s, n] for s in range(seqs)]
        slab = jnp.concatenate([piece.astype(jnp.float32) for piece in pieces], axis=0)
        full_ref[(n, *flags[::-1], core)] = slab.astype(jnp.bfloat16)
        return carry

    lax.fori_loop(0, count, join, 0)

    orders = [list(range(bits)), list(range(bits - 1, -1, -1))]
    onward, across = [], []
    held = [[tuple(flags)] for _ in range(2)]

    def slab_at(h, place, at_core):
        low, high = halves[h]
        return full_ref.at[(pl.ds(low, high - low), *place[::-1], at_core)]

    def pass_on(h, place):
        spot = slab_at(h, place, core)
        move = copy(spot, spot, sibling)
        move.start()
        across.append(move)

    for h in range(2):
        pass_on(h, held[h][0])
    for level in range(bits):
        for h in range(2):
            bit = orders[h][level]
            moves = []
            for place in held[h]:
                spot = slab_at(h, place, core)
                move = copy(spot, spot, peers[bit])
                moves.append((place, move))
            for place, move in moves:
                move.start()
            onward.append((h, bit, moves))
        if level + 1 < seqs:
            chain(level + 1)
        for h, bit, moves in onward[-2:]:
            for place, move in moves:
                move.wait_recv()
                other = list(place)
                other[bit] = 1 - flags[bit]
                held[h].append(tuple(other))
                pass_on(h, tuple(other))
    for step in range(bits + 1, seqs):
        chain(step)
    for _, _, moves in onward:
        for _, move in moves:
            move.wait_send()
    for move in across:
        move.wait()
    keep_tokens.wait()
    for step in range(seqs):
        for to_right in (True, False):
            there, more = ends(to_right, step)

            @pl.when(there & more)
            def _():
                hop(to_right, step)[1].wait_send()


def gather_rows(pieces, tokens, rows, seqs, collective):
    count, part, _ = pieces.shape
    bits = (rows // 2).bit_length() - 1
    slab = BS // rows
    twos = (2,) * bits
    low = jnp.bfloat16
    whole = pl.BlockSpec(memory_space=VMEM)
    sems = seqs - 1 + 2 * (2 ** bits - 1) + 2 * 2 ** bits
    full, token_row = pl.pallas_call(
        functools.partial(gather_rows_body, bits, seqs, (count + 1) // 2),
        name="gather_rows",
        out_shape=(
            jax.ShapeDtypeStruct((count, *twos, 2, slab, BS), low),
            jax.ShapeDtypeStruct((seqs, *tokens.shape), low),
        ),
        in_specs=[whole] * 2,
        out_specs=[whole] * 2,
        scratch_shapes=[
            VMEM((seqs, count, part, BS), low),
            pltpu.SemaphoreType.DMA((sems,)),
            pltpu.SemaphoreType.DMA((sems,)),
            pltpu.SemaphoreType.DMA((2, seqs)),
            pltpu.SemaphoreType.DMA((seqs,)),
            pltpu.SemaphoreType.DMA,
        ],
        compiler_params=pltpu.CompilerParams(
            collective_id=collective, has_side_effects=True, vmem_limit_bytes=40 << 20
        ),
        cost_estimate=pl.CostEstimate(flops=0, bytes_accessed=4 * count * BS * BS, transcendentals=0),
    )(pieces, tokens)
    return full.reshape(count, BS, BS), token_row.reshape(-1, tokens.shape[1])


def normalize(values):
    centered = values - jnp.mean(values, axis=-1, keepdims=True)
    inverse = lax.rsqrt(jnp.mean(centered * centered, axis=-1, keepdims=True) + NORM_EPS)
    return centered * inverse, inverse


def column(k):
    return slice(k * BS, (k + 1) * BS)


def gate(values):
    return 1.0 / (1.0 + jnp.exp(-values))


def enter_body(spots, token_ref, row_ref, weight_ref, vector_ref, hid_ref, pre_ref, own_t_ref, value_ref, row_t_ref):
    first_at, value_at = spots
    wide = vector_ref.shape[1] // BS
    gain, shift, bias = vector_ref[0:1], vector_ref[1:2], vector_ref[4:5]

    def project(inputs, at, j):
        total = dot_nn(inputs[:, column(0)], weight_ref[at + j])
        for i in range(1, wide):
            total = total + dot_nn(inputs[:, column(i)], weight_ref[at + i * wide + j])
        return total

    def own(c, carry):
        rows = pl.ds(pl.multiple_of(c * BS, BS), BS)
        normed = normalize(token_ref[rows, :].astype(jnp.float32))[0] * gain + shift
        inputs = normed.astype(jnp.bfloat16)
        own_t_ref[:, rows] = normed.T.astype(jnp.bfloat16)
        for j in range(wide):
            pre = project(inputs, first_at, j) + bias[:, column(j)]
            pre_ref[rows, column(j)] = pre
            hid_ref[rows, column(j)] = (pre * gate(pre)).astype(jnp.bfloat16)
        return carry

    lax.fori_loop(0, token_ref.shape[0] // BS, own, 0)

    def whole_row(c, carry):
        rows = pl.ds(pl.multiple_of(c * BS, BS), BS)
        normed = normalize(row_ref[rows, :].astype(jnp.float32))[0] * gain + shift
        inputs = normed.astype(jnp.bfloat16)
        row_t_ref[:, rows] = normed.T.astype(jnp.bfloat16)
        for j in range(wide):
            value_ref[rows, column(j)] = project(inputs, value_at, j).astype(jnp.bfloat16)
        return carry

    lax.fori_loop(0, row_ref.shape[0] // BS, whole_row, 0)


def enter(tokens, token_row, weights, vectors, spots):
    positions, width = tokens.shape
    length = token_row.shape[0]
    whole = pl.BlockSpec(memory_space=VMEM)
    low = jnp.bfloat16
    return pl.pallas_call(
        functools.partial(enter_body, spots),
        name="enter",
        out_shape=(
            jax.ShapeDtypeStruct((positions, width), low),
            jax.ShapeDtypeStruct((positions, width), jnp.float32),
            jax.ShapeDtypeStruct((width, positions), low),
            jax.ShapeDtypeStruct((length, width), low),
            jax.ShapeDtypeStruct((width, length), low),
        ),
        in_specs=[whole] * 4,
        out_specs=[whole] * 5,
        compiler_params=pltpu.CompilerParams(vmem_limit_bytes=40 << 20),
        cost_estimate=pl.CostEstimate(flops=2 * (positions + length) * width * width, bytes_accessed=24 << 20, transcendentals=positions * width),
    )(tokens, token_row, weights, vectors)


def middle_body(token_ref, cotangent_ref, mixed_ref, output_ref, up_a, up_b, up_c, down_ref, vector_ref,
                out_ref, terms_ref, dmix_ref, dmiddle_ref, sums_ref, bias_ref,
                middle, normed_in, normed_t, back_t, total, back, made, made_output, sems, output_sem):
    f, last = pl.program_id(0), pl.num_programs(0) - 1
    ups = (up_a, up_b, up_c)
    wide = len(ups)
    first_up, first_down = wide * wide, wide * wide + wide * (last + 1)
    slot = f % 2

    @pl.when(f == 0)
    def _():
        mixed = mixed_ref[...].astype(jnp.bfloat16)
        for j in range(wide):
            part = token_ref[:, column(j)].astype(jnp.float32)
            for i in range(wide):
                part = part + dot_nn(mixed[:, column(i)], output_ref[i * wide + j])
            middle[:, column(j)] = part
        hat, _ = normalize(middle[...])
        inputs = hat * vector_ref[2:3] + vector_ref[3:4]
        normed_in[...] = inputs.astype(jnp.bfloat16)
        normed_t[...] = inputs.T.astype(jnp.bfloat16)
        total[...] = middle[...]
        back[...] = jnp.zeros_like(back)

    def copies(at, step):
        out = []
        for i in range(wide):
            out.append(pltpu.make_async_copy(made.at[at, i], terms_ref.at[first_up + i * (last + 1) + step], sems.at[at, i]))
        for j in range(wide):
            out.append(pltpu.make_async_copy(made.at[at, wide + j], terms_ref.at[first_down + step * wide + j], sems.at[at, wide + j]))
        return out

    @pl.when(f >= 2)
    def _():
        for move in copies(slot, f - 2):
            move.wait()

    inputs = normed_in[...]
    pre = vector_ref[pl.ds(5 + f // wide, 1), pl.ds(pl.multiple_of(f % wide * BS, BS), BS)]
    for i in range(wide):
        pre = pre + dot_nn(inputs[:, column(i)], ups[i][0])
    share = gate(pre)
    hidden = pre * share
    low_hidden = hidden.astype(jnp.bfloat16)
    hidden_t = hidden.T.astype(jnp.bfloat16)
    dhidden = None
    for j in range(wide):
        total[:, column(j)] += dot_nn(low_hidden, down_ref[j])
        made[slot, wide + j] = dot_nn(hidden_t, cotangent_ref[:, column(j)]).astype(jnp.bfloat16)
        part = dot_nt(cotangent_ref[:, column(j)], down_ref[j])
        dhidden = part if dhidden is None else dhidden + part
    dhidden = dhidden.astype(jnp.bfloat16).astype(jnp.float32)
    dpre = (dhidden * (share * (1.0 + pre * (1.0 - share)))).astype(jnp.bfloat16)
    bias_ref[pl.ds(f, 1), :] = jnp.sum(dpre.astype(jnp.float32), axis=0, keepdims=True)
    for i in range(wide):
        made[slot, i] = dot_nn(normed_t[column(i), :], dpre).astype(jnp.bfloat16)
        back[:, column(i)] += dot_nt(dpre, ups[i][0])
    for move in copies(slot, f):
        move.start()

    @pl.when(f == last)
    def _():
        out_ref[...] = total[...].astype(jnp.bfloat16)
        hat, inverse = normalize(middle[...])
        dnormed = back[...]
        sums_ref[...] = jnp.zeros_like(sums_ref)
        sums_ref[0:1] = jnp.sum(dnormed * hat, axis=0, keepdims=True)
        sums_ref[1:2] = jnp.sum(dnormed, axis=0, keepdims=True)
        scaled = dnormed * vector_ref[2:3]
        dmiddle = cotangent_ref[...].astype(jnp.float32) + inverse * (
            scaled
            - jnp.mean(scaled, axis=-1, keepdims=True)
            - hat * jnp.mean(scaled * hat, axis=-1, keepdims=True)
        )
        dmiddle_ref[...] = dmiddle
        low = dmiddle.astype(jnp.bfloat16)
        back_t[...] = mixed_ref[...].T.astype(jnp.bfloat16)
        for i in range(wide):
            part = None
            for j in range(wide):
                made_output[i * wide + j] = dot_nn(back_t[column(i), :], low[:, column(j)]).astype(jnp.bfloat16)
                term = dot_nt(low[:, column(j)], output_ref[i * wide + j])
                part = term if part is None else part + term
            dmix_ref[:, column(i)] = part.astype(jnp.bfloat16)
        move = pltpu.make_async_copy(made_output, terms_ref.at[0:wide * wide], output_sem)
        move.start()
        for one in copies(1 - slot, f - 1):
            one.wait()
        for one in copies(slot, f):
            one.wait()
        move.wait()


def middle_stage(tokens, cotangent, mixed, weights, vectors):
    positions, width = tokens.shape
    wide = width // BS
    steps = (weights.shape[0] - wide * wide) // (2 * wide)
    assert (wide * wide + wide * steps) % wide == 0
    low = jnp.bfloat16
    tok = pl.BlockSpec((positions, width), lambda f: (0, 0))

    def up(i):
        return pl.BlockSpec((1, BS, BS), lambda f: (wide * wide + i * steps + f, 0, 0))

    return pl.pallas_call(
        middle_body,
        name="middle_stage",
        out_shape=(
            jax.ShapeDtypeStruct((positions, width), low),
            jax.ShapeDtypeStruct(weights.shape, low),
            jax.ShapeDtypeStruct((positions, width), low),
            jax.ShapeDtypeStruct((positions, width), jnp.float32),
            jax.ShapeDtypeStruct((8, width), jnp.float32),
            jax.ShapeDtypeStruct((steps, BS), jnp.float32),
        ),
        grid=(steps,),
        in_specs=[
            tok,
            tok,
            tok,
            pl.BlockSpec((wide * wide, BS, BS), lambda f: (0, 0, 0)),
            up(0),
            up(1),
            up(2),
            pl.BlockSpec((wide, BS, BS), lambda f: (wide + steps + f, 0, 0)),
            pl.BlockSpec(vectors.shape, lambda f: (0, 0)),
        ],
        out_specs=[
            tok,
            pl.BlockSpec(memory_space=pl.ANY),
            tok,
            tok,
            pl.BlockSpec((8, width), lambda f: (0, 0)),
            pl.BlockSpec((steps, BS), lambda f: (0, 0)),
        ],
        scratch_shapes=[
            VMEM((positions, width), jnp.float32),
            VMEM((positions, width), low),
            VMEM((width, positions), low),
            VMEM((width, positions), low),
            VMEM((positions, width), jnp.float32),
            VMEM((positions, width), jnp.float32),
            VMEM((2, 2 * wide, BS, BS), low),
            VMEM((wide * wide, BS, BS), low),
            pltpu.SemaphoreType.DMA((2, 2 * wide)),
            pltpu.SemaphoreType.DMA,
        ],
        compiler_params=pltpu.CompilerParams(vmem_limit_bytes=48 << 20, dimension_semantics=("arbitrary",)),
        cost_estimate=pl.CostEstimate(flops=36 * positions * width * width, bytes_accessed=40 << 20, transcendentals=positions * width * 4),
    )(tokens, cotangent, mixed, weights, weights, weights, weights, weights, vectors)


def leave_body(spots, dhid_ref, pre_ref, own_t_ref, token_ref, row_ref, row_t_ref, dvalue_ref, weight_ref, vector_ref, sums_ref, bias_ref,
               dfirst_ref, dweight_ref, block_ref, back_ref, dpre_all, rows32):
    first_at, value_at = spots
    positions, width = dhid_ref.shape
    wide = width // BS
    sums = [jnp.zeros((1, width), jnp.float32) for _ in range(3)]

    def unproject(grads, at, i):
        total = None
        for j in range(wide):
            part = dot_nt(grads[:, column(j)], weight_ref[at + i * wide + j])
            total = part if total is None else total + part
        return total

    def own(c, sums):
        rows = pl.ds(pl.multiple_of(c * BS, BS), BS)
        pre = pre_ref[rows, :]
        share = gate(pre)
        dpre = (dhid_ref[rows, :].astype(jnp.float32) * (share * (1.0 + pre * (1.0 - share)))).astype(jnp.bfloat16)
        dpre_all[rows, :] = dpre
        hat, _ = normalize(token_ref[rows, :].astype(jnp.float32))
        back = jnp.concatenate([unproject(dpre, first_at, i) for i in range(wide)], axis=1)
        back_ref[rows, :] = back
        return (
            sums[0] + jnp.sum(back * hat, axis=0, keepdims=True),
            sums[1] + jnp.sum(back, axis=0, keepdims=True),
            sums[2] + jnp.sum(dpre.astype(jnp.float32), axis=0, keepdims=True),
        )

    sums = lax.fori_loop(0, positions // BS, own, tuple(sums))

    def whole_row(c, sums):
        rows = pl.ds(pl.multiple_of(c * BS, BS), BS)
        dvalue = dvalue_ref[rows, :]
        hat, _ = normalize(row_ref[rows, :].astype(jnp.float32))
        back = jnp.concatenate([unproject(dvalue, value_at, i) for i in range(wide)], axis=1)
        return (
            sums[0] + jnp.sum(back * hat, axis=0, keepdims=True),
            sums[1] + jnp.sum(back, axis=0, keepdims=True),
            sums[2],
        )

    sums = lax.fori_loop(0, row_ref.shape[0] // BS, whole_row, sums)
    for i in range(wide):
        for j in range(wide):
            dfirst_ref[i * wide + j] = dot_nn(own_t_ref[column(i), :], dpre_all[:, column(j)]).astype(jnp.bfloat16)
            dweight_ref[i * wide + j] = dot_nn(row_t_ref[column(i), :], dvalue_ref[:, column(j)]).astype(jnp.bfloat16)
    rows32[...] = jnp.zeros_like(rows32)
    lines = (sums[0], sums[1], sums_ref[0:1], sums_ref[1:2], sums[2])
    for r, line in enumerate(lines):
        for i in range(wide):
            rows32[r * wide + i:r * wide + i + 1, :] = line[:, column(i)]
    at = len(lines) * wide
    rows32[at:at + bias_ref.shape[0], :] = bias_ref[...]
    block_ref[0] = jnp.zeros_like(block_ref[0])
    block_ref[0, 0:rows32.shape[0], :] = rows32[...].astype(jnp.bfloat16)


def leave(dhid, pre, own_t, tokens, token_row, row_t, dvalue, weights, vectors, sums, bias, spots):
    positions, width = dhid.shape
    wide = width // BS
    whole = pl.BlockSpec(memory_space=VMEM)
    low = jnp.bfloat16
    tall = -(-(5 * wide + bias.shape[0]) // 16) * 16
    return pl.pallas_call(
        functools.partial(leave_body, spots),
        name="leave",
        out_shape=(
            jax.ShapeDtypeStruct((wide * wide, BS, BS), low),
            jax.ShapeDtypeStruct((wide * wide, BS, BS), low),
            jax.ShapeDtypeStruct((1, BS, BS), low),
            jax.ShapeDtypeStruct((positions, width), jnp.float32),
        ),
        in_specs=[whole] * 11,
        out_specs=[whole] * 4,
        scratch_shapes=[VMEM((positions, width), low), VMEM((tall, BS), jnp.float32)],
        compiler_params=pltpu.CompilerParams(vmem_limit_bytes=48 << 20),
        cost_estimate=pl.CostEstimate(flops=4 * (positions + token_row.shape[0]) * width * width, bytes_accessed=24 << 20, transcendentals=positions * width),
    )(dhid, pre, own_t, tokens, token_row, row_t, dvalue, weights, vectors, sums, bias)


def finish_body(value_at, dvalue_ref, first_ref, dmiddle_ref, token_ref, weight_ref, vector_ref, out_ref):
    wide = vector_ref.shape[1] // BS

    def chunk(c, carry):
        rows = pl.ds(pl.multiple_of(c * BS, BS), BS)
        dvalue = dvalue_ref[rows, :]
        parts = []
        for i in range(wide):
            total = first_ref[rows, column(i)]
            for j in range(wide):
                total = total + dot_nt(dvalue[:, column(j)], weight_ref[value_at + i * wide + j])
            parts.append(total)
        scaled = jnp.concatenate(parts, axis=1) * vector_ref[0:1]
        hat, inverse = normalize(token_ref[rows, :].astype(jnp.float32))
        out_ref[rows, :] = dmiddle_ref[rows, :] + inverse * (
            scaled
            - jnp.mean(scaled, axis=-1, keepdims=True)
            - hat * jnp.mean(scaled * hat, axis=-1, keepdims=True)
        )
        return carry

    lax.fori_loop(0, token_ref.shape[0] // BS, chunk, 0)


def finish_inputs(dvalue, from_first, dmiddle, tokens, weights, vectors, value_at):
    whole = pl.BlockSpec(memory_space=VMEM)
    positions, width = tokens.shape
    return pl.pallas_call(
        functools.partial(finish_body, value_at),
        name="finish_inputs",
        out_shape=jax.ShapeDtypeStruct((positions, width), jnp.float32),
        in_specs=[whole] * 6,
        out_specs=whole,
        compiler_params=pltpu.CompilerParams(vmem_limit_bytes=40 << 20),
        cost_estimate=pl.CostEstimate(flops=2 * positions * width * width, bytes_accessed=12 << 20, transcendentals=0),
    )(dvalue, from_first, dmiddle, tokens, weights, vectors)


def block_bounds():
    model_blocks = D // BS
    first_end = model_blocks * model_blocks
    synth_end = first_end + model_blocks * (LEN // BS)
    value_end = synth_end + first_end
    output_end = value_end + first_end
    expand_end = output_end + model_blocks * (FF // BS)
    return (first_end, synth_end, value_end, output_end, expand_end)


def block_scales():
    first_end, synth_end, value_end, output_end, expand_end = block_bounds()
    spots = jnp.arange(BLOCKS)
    scales = jnp.where(
        spots < first_end,
        D ** (-0.5),
        jnp.where(
            spots < synth_end,
            3.0 * HD ** (-0.5),
            jnp.where(
                spots < value_end,
                D ** (-0.5),
                jnp.where(
                    spots < output_end,
                    4.0 * D ** (-0.5),
                    jnp.where(spots < expand_end, D ** (-0.5), FF ** (-0.5)),
                ),
            ),
        ),
    )
    return scales.astype(jnp.float32)


def slot_table(owners, own_most, slot_total):
    block_count = owners.shape[0]
    block_index = jnp.arange(block_count, dtype=jnp.int32)
    same_owner = owners[:, None] == owners[None, :]
    earlier = block_index[None, :] < block_index[:, None]
    rank_within = jnp.sum(jnp.where(same_owner & earlier, 1, 0), axis=1).astype(jnp.int32)
    slot_id = owners * own_most + rank_within
    slot_hit = slot_id[:, None] == jnp.arange(slot_total, dtype=jnp.int32)[None, :]
    used = jnp.any(slot_hit, axis=0)
    block_of = jnp.sum(jnp.where(slot_hit, block_index[:, None], 0), axis=0)
    return (slot_id, used, block_of)


def vector_adam(vectors, vec_moments, grad_rows, mom_fix, sec_fix):
    first_moment = BETA_MOM * vec_moments[0] + (1 - BETA_MOM) * grad_rows
    second = BETA_SEC * vec_moments[1] + (1 - BETA_SEC) * grad_rows * grad_rows
    step_rows = first_moment / mom_fix / (jnp.sqrt(second / sec_fix) + EPSILON)
    return (vectors - VECTOR_RATE * step_rows, jnp.stack([first_moment, second]))


def local(
    tokens,
    cotangent,
    seg_ids,
    seg_lengths,
    weights,
    vectors,
    vec_moments,
    moments,
    stats,
    bases,
    owners,
    step_count,
):
    rows_here, positions, width = tokens.shape
    owner_count = lax.axis_size("row") * lax.axis_size("seq")
    own_most = moments.shape[0]
    slot_count = owner_count * own_most
    block_count = weights.shape[0]
    piece_rows = weights.shape[1] // BS
    first_end, synth_end, value_end, _, _ = block_bounds()
    synth_count = synth_end - first_end
    tokens = tokens.reshape(positions, width)
    pieces_one, pieces_two = spread_pieces(
        weights, ((first_end, synth_end), (0, first_end), (synth_end, value_end))
    )
    spots = (synth_count, synth_end)
    rows_total, seqs_total = lax.axis_size("row"), lax.axis_size("seq")
    gathered_one, token_row = gather_rows(pieces_one, tokens, rows_total, seqs_total, 3)
    gathered_one, pieces_two = lax.optimization_barrier((gathered_one, pieces_two))
    gathered_two = lax.all_gather(pieces_two, AXES, axis=1, tiled=True)

    slot_range = jnp.arange(seg_lengths.shape[1], dtype=jnp.int32)
    before = slot_range[None, :] < slot_range[:, None]
    starts = jnp.sum(jnp.where(before, seg_lengths[0][None, :], 0), axis=1)
    tq = tile_rows(positions)
    tile_ids = seg_ids[0].reshape(positions // tq, tq)
    offset = lax.axis_index("seq") * positions
    tables = jnp.concatenate(
        [
            starts,
            seg_lengths[0],
            tile_ids[:, 0],
            tile_ids[:, tq - 1] + 1,
            jnp.full((1,), offset, jnp.int32),
        ]
    ).astype(jnp.int32)

    hidden, first_pre, own_t, values, row_t = enter(tokens, token_row, gathered_one, vectors, spots)
    mixed, log_total = attn_forward(tables, hidden, gathered_one, values)
    layer_out, early_terms, back_mixed, back_middle, norm_sums, grad_ffn_bias = middle_stage(
        tokens, cotangent.reshape(positions, width), mixed, gathered_two, vectors
    )
    early_part = lax.psum_scatter(early_terms, "row", scatter_dimension=1, tiled=True)
    synth_grad, back_hidden, value_terms = attn_backward(
        tables, hidden, gathered_one, values, back_mixed, mixed, log_total
    )
    grad_first, grad_value, vector_block, back_from_first = leave(
        back_hidden,
        first_pre,
        own_t,
        tokens,
        token_row,
        row_t,
        value_terms,
        gathered_one,
        vectors,
        norm_sums,
        grad_ffn_bias,
        spots,
    )
    late_terms = [grad_first, grad_value, vector_block, synth_grad]
    late_terms, early_part = lax.optimization_barrier((late_terms, early_part))
    early = lax.psum_scatter(early_part, "seq", scatter_dimension=1, tiled=True)
    vector_rows = vectors.shape[0] * vectors.shape[1] // BS
    late = reduce_rows(late_terms, rows_total, seqs_total, 1)
    slot_id, used, block_of = slot_table(owners, own_most, slot_count)
    device_index = lax.axis_index(AXES)
    mine_used = lax.dynamic_slice_in_dim(used, device_index * own_most, own_most)
    mine_block = lax.dynamic_slice_in_dim(block_of, device_index * own_most, own_most)
    vector_spot = 2 * first_end
    spot_of = jnp.where(
        block_of < first_end,
        block_of,
        jnp.where(
            block_of < synth_end,
            block_of + first_end + 1,
            jnp.where(block_of < value_end, block_of - synth_end + first_end, block_of + 1),
        ),
    )
    got, square_parts, vector_parts = exchange(
        spot_of, late, early, rows_total, seqs_total, vector_spot, vector_rows, 2
    )
    got, value_late = lax.optimization_barrier((got, value_terms))
    value_sums = lax.psum_scatter(value_late, "seq", scatter_dimension=0, tiled=True)
    x_grad = finish_inputs(
        value_sums, back_from_first, back_middle, tokens, gathered_one, vectors, synth_end
    )
    vector_total = vector_parts.reshape(-1, BS)[:vector_rows].reshape(vectors.shape)
    grad_norm = jnp.sqrt(jnp.sum(square_parts))
    clip_max = math.sqrt(block_count * BS * BS + vectors.shape[0] * vectors.shape[1])
    scale = jnp.minimum(1.0, clip_max / grad_norm)
    step_value = step_count[0].astype(jnp.float32)
    mom_fix = 1.0 - jnp.power(BETA_MOM, step_value)
    sec_fix = 1.0 - jnp.power(BETA_SEC, step_value)
    new_vectors, new_vec_moments = vector_adam(
        vectors, vec_moments, vector_total * scale, mom_fix, sec_fix
    )
    rate_table = RATE_FACTOR * block_scales()
    slot_rates = jnp.sum(
        jnp.where(
            mine_block[:, None] == jnp.arange(block_count, dtype=jnp.int32)[None, :],
            rate_table[None, :],
            0.0,
        ),
        axis=1,
    )
    floats = jnp.concatenate([jnp.stack([scale, mom_fix, sec_fix]), slot_rates])
    mine_spot = jnp.where(
        mine_block < first_end,
        mine_block + synth_count,
        jnp.where(mine_block < synth_end, mine_block - first_end, mine_block),
    )
    ints = jnp.concatenate([mine_used.astype(jnp.int32), mine_spot])
    new_master, new_moments, new_stats, wide = soap_update(
        ints, floats, got, gathered_one, gathered_two, moments, stats, bases
    )
    new_bases = soap_bases(ints, wide, bases)
    returned = lax.all_to_all(
        new_master.reshape(1, own_most, BS, BS), AXES, split_axis=2, concat_axis=0, tiled=True
    )
    new_weights = collect(slot_id, returned.reshape(slot_count, piece_rows, BS))
    return (
        layer_out.reshape(rows_here, positions, width),
        x_grad.reshape(rows_here, positions, width),
        new_weights,
        new_moments,
        new_stats,
        new_bases,
        new_vectors,
        new_vec_moments,
        grad_norm.reshape(1),
    )


def solution(mesh):
    placed = (
        P("row", "seq", None),
        P("row", "seq", None),
        P("row", "seq"),
        P("row", None),
        P(None, ("row", "seq")),
        P(),
        P(),
        P(("row", "seq"), None, None, None),
        P(("row", "seq"), None, None, None),
        P(("row", "seq"), None, None, None),
        P(),
        P(),
    )
    return jax.shard_map(
        local,
        mesh=mesh,
        in_specs=placed,
        out_specs=(
            P("row", "seq", None),
            P("row", "seq", None),
            P(None, ("row", "seq")),
            P(("row", "seq"), None, None, None),
            P(("row", "seq"), None, None, None),
            P(("row", "seq"), None, None, None),
            P(),
            P(),
            P(),
        ),
        check_vma=False,
    )
```

```python
import functools
import math

import jax
import jax.numpy as jnp
from jax import lax
from jax.experimental import pallas as pl
from jax.experimental.pallas import tpu as pltpu
from jax.sharding import PartitionSpec as P

D = 768
HEADS = 12
HD = 64
FF = 3072
LEN = 2048
BS = 256
BLOCKS = 123

BETA_MOM = 0.95
BETA_SEC = 0.95
EPSILON = 1e-08
DECAY = 0.01
VECTOR_RATE = 0.3
RATE_FACTOR = 2.0
NORM_EPS = 1e-05
NEG = -1e30
PANEL = 32
HIGHEST = lax.Precision.HIGHEST
VMEM = pltpu.VMEM
AXES = ("row", "seq")
MESH = pl.DeviceIdType.MESH


def dot_nn(a,b): return lax.dot_general(a,b,(((1,),(0,)),((),())),preferred_element_type=jnp.float32)
def dot_nt(a,b): return lax.dot_general(a,b,(((1,),(1,)),((),())),preferred_element_type=jnp.float32)

TILE = 512

def tile_rows(positions): return min(positions, TILE)

def attn_forward_body(tq, tables, hid_ref, synth_ref, value_ref, mixed_ref, lse_ref, f2m, v32, lbuf):
    length = value_ref.shape[0]
    tiles = hid_ref.shape[0] // tq
    blocks = synth_ref.shape[0]
    segs = (tables.shape[0] - 2 * tiles - 1) // 2
    low_rows = lax.broadcasted_iota(jnp.int32, (2 * HD, BS), 0) < HD
    for j in range(blocks):
        tile = synth_ref[j]
        zero = jnp.zeros_like(tile)
        f2m[0, j] = jnp.where(low_rows, tile, zero)
        f2m[1, j] = jnp.where(low_rows, zero, tile)
    v32[0:length] = value_ref[...].astype(jnp.float32)
    v32[length:] = jnp.zeros((BS, 2 * HD), jnp.float32)
    left = lax.broadcasted_iota(jnp.int32, (tq, 2 * HD), 1) < HD
    lane = lax.broadcasted_iota(jnp.int32, (1, BS), 1)
    row = lax.broadcasted_iota(jnp.int32, (tq, 1), 0)
    for t in range(tiles):
        hid = hid_ref[t * tq:(t + 1) * tq]
        base = tables[2 * segs + 2 * tiles] + t * tq

        def segment(s, carry):
            start, count = tables[s], tables[segs + s]
            used = (count + BS - 1) // BS

            def scores(j, tops):
                keep = lane < count - j * BS
                out = []
                for h in range(2):
                    part = jnp.where(keep, dot_nn(hid, f2m[h, j]), NEG)
                    lbuf[h, j] = part
                    out.append(jnp.maximum(tops[h], jnp.maximum(part[:, :128], part[:, 128:])))
                return tuple(out)

            none = jnp.full((tq, 128), NEG, jnp.float32)
            tops = lax.fori_loop(0, used, scores, (none, none))
            tops = [jnp.max(top, axis=1, keepdims=True) for top in tops]

            def weigh(j, carried):
                value = v32[pl.ds(start + j * BS, BS), :].astype(jnp.bfloat16)
                out = []
                for h in range(2):
                    total, mix = carried[h]
                    part = jnp.exp(lbuf[h, j] - tops[h])
                    total = total + part[:, :128] + part[:, 128:]
                    mix = mix + dot_nn(part.astype(jnp.bfloat16), value)
                    out.append((total, mix))
                return tuple(out)

            blank = jnp.zeros((tq, 128), jnp.float32)
            pair = lax.fori_loop(0, used, weigh, ((blank, blank), (blank, blank)))
            sums = [jnp.sum(total, axis=1, keepdims=True) for total, _ in pair]
            mix = jnp.where(left, pair[0][1] / sums[0], pair[1][1] / sums[1])
            log = jnp.where(left, tops[0] + jnp.log(sums[0]), tops[1] + jnp.log(sums[1]))
            here = (row + base >= start) & (row + base < start + count)
            rows = pl.ds(t * tq, tq)
            mixed_ref[rows] = jnp.where(here, mix, mixed_ref[rows])
            lse_ref[rows] = jnp.where(here, log, lse_ref[rows])
            return carry

        lax.fori_loop(tables[2 * segs + t], tables[2 * segs + tiles + t], segment, 0)

def attn_forward(tables, hidden, synth, values):
    positions, width = hidden.shape
    length = values.shape[0]
    tq = tile_rows(positions)
    pairs = width // (2 * HD)
    blocks = length // BS
    per = BS // (2 * HD)
    return pl.pallas_call(
        functools.partial(attn_forward_body, tq),
        name="attn_forward",
        out_shape=(jax.ShapeDtypeStruct((positions, width), jnp.float32),) * 2,
        grid_spec=pltpu.PrefetchScalarGridSpec(
            num_scalar_prefetch=1,
            grid=(pairs,),
            in_specs=[
                pl.BlockSpec((positions, 2 * HD), lambda p, t: (0, p)),
                pl.BlockSpec((blocks, 2 * HD, BS), lambda p, t: (p // per, p % per, 0)),
                pl.BlockSpec((length, 2 * HD), lambda p, t: (0, p)),
            ],
            out_specs=[pl.BlockSpec((positions, 2 * HD), lambda p, t: (0, p))] * 2,
            scratch_shapes=[
                pltpu.VMEM((2, blocks, 2 * HD, BS), jnp.bfloat16),
                pltpu.VMEM((length + BS, 2 * HD), jnp.float32),
                pltpu.VMEM((2, blocks, tq, BS), jnp.float32),
            ],
        ),
        compiler_params=pltpu.CompilerParams(vmem_limit_bytes=40 << 20, dimension_semantics=("arbitrary",)),
        cost_estimate=pl.CostEstimate(flops=4 * positions * length * width * 2, bytes_accessed=12 << 20, transcendentals=positions * length * 12),
    )(tables, hidden, synth, values)

def attn_backward_body(tq, tables, hid_ref, synth_ref, value_ref, dmix_ref, mixed_ref, lse_ref,
                       dsynth_ref, dhid_ref, dvalue_ref, f2m, v32, dv32, dmm, dacc, df2):
    length = value_ref.shape[0]
    tiles = hid_ref.shape[0] // tq
    blocks = synth_ref.shape[0]
    segs = (tables.shape[0] - 2 * tiles - 1) // 2
    low_rows = lax.broadcasted_iota(jnp.int32, (2 * HD, BS), 0) < HD
    for j in range(blocks):
        tile = synth_ref[j]
        zero = jnp.zeros_like(tile)
        f2m[0, j] = jnp.where(low_rows, tile, zero)
        f2m[1, j] = jnp.where(low_rows, zero, tile)
    v32[0:length] = value_ref[...].astype(jnp.float32)
    v32[length:] = jnp.zeros((BS, 2 * HD), jnp.float32)
    dv32[...] = jnp.zeros_like(dv32)
    df2[...] = jnp.zeros_like(df2)
    left = lax.broadcasted_iota(jnp.int32, (tq, 2 * HD), 1) < HD
    lane = lax.broadcasted_iota(jnp.int32, (1, BS), 1)
    row = lax.broadcasted_iota(jnp.int32, (tq, 1), 0)
    for t in range(tiles):
        rows = pl.ds(t * tq, tq)
        hid = hid_ref[rows]
        hid_t = hid.astype(jnp.float32).T.astype(jnp.bfloat16)
        dmix32 = dmix_ref[rows].astype(jnp.float32)
        dmix_t = dmix32.T.astype(jnp.bfloat16)
        dot_pair = dmix32 * mixed_ref[rows]
        nil = jnp.zeros_like(dmix32)
        deltas = (
            jnp.sum(jnp.where(left, dot_pair, nil), axis=1, keepdims=True),
            jnp.sum(jnp.where(left, nil, dot_pair), axis=1, keepdims=True),
        )
        dmm[0] = jnp.where(left, dmix32, nil).astype(jnp.bfloat16)
        dmm[1] = jnp.where(left, nil, dmix32).astype(jnp.bfloat16)
        base = tables[2 * segs + 2 * tiles] + t * tq
        logs = lse_ref[rows]
        dacc[...] = jnp.zeros_like(dacc)

        def segment(s, carry):
            start, count = tables[s], tables[segs + s]
            used = (count + BS - 1) // BS
            here = (row + base >= start) & (row + base < start + count)
            lse = [jnp.where(here, logs[:, h * HD:h * HD + 1], -NEG) for h in range(2)]

            def block(j, carry):
                keep = lane < count - j * BS
                value = v32[pl.ds(start + j * BS, BS), :].astype(jnp.bfloat16)
                parts = []
                total = None
                for h in range(2):
                    synth = f2m[h, j]
                    prob = jnp.where(keep, jnp.exp(dot_nn(hid, synth) - lse[h]), 0.0)
                    dprob = dot_nt(dmm[h], value)
                    dlog = (prob * (dprob - deltas[h])).astype(jnp.bfloat16)
                    head = slice(h * HD, (h + 1) * HD)
                    df2[j, head, :] += dot_nn(hid_t[head], dlog)
                    back = dot_nt(dlog, synth)
                    total = back if total is None else total + back
                    parts.append(dot_nn(dmix_t[head], prob.astype(jnp.bfloat16)))
                dacc[...] += total
                dv32[pl.ds(start + j * BS, BS), :] += jnp.concatenate(parts, axis=0).T
                return carry

            lax.fori_loop(0, used, block, 0)
            return carry

        lax.fori_loop(tables[2 * segs + t], tables[2 * segs + tiles + t], segment, 0)
        dhid_ref[rows] = dacc[...].astype(jnp.bfloat16)
    dvalue_ref[...] = dv32[0:length].astype(jnp.bfloat16)
    dsynth_ref[...] = df2[...].astype(jnp.bfloat16)

def attn_backward(tables, hidden, synth, values, dmix, mixed, lse):
    positions, width = hidden.shape
    length = values.shape[0]
    tq = tile_rows(positions)
    pairs = width // (2 * HD)
    blocks = length // BS
    per = BS // (2 * HD)
    tok = pl.BlockSpec((positions, 2 * HD), lambda p, t: (0, p))
    f2 = pl.BlockSpec((blocks, 2 * HD, BS), lambda p, t: (p // per, p % per, 0))
    val = pl.BlockSpec((length, 2 * HD), lambda p, t: (0, p))
    return pl.pallas_call(
        functools.partial(attn_backward_body, tq),
        name="attn_backward",
        out_shape=(
            jax.ShapeDtypeStruct((pairs // per * blocks, BS, BS), jnp.bfloat16),
            jax.ShapeDtypeStruct((positions, width), jnp.bfloat16),
            jax.ShapeDtypeStruct((length, width), jnp.bfloat16),
        ),
        grid_spec=pltpu.PrefetchScalarGridSpec(
            num_scalar_prefetch=1,
            grid=(pairs,),
            in_specs=[tok, f2, val, tok, tok, tok],
            out_specs=[f2, tok, val],
            scratch_shapes=[
                pltpu.VMEM((2, blocks, 2 * HD, BS), jnp.bfloat16),
                pltpu.VMEM((length + BS, 2 * HD), jnp.float32),
                pltpu.VMEM((length + BS, 2 * HD), jnp.float32),
                pltpu.VMEM((2, tq, 2 * HD), jnp.bfloat16),
                pltpu.VMEM((tq, 2 * HD), jnp.float32),
                pltpu.VMEM((blocks, 2 * HD, BS), jnp.float32),
            ],
        ),
        compiler_params=pltpu.CompilerParams(vmem_limit_bytes=40 << 20, dimension_semantics=("arbitrary",)),
        cost_estimate=pl.CostEstimate(flops=10 * positions * length * width * 2, bytes_accessed=24 << 20, transcendentals=positions * length * 12),
    )(tables, hidden, synth, values, dmix, mixed, lse)


def exact(a, b, da=1, db=0):
    return lax.dot_general(a, b, (((da,), (db,)), ((), ())), precision=HIGHEST, preferred_element_type=jnp.float32)

def parts_of(values):
    first = values.astype(jnp.bfloat16)
    rest = values - first.astype(jnp.float32)
    second = rest.astype(jnp.bfloat16)
    return first, second, (rest - second.astype(jnp.float32)).astype(jnp.bfloat16)


LEFT_PARTS, RIGHT_PARTS = (0, 0, 1, 0, 1, 2), (0, 1, 0, 2, 1, 0)


def exact_thin(left, right, axis):
    lefts, rights = parts_of(left), parts_of(right)
    return lax.dot_general(
        jnp.concatenate([lefts[k] for k in LEFT_PARTS], axis=axis),
        jnp.concatenate([rights[k] for k in RIGHT_PARTS], axis=0),
        (((axis,), (0,)), ((), ())),
        preferred_element_type=jnp.float32,
    )


def soap_update_body(ints, floats, got_ref, one_ref, two_ref, three_ref, moment_ref, stat_ref, basis_ref,
                     new_master_ref, new_moment_ref, new_stat_ref, wide_ref, grad_ref, master_ref, sems):
    devices, slots, part = got_ref.shape[0], got_ref.shape[1], got_ref.shape[2]
    sources, at = [], 0
    for ref in (one_ref, two_ref, three_ref):
        sources.append((ref, at, at + ref.shape[0]))
        at += ref.shape[0]

    def master_copy(k, source):
        return pltpu.make_async_copy(source, master_ref.at[k], sems.at[k])

    for k in range(slots):
        block = ints[slots + k]
        for ref, low, high in sources:

            @pl.when((block >= low) & (block < high))
            def _():
                master_copy(k, ref.at[block - low]).start()

    scale, mom_fix, sec_fix = floats[0], floats[1], floats[2]

    per = max(1, 8 // part)

    def join(d, carry):
        rows = pl.ds(pl.multiple_of(d * (per * part), per * part), per * part)
        for k in range(slots):
            pieces = [got_ref[d * per + i, k].astype(jnp.float32) for i in range(per)]
            grad_ref[k, rows, :] = pieces[0] if per == 1 else jnp.concatenate(pieces, axis=0)
        return carry

    lax.fori_loop(0, devices // per, join, 0)
    for k in range(slots):
        master_copy(k, one_ref.at[0]).wait()

    def prepare(k, carry):
        used = ints[k] > 0
        grad = jnp.where(used, grad_ref[k] * scale, 0.0)
        left, right = basis_ref[k, 0], basis_ref[k, 1]
        old_left, old_right = stat_ref[k, 0], stat_ref[k, 1]
        left_stat = BETA_SEC * old_left + (1 - BETA_SEC) * exact(grad, grad, 1, 1)
        right_stat = BETA_SEC * old_right + (1 - BETA_SEC) * exact(grad, grad, 0, 0)
        new_stat_ref[k, 0] = jnp.where(used, left_stat, old_left)
        new_stat_ref[k, 1] = jnp.where(used, right_stat, old_right)
        left_t = left.T
        for side, (turn, stat) in enumerate(((left_t, left_stat), (right.T, right_stat))):
            cross = exact(turn, stat)
            wide_ref[2 * k + side, :, 0:BS] = exact(cross, cross, 1, 1)
            wide_ref[2 * k + side, :, BS:] = cross
        momentum = BETA_MOM * moment_ref[k, 0] + (1 - BETA_MOM) * grad
        turned_grad = exact(exact(left_t, grad), right)
        turned_mom = exact(exact(left_t, momentum), right)
        old_second = moment_ref[k, 1]
        second = BETA_SEC * old_second + (1 - BETA_SEC) * turned_grad * turned_grad
        step = turned_mom / mom_fix / (jnp.sqrt(second / sec_fix) + EPSILON)
        update = exact(exact(left, step), right, 1, 1)
        master = master_ref[k].astype(jnp.float32)
        new_master_ref[k] = (master - floats[3 + k] * (update + DECAY * master)).astype(jnp.bfloat16)
        new_moment_ref[k, 0] = jnp.where(used, momentum, moment_ref[k, 0])
        new_moment_ref[k, 1] = jnp.where(used, second, old_second)
        return carry

    lax.fori_loop(0, slots, prepare, 0)


def soap_update(ints, floats, got, one, two, three, moments, stats, bases):
    slots = got.shape[1]
    whole = pl.BlockSpec(memory_space=VMEM)
    scalar = pl.BlockSpec(memory_space=pltpu.SMEM)
    anywhere = pl.BlockSpec(memory_space=pl.ANY)
    pair = jax.ShapeDtypeStruct(moments.shape, jnp.float32)
    return pl.pallas_call(
        soap_update_body,
        name="soap_update",
        out_shape=(
            jax.ShapeDtypeStruct((slots, BS, BS), jnp.bfloat16),
            pair,
            pair,
            jax.ShapeDtypeStruct((2 * slots, BS, 2 * BS), jnp.float32),
        ),
        in_specs=[scalar, scalar, whole, anywhere, anywhere, anywhere] + [whole] * 3,
        out_specs=[whole] * 4,
        scratch_shapes=[
            VMEM((slots, BS, BS), jnp.float32),
            VMEM((slots, BS, BS), jnp.bfloat16),
            pltpu.SemaphoreType.DMA((slots,)),
        ],
        compiler_params=pltpu.CompilerParams(vmem_limit_bytes=48 << 20),
        cost_estimate=pl.CostEstimate(flops=slots * 12 * 6 * 2 * BS ** 3, bytes_accessed=slots * 14 * 4 * BS * BS, transcendentals=slots * BS * BS),
    )(ints, floats, got, one, two, three, moments, stats, bases)


def soap_bases_body(ints, given_ref, basis_ref, new_basis_ref, wide):
    slots = basis_ref.shape[0]
    count = 2 * slots
    wide[...] = given_ref[...]
    group = 128 // PANEL
    groups = count // group
    row = lax.broadcasted_iota(jnp.int32, (PANEL, 128), 0)
    lane = lax.broadcasted_iota(jnp.int32, (PANEL, 128), 1)
    unit = jnp.where(row == lane % PANEL, 1.0, 0.0)
    spot = lane // PANEL * PANEL
    for p in range(BS // PANEL):
        low = p * PANEL
        rows = slice(low, low + PANEL)
        schur, inverse, pivots = [], [], []
        for q in range(groups):
            schur.append(jnp.concatenate([wide[q * group + i, rows, low:low + PANEL] for i in range(group)], axis=1))
            inverse.append(unit)
            pivots.append(unit)

        for k in range(PANEL):
            below = row > k
            for q in range(groups):
                a, b = schur[q], inverse[q]
                column = jnp.take_along_axis(a, spot + k, axis=1)
                pivot = jnp.take_along_axis(jnp.broadcast_to(a[k:k + 1], (8, 128)), spot[:8] + k, axis=1)[0:1]
                factor = jnp.where(below, column * (1.0 / pivot), 0.0)
                schur[q] = a - factor * a[k:k + 1]
                inverse[q] = b - factor * b[k:k + 1]
                pivots[q] = jnp.where(row == k, pivot, pivots[q])
        for q in range(groups):
            whole = inverse[q] * lax.rsqrt(pivots[q])
            for i in range(group):
                m = q * group + i
                near = low // 128 * 128
                limit = near + 128
                part = exact_thin(whole[:, i * PANEL:(i + 1) * PANEL], wide[m, rows, near:], 1)
                wide[m, rows, near:] = part
                if low + PANEL < limit:
                    wide[m, low + PANEL:limit, near:] -= exact_thin(
                        part[:, low + PANEL - near:limit - near], part, 0
                    )
                elif limit < BS:
                    above = wide[m, near:limit, limit:]
                    wide[m, limit:, limit:] -= exact(above[:, :BS - limit], above, 0, 0)

    def finish(k, carry):
        used = ints[k] > 0
        for side in range(2):
            new_basis_ref[k, side] = jnp.where(used, wide[2 * k + side, :, BS:].T, basis_ref[k, side])
        return carry

    lax.fori_loop(0, slots, finish, 0)


def soap_bases(ints, wide, bases):
    slots = bases.shape[0]
    whole = pl.BlockSpec(memory_space=VMEM)
    return pl.pallas_call(
        soap_bases_body,
        name="soap_bases",
        out_shape=jax.ShapeDtypeStruct(bases.shape, jnp.float32),
        in_specs=[pl.BlockSpec(memory_space=pltpu.SMEM), whole, whole],
        out_specs=whole,
        scratch_shapes=[VMEM(wide.shape, jnp.float32)],
        compiler_params=pltpu.CompilerParams(vmem_limit_bytes=48 << 20),
        cost_estimate=pl.CostEstimate(flops=slots * 4 * 6 * 2 * BS ** 3, bytes_accessed=slots * 8 * 4 * BS * BS, transcendentals=slots * BS * BS),
    )(ints, wide, bases)


def spread_pieces_body(orders, weight_ref, *refs):
    *out_refs, lay = refs
    for i in range(lay.shape[1]):
        lay[:, i, :] = weight_ref[:, i * BS:(i + 1) * BS]
    for out_ref, order in zip(out_refs, orders):
        at = 0
        for low, high in order:
            out_ref[at:at + high - low] = lay[low:high].astype(jnp.bfloat16)
            at += high - low


def spread_pieces(weights, orders):
    count, rows = weights.shape[0], weights.shape[1] // BS
    sizes = [sum(high - low for low, high in order) for order in orders]
    whole = pl.BlockSpec(memory_space=VMEM)
    return pl.pallas_call(
        functools.partial(spread_pieces_body, orders),
        name="spread_pieces",
        out_shape=[jax.ShapeDtypeStruct((size, rows, BS), jnp.bfloat16) for size in sizes],
        in_specs=[whole],
        out_specs=[whole] * len(sizes),
        scratch_shapes=[VMEM((count, rows, BS), jnp.float32)],
        compiler_params=pltpu.CompilerParams(vmem_limit_bytes=32 << 20),
    )(weights)


def collect_body(slot_id, piece_ref, out_ref):
    rows = piece_ref.shape[1]

    def place(m, carry):
        piece = piece_ref[slot_id[m]].astype(jnp.float32)
        for i in range(rows):
            out_ref[pl.ds(m, 1), i * BS:(i + 1) * BS] = piece[i:i + 1]
        return carry

    lax.fori_loop(0, out_ref.shape[0], place, 0)


def collect(slot_id, pieces):
    count, rows = slot_id.shape[0], pieces.shape[1]
    whole = pl.BlockSpec(memory_space=VMEM)
    return pl.pallas_call(
        collect_body,
        name="collect",
        out_shape=jax.ShapeDtypeStruct((count, rows * BS), jnp.float32),
        in_specs=[pl.BlockSpec(memory_space=pltpu.SMEM), whole],
        out_specs=whole,
        compiler_params=pltpu.CompilerParams(vmem_limit_bytes=32 << 20),
    )(slot_id, pieces)


def partners(bits):
    row, seq = lax.axis_index("row"), lax.axis_index("seq")
    core, flags, peers = row % 2, [], []
    for k in range(bits):
        flag = row // 2 ** (k + 1) % 2
        flags.append(flag)
        peers.append((row + (1 - 2 * flag) * 2 ** (k + 1), seq))
    return core, (row + 1 - 2 * core, seq), flags, peers


def greet(devices):
    barrier = pltpu.get_barrier_semaphore()
    for device in devices:
        pl.semaphore_signal(barrier, inc=1, device_id=device, device_id_type=MESH)
    pl.semaphore_wait(barrier, len(devices))


def in_turns(works):
    live = []
    works = list(works)
    while works or live:
        if works:
            live.append(works.pop(0))
        live = [work for work in reversed(live) if next(work, None) is not None][::-1]


def group_bounds(count, groups):
    return [(count * k // groups, count * (k + 1) // groups) for k in range(groups)]


def reduce_rows_body(bits, seqs, groups, given, *refs):
    in_refs, summed_ref, (out_ref, mine, near, *rest) = refs[:given], refs[given], refs[given + 1:]
    far = rest[:bits]
    spread, arrived, own_summed, got_summed, keep_sems, send, recv = rest[bits:]
    count, extra = mine.shape[0], own_summed.shape[0]
    part = out_ref.shape[1]
    core, sibling, flags, peers = partners(bits)
    row, seq = lax.axis_index("row"), lax.axis_index("seq")
    beside = [(row, (seq + k) % seqs) for k in range(1, seqs)]
    greet([sibling, *peers, *beside])
    used = [0]

    def copy(source, target, device):
        at = used[0]
        used[0] += 1
        return pltpu.make_async_remote_copy(
            src_ref=source, dst_ref=target, send_sem=send.at[at], recv_sem=recv.at[at],
            device_id=device, device_id_type=MESH,
        )

    some = slice(None)
    every = (some,) * bits
    bounds = group_bounds(count, groups)
    starts, kept = [[] for _ in bounds], [[] for _ in bounds]
    at = local = 0
    for ref in in_refs:
        for g, (low, high) in enumerate(bounds):
            begin, end = max(low, at), min(high, at + ref.shape[0])
            if begin < end:
                span, to = pl.ds(begin - at, end - begin), pl.ds(begin, end - begin)
                starts[g].append(copy(ref.at[(span, *every, 1 - core)], near.at[to], sibling))
                kept[g].append(pltpu.make_async_copy(ref.at[(span, *every, core)], mine.at[to], keep_sems.at[local]))
                local += 1
        at += ref.shape[0]
    for g in range(groups):
        for move in starts[g] + kept[g]:
            move.start()
    extras = [copy(summed_ref.at[:, device[1]], got_summed.at[k], device) for k, device in enumerate(beside)]
    own_extra = pltpu.make_async_copy(summed_ref.at[:, seq], own_summed, keep_sems.at[local])
    for move in (*extras, own_extra):
        move.start()

    def work(g):
        low, high = bounds[g]
        span = pl.ds(low, high - low)
        order = list(range(bits)) if g % 2 == 0 else list(range(bits - 1, -1, -1))
        place = [some] * bits
        for move in starts[g] + kept[g]:
            move.wait()

        def first(n, carry):
            total = mine[n].astype(jnp.float32) + near[n].astype(jnp.float32)
            mine[n] = total.astype(jnp.bfloat16)
            return carry

        lax.fori_loop(low, high, first, 0)
        for step, bit in enumerate(order):
            spot = bits - 1 - bit
            theirs = list(place)
            theirs[spot] = 1 - flags[bit]
            place[spot] = flags[bit]
            move = copy(mine.at[(span, *theirs)], far[step].at[span], peers[bit])
            move.start()
            yield True
            move.wait()
            last = step == bits - 1
            where = tuple(place)

            def add(n, carry, step=step, where=where, last=last):
                total = mine[(n, *where)].astype(jnp.float32) + far[step][n].astype(jnp.float32)
                if last:
                    for s in range(seqs):
                        spread[s, n] = total[s * part:(s + 1) * part].astype(jnp.bfloat16)
                else:
                    mine[(n, *where)] = total.astype(jnp.bfloat16)
                return carry

            lax.fori_loop(low, high, add, 0)
        final = [
            copy(spread.at[device[1], span], arrived.at[k, span], device) for k, device in enumerate(beside)
        ]
        for move in final:
            move.start()
        yield True
        for move in final:
            move.wait()

        def finish(n, carry):
            total = spread[seq, n].astype(jnp.float32)
            for k in range(seqs - 1):
                total = total + arrived[k, n].astype(jnp.float32)
            out_ref[n] = total
            return carry

        lax.fori_loop(low, high, finish, 0)

    in_turns([work(g) for g in range(groups)])
    for move in (*extras, own_extra):
        move.wait()

    def add_extra(n, carry):
        total = own_summed[n].astype(jnp.float32)
        for k in range(seqs - 1):
            total = total + got_summed[k, n].astype(jnp.float32)
        out_ref[count + n] = total
        return carry

    lax.fori_loop(0, extra, add_extra, 0)


def reduce_rows(terms, summed, rows, seqs, groups, collective):
    count = sum(term.shape[0] for term in terms)
    bits = (rows // 2).bit_length() - 1
    slab = BS // rows
    part = slab // seqs
    twos = (2,) * bits
    low = jnp.bfloat16
    most = len(terms) + groups + 1
    sems = groups * (bits + seqs - 1) + most + seqs
    extra = summed.shape[0]
    return pl.pallas_call(
        functools.partial(reduce_rows_body, bits, seqs, groups, len(terms)),
        name="reduce_rows",
        out_shape=jax.ShapeDtypeStruct((count + extra, part, BS), jnp.float32),
        in_specs=[pl.BlockSpec(memory_space=pl.ANY)] * (len(terms) + 1),
        out_specs=pl.BlockSpec(memory_space=VMEM),
        scratch_shapes=[
            VMEM((count, *twos, slab, BS), low),
            VMEM((count, *twos, slab, BS), low),
            *[VMEM((count, *twos[k + 1:], slab, BS), low) for k in range(bits)],
            VMEM((seqs, count, part, BS), low),
            VMEM((seqs - 1, count, part, BS), low),
            VMEM((extra, part, BS), low),
            VMEM((seqs - 1, extra, part, BS), low),
            pltpu.SemaphoreType.DMA((most,)),
            pltpu.SemaphoreType.DMA((sems,)),
            pltpu.SemaphoreType.DMA((sems,)),
        ],
        compiler_params=pltpu.CompilerParams(
            collective_id=collective, has_side_effects=True, vmem_limit_bytes=56 << 20
        ),
        cost_estimate=pl.CostEstimate(flops=count * BS * BS, bytes_accessed=4 * count * BS * BS, transcendentals=0),
    )(*[term.reshape(-1, *twos, 2, slab, BS) for term in terms], summed.reshape(-1, seqs, part, BS))


def exchange_body(seqs, sources, spot_of, late_ref, got_ref, square_ref, vector_ref, out, mine, send, recv):
    devices, own = got_ref.shape[0], got_ref.shape[1]
    part = late_ref.shape[1]
    me = lax.axis_index("row") * seqs + lax.axis_index("seq")
    barrier = pltpu.get_barrier_semaphore()

    def peer(k):
        to = (me + k) % devices
        return to, (to // seqs, to % seqs)

    def hello(k, carry):
        pl.semaphore_signal(barrier, inc=1, device_id=peer(k)[1], device_id_type=MESH)
        return carry

    lax.fori_loop(1, devices, hello, 0)

    def place(d, carry):
        for s in range(own):
            out[d, s] = late_ref[spot_of[d * own + s]].astype(jnp.bfloat16)
        return carry

    lax.fori_loop(0, devices, place, 0)

    def add(ref, total):
        def step(m, total):
            value = ref[m].astype(jnp.float32)
            return total + value * value

        return lax.fori_loop(0, ref.shape[0], step, total)

    total = add(late_ref, jnp.zeros((part, BS), jnp.float32))
    mine[...] = total[:, :128] + total[:, 128:]
    pl.semaphore_wait(barrier, devices - 1)

    def move(source, target, kind, k, device):
        return pltpu.make_async_remote_copy(
            src_ref=source, dst_ref=target, send_sem=send.at[kind, k], recv_sem=recv.at[kind, k],
            device_id=device, device_id_type=MESH,
        )

    def moves(k):
        to, device = peer(k)
        return (
            move(out.at[to], got_ref.at[me], 0, k, device),
            move(mine, square_ref.at[me], 1, k, device),
        )

    def launch(k, carry):
        for one in moves(k):
            one.start()
        return carry

    lax.fori_loop(1, devices, launch, 0)

    @pl.when(me < sources[0])
    def _():
        def tell(k, carry):
            move(late_ref.at[sources[1]], vector_ref.at[me], 2, k, peer(k)[1]).start()
            return carry

        lax.fori_loop(1, devices, tell, 0)
        vector_ref[me] = late_ref[sources[1]]

    got_ref[me] = out[me]
    square_ref[me] = mine[...]

    def finish(k, carry):
        for one in moves(k):
            one.wait()
        return carry

    lax.fori_loop(1, devices, finish, 0)

    @pl.when(me < sources[0])
    def _():
        def told(k, carry):
            move(late_ref.at[sources[1]], vector_ref.at[me], 2, k, peer(k)[1]).wait_send()
            return carry

        lax.fori_loop(1, devices, told, 0)

    for d in range(sources[0]):
        @pl.when(me != d)
        def _():
            k = (me - d + devices) % devices
            move(late_ref.at[sources[1]], vector_ref.at[d], 2, k, peer(k)[1]).wait_recv()


def exchange(spot_of, late, rows, seqs, vector_spot, vector_rows, collective):
    devices = rows * seqs
    part = late.shape[1]
    own = spot_of.shape[0] // devices
    told = -(-vector_rows // part)
    whole = pl.BlockSpec(memory_space=VMEM)
    return pl.pallas_call(
        functools.partial(exchange_body, seqs, (told, vector_spot)),
        name="exchange",
        out_shape=(
            jax.ShapeDtypeStruct((devices, own, part, BS), jnp.bfloat16),
            jax.ShapeDtypeStruct((devices, part, 128), jnp.float32),
            jax.ShapeDtypeStruct((told, part, BS), jnp.float32),
        ),
        in_specs=[pl.BlockSpec(memory_space=pltpu.SMEM), whole],
        out_specs=[whole] * 3,
        scratch_shapes=[
            VMEM((devices, own, part, BS), jnp.bfloat16),
            VMEM((part, 128), jnp.float32),
            pltpu.SemaphoreType.DMA((3, devices)),
            pltpu.SemaphoreType.DMA((3, devices)),
        ],
        compiler_params=pltpu.CompilerParams(
            collective_id=collective, has_side_effects=True, vmem_limit_bytes=32 << 20
        ),
    )(spot_of, late)


def gather_rows_body(bits, seqs, groups, ahead, parts, pace, given, *refs):
    piece_refs, token_ref = refs[:given], refs[given]
    full_refs, row_ref = refs[given + 1:2 * given + 1], refs[2 * given + 1]
    near, send, recv, chain_send, chain_recv, own_sem = refs[2 * given + 2:]
    core, sibling, flags, peers = partners(bits)
    row, seq = lax.axis_index("row"), lax.axis_index("seq")
    greet([sibling, *peers, *[(row, (seq + k) % seqs) for k in range(1, seqs)]])
    used = [0]

    def copy(source, target, device):
        at = used[0]
        used[0] += 1
        return pltpu.make_async_remote_copy(
            src_ref=source, dst_ref=target, send_sem=send.at[at], recv_sem=recv.at[at],
            device_id=device, device_id_type=MESH,
        )

    def hop(source, here, sems_out, sems_in, to_right, step):
        spot = seq - step if to_right else seq + step
        side = 0 if to_right else 1
        return pltpu.make_async_remote_copy(
            src_ref=source if step == 0 else here(spot), dst_ref=here(spot), send_sem=sems_out(side, step),
            recv_sem=sems_in(spot), device_id=(row, seq + (1 if to_right else -1)), device_id_type=MESH,
        )

    def ends(to_right, step):
        there = seq - step >= 0 if to_right else seq + step < seqs
        onward = seq + 1 < seqs if to_right else seq - 1 >= 0
        return there, onward

    def chain(line, step, finish=False):
        for to_right in (True, False):
            there, onward = ends(to_right, step)
            if step > 0 and not finish:

                @pl.when(there)
                def _():
                    hop(*line, to_right, step).wait_recv()

            @pl.when(there & onward)
            def _():
                move = hop(*line, to_right, step)
                if finish:
                    move.wait_send()
                else:
                    move.start()

    lines = []
    for g, (ref, low, high, to, _) in enumerate(groups):
        span, near_span = pl.ds(low, high - low), pl.ds(to, high - low)
        lines.append((
            piece_refs[ref].at[span],
            lambda spot, near_span=near_span: near.at[spot, near_span],
            lambda side, step, g=g: chain_send.at[g, side, step],
            lambda spot, g=g: chain_recv.at[g, spot],
        ))
    share = token_ref.shape[0] // parts

    def token_line(k):
        rows, at = pl.ds(k * share, share), len(groups) + k
        return (
            token_ref.at[rows],
            lambda spot: row_ref.at[spot, rows],
            lambda side, step: chain_send.at[at, side, step],
            lambda spot: chain_recv.at[at, spot],
        )

    token_lines = [token_line(k) for k in range(parts)]
    for line in lines:
        chain(line, 0)
    keep_tokens = pltpu.make_async_copy(token_ref, row_ref.at[seq], own_sem)
    keep_tokens.start()
    sent = []

    def work(g):
        ref, low, high, to, backwards = groups[g]
        full_ref = full_refs[ref]
        span = pl.ds(low, high - low)
        order = list(range(bits - 1, -1, -1)) if backwards else list(range(bits))
        for step in range(1, seqs):
            chain(lines[g], step)
            yield True

        def join(n, carry):
            pieces = [
                jnp.where(seq == s, piece_refs[ref][low + n], near[s, to + n]).astype(jnp.float32)
                for s in range(seqs)
            ]
            slab = jnp.concatenate(pieces, axis=0)
            full_ref[(low + n, *flags[::-1], core)] = slab.astype(jnp.bfloat16)
            return carry

        lax.fori_loop(0, high - low, join, 0)
        coming = [[] for _ in order]

        def pass_on(place, level):
            spot = full_ref.at[(span, *place[::-1], core)]
            for later in range(level + 1, bits):
                bit = order[later]
                move = copy(spot, spot, peers[bit])
                move.start()
                there = list(place)
                there[bit] = 1 - flags[bit]
                coming[later].append((tuple(there), move))
                sent.append(move)
            move = copy(spot, spot, sibling)
            move.start()
            across.append(move)

        pass_on(tuple(flags), -1)
        for level in range(bits):
            yield True
            for place, move in coming[level]:
                move.wait_recv()
                pass_on(place, level)

    across = []

    works = [work(g) for g in range(len(groups))]
    hops = [(line, step) for step in range(seqs) for line in token_lines]
    for turn in range(bits + seqs):
        for one in works:
            next(one, None)
        if turn >= ahead:
            for line, step in hops[:parts if turn == ahead else pace]:
                chain(line, step)
                hops = hops[1:]
    for line, step in hops:
        chain(line, step)
    for move in sent:
        move.wait_send()
    for move in across:
        move.wait()
    keep_tokens.wait()
    for line in [*lines, *token_lines]:
        for step in range(seqs):
            chain(line, step, True)


def gather_rows(pieces, tokens, rows, seqs, cuts, collective, ahead=2, parts=1, pace=1):
    part = pieces[0].shape[1]
    bits = (rows // 2).bit_length() - 1
    slab = BS // rows
    twos = (2,) * bits
    low = jnp.bfloat16
    whole = pl.BlockSpec(memory_space=VMEM)
    groups, at = [], 0
    for ref, piece in enumerate(pieces):
        for begin, end in group_bounds(piece.shape[0], cuts[ref]):
            groups.append((ref, begin, end, at, len(groups) % 2 == 1))
            at += end - begin
    sems = len(groups) * (2 * 2 ** bits - 1)
    *full, token_row = pl.pallas_call(
        functools.partial(gather_rows_body, bits, seqs, groups, ahead, parts, pace, len(pieces)),
        name="gather_rows",
        out_shape=(
            *[jax.ShapeDtypeStruct((piece.shape[0], *twos, 2, slab, BS), low) for piece in pieces],
            jax.ShapeDtypeStruct((seqs, *tokens.shape), low),
        ),
        in_specs=[whole] * (len(pieces) + 1),
        out_specs=[whole] * (len(pieces) + 1),
        scratch_shapes=[
            VMEM((seqs, at, part, BS), low),
            pltpu.SemaphoreType.DMA((sems,)),
            pltpu.SemaphoreType.DMA((sems,)),
            pltpu.SemaphoreType.DMA((len(groups) + parts, 2, seqs)),
            pltpu.SemaphoreType.DMA((len(groups) + parts, seqs)),
            pltpu.SemaphoreType.DMA,
        ],
        compiler_params=pltpu.CompilerParams(
            collective_id=collective, has_side_effects=True, vmem_limit_bytes=56 << 20
        ),
        cost_estimate=pl.CostEstimate(flops=0, bytes_accessed=4 * at * BS * BS, transcendentals=0),
    )(*pieces, tokens)
    return [one.reshape(-1, BS, BS) for one in full], token_row.reshape(-1, tokens.shape[1])


def normalize(values):
    centered = values - jnp.mean(values, axis=-1, keepdims=True)
    inverse = lax.rsqrt(jnp.mean(centered * centered, axis=-1, keepdims=True) + NORM_EPS)
    return centered * inverse, inverse


def column(k):
    return slice(k * BS, (k + 1) * BS)


def gate(values):
    return 1.0 / (1.0 + jnp.exp(-values))


def enter_body(spots, token_ref, row_ref, weight_ref, vector_ref, hid_ref, pre_ref, own_t_ref, value_ref, row_t_ref):
    first_at, value_at = spots
    wide = vector_ref.shape[1] // BS
    gain, shift, bias = vector_ref[0:1], vector_ref[1:2], vector_ref[4:5]

    def project(inputs, at, j):
        total = dot_nn(inputs[:, column(0)], weight_ref[at + j])
        for i in range(1, wide):
            total = total + dot_nn(inputs[:, column(i)], weight_ref[at + i * wide + j])
        return total

    def own(c, carry):
        rows = pl.ds(pl.multiple_of(c * BS, BS), BS)
        normed = normalize(token_ref[rows, :].astype(jnp.float32))[0] * gain + shift
        inputs = normed.astype(jnp.bfloat16)
        own_t_ref[:, rows] = normed.T.astype(jnp.bfloat16)
        for j in range(wide):
            pre = project(inputs, first_at, j) + bias[:, column(j)]
            pre_ref[rows, column(j)] = pre
            hid_ref[rows, column(j)] = (pre * gate(pre)).astype(jnp.bfloat16)
        return carry

    lax.fori_loop(0, token_ref.shape[0] // BS, own, 0)

    def whole_row(c, carry):
        rows = pl.ds(pl.multiple_of(c * BS, BS), BS)
        normed = normalize(row_ref[rows, :].astype(jnp.float32))[0] * gain + shift
        inputs = normed.astype(jnp.bfloat16)
        row_t_ref[:, rows] = normed.T.astype(jnp.bfloat16)
        for j in range(wide):
            value_ref[rows, column(j)] = project(inputs, value_at, j).astype(jnp.bfloat16)
        return carry

    lax.fori_loop(0, row_ref.shape[0] // BS, whole_row, 0)


def enter(tokens, token_row, weights, vectors, spots):
    positions, width = tokens.shape
    length = token_row.shape[0]
    whole = pl.BlockSpec(memory_space=VMEM)
    low = jnp.bfloat16
    return pl.pallas_call(
        functools.partial(enter_body, spots),
        name="enter",
        out_shape=(
            jax.ShapeDtypeStruct((positions, width), low),
            jax.ShapeDtypeStruct((positions, width), jnp.float32),
            jax.ShapeDtypeStruct((width, positions), low),
            jax.ShapeDtypeStruct((length, width), low),
            jax.ShapeDtypeStruct((width, length), low),
        ),
        in_specs=[whole] * 4,
        out_specs=[whole] * 5,
        compiler_params=pltpu.CompilerParams(vmem_limit_bytes=40 << 20),
        cost_estimate=pl.CostEstimate(flops=2 * (positions + length) * width * width, bytes_accessed=24 << 20, transcendentals=positions * width),
    )(tokens, token_row, weights, vectors)


def middle_body(cut, token_ref, cotangent_ref, mixed_ref, output_ref, up_a, up_b, up_c, down_ref, vector_ref,
                out_ref, terms_ref, apart_ref, dmix_ref, dmiddle_ref, sums_ref, bias_ref,
                middle, normed_in, normed_t, back_t, total, back, made, made_output, sems, output_sem):
    f, last = pl.program_id(0), pl.num_programs(0) - 1
    ups = (up_a, up_b, up_c)
    wide = len(ups)
    first_up, steps = wide * wide, bias_ref.shape[0]
    slot = f % 2

    def spot(base, step):
        return apart_ref.at[base - cut + step] if base >= cut else terms_ref.at[base + step]

    @pl.when(f == 0)
    def _():
        mixed = mixed_ref[...].astype(jnp.bfloat16)
        for j in range(wide):
            part = token_ref[:, column(j)].astype(jnp.float32)
            for i in range(wide):
                part = part + dot_nn(mixed[:, column(i)], output_ref[i * wide + j])
            middle[:, column(j)] = part
        hat, _ = normalize(middle[...])
        inputs = hat * vector_ref[2:3] + vector_ref[3:4]
        normed_in[...] = inputs.astype(jnp.bfloat16)
        normed_t[...] = inputs.T.astype(jnp.bfloat16)
        total[...] = middle[...]
        back[...] = jnp.zeros_like(back)

    def copies(at, step):
        out = []
        for i in range(wide):
            out.append(pltpu.make_async_copy(made.at[at, i], spot(first_up + i * steps, step), sems.at[at, i]))
        for j in range(wide):
            out.append(pltpu.make_async_copy(made.at[at, wide + j], spot(first_up + wide * steps, step * wide + j), sems.at[at, wide + j]))
        return out

    @pl.when(f >= 2)
    def _():
        for move in copies(slot, f - 2):
            move.wait()

    inputs = normed_in[...]
    pre = vector_ref[pl.ds(5 + f // wide, 1), pl.ds(pl.multiple_of(f % wide * BS, BS), BS)]
    for i in range(wide):
        pre = pre + dot_nn(inputs[:, column(i)], ups[i][0])
    share = gate(pre)
    hidden = pre * share
    low_hidden = hidden.astype(jnp.bfloat16)
    hidden_t = hidden.T.astype(jnp.bfloat16)
    dhidden = None
    for j in range(wide):
        total[:, column(j)] += dot_nn(low_hidden, down_ref[j])
        made[slot, wide + j] = dot_nn(hidden_t, cotangent_ref[:, column(j)]).astype(jnp.bfloat16)
        part = dot_nt(cotangent_ref[:, column(j)], down_ref[j])
        dhidden = part if dhidden is None else dhidden + part
    dhidden = dhidden.astype(jnp.bfloat16).astype(jnp.float32)
    dpre = (dhidden * (share * (1.0 + pre * (1.0 - share)))).astype(jnp.bfloat16)
    bias_ref[pl.ds(f, 1), :] = jnp.sum(dpre.astype(jnp.float32), axis=0, keepdims=True)
    for i in range(wide):
        made[slot, i] = dot_nn(normed_t[column(i), :], dpre).astype(jnp.bfloat16)
        back[:, column(i)] += dot_nt(dpre, ups[i][0])
    for move in copies(slot, f):
        move.start()

    @pl.when(f == last)
    def _():
        out_ref[...] = total[...].astype(jnp.bfloat16)
        hat, inverse = normalize(middle[...])
        dnormed = back[...]
        sums_ref[...] = jnp.zeros_like(sums_ref)
        sums_ref[0:1] = jnp.sum(dnormed * hat, axis=0, keepdims=True)
        sums_ref[1:2] = jnp.sum(dnormed, axis=0, keepdims=True)
        scaled = dnormed * vector_ref[2:3]
        dmiddle = cotangent_ref[...].astype(jnp.float32) + inverse * (
            scaled
            - jnp.mean(scaled, axis=-1, keepdims=True)
            - hat * jnp.mean(scaled * hat, axis=-1, keepdims=True)
        )
        dmiddle_ref[...] = dmiddle
        low = dmiddle.astype(jnp.bfloat16)
        back_t[...] = mixed_ref[...].T.astype(jnp.bfloat16)
        for i in range(wide):
            part = None
            for j in range(wide):
                made_output[i * wide + j] = dot_nn(back_t[column(i), :], low[:, column(j)]).astype(jnp.bfloat16)
                term = dot_nt(low[:, column(j)], output_ref[i * wide + j])
                part = term if part is None else part + term
            dmix_ref[:, column(i)] = part.astype(jnp.bfloat16)
        move = pltpu.make_async_copy(made_output, terms_ref.at[0:wide * wide], output_sem)
        move.start()
        for one in copies(1 - slot, f - 1):
            one.wait()
        for one in copies(slot, f):
            one.wait()
        move.wait()


def middle_stage(tokens, cotangent, mixed, weights, down_weights, vectors, apart):
    positions, width = tokens.shape
    wide = width // BS
    steps = down_weights.shape[0] // wide
    cut = wide * wide + (wide - apart) * steps
    low = jnp.bfloat16
    tok = pl.BlockSpec((positions, width), lambda f: (0, 0))

    def up(i):
        return pl.BlockSpec((1, BS, BS), lambda f: (wide * wide + i * steps + f, 0, 0))

    return pl.pallas_call(
        functools.partial(middle_body, cut),
        name="middle_stage",
        out_shape=(
            jax.ShapeDtypeStruct((positions, width), low),
            jax.ShapeDtypeStruct((cut, BS, BS), low),
            jax.ShapeDtypeStruct((wide * wide + 2 * wide * steps - cut, BS, BS), low),
            jax.ShapeDtypeStruct((positions, width), low),
            jax.ShapeDtypeStruct((positions, width), jnp.float32),
            jax.ShapeDtypeStruct((8, width), jnp.float32),
            jax.ShapeDtypeStruct((steps, BS), jnp.float32),
        ),
        grid=(steps,),
        in_specs=[
            tok,
            tok,
            tok,
            pl.BlockSpec((wide * wide, BS, BS), lambda f: (0, 0, 0)),
            up(0),
            up(1),
            up(2),
            pl.BlockSpec((wide, BS, BS), lambda f: (f, 0, 0)),
            pl.BlockSpec(vectors.shape, lambda f: (0, 0)),
        ],
        out_specs=[
            tok,
            pl.BlockSpec(memory_space=pl.ANY),
            pl.BlockSpec(memory_space=pl.ANY),
            tok,
            tok,
            pl.BlockSpec((8, width), lambda f: (0, 0)),
            pl.BlockSpec((steps, BS), lambda f: (0, 0)),
        ],
        scratch_shapes=[
            VMEM((positions, width), jnp.float32),
            VMEM((positions, width), low),
            VMEM((width, positions), low),
            VMEM((width, positions), low),
            VMEM((positions, width), jnp.float32),
            VMEM((positions, width), jnp.float32),
            VMEM((2, 2 * wide, BS, BS), low),
            VMEM((wide * wide, BS, BS), low),
            pltpu.SemaphoreType.DMA((2, 2 * wide)),
            pltpu.SemaphoreType.DMA,
        ],
        compiler_params=pltpu.CompilerParams(vmem_limit_bytes=48 << 20, dimension_semantics=("arbitrary",)),
        cost_estimate=pl.CostEstimate(flops=36 * positions * width * width, bytes_accessed=40 << 20, transcendentals=positions * width * 4),
    )(tokens, cotangent, mixed, weights, weights, weights, weights, down_weights, vectors)


def leave_body(spots, dhid_ref, pre_ref, own_t_ref, token_ref, row_ref, row_t_ref, dvalue_ref, weight_ref, vector_ref, sums_ref, bias_ref,
               dfirst_ref, dweight_ref, block_ref, back_ref, dpre_all, rows32):
    first_at, value_at = spots
    positions, width = dhid_ref.shape
    wide = width // BS
    sums = [jnp.zeros((1, width), jnp.float32) for _ in range(3)]

    def unproject(grads, at, i):
        total = None
        for j in range(wide):
            part = dot_nt(grads[:, column(j)], weight_ref[at + i * wide + j])
            total = part if total is None else total + part
        return total

    def own(c, sums):
        rows = pl.ds(pl.multiple_of(c * BS, BS), BS)
        pre = pre_ref[rows, :]
        share = gate(pre)
        dpre = (dhid_ref[rows, :].astype(jnp.float32) * (share * (1.0 + pre * (1.0 - share)))).astype(jnp.bfloat16)
        dpre_all[rows, :] = dpre
        hat, _ = normalize(token_ref[rows, :].astype(jnp.float32))
        back = jnp.concatenate([unproject(dpre, first_at, i) for i in range(wide)], axis=1)
        back_ref[rows, :] = back
        return (
            sums[0] + jnp.sum(back * hat, axis=0, keepdims=True),
            sums[1] + jnp.sum(back, axis=0, keepdims=True),
            sums[2] + jnp.sum(dpre.astype(jnp.float32), axis=0, keepdims=True),
        )

    sums = lax.fori_loop(0, positions // BS, own, tuple(sums))

    def whole_row(c, sums):
        rows = pl.ds(pl.multiple_of(c * BS, BS), BS)
        dvalue = dvalue_ref[rows, :]
        hat, _ = normalize(row_ref[rows, :].astype(jnp.float32))
        back = jnp.concatenate([unproject(dvalue, value_at, i) for i in range(wide)], axis=1)
        return (
            sums[0] + jnp.sum(back * hat, axis=0, keepdims=True),
            sums[1] + jnp.sum(back, axis=0, keepdims=True),
            sums[2],
        )

    sums = lax.fori_loop(0, row_ref.shape[0] // BS, whole_row, sums)
    for i in range(wide):
        for j in range(wide):
            dfirst_ref[i * wide + j] = dot_nn(own_t_ref[column(i), :], dpre_all[:, column(j)]).astype(jnp.bfloat16)
            dweight_ref[i * wide + j] = dot_nn(row_t_ref[column(i), :], dvalue_ref[:, column(j)]).astype(jnp.bfloat16)
    rows32[...] = jnp.zeros_like(rows32)
    lines = (sums[0], sums[1], sums_ref[0:1], sums_ref[1:2], sums[2])
    for r, line in enumerate(lines):
        for i in range(wide):
            rows32[r * wide + i:r * wide + i + 1, :] = line[:, column(i)]
    at = len(lines) * wide
    rows32[at:at + bias_ref.shape[0], :] = bias_ref[...]
    block_ref[0] = jnp.zeros_like(block_ref[0])
    block_ref[0, 0:rows32.shape[0], :] = rows32[...].astype(jnp.bfloat16)


def leave(dhid, pre, own_t, tokens, token_row, row_t, dvalue, weights, vectors, sums, bias, spots):
    positions, width = dhid.shape
    wide = width // BS
    whole = pl.BlockSpec(memory_space=VMEM)
    low = jnp.bfloat16
    tall = -(-(5 * wide + bias.shape[0]) // 16) * 16
    return pl.pallas_call(
        functools.partial(leave_body, spots),
        name="leave",
        out_shape=(
            jax.ShapeDtypeStruct((wide * wide, BS, BS), low),
            jax.ShapeDtypeStruct((wide * wide, BS, BS), low),
            jax.ShapeDtypeStruct((1, BS, BS), low),
            jax.ShapeDtypeStruct((positions, width), jnp.float32),
        ),
        in_specs=[whole] * 11,
        out_specs=[whole] * 4,
        scratch_shapes=[VMEM((positions, width), low), VMEM((tall, BS), jnp.float32)],
        compiler_params=pltpu.CompilerParams(vmem_limit_bytes=48 << 20),
        cost_estimate=pl.CostEstimate(flops=4 * (positions + token_row.shape[0]) * width * width, bytes_accessed=24 << 20, transcendentals=positions * width),
    )(dhid, pre, own_t, tokens, token_row, row_t, dvalue, weights, vectors, sums, bias)


def finish_body(value_at, dvalue_ref, first_ref, dmiddle_ref, token_ref, weight_ref, vector_ref, out_ref):
    wide = vector_ref.shape[1] // BS

    def chunk(c, carry):
        rows = pl.ds(pl.multiple_of(c * BS, BS), BS)
        dvalue = dvalue_ref[rows, :]
        parts = []
        for i in range(wide):
            total = first_ref[rows, column(i)]
            for j in range(wide):
                total = total + dot_nt(dvalue[:, column(j)], weight_ref[value_at + i * wide + j])
            parts.append(total)
        scaled = jnp.concatenate(parts, axis=1) * vector_ref[0:1]
        hat, inverse = normalize(token_ref[rows, :].astype(jnp.float32))
        out_ref[rows, :] = dmiddle_ref[rows, :] + inverse * (
            scaled
            - jnp.mean(scaled, axis=-1, keepdims=True)
            - hat * jnp.mean(scaled * hat, axis=-1, keepdims=True)
        )
        return carry

    lax.fori_loop(0, token_ref.shape[0] // BS, chunk, 0)


def finish_inputs(dvalue, from_first, dmiddle, tokens, weights, vectors, value_at):
    whole = pl.BlockSpec(memory_space=VMEM)
    positions, width = tokens.shape
    return pl.pallas_call(
        functools.partial(finish_body, value_at),
        name="finish_inputs",
        out_shape=jax.ShapeDtypeStruct((positions, width), jnp.float32),
        in_specs=[whole] * 6,
        out_specs=whole,
        compiler_params=pltpu.CompilerParams(vmem_limit_bytes=40 << 20),
        cost_estimate=pl.CostEstimate(flops=2 * positions * width * width, bytes_accessed=12 << 20, transcendentals=0),
    )(dvalue, from_first, dmiddle, tokens, weights, vectors)


def block_bounds():
    model_blocks = D // BS
    first_end = model_blocks * model_blocks
    synth_end = first_end + model_blocks * (LEN // BS)
    value_end = synth_end + first_end
    output_end = value_end + first_end
    expand_end = output_end + model_blocks * (FF // BS)
    return (first_end, synth_end, value_end, output_end, expand_end)


def block_scales():
    first_end, synth_end, value_end, output_end, expand_end = block_bounds()
    spots = jnp.arange(BLOCKS)
    scales = jnp.where(
        spots < first_end,
        D ** (-0.5),
        jnp.where(
            spots < synth_end,
            3.0 * HD ** (-0.5),
            jnp.where(
                spots < value_end,
                D ** (-0.5),
                jnp.where(
                    spots < output_end,
                    4.0 * D ** (-0.5),
                    jnp.where(spots < expand_end, D ** (-0.5), FF ** (-0.5)),
                ),
            ),
        ),
    )
    return scales.astype(jnp.float32)


def slot_table(owners, own_most, slot_total):
    block_count = owners.shape[0]
    block_index = jnp.arange(block_count, dtype=jnp.int32)
    same_owner = owners[:, None] == owners[None, :]
    earlier = block_index[None, :] < block_index[:, None]
    rank_within = jnp.sum(jnp.where(same_owner & earlier, 1, 0), axis=1).astype(jnp.int32)
    slot_id = owners * own_most + rank_within
    slot_hit = slot_id[:, None] == jnp.arange(slot_total, dtype=jnp.int32)[None, :]
    used = jnp.any(slot_hit, axis=0)
    block_of = jnp.sum(jnp.where(slot_hit, block_index[:, None], 0), axis=0)
    return (slot_id, used, block_of)


def vector_adam(vectors, vec_moments, grad_rows, mom_fix, sec_fix):
    first_moment = BETA_MOM * vec_moments[0] + (1 - BETA_MOM) * grad_rows
    second = BETA_SEC * vec_moments[1] + (1 - BETA_SEC) * grad_rows * grad_rows
    step_rows = first_moment / mom_fix / (jnp.sqrt(second / sec_fix) + EPSILON)
    return (vectors - VECTOR_RATE * step_rows, jnp.stack([first_moment, second]))


def local(
    tokens,
    cotangent,
    seg_ids,
    seg_lengths,
    weights,
    vectors,
    vec_moments,
    moments,
    stats,
    bases,
    owners,
    step_count,
):
    rows_here, positions, width = tokens.shape
    owner_count = lax.axis_size("row") * lax.axis_size("seq")
    own_most = moments.shape[0]
    slot_count = owner_count * own_most
    block_count = weights.shape[0]
    piece_rows = weights.shape[1] // BS
    first_end, synth_end, value_end, _, expand_end = block_bounds()
    synth_count = synth_end - first_end
    tokens = tokens.reshape(positions, width)
    pieces_one, pieces_two, pieces_three = spread_pieces(
        weights,
        (
            ((first_end, synth_end), (0, first_end), (synth_end, value_end)),
            ((value_end, expand_end),),
            ((expand_end, block_count),),
        ),
    )
    spots = (synth_count, synth_end)
    rows_total, seqs_total = lax.axis_size("row"), lax.axis_size("seq")
    (gathered_one, gathered_two), token_row = gather_rows(
        [pieces_one, pieces_two], tokens, rows_total, seqs_total, (2, 2), 3
    )
    gathered_one, pieces_three = lax.optimization_barrier((gathered_one, pieces_three))
    gathered_three = lax.all_gather(pieces_three, AXES, axis=1, tiled=True)

    slot_range = jnp.arange(seg_lengths.shape[1], dtype=jnp.int32)
    before = slot_range[None, :] < slot_range[:, None]
    starts = jnp.sum(jnp.where(before, seg_lengths[0][None, :], 0), axis=1)
    tq = tile_rows(positions)
    tile_ids = seg_ids[0].reshape(positions // tq, tq)
    offset = lax.axis_index("seq") * positions
    tables = jnp.concatenate(
        [
            starts,
            seg_lengths[0],
            tile_ids[:, 0],
            tile_ids[:, tq - 1] + 1,
            jnp.full((1,), offset, jnp.int32),
        ]
    ).astype(jnp.int32)

    hidden, first_pre, own_t, values, row_t = enter(tokens, token_row, gathered_one, vectors, spots)
    mixed, log_total = attn_forward(tables, hidden, gathered_one, values)
    layer_out, terms_two, early_terms, back_mixed, back_middle, norm_sums, grad_ffn_bias = middle_stage(
        tokens, cotangent.reshape(positions, width), mixed, gathered_two, gathered_three, vectors, 2
    )
    early_part = lax.psum_scatter(early_terms, "row", scatter_dimension=1, tiled=True)
    synth_grad, back_hidden, value_terms = attn_backward(
        tables, hidden, gathered_one, values, back_mixed, mixed, log_total
    )
    grad_first, grad_value, vector_block, back_from_first = leave(
        back_hidden,
        first_pre,
        own_t,
        tokens,
        token_row,
        row_t,
        value_terms,
        gathered_one,
        vectors,
        norm_sums,
        grad_ffn_bias,
        spots,
    )
    late_terms = [grad_first, grad_value, vector_block, synth_grad, terms_two]
    vector_rows = vectors.shape[0] * vectors.shape[1] // BS
    sums = reduce_rows(late_terms, early_part, rows_total, seqs_total, 6, 1)
    slot_id, used, block_of = slot_table(owners, own_most, slot_count)
    device_index = lax.axis_index(AXES)
    mine_used = lax.dynamic_slice_in_dim(used, device_index * own_most, own_most)
    mine_block = lax.dynamic_slice_in_dim(block_of, device_index * own_most, own_most)
    vector_spot = 2 * first_end
    spot_of = jnp.where(
        block_of < first_end,
        block_of,
        jnp.where(
            block_of < synth_end,
            block_of + first_end + 1,
            jnp.where(block_of < value_end, block_of - synth_end + first_end, block_of + 1),
        ),
    )
    got, square_parts, vector_parts = exchange(
        spot_of, sums, rows_total, seqs_total, vector_spot, vector_rows, 2
    )
    got, value_late = lax.optimization_barrier((got, value_terms))
    value_sums = lax.psum_scatter(value_late, "seq", scatter_dimension=0, tiled=True)
    x_grad = finish_inputs(
        value_sums, back_from_first, back_middle, tokens, gathered_one, vectors, synth_end
    )
    vector_total = vector_parts.reshape(-1, BS)[:vector_rows].reshape(vectors.shape)
    grad_norm = jnp.sqrt(jnp.sum(square_parts))
    clip_max = math.sqrt(block_count * BS * BS + vectors.shape[0] * vectors.shape[1])
    scale = jnp.minimum(1.0, clip_max / grad_norm)
    step_value = step_count[0].astype(jnp.float32)
    mom_fix = 1.0 - jnp.power(BETA_MOM, step_value)
    sec_fix = 1.0 - jnp.power(BETA_SEC, step_value)
    new_vectors, new_vec_moments = vector_adam(
        vectors, vec_moments, vector_total * scale, mom_fix, sec_fix
    )
    rate_table = RATE_FACTOR * block_scales()
    slot_rates = jnp.sum(
        jnp.where(
            mine_block[:, None] == jnp.arange(block_count, dtype=jnp.int32)[None, :],
            rate_table[None, :],
            0.0,
        ),
        axis=1,
    )
    floats = jnp.concatenate([jnp.stack([scale, mom_fix, sec_fix]), slot_rates])
    mine_spot = jnp.where(
        mine_block < first_end,
        mine_block + synth_count,
        jnp.where(mine_block < synth_end, mine_block - first_end, mine_block),
    )
    ints = jnp.concatenate([mine_used.astype(jnp.int32), mine_spot])
    new_master, new_moments, new_stats, wide = soap_update(
        ints, floats, got, gathered_one, gathered_two, gathered_three, moments, stats, bases
    )
    new_bases = soap_bases(ints, wide, bases)
    returned = lax.all_to_all(
        new_master.reshape(1, own_most, BS, BS), AXES, split_axis=2, concat_axis=0, tiled=True
    )
    new_weights = collect(slot_id, returned.reshape(slot_count, piece_rows, BS))
    return (
        layer_out.reshape(rows_here, positions, width),
        x_grad.reshape(rows_here, positions, width),
        new_weights,
        new_moments,
        new_stats,
        new_bases,
        new_vectors,
        new_vec_moments,
        grad_norm.reshape(1),
    )


def solution(mesh):
    placed = (
        P("row", "seq", None),
        P("row", "seq", None),
        P("row", "seq"),
        P("row", None),
        P(None, ("row", "seq")),
        P(),
        P(),
        P(("row", "seq"), None, None, None),
        P(("row", "seq"), None, None, None),
        P(("row", "seq"), None, None, None),
        P(),
        P(),
    )
    return jax.shard_map(
        local,
        mesh=mesh,
        in_specs=placed,
        out_specs=(
            P("row", "seq", None),
            P("row", "seq", None),
            P(None, ("row", "seq")),
            P(("row", "seq"), None, None, None),
            P(("row", "seq"), None, None, None),
            P(("row", "seq"), None, None, None),
            P(),
            P(),
            P(),
        ),
        check_vma=False,
    )
```

```python
import functools
import math

import jax
import jax.numpy as jnp
from jax import lax
from jax.experimental import pallas as pl
from jax.experimental.pallas import tpu as pltpu
from jax.sharding import PartitionSpec as P

D = 768
HEADS = 12
HD = 64
FF = 3072
LEN = 2048
BS = 256
BLOCKS = 123

BETA_MOM = 0.95
BETA_SEC = 0.95
EPSILON = 1e-08
DECAY = 0.01
VECTOR_RATE = 0.3
RATE_FACTOR = 2.0
NORM_EPS = 1e-05
NEG = -1e30
PANEL = 32
HIGHEST = lax.Precision.HIGHEST
VMEM = pltpu.VMEM
AXES = ("row", "seq")
MESH = pl.DeviceIdType.MESH


def dot_nn(a, b):
    return lax.dot_general(a, b, (((1,), (0,)), ((), ())), preferred_element_type=jnp.float32)


def dot_nt(a, b):
    return lax.dot_general(a, b, (((1,), (1,)), ((), ())), preferred_element_type=jnp.float32)


SMALL = 128


def tables_of(starts, lengths, ids, offset):
    ends = jnp.stack([ids[0], ids[-1] + 1, offset])
    return jnp.concatenate([starts, lengths, ends]).astype(jnp.int32)


def split_heads(synth_ref, value_ref, f2m, v32):
    length = value_ref.shape[0]
    low_rows = lax.broadcasted_iota(jnp.int32, (2 * HD, BS), 0) < HD
    for j in range(synth_ref.shape[0]):
        tile = synth_ref[j]
        zero = jnp.zeros_like(tile)
        f2m[0, j] = jnp.where(low_rows, tile, zero)
        f2m[1, j] = jnp.where(low_rows, zero, tile)
    v32[0:length] = value_ref[...].astype(jnp.float32)
    v32[length:] = jnp.zeros((BS, 2 * HD), jnp.float32)


def each_segment(tables, positions, visit):
    segs = (tables.shape[0] - 3) // 2
    offset = tables[2 * segs + 2]

    def segment(s, carry):
        start, count = tables[s], tables[segs + s]
        low = jnp.maximum(start - offset, 0)
        high = jnp.minimum(start + count - offset, positions)

        first = low // 16 * 16

        @pl.when(high - first > SMALL)
        def _():
            visit(start, count, positions, 0, low, high)

        @pl.when(high - first <= SMALL)
        def _():
            at = pl.multiple_of(jnp.minimum(first, positions - SMALL), 16)
            visit(start, count, SMALL, at, low, high)

        return carry

    lax.fori_loop(tables[2 * segs], tables[2 * segs + 1], segment, 0)


def attn_forward_body(tables, hid_ref, synth_ref, value_ref, mixed_ref, lse_ref, f2m, v32, lbuf):
    split_heads(synth_ref, value_ref, f2m, v32)
    lane = lax.broadcasted_iota(jnp.int32, (1, BS), 1)

    def visit(start, count, size, at, low, high):
        rows = pl.ds(at, size)
        hid = hid_ref[rows, :]
        used = (count + BS - 1) // BS

        def scores(j, tops):
            keep = lane < count - j * BS
            out = []
            for h in range(2):
                part = jnp.where(keep, dot_nn(hid, f2m[h, j]), NEG)
                lbuf[h, j, 0:size] = part
                out.append(jnp.maximum(tops[h], jnp.maximum(part[:, :128], part[:, 128:])))
            return tuple(out)

        none = jnp.full((size, 128), NEG, jnp.float32)
        tops = lax.fori_loop(0, used, scores, (none, none))
        tops = [jnp.max(top, axis=1, keepdims=True) for top in tops]

        def weigh(j, carried):
            value = v32[pl.ds(start + j * BS, BS), :].astype(jnp.bfloat16)
            out = []
            for h in range(2):
                total, mix = carried[h]
                part = jnp.exp(lbuf[h, j, 0:size] - tops[h])
                total = total + part[:, :128] + part[:, 128:]
                mix = mix + dot_nn(part.astype(jnp.bfloat16), value)
                out.append((total, mix))
            return tuple(out)

        blank = jnp.zeros((size, 128), jnp.float32)
        pair = lax.fori_loop(0, used, weigh, ((blank, blank), (blank, blank)))
        sums = [jnp.sum(total, axis=1, keepdims=True) for total, _ in pair]
        left = lax.broadcasted_iota(jnp.int32, (size, 2 * HD), 1) < HD
        mix = jnp.where(left, pair[0][1], pair[1][1]) / jnp.where(left, sums[0], sums[1])
        log = jnp.where(left, tops[0] + jnp.log(sums[0]), tops[1] + jnp.log(sums[1]))
        row = lax.broadcasted_iota(jnp.int32, (size, 1), 0) + at
        here = (row >= low) & (row < high)
        mixed_ref[rows, :] = jnp.where(here, mix, mixed_ref[rows, :])
        lse_ref[rows, :] = jnp.where(here, log, lse_ref[rows, :])

    each_segment(tables, hid_ref.shape[0], visit)


def attn_specs(positions, length):
    blocks, per = length // BS, BS // (2 * HD)
    return (
        pl.BlockSpec((positions, 2 * HD), lambda p, t: (0, p)),
        pl.BlockSpec((blocks, 2 * HD, BS), lambda p, t: (p // per, p % per, 0)),
        pl.BlockSpec((length, 2 * HD), lambda p, t: (0, p)),
    )


def attn_forward(tables, hidden, synth, values):
    positions, width = hidden.shape
    length = values.shape[0]
    blocks = length // BS
    tok, f2, val = attn_specs(positions, length)
    return pl.pallas_call(
        attn_forward_body,
        name="attn_forward",
        out_shape=(jax.ShapeDtypeStruct((positions, width), jnp.float32),) * 2,
        grid_spec=pltpu.PrefetchScalarGridSpec(
            num_scalar_prefetch=1,
            grid=(width // (2 * HD),),
            in_specs=[tok, f2, val],
            out_specs=[tok] * 2,
            scratch_shapes=[
                pltpu.VMEM((2, blocks, 2 * HD, BS), jnp.bfloat16),
                pltpu.VMEM((length + BS, 2 * HD), jnp.float32),
                pltpu.VMEM((2, blocks, positions, BS), jnp.float32),
            ],
        ),
        compiler_params=pltpu.CompilerParams(vmem_limit_bytes=60 << 20, dimension_semantics=("arbitrary",)),
        cost_estimate=pl.CostEstimate(flops=4 * positions * length * width * 2, bytes_accessed=12 << 20, transcendentals=positions * length * 12),
    )(tables, hidden, synth, values)


def attn_backward_body(tables, hid_ref, synth_ref, value_ref, dmix_ref, mixed_ref, lse_ref,
                       dsynth_ref, dhid_ref, dvalue_ref, f2m, v32, dv32, dmm, dacc, df2):
    length = value_ref.shape[0]
    split_heads(synth_ref, value_ref, f2m, v32)
    dv32[...] = jnp.zeros_like(dv32)
    df2[...] = jnp.zeros_like(df2)
    lane = lax.broadcasted_iota(jnp.int32, (1, BS), 1)

    def visit(start, count, size, at, low, high):
        rows = pl.ds(at, size)
        left = lax.broadcasted_iota(jnp.int32, (size, 2 * HD), 1) < HD
        row = lax.broadcasted_iota(jnp.int32, (size, 1), 0) + at
        here = (row >= low) & (row < high)
        hid = hid_ref[rows, :]
        hid_t = hid.astype(jnp.float32).T.astype(jnp.bfloat16)
        dmix32 = dmix_ref[rows, :].astype(jnp.float32)
        dmix_t = dmix32.T.astype(jnp.bfloat16)
        dot_pair = dmix32 * mixed_ref[rows, :]
        nil = jnp.zeros_like(dmix32)
        deltas = (
            jnp.sum(jnp.where(left, dot_pair, nil), axis=1, keepdims=True),
            jnp.sum(jnp.where(left, nil, dot_pair), axis=1, keepdims=True),
        )
        dmm[0, 0:size] = jnp.where(left, dmix32, nil).astype(jnp.bfloat16)
        dmm[1, 0:size] = jnp.where(left, nil, dmix32).astype(jnp.bfloat16)
        logs = lse_ref[rows, :]
        lse = [jnp.where(here, logs[:, h * HD:h * HD + 1], -NEG) for h in range(2)]
        dacc[0:size] = jnp.zeros((size, 2 * HD), jnp.float32)

        def block(j, carry):
            keep = lane < count - j * BS
            value = v32[pl.ds(start + j * BS, BS), :].astype(jnp.bfloat16)
            parts = []
            total = None
            for h in range(2):
                synth = f2m[h, j]
                prob = jnp.where(keep, jnp.exp(dot_nn(hid, synth) - lse[h]), 0.0)
                dprob = dot_nt(dmm[h, 0:size], value)
                dlog = (prob * (dprob - deltas[h])).astype(jnp.bfloat16)
                head = slice(h * HD, (h + 1) * HD)
                df2[j, head, :] += dot_nn(hid_t[head], dlog)
                back = dot_nt(dlog, synth)
                total = back if total is None else total + back
                parts.append(dot_nn(dmix_t[head], prob.astype(jnp.bfloat16)))
            dacc[0:size] += total
            dv32[pl.ds(start + j * BS, BS), :] += jnp.concatenate(parts, axis=0).T
            return carry

        lax.fori_loop(0, (count + BS - 1) // BS, block, 0)
        dhid_ref[rows, :] = jnp.where(here, dacc[0:size], dhid_ref[rows, :].astype(jnp.float32)).astype(jnp.bfloat16)

    each_segment(tables, hid_ref.shape[0], visit)
    dvalue_ref[...] = dv32[0:length].astype(jnp.bfloat16)
    dsynth_ref[...] = df2[...].astype(jnp.bfloat16)


def attn_backward(tables, hidden, synth, values, dmix, mixed, lse):
    positions, width = hidden.shape
    length = values.shape[0]
    blocks = length // BS
    tok, f2, val = attn_specs(positions, length)
    return pl.pallas_call(
        attn_backward_body,
        name="attn_backward",
        out_shape=(
            jax.ShapeDtypeStruct((width // BS * blocks, BS, BS), jnp.bfloat16),
            jax.ShapeDtypeStruct((positions, width), jnp.bfloat16),
            jax.ShapeDtypeStruct((length, width), jnp.bfloat16),
        ),
        grid_spec=pltpu.PrefetchScalarGridSpec(
            num_scalar_prefetch=1,
            grid=(width // (2 * HD),),
            in_specs=[tok, f2, val, tok, tok, tok],
            out_specs=[f2, tok, val],
            scratch_shapes=[
                pltpu.VMEM((2, blocks, 2 * HD, BS), jnp.bfloat16),
                pltpu.VMEM((length + BS, 2 * HD), jnp.float32),
                pltpu.VMEM((length + BS, 2 * HD), jnp.float32),
                pltpu.VMEM((2, positions, 2 * HD), jnp.bfloat16),
                pltpu.VMEM((positions, 2 * HD), jnp.float32),
                pltpu.VMEM((blocks, 2 * HD, BS), jnp.float32),
            ],
        ),
        compiler_params=pltpu.CompilerParams(vmem_limit_bytes=60 << 20, dimension_semantics=("arbitrary",)),
        cost_estimate=pl.CostEstimate(flops=10 * positions * length * width * 2, bytes_accessed=24 << 20, transcendentals=positions * length * 12),
    )(tables, hidden, synth, values, dmix, mixed, lse)


def exact(a, b, da=1, db=0):
    return lax.dot_general(a, b, (((da,), (db,)), ((), ())), precision=HIGHEST, preferred_element_type=jnp.float32)

def parts_of(values):
    first = values.astype(jnp.bfloat16)
    rest = values - first.astype(jnp.float32)
    second = rest.astype(jnp.bfloat16)
    return first, second, (rest - second.astype(jnp.float32)).astype(jnp.bfloat16)


LEFT_PARTS, RIGHT_PARTS = (0, 0, 1, 0, 1, 2), (0, 1, 0, 2, 1, 0)


def exact_thin(left, right, axis):
    lefts, rights = parts_of(left), parts_of(right)
    return lax.dot_general(
        jnp.concatenate([lefts[k] for k in LEFT_PARTS], axis=axis),
        jnp.concatenate([rights[k] for k in RIGHT_PARTS], axis=0),
        (((axis,), (0,)), ((), ())),
        preferred_element_type=jnp.float32,
    )


def soap_update_body(ints, floats, got_ref, one_ref, two_ref, three_ref, moment_ref, stat_ref, basis_ref,
                     new_master_ref, new_moment_ref, new_stat_ref, wide_ref, grad_ref, master_ref, sems):
    devices, slots, part = got_ref.shape[0], got_ref.shape[1], got_ref.shape[2]
    sources, at = [], 0
    for ref in (one_ref, two_ref, three_ref):
        sources.append((ref, at, at + ref.shape[0]))
        at += ref.shape[0]

    def master_copy(k, source):
        return pltpu.make_async_copy(source, master_ref.at[k], sems.at[k])

    for k in range(slots):
        block = ints[slots + k]
        for ref, low, high in sources:

            @pl.when((block >= low) & (block < high))
            def _():
                master_copy(k, ref.at[block - low]).start()

    scale, mom_fix, sec_fix = floats[0], floats[1], floats[2]

    per = max(1, 8 // part)

    def join(d, carry):
        rows = pl.ds(pl.multiple_of(d * (per * part), per * part), per * part)
        for k in range(slots):
            pieces = [got_ref[d * per + i, k].astype(jnp.float32) for i in range(per)]
            grad_ref[k, rows, :] = pieces[0] if per == 1 else jnp.concatenate(pieces, axis=0)
        return carry

    lax.fori_loop(0, devices // per, join, 0)
    for k in range(slots):
        master_copy(k, one_ref.at[0]).wait()

    def prepare(k, carry):
        used = ints[k] > 0
        grad = jnp.where(used, grad_ref[k] * scale, 0.0)
        left, right = basis_ref[k, 0], basis_ref[k, 1]
        old_left, old_right = stat_ref[k, 0], stat_ref[k, 1]
        left_stat = BETA_SEC * old_left + (1 - BETA_SEC) * exact(grad, grad, 1, 1)
        right_stat = BETA_SEC * old_right + (1 - BETA_SEC) * exact(grad, grad, 0, 0)
        new_stat_ref[k, 0] = jnp.where(used, left_stat, old_left)
        new_stat_ref[k, 1] = jnp.where(used, right_stat, old_right)
        left_t = left.T
        for side, (turn, stat) in enumerate(((left_t, left_stat), (right.T, right_stat))):
            cross = exact(turn, stat)
            wide_ref[2 * k + side, :, 0:BS] = exact(cross, cross, 1, 1)
            wide_ref[2 * k + side, :, BS:] = cross
        momentum = BETA_MOM * moment_ref[k, 0] + (1 - BETA_MOM) * grad
        turned_grad = exact(exact(left_t, grad), right)
        turned_mom = exact(exact(left_t, momentum), right)
        old_second = moment_ref[k, 1]
        second = BETA_SEC * old_second + (1 - BETA_SEC) * turned_grad * turned_grad
        step = turned_mom / mom_fix / (jnp.sqrt(second / sec_fix) + EPSILON)
        update = exact(exact(left, step), right, 1, 1)
        master = master_ref[k].astype(jnp.float32)
        new_master_ref[k] = (master - floats[3 + k] * (update + DECAY * master)).astype(jnp.bfloat16)
        new_moment_ref[k, 0] = jnp.where(used, momentum, moment_ref[k, 0])
        new_moment_ref[k, 1] = jnp.where(used, second, old_second)
        return carry

    lax.fori_loop(0, slots, prepare, 0)


def soap_update(ints, floats, got, one, two, three, moments, stats, bases):
    slots = got.shape[1]
    whole = pl.BlockSpec(memory_space=VMEM)
    scalar = pl.BlockSpec(memory_space=pltpu.SMEM)
    anywhere = pl.BlockSpec(memory_space=pl.ANY)
    pair = jax.ShapeDtypeStruct(moments.shape, jnp.float32)
    return pl.pallas_call(
        soap_update_body,
        name="soap_update",
        out_shape=(
            jax.ShapeDtypeStruct((slots, BS, BS), jnp.bfloat16),
            pair,
            pair,
            jax.ShapeDtypeStruct((2 * slots, BS, 2 * BS), jnp.float32),
        ),
        in_specs=[scalar, scalar, whole, anywhere, anywhere, anywhere] + [whole] * 3,
        out_specs=[whole] * 4,
        scratch_shapes=[
            VMEM((slots, BS, BS), jnp.float32),
            VMEM((slots, BS, BS), jnp.bfloat16),
            pltpu.SemaphoreType.DMA((slots,)),
        ],
        compiler_params=pltpu.CompilerParams(vmem_limit_bytes=60 << 20),
        cost_estimate=pl.CostEstimate(flops=slots * 12 * 6 * 2 * BS ** 3, bytes_accessed=slots * 14 * 4 * BS * BS, transcendentals=slots * BS * BS),
    )(ints, floats, got, one, two, three, moments, stats, bases)


def soap_bases_body(ints, given_ref, basis_ref, new_basis_ref, wide):
    slots = basis_ref.shape[0]
    count = 2 * slots
    wide[...] = given_ref[...]
    group = 128 // PANEL
    groups = count // group
    row = lax.broadcasted_iota(jnp.int32, (PANEL, 128), 0)
    lane = lax.broadcasted_iota(jnp.int32, (PANEL, 128), 1)
    unit = jnp.where(row == lane % PANEL, 1.0, 0.0)
    spot = lane // PANEL * PANEL
    for p in range(BS // PANEL):
        low = p * PANEL
        rows = slice(low, low + PANEL)
        schur, inverse, pivots = [], [], []
        for q in range(groups):
            schur.append(jnp.concatenate([wide[q * group + i, rows, low:low + PANEL] for i in range(group)], axis=1))
            inverse.append(unit)
            pivots.append(unit)

        for k in range(PANEL):
            below = row > k
            for q in range(groups):
                a, b = schur[q], inverse[q]
                column = jnp.take_along_axis(a, spot + k, axis=1)
                pivot = jnp.take_along_axis(jnp.broadcast_to(a[k:k + 1], (8, 128)), spot[:8] + k, axis=1)[0:1]
                factor = jnp.where(below, column * (1.0 / pivot), 0.0)
                schur[q] = a - factor * a[k:k + 1]
                inverse[q] = b - factor * b[k:k + 1]
                pivots[q] = jnp.where(row == k, pivot, pivots[q])
        for q in range(groups):
            whole = inverse[q] * lax.rsqrt(pivots[q])
            for i in range(group):
                m = q * group + i
                near = low // 128 * 128
                limit = near + 128
                part = exact_thin(whole[:, i * PANEL:(i + 1) * PANEL], wide[m, rows, near:], 1)
                wide[m, rows, near:] = part
                if low + PANEL < limit:
                    wide[m, low + PANEL:limit, near:] -= exact_thin(
                        part[:, low + PANEL - near:limit - near], part, 0
                    )
                elif limit < BS:
                    above = wide[m, near:limit, limit:]
                    wide[m, limit:, limit:] -= exact(above[:, :BS - limit], above, 0, 0)

    def finish(k, carry):
        used = ints[k] > 0
        for side in range(2):
            new_basis_ref[k, side] = jnp.where(used, wide[2 * k + side, :, BS:].T, basis_ref[k, side])
        return carry

    lax.fori_loop(0, slots, finish, 0)


def soap_bases(ints, wide, bases):
    slots = bases.shape[0]
    whole = pl.BlockSpec(memory_space=VMEM)
    return pl.pallas_call(
        soap_bases_body,
        name="soap_bases",
        out_shape=jax.ShapeDtypeStruct(bases.shape, jnp.float32),
        in_specs=[pl.BlockSpec(memory_space=pltpu.SMEM), whole, whole],
        out_specs=whole,
        scratch_shapes=[VMEM(wide.shape, jnp.float32)],
        compiler_params=pltpu.CompilerParams(vmem_limit_bytes=60 << 20),
        cost_estimate=pl.CostEstimate(flops=slots * 4 * 6 * 2 * BS ** 3, bytes_accessed=slots * 8 * 4 * BS * BS, transcendentals=slots * BS * BS),
    )(ints, wide, bases)


def spread_pieces_body(orders, weight_ref, *refs):
    *out_refs, lay = refs
    for i in range(lay.shape[1]):
        lay[:, i, :] = weight_ref[:, i * BS:(i + 1) * BS]
    for out_ref, order in zip(out_refs, orders):
        at = 0
        for low, high in order:
            out_ref[at:at + high - low] = lay[low:high].astype(jnp.bfloat16)
            at += high - low


def spread_pieces(weights, orders):
    count, rows = weights.shape[0], weights.shape[1] // BS
    sizes = [sum(high - low for low, high in order) for order in orders]
    whole = pl.BlockSpec(memory_space=VMEM)
    return pl.pallas_call(
        functools.partial(spread_pieces_body, orders),
        name="spread_pieces",
        out_shape=[jax.ShapeDtypeStruct((size, rows, BS), jnp.bfloat16) for size in sizes],
        in_specs=[whole],
        out_specs=[whole] * len(sizes),
        scratch_shapes=[VMEM((count, rows, BS), jnp.float32)],
        compiler_params=pltpu.CompilerParams(vmem_limit_bytes=60 << 20),
    )(weights)


def collect_body(slot_id, piece_ref, out_ref):
    rows = piece_ref.shape[1]

    def place(m, carry):
        piece = piece_ref[slot_id[m]].astype(jnp.float32)
        for i in range(rows):
            out_ref[pl.ds(m, 1), i * BS:(i + 1) * BS] = piece[i:i + 1]
        return carry

    lax.fori_loop(0, out_ref.shape[0], place, 0)


def collect(slot_id, pieces):
    count, rows = slot_id.shape[0], pieces.shape[1]
    whole = pl.BlockSpec(memory_space=VMEM)
    return pl.pallas_call(
        collect_body,
        name="collect",
        out_shape=jax.ShapeDtypeStruct((count, rows * BS), jnp.float32),
        in_specs=[pl.BlockSpec(memory_space=pltpu.SMEM), whole],
        out_specs=whole,
        compiler_params=pltpu.CompilerParams(vmem_limit_bytes=60 << 20),
    )(slot_id, pieces)


def partners(bits):
    row, seq = lax.axis_index("row"), lax.axis_index("seq")
    core, flags, peers = row % 2, [], []
    for k in range(bits):
        flag = row // 2 ** (k + 1) % 2
        flags.append(flag)
        peers.append((row + (1 - 2 * flag) * 2 ** (k + 1), seq))
    return core, (row + 1 - 2 * core, seq), flags, peers


def greet(devices):
    barrier = pltpu.get_barrier_semaphore()
    for device in devices:
        pl.semaphore_signal(barrier, inc=1, device_id=device, device_id_type=MESH)
    pl.semaphore_wait(barrier, len(devices))


def in_turns(works):
    live = []
    works = list(works)
    while works or live:
        if works:
            live.append(works.pop(0))
        live = [work for work in reversed(live) if next(work, None) is not None][::-1]


def group_bounds(count, groups):
    return [(count * k // groups, count * (k + 1) // groups) for k in range(groups)]


def reduce_rows_body(bits, seqs, groups, given, *refs):
    in_refs, summed_ref, (out_ref, mine, near, *rest) = refs[:given], refs[given], refs[given + 1:]
    far = rest[:bits]
    spread, arrived, own_summed, got_summed, keep_sems, send, recv = rest[bits:]
    count, extra = mine.shape[0], own_summed.shape[0]
    part = out_ref.shape[1]
    core, sibling, flags, peers = partners(bits)
    row, seq = lax.axis_index("row"), lax.axis_index("seq")
    beside = [(row, (seq + k) % seqs) for k in range(1, seqs)]
    greet([sibling, *peers, *beside])
    used = [0]

    def copy(source, target, device):
        at = used[0]
        used[0] += 1
        return pltpu.make_async_remote_copy(
            src_ref=source, dst_ref=target, send_sem=send.at[at], recv_sem=recv.at[at],
            device_id=device, device_id_type=MESH,
        )

    some = slice(None)
    every = (some,) * bits
    bounds = group_bounds(count, groups)
    starts, kept = [[] for _ in bounds], [[] for _ in bounds]
    at = local = 0
    for ref in in_refs:
        for g, (low, high) in enumerate(bounds):
            begin, end = max(low, at), min(high, at + ref.shape[0])
            if begin < end:
                span, to = pl.ds(begin - at, end - begin), pl.ds(begin, end - begin)
                starts[g].append(copy(ref.at[(span, *every, 1 - core)], near.at[to], sibling))
                kept[g].append(pltpu.make_async_copy(ref.at[(span, *every, core)], mine.at[to], keep_sems.at[local]))
                local += 1
        at += ref.shape[0]
    for g in range(groups):
        for move in starts[g] + kept[g]:
            move.start()
    extras = [copy(summed_ref.at[:, device[1]], got_summed.at[k], device) for k, device in enumerate(beside)]
    own_extra = pltpu.make_async_copy(summed_ref.at[:, seq], own_summed, keep_sems.at[local])
    for move in (*extras, own_extra):
        move.start()

    def work(g):
        low, high = bounds[g]
        span = pl.ds(low, high - low)
        order = list(range(bits)) if g % 2 == 0 else list(range(bits - 1, -1, -1))
        place = [some] * bits
        for move in starts[g] + kept[g]:
            move.wait()

        def first(n, carry):
            total = mine[n].astype(jnp.float32) + near[n].astype(jnp.float32)
            mine[n] = total.astype(jnp.bfloat16)
            return carry

        lax.fori_loop(low, high, first, 0)
        for step, bit in enumerate(order):
            spot = bits - 1 - bit
            theirs = list(place)
            theirs[spot] = 1 - flags[bit]
            place[spot] = flags[bit]
            move = copy(mine.at[(span, *theirs)], far[step].at[span], peers[bit])
            move.start()
            yield True
            move.wait()
            last = step == bits - 1
            where = tuple(place)

            def add(n, carry, step=step, where=where, last=last):
                total = mine[(n, *where)].astype(jnp.float32) + far[step][n].astype(jnp.float32)
                if last:
                    for s in range(seqs):
                        spread[s, n] = total[s * part:(s + 1) * part].astype(jnp.bfloat16)
                else:
                    mine[(n, *where)] = total.astype(jnp.bfloat16)
                return carry

            lax.fori_loop(low, high, add, 0)
        final = [
            copy(spread.at[device[1], span], arrived.at[k, span], device) for k, device in enumerate(beside)
        ]
        for move in final:
            move.start()
        yield True
        for move in final:
            move.wait()

        def finish(n, carry):
            total = spread[seq, n].astype(jnp.float32)
            for k in range(seqs - 1):
                total = total + arrived[k, n].astype(jnp.float32)
            out_ref[n] = total
            return carry

        lax.fori_loop(low, high, finish, 0)

    in_turns([work(g) for g in range(groups)])
    for move in (*extras, own_extra):
        move.wait()

    def add_extra(n, carry):
        total = own_summed[n].astype(jnp.float32)
        for k in range(seqs - 1):
            total = total + got_summed[k, n].astype(jnp.float32)
        out_ref[count + n] = total
        return carry

    lax.fori_loop(0, extra, add_extra, 0)


def reduce_rows(terms, summed, rows, seqs, groups, collective):
    count = sum(term.shape[0] for term in terms)
    bits = (rows // 2).bit_length() - 1
    slab = BS // rows
    part = slab // seqs
    twos = (2,) * bits
    low = jnp.bfloat16
    most = len(terms) + groups + 1
    sems = groups * (bits + seqs - 1) + most + seqs
    extra = summed.shape[0]
    return pl.pallas_call(
        functools.partial(reduce_rows_body, bits, seqs, groups, len(terms)),
        name="reduce_rows",
        out_shape=jax.ShapeDtypeStruct((count + extra, part, BS), jnp.float32),
        in_specs=[pl.BlockSpec(memory_space=pl.ANY)] * (len(terms) + 1),
        out_specs=pl.BlockSpec(memory_space=VMEM),
        scratch_shapes=[
            VMEM((count, *twos, slab, BS), low),
            VMEM((count, *twos, slab, BS), low),
            *[VMEM((count, *twos[k + 1:], slab, BS), low) for k in range(bits)],
            VMEM((seqs, count, part, BS), low),
            VMEM((seqs - 1, count, part, BS), low),
            VMEM((extra, part, BS), low),
            VMEM((seqs - 1, extra, part, BS), low),
            pltpu.SemaphoreType.DMA((most,)),
            pltpu.SemaphoreType.DMA((sems,)),
            pltpu.SemaphoreType.DMA((sems,)),
        ],
        compiler_params=pltpu.CompilerParams(
            collective_id=collective, has_side_effects=True, vmem_limit_bytes=60 << 20
        ),
        cost_estimate=pl.CostEstimate(flops=count * BS * BS, bytes_accessed=4 * count * BS * BS, transcendentals=0),
    )(*[term.reshape(-1, *twos, 2, slab, BS) for term in terms], summed.reshape(-1, seqs, part, BS))


def exchange_body(seqs, sources, spot_of, late_ref, got_ref, square_ref, vector_ref, out, mine, send, recv):
    devices, own = got_ref.shape[0], got_ref.shape[1]
    part = late_ref.shape[1]
    me = lax.axis_index("row") * seqs + lax.axis_index("seq")
    barrier = pltpu.get_barrier_semaphore()

    def peer(k):
        to = (me + k) % devices
        return to, (to // seqs, to % seqs)

    def hello(k, carry):
        pl.semaphore_signal(barrier, inc=1, device_id=peer(k)[1], device_id_type=MESH)
        return carry

    lax.fori_loop(1, devices, hello, 0)

    def place(d, carry):
        for s in range(own):
            out[d, s] = late_ref[spot_of[d * own + s]].astype(jnp.bfloat16)
        return carry

    lax.fori_loop(0, devices, place, 0)

    def add(ref, total):
        def step(m, total):
            value = ref[m].astype(jnp.float32)
            return total + value * value

        return lax.fori_loop(0, ref.shape[0], step, total)

    total = add(late_ref, jnp.zeros((part, BS), jnp.float32))
    mine[...] = total[:, :128] + total[:, 128:]
    pl.semaphore_wait(barrier, devices - 1)

    def move(source, target, kind, k, device):
        return pltpu.make_async_remote_copy(
            src_ref=source, dst_ref=target, send_sem=send.at[kind, k], recv_sem=recv.at[kind, k],
            device_id=device, device_id_type=MESH,
        )

    def moves(k):
        to, device = peer(k)
        return (
            move(out.at[to], got_ref.at[me], 0, k, device),
            move(mine, square_ref.at[me], 1, k, device),
        )

    def launch(k, carry):
        for one in moves(k):
            one.start()
        return carry

    lax.fori_loop(1, devices, launch, 0)

    @pl.when(me < sources[0])
    def _():
        def tell(k, carry):
            move(late_ref.at[sources[1]], vector_ref.at[me], 2, k, peer(k)[1]).start()
            return carry

        lax.fori_loop(1, devices, tell, 0)
        vector_ref[me] = late_ref[sources[1]]

    got_ref[me] = out[me]
    square_ref[me] = mine[...]

    def finish(k, carry):
        for one in moves(k):
            one.wait()
        return carry

    lax.fori_loop(1, devices, finish, 0)

    @pl.when(me < sources[0])
    def _():
        def told(k, carry):
            move(late_ref.at[sources[1]], vector_ref.at[me], 2, k, peer(k)[1]).wait_send()
            return carry

        lax.fori_loop(1, devices, told, 0)

    for d in range(sources[0]):
        @pl.when(me != d)
        def _():
            k = (me - d + devices) % devices
            move(late_ref.at[sources[1]], vector_ref.at[d], 2, k, peer(k)[1]).wait_recv()


def exchange(spot_of, late, rows, seqs, vector_spot, vector_rows, collective):
    devices = rows * seqs
    part = late.shape[1]
    own = spot_of.shape[0] // devices
    told = -(-vector_rows // part)
    whole = pl.BlockSpec(memory_space=VMEM)
    return pl.pallas_call(
        functools.partial(exchange_body, seqs, (told, vector_spot)),
        name="exchange",
        out_shape=(
            jax.ShapeDtypeStruct((devices, own, part, BS), jnp.bfloat16),
            jax.ShapeDtypeStruct((devices, part, 128), jnp.float32),
            jax.ShapeDtypeStruct((told, part, BS), jnp.float32),
        ),
        in_specs=[pl.BlockSpec(memory_space=pltpu.SMEM), whole],
        out_specs=[whole] * 3,
        scratch_shapes=[
            VMEM((devices, own, part, BS), jnp.bfloat16),
            VMEM((part, 128), jnp.float32),
            pltpu.SemaphoreType.DMA((3, devices)),
            pltpu.SemaphoreType.DMA((3, devices)),
        ],
        compiler_params=pltpu.CompilerParams(
            collective_id=collective, has_side_effects=True, vmem_limit_bytes=60 << 20
        ),
    )(spot_of, late)


def gather_rows_body(bits, seqs, groups, ahead, parts, pace, given, *refs):
    piece_refs, token_ref = refs[:given], refs[given]
    full_refs, row_ref = refs[given + 1:2 * given + 1], refs[2 * given + 1]
    near, send, recv, chain_send, chain_recv, own_sem = refs[2 * given + 2:]
    core, sibling, flags, peers = partners(bits)
    row, seq = lax.axis_index("row"), lax.axis_index("seq")
    greet([sibling, *peers, *[(row, (seq + k) % seqs) for k in range(1, seqs)]])
    used = [0]

    def copy(source, target, device):
        at = used[0]
        used[0] += 1
        return pltpu.make_async_remote_copy(
            src_ref=source, dst_ref=target, send_sem=send.at[at], recv_sem=recv.at[at],
            device_id=device, device_id_type=MESH,
        )

    def hop(source, here, sems_out, sems_in, to_right, step):
        spot = seq - step if to_right else seq + step
        side = 0 if to_right else 1
        return pltpu.make_async_remote_copy(
            src_ref=source if step == 0 else here(spot), dst_ref=here(spot), send_sem=sems_out(side, step),
            recv_sem=sems_in(spot), device_id=(row, seq + (1 if to_right else -1)), device_id_type=MESH,
        )

    def ends(to_right, step):
        there = seq - step >= 0 if to_right else seq + step < seqs
        onward = seq + 1 < seqs if to_right else seq - 1 >= 0
        return there, onward

    def chain(line, step, finish=False):
        for to_right in (True, False):
            there, onward = ends(to_right, step)
            if step > 0 and not finish:

                @pl.when(there)
                def _():
                    hop(*line, to_right, step).wait_recv()

            @pl.when(there & onward)
            def _():
                move = hop(*line, to_right, step)
                if finish:
                    move.wait_send()
                else:
                    move.start()

    lines = []
    for g, (ref, low, high, to, _) in enumerate(groups):
        span, near_span = pl.ds(low, high - low), pl.ds(to, high - low)
        lines.append((
            piece_refs[ref].at[span],
            lambda spot, near_span=near_span: near.at[spot, near_span],
            lambda side, step, g=g: chain_send.at[g, side, step],
            lambda spot, g=g: chain_recv.at[g, spot],
        ))
    share = token_ref.shape[0] // parts

    def token_line(k):
        rows, at = pl.ds(k * share, share), len(groups) + k
        return (
            token_ref.at[rows],
            lambda spot: row_ref.at[spot, rows],
            lambda side, step: chain_send.at[at, side, step],
            lambda spot: chain_recv.at[at, spot],
        )

    token_lines = [token_line(k) for k in range(parts)]
    for line in lines:
        chain(line, 0)
    keep_tokens = pltpu.make_async_copy(token_ref, row_ref.at[seq], own_sem)
    keep_tokens.start()
    sent = []

    def work(g):
        ref, low, high, to, backwards = groups[g]
        full_ref = full_refs[ref]
        span = pl.ds(low, high - low)
        order = list(range(bits - 1, -1, -1)) if backwards else list(range(bits))
        for step in range(1, seqs):
            chain(lines[g], step)
            yield True

        def join(n, carry):
            pieces = [
                jnp.where(seq == s, piece_refs[ref][low + n], near[s, to + n]).astype(jnp.float32)
                for s in range(seqs)
            ]
            slab = jnp.concatenate(pieces, axis=0)
            full_ref[(low + n, *flags[::-1], core)] = slab.astype(jnp.bfloat16)
            return carry

        lax.fori_loop(0, high - low, join, 0)
        coming = [[] for _ in order]

        def pass_on(place, level):
            spot = full_ref.at[(span, *place[::-1], core)]
            for later in range(level + 1, bits):
                bit = order[later]
                move = copy(spot, spot, peers[bit])
                move.start()
                there = list(place)
                there[bit] = 1 - flags[bit]
                coming[later].append((tuple(there), move))
                sent.append(move)
            move = copy(spot, spot, sibling)
            move.start()
            across.append(move)

        pass_on(tuple(flags), -1)
        for level in range(bits):
            yield True
            for place, move in coming[level]:
                move.wait_recv()
                pass_on(place, level)

    across = []

    works = [work(g) for g in range(len(groups))]
    hops = [(line, step) for step in range(seqs) for line in token_lines]
    for turn in range(bits + seqs):
        for one in works:
            next(one, None)
        if turn >= ahead:
            for line, step in hops[:parts if turn == ahead else pace]:
                chain(line, step)
                hops = hops[1:]
    for line, step in hops:
        chain(line, step)
    for move in sent:
        move.wait_send()
    for move in across:
        move.wait()
    keep_tokens.wait()
    for line in [*lines, *token_lines]:
        for step in range(seqs):
            chain(line, step, True)


def gather_rows(pieces, tokens, rows, seqs, cuts, collective, ahead=2, parts=1, pace=1):
    part = pieces[0].shape[1]
    bits = (rows // 2).bit_length() - 1
    slab = BS // rows
    twos = (2,) * bits
    low = jnp.bfloat16
    whole = pl.BlockSpec(memory_space=VMEM)
    groups, at = [], 0
    for ref, piece in enumerate(pieces):
        for begin, end in group_bounds(piece.shape[0], cuts[ref]):
            groups.append((ref, begin, end, at, len(groups) % 2 == 1))
            at += end - begin
    sems = len(groups) * (2 * 2 ** bits - 1)
    *full, token_row = pl.pallas_call(
        functools.partial(gather_rows_body, bits, seqs, groups, ahead, parts, pace, len(pieces)),
        name="gather_rows",
        out_shape=(
            *[jax.ShapeDtypeStruct((piece.shape[0], *twos, 2, slab, BS), low) for piece in pieces],
            jax.ShapeDtypeStruct((seqs, *tokens.shape), low),
        ),
        in_specs=[whole] * (len(pieces) + 1),
        out_specs=[whole] * (len(pieces) + 1),
        scratch_shapes=[
            VMEM((seqs, at, part, BS), low),
            pltpu.SemaphoreType.DMA((sems,)),
            pltpu.SemaphoreType.DMA((sems,)),
            pltpu.SemaphoreType.DMA((len(groups) + parts, 2, seqs)),
            pltpu.SemaphoreType.DMA((len(groups) + parts, seqs)),
            pltpu.SemaphoreType.DMA,
        ],
        compiler_params=pltpu.CompilerParams(
            collective_id=collective, has_side_effects=True, vmem_limit_bytes=60 << 20
        ),
        cost_estimate=pl.CostEstimate(flops=0, bytes_accessed=4 * at * BS * BS, transcendentals=0),
    )(*pieces, tokens)
    return [one.reshape(-1, BS, BS) for one in full], token_row.reshape(-1, tokens.shape[1])


def normalize(values):
    centered = values - jnp.mean(values, axis=-1, keepdims=True)
    inverse = lax.rsqrt(jnp.mean(centered * centered, axis=-1, keepdims=True) + NORM_EPS)
    return centered * inverse, inverse


def column(k):
    return slice(k * BS, (k + 1) * BS)


def gate(values):
    return 1.0 / (1.0 + jnp.exp(-values))


def enter_body(spots, token_ref, row_ref, weight_ref, vector_ref, hid_ref, pre_ref, own_t_ref, value_ref, row_t_ref):
    first_at, value_at = spots
    wide = vector_ref.shape[1] // BS
    gain, shift, bias = vector_ref[0:1], vector_ref[1:2], vector_ref[4:5]

    def project(inputs, at, j):
        total = dot_nn(inputs[:, column(0)], weight_ref[at + j])
        for i in range(1, wide):
            total = total + dot_nn(inputs[:, column(i)], weight_ref[at + i * wide + j])
        return total

    def own(c, carry):
        rows = pl.ds(pl.multiple_of(c * BS, BS), BS)
        normed = normalize(token_ref[rows, :].astype(jnp.float32))[0] * gain + shift
        inputs = normed.astype(jnp.bfloat16)
        own_t_ref[:, rows] = normed.T.astype(jnp.bfloat16)
        for j in range(wide):
            pre = project(inputs, first_at, j) + bias[:, column(j)]
            pre_ref[rows, column(j)] = pre
            hid_ref[rows, column(j)] = (pre * gate(pre)).astype(jnp.bfloat16)
        return carry

    lax.fori_loop(0, token_ref.shape[0] // BS, own, 0)

    def whole_row(c, carry):
        rows = pl.ds(pl.multiple_of(c * BS, BS), BS)
        normed = normalize(row_ref[rows, :].astype(jnp.float32))[0] * gain + shift
        inputs = normed.astype(jnp.bfloat16)
        row_t_ref[:, rows] = normed.T.astype(jnp.bfloat16)
        for j in range(wide):
            value_ref[rows, column(j)] = project(inputs, value_at, j).astype(jnp.bfloat16)
        return carry

    lax.fori_loop(0, row_ref.shape[0] // BS, whole_row, 0)


def enter(tokens, token_row, weights, vectors, spots):
    positions, width = tokens.shape
    length = token_row.shape[0]
    whole = pl.BlockSpec(memory_space=VMEM)
    low = jnp.bfloat16
    return pl.pallas_call(
        functools.partial(enter_body, spots),
        name="enter",
        out_shape=(
            jax.ShapeDtypeStruct((positions, width), low),
            jax.ShapeDtypeStruct((positions, width), jnp.float32),
            jax.ShapeDtypeStruct((width, positions), low),
            jax.ShapeDtypeStruct((length, width), low),
            jax.ShapeDtypeStruct((width, length), low),
        ),
        in_specs=[whole] * 4,
        out_specs=[whole] * 5,
        compiler_params=pltpu.CompilerParams(vmem_limit_bytes=60 << 20),
        cost_estimate=pl.CostEstimate(flops=2 * (positions + length) * width * width, bytes_accessed=24 << 20, transcendentals=positions * width),
    )(tokens, token_row, weights, vectors)


def middle_body(cut, token_ref, cotangent_ref, mixed_ref, output_ref, up_a, up_b, up_c, down_ref, vector_ref,
                out_ref, terms_ref, apart_ref, dmix_ref, dmiddle_ref, sums_ref, bias_ref,
                middle, normed_in, normed_t, back_t, total, back, made, made_output, sems, output_sem):
    f, last = pl.program_id(0), pl.num_programs(0) - 1
    ups = (up_a, up_b, up_c)
    wide = len(ups)
    first_up, steps = wide * wide, bias_ref.shape[0]
    slot = f % 2

    def spot(base, step):
        return apart_ref.at[base - cut + step] if base >= cut else terms_ref.at[base + step]

    @pl.when(f == 0)
    def _():
        mixed = mixed_ref[...].astype(jnp.bfloat16)
        for j in range(wide):
            part = token_ref[:, column(j)].astype(jnp.float32)
            for i in range(wide):
                part = part + dot_nn(mixed[:, column(i)], output_ref[i * wide + j])
            middle[:, column(j)] = part
        hat, _ = normalize(middle[...])
        inputs = hat * vector_ref[2:3] + vector_ref[3:4]
        normed_in[...] = inputs.astype(jnp.bfloat16)
        normed_t[...] = inputs.T.astype(jnp.bfloat16)
        total[...] = middle[...]
        back[...] = jnp.zeros_like(back)

    def copies(at, step):
        out = []
        for i in range(wide):
            out.append(pltpu.make_async_copy(made.at[at, i], spot(first_up + i * steps, step), sems.at[at, i]))
        for j in range(wide):
            out.append(pltpu.make_async_copy(made.at[at, wide + j], spot(first_up + wide * steps, step * wide + j), sems.at[at, wide + j]))
        return out

    @pl.when(f >= 2)
    def _():
        for move in copies(slot, f - 2):
            move.wait()

    inputs = normed_in[...]
    pre = vector_ref[pl.ds(5 + f // wide, 1), pl.ds(pl.multiple_of(f % wide * BS, BS), BS)]
    for i in range(wide):
        pre = pre + dot_nn(inputs[:, column(i)], ups[i][0])
    share = gate(pre)
    hidden = pre * share
    low_hidden = hidden.astype(jnp.bfloat16)
    hidden_t = hidden.T.astype(jnp.bfloat16)
    dhidden = None
    for j in range(wide):
        total[:, column(j)] += dot_nn(low_hidden, down_ref[j])
        made[slot, wide + j] = dot_nn(hidden_t, cotangent_ref[:, column(j)]).astype(jnp.bfloat16)
        part = dot_nt(cotangent_ref[:, column(j)], down_ref[j])
        dhidden = part if dhidden is None else dhidden + part
    dhidden = dhidden.astype(jnp.bfloat16).astype(jnp.float32)
    dpre = (dhidden * (share * (1.0 + pre * (1.0 - share)))).astype(jnp.bfloat16)
    bias_ref[pl.ds(f, 1), :] = jnp.sum(dpre.astype(jnp.float32), axis=0, keepdims=True)
    for i in range(wide):
        made[slot, i] = dot_nn(normed_t[column(i), :], dpre).astype(jnp.bfloat16)
        back[:, column(i)] += dot_nt(dpre, ups[i][0])
    for move in copies(slot, f):
        move.start()

    @pl.when(f == last)
    def _():
        out_ref[...] = total[...].astype(jnp.bfloat16)
        hat, inverse = normalize(middle[...])
        dnormed = back[...]
        sums_ref[...] = jnp.zeros_like(sums_ref)
        sums_ref[0:1] = jnp.sum(dnormed * hat, axis=0, keepdims=True)
        sums_ref[1:2] = jnp.sum(dnormed, axis=0, keepdims=True)
        scaled = dnormed * vector_ref[2:3]
        dmiddle = cotangent_ref[...].astype(jnp.float32) + inverse * (
            scaled
            - jnp.mean(scaled, axis=-1, keepdims=True)
            - hat * jnp.mean(scaled * hat, axis=-1, keepdims=True)
        )
        dmiddle_ref[...] = dmiddle
        low = dmiddle.astype(jnp.bfloat16)
        back_t[...] = mixed_ref[...].T.astype(jnp.bfloat16)
        for i in range(wide):
            part = None
            for j in range(wide):
                made_output[i * wide + j] = dot_nn(back_t[column(i), :], low[:, column(j)]).astype(jnp.bfloat16)
                term = dot_nt(low[:, column(j)], output_ref[i * wide + j])
                part = term if part is None else part + term
            dmix_ref[:, column(i)] = part.astype(jnp.bfloat16)
        move = pltpu.make_async_copy(made_output, terms_ref.at[0:wide * wide], output_sem)
        move.start()
        for one in copies(1 - slot, f - 1):
            one.wait()
        for one in copies(slot, f):
            one.wait()
        move.wait()


def middle_stage(tokens, cotangent, mixed, weights, down_weights, vectors, apart):
    positions, width = tokens.shape
    wide = width // BS
    steps = down_weights.shape[0] // wide
    cut = wide * wide + (wide - apart) * steps
    low = jnp.bfloat16
    tok = pl.BlockSpec((positions, width), lambda f: (0, 0))

    def up(i):
        return pl.BlockSpec((1, BS, BS), lambda f: (wide * wide + i * steps + f, 0, 0))

    return pl.pallas_call(
        functools.partial(middle_body, cut),
        name="middle_stage",
        out_shape=(
            jax.ShapeDtypeStruct((positions, width), low),
            jax.ShapeDtypeStruct((cut, BS, BS), low),
            jax.ShapeDtypeStruct((wide * wide + 2 * wide * steps - cut, BS, BS), low),
            jax.ShapeDtypeStruct((positions, width), low),
            jax.ShapeDtypeStruct((positions, width), jnp.float32),
            jax.ShapeDtypeStruct((8, width), jnp.float32),
            jax.ShapeDtypeStruct((steps, BS), jnp.float32),
        ),
        grid=(steps,),
        in_specs=[
            tok,
            tok,
            tok,
            pl.BlockSpec((wide * wide, BS, BS), lambda f: (0, 0, 0)),
            up(0),
            up(1),
            up(2),
            pl.BlockSpec((wide, BS, BS), lambda f: (f, 0, 0)),
            pl.BlockSpec(vectors.shape, lambda f: (0, 0)),
        ],
        out_specs=[
            tok,
            pl.BlockSpec(memory_space=pl.ANY),
            pl.BlockSpec(memory_space=pl.ANY),
            tok,
            tok,
            pl.BlockSpec((8, width), lambda f: (0, 0)),
            pl.BlockSpec((steps, BS), lambda f: (0, 0)),
        ],
        scratch_shapes=[
            VMEM((positions, width), jnp.float32),
            VMEM((positions, width), low),
            VMEM((width, positions), low),
            VMEM((width, positions), low),
            VMEM((positions, width), jnp.float32),
            VMEM((positions, width), jnp.float32),
            VMEM((2, 2 * wide, BS, BS), low),
            VMEM((wide * wide, BS, BS), low),
            pltpu.SemaphoreType.DMA((2, 2 * wide)),
            pltpu.SemaphoreType.DMA,
        ],
        compiler_params=pltpu.CompilerParams(vmem_limit_bytes=60 << 20, dimension_semantics=("arbitrary",)),
        cost_estimate=pl.CostEstimate(flops=36 * positions * width * width, bytes_accessed=40 << 20, transcendentals=positions * width * 4),
    )(tokens, cotangent, mixed, weights, weights, weights, weights, down_weights, vectors)


def leave_body(spots, dhid_ref, pre_ref, own_t_ref, token_ref, row_ref, row_t_ref, dvalue_ref, weight_ref, vector_ref, sums_ref, bias_ref,
               dfirst_ref, dweight_ref, block_ref, back_ref, dpre_all, rows32):
    first_at, value_at = spots
    positions, width = dhid_ref.shape
    wide = width // BS
    sums = [jnp.zeros((1, width), jnp.float32) for _ in range(3)]

    def unproject(grads, at, i):
        total = None
        for j in range(wide):
            part = dot_nt(grads[:, column(j)], weight_ref[at + i * wide + j])
            total = part if total is None else total + part
        return total

    def own(c, sums):
        rows = pl.ds(pl.multiple_of(c * BS, BS), BS)
        pre = pre_ref[rows, :]
        share = gate(pre)
        dpre = (dhid_ref[rows, :].astype(jnp.float32) * (share * (1.0 + pre * (1.0 - share)))).astype(jnp.bfloat16)
        dpre_all[rows, :] = dpre
        hat, _ = normalize(token_ref[rows, :].astype(jnp.float32))
        back = jnp.concatenate([unproject(dpre, first_at, i) for i in range(wide)], axis=1)
        back_ref[rows, :] = back
        return (
            sums[0] + jnp.sum(back * hat, axis=0, keepdims=True),
            sums[1] + jnp.sum(back, axis=0, keepdims=True),
            sums[2] + jnp.sum(dpre.astype(jnp.float32), axis=0, keepdims=True),
        )

    sums = lax.fori_loop(0, positions // BS, own, tuple(sums))

    def whole_row(c, sums):
        rows = pl.ds(pl.multiple_of(c * BS, BS), BS)
        dvalue = dvalue_ref[rows, :]
        hat, _ = normalize(row_ref[rows, :].astype(jnp.float32))
        back = jnp.concatenate([unproject(dvalue, value_at, i) for i in range(wide)], axis=1)
        return (
            sums[0] + jnp.sum(back * hat, axis=0, keepdims=True),
            sums[1] + jnp.sum(back, axis=0, keepdims=True),
            sums[2],
        )

    sums = lax.fori_loop(0, row_ref.shape[0] // BS, whole_row, sums)
    for i in range(wide):
        for j in range(wide):
            dfirst_ref[i * wide + j] = dot_nn(own_t_ref[column(i), :], dpre_all[:, column(j)]).astype(jnp.bfloat16)
            dweight_ref[i * wide + j] = dot_nn(row_t_ref[column(i), :], dvalue_ref[:, column(j)]).astype(jnp.bfloat16)
    rows32[...] = jnp.zeros_like(rows32)
    lines = (sums[0], sums[1], sums_ref[0:1], sums_ref[1:2], sums[2])
    for r, line in enumerate(lines):
        for i in range(wide):
            rows32[r * wide + i:r * wide + i + 1, :] = line[:, column(i)]
    at = len(lines) * wide
    rows32[at:at + bias_ref.shape[0], :] = bias_ref[...]
    block_ref[0] = jnp.zeros_like(block_ref[0])
    block_ref[0, 0:rows32.shape[0], :] = rows32[...].astype(jnp.bfloat16)


def leave(dhid, pre, own_t, tokens, token_row, row_t, dvalue, weights, vectors, sums, bias, spots):
    positions, width = dhid.shape
    wide = width // BS
    whole = pl.BlockSpec(memory_space=VMEM)
    low = jnp.bfloat16
    tall = -(-(5 * wide + bias.shape[0]) // 16) * 16
    return pl.pallas_call(
        functools.partial(leave_body, spots),
        name="leave",
        out_shape=(
            jax.ShapeDtypeStruct((wide * wide, BS, BS), low),
            jax.ShapeDtypeStruct((wide * wide, BS, BS), low),
            jax.ShapeDtypeStruct((1, BS, BS), low),
            jax.ShapeDtypeStruct((positions, width), jnp.float32),
        ),
        in_specs=[whole] * 11,
        out_specs=[whole] * 4,
        scratch_shapes=[VMEM((positions, width), low), VMEM((tall, BS), jnp.float32)],
        compiler_params=pltpu.CompilerParams(vmem_limit_bytes=60 << 20),
        cost_estimate=pl.CostEstimate(flops=4 * (positions + token_row.shape[0]) * width * width, bytes_accessed=24 << 20, transcendentals=positions * width),
    )(dhid, pre, own_t, tokens, token_row, row_t, dvalue, weights, vectors, sums, bias)


def finish_body(value_at, dvalue_ref, first_ref, dmiddle_ref, token_ref, weight_ref, vector_ref, out_ref):
    wide = vector_ref.shape[1] // BS

    def chunk(c, carry):
        rows = pl.ds(pl.multiple_of(c * BS, BS), BS)
        dvalue = dvalue_ref[rows, :]
        parts = []
        for i in range(wide):
            total = first_ref[rows, column(i)]
            for j in range(wide):
                total = total + dot_nt(dvalue[:, column(j)], weight_ref[value_at + i * wide + j])
            parts.append(total)
        scaled = jnp.concatenate(parts, axis=1) * vector_ref[0:1]
        hat, inverse = normalize(token_ref[rows, :].astype(jnp.float32))
        out_ref[rows, :] = dmiddle_ref[rows, :] + inverse * (
            scaled
            - jnp.mean(scaled, axis=-1, keepdims=True)
            - hat * jnp.mean(scaled * hat, axis=-1, keepdims=True)
        )
        return carry

    lax.fori_loop(0, token_ref.shape[0] // BS, chunk, 0)


def finish_inputs(dvalue, from_first, dmiddle, tokens, weights, vectors, value_at):
    whole = pl.BlockSpec(memory_space=VMEM)
    positions, width = tokens.shape
    return pl.pallas_call(
        functools.partial(finish_body, value_at),
        name="finish_inputs",
        out_shape=jax.ShapeDtypeStruct((positions, width), jnp.float32),
        in_specs=[whole] * 6,
        out_specs=whole,
        compiler_params=pltpu.CompilerParams(vmem_limit_bytes=60 << 20),
        cost_estimate=pl.CostEstimate(flops=2 * positions * width * width, bytes_accessed=12 << 20, transcendentals=0),
    )(dvalue, from_first, dmiddle, tokens, weights, vectors)


def block_bounds():
    model_blocks = D // BS
    first_end = model_blocks * model_blocks
    synth_end = first_end + model_blocks * (LEN // BS)
    value_end = synth_end + first_end
    output_end = value_end + first_end
    expand_end = output_end + model_blocks * (FF // BS)
    return (first_end, synth_end, value_end, output_end, expand_end)


def block_scales():
    first_end, synth_end, value_end, output_end, expand_end = block_bounds()
    spots = jnp.arange(BLOCKS)
    scales = jnp.where(
        spots < first_end,
        D ** (-0.5),
        jnp.where(
            spots < synth_end,
            3.0 * HD ** (-0.5),
            jnp.where(
                spots < value_end,
                D ** (-0.5),
                jnp.where(
                    spots < output_end,
                    4.0 * D ** (-0.5),
                    jnp.where(spots < expand_end, D ** (-0.5), FF ** (-0.5)),
                ),
            ),
        ),
    )
    return scales.astype(jnp.float32)


def slot_table(owners, own_most, slot_total):
    block_count = owners.shape[0]
    block_index = jnp.arange(block_count, dtype=jnp.int32)
    same_owner = owners[:, None] == owners[None, :]
    earlier = block_index[None, :] < block_index[:, None]
    rank_within = jnp.sum(jnp.where(same_owner & earlier, 1, 0), axis=1).astype(jnp.int32)
    slot_id = owners * own_most + rank_within
    slot_hit = slot_id[:, None] == jnp.arange(slot_total, dtype=jnp.int32)[None, :]
    used = jnp.any(slot_hit, axis=0)
    block_of = jnp.sum(jnp.where(slot_hit, block_index[:, None], 0), axis=0)
    return (slot_id, used, block_of)


def vector_adam(vectors, vec_moments, grad_rows, mom_fix, sec_fix):
    first_moment = BETA_MOM * vec_moments[0] + (1 - BETA_MOM) * grad_rows
    second = BETA_SEC * vec_moments[1] + (1 - BETA_SEC) * grad_rows * grad_rows
    step_rows = first_moment / mom_fix / (jnp.sqrt(second / sec_fix) + EPSILON)
    return (vectors - VECTOR_RATE * step_rows, jnp.stack([first_moment, second]))


def local(
    tokens,
    cotangent,
    seg_ids,
    seg_lengths,
    weights,
    vectors,
    vec_moments,
    moments,
    stats,
    bases,
    owners,
    step_count,
):
    rows_here, positions, width = tokens.shape
    owner_count = lax.axis_size("row") * lax.axis_size("seq")
    own_most = moments.shape[0]
    slot_count = owner_count * own_most
    block_count = weights.shape[0]
    piece_rows = weights.shape[1] // BS
    first_end, synth_end, value_end, _, expand_end = block_bounds()
    synth_count = synth_end - first_end
    tokens = tokens.reshape(positions, width)
    pieces_one, pieces_two, pieces_three = spread_pieces(
        weights,
        (
            ((first_end, synth_end), (0, first_end), (synth_end, value_end)),
            ((value_end, expand_end),),
            ((expand_end, block_count),),
        ),
    )
    spots = (synth_count, synth_end)
    rows_total, seqs_total = lax.axis_size("row"), lax.axis_size("seq")
    (gathered_one, gathered_two), token_row = gather_rows(
        [pieces_one, pieces_two], tokens, rows_total, seqs_total, (2, 2), 3
    )
    gathered_one, pieces_three = lax.optimization_barrier((gathered_one, pieces_three))
    gathered_three = lax.all_gather(pieces_three, AXES, axis=1, tiled=True)

    slot_range = jnp.arange(seg_lengths.shape[1], dtype=jnp.int32)
    before = slot_range[None, :] < slot_range[:, None]
    starts = jnp.sum(jnp.where(before, seg_lengths[0][None, :], 0), axis=1)
    offset = lax.axis_index("seq") * positions
    tables = tables_of(starts, seg_lengths[0], seg_ids[0], offset)

    hidden, first_pre, own_t, values, row_t = enter(tokens, token_row, gathered_one, vectors, spots)
    mixed, log_total = attn_forward(tables, hidden, gathered_one, values)
    layer_out, terms_two, early_terms, back_mixed, back_middle, norm_sums, grad_ffn_bias = middle_stage(
        tokens, cotangent.reshape(positions, width), mixed, gathered_two, gathered_three, vectors, 2
    )
    early_part = lax.psum_scatter(early_terms, "row", scatter_dimension=1, tiled=True)
    synth_grad, back_hidden, value_terms = attn_backward(
        tables, hidden, gathered_one, values, back_mixed, mixed, log_total
    )
    grad_first, grad_value, vector_block, back_from_first = leave(
        back_hidden,
        first_pre,
        own_t,
        tokens,
        token_row,
        row_t,
        value_terms,
        gathered_one,
        vectors,
        norm_sums,
        grad_ffn_bias,
        spots,
    )
    late_terms = [grad_first, grad_value, vector_block, synth_grad, terms_two]
    vector_rows = vectors.shape[0] * vectors.shape[1] // BS
    sums = reduce_rows(late_terms, early_part, rows_total, seqs_total, 6, 1)
    slot_id, used, block_of = slot_table(owners, own_most, slot_count)
    device_index = lax.axis_index(AXES)
    mine_used = lax.dynamic_slice_in_dim(used, device_index * own_most, own_most)
    mine_block = lax.dynamic_slice_in_dim(block_of, device_index * own_most, own_most)
    vector_spot = 2 * first_end
    spot_of = jnp.where(
        block_of < first_end,
        block_of,
        jnp.where(
            block_of < synth_end,
            block_of + first_end + 1,
            jnp.where(block_of < value_end, block_of - synth_end + first_end, block_of + 1),
        ),
    )
    got, square_parts, vector_parts = exchange(
        spot_of, sums, rows_total, seqs_total, vector_spot, vector_rows, 2
    )
    got, value_late = lax.optimization_barrier((got, value_terms))
    value_sums = lax.psum_scatter(value_late, "seq", scatter_dimension=0, tiled=True)
    x_grad = finish_inputs(
        value_sums, back_from_first, back_middle, tokens, gathered_one, vectors, synth_end
    )
    vector_total = vector_parts.reshape(-1, BS)[:vector_rows].reshape(vectors.shape)
    grad_norm = jnp.sqrt(jnp.sum(square_parts))
    clip_max = math.sqrt(block_count * BS * BS + vectors.shape[0] * vectors.shape[1])
    scale = jnp.minimum(1.0, clip_max / grad_norm)
    step_value = step_count[0].astype(jnp.float32)
    mom_fix = 1.0 - jnp.power(BETA_MOM, step_value)
    sec_fix = 1.0 - jnp.power(BETA_SEC, step_value)
    new_vectors, new_vec_moments = vector_adam(
        vectors, vec_moments, vector_total * scale, mom_fix, sec_fix
    )
    rate_table = RATE_FACTOR * block_scales()
    slot_rates = jnp.sum(
        jnp.where(
            mine_block[:, None] == jnp.arange(block_count, dtype=jnp.int32)[None, :],
            rate_table[None, :],
            0.0,
        ),
        axis=1,
    )
    floats = jnp.concatenate([jnp.stack([scale, mom_fix, sec_fix]), slot_rates])
    mine_spot = jnp.where(
        mine_block < first_end,
        mine_block + synth_count,
        jnp.where(mine_block < synth_end, mine_block - first_end, mine_block),
    )
    ints = jnp.concatenate([mine_used.astype(jnp.int32), mine_spot])
    new_master, new_moments, new_stats, wide = soap_update(
        ints, floats, got, gathered_one, gathered_two, gathered_three, moments, stats, bases
    )
    new_bases = soap_bases(ints, wide, bases)
    returned = lax.all_to_all(
        new_master.reshape(1, own_most, BS, BS), AXES, split_axis=2, concat_axis=0, tiled=True
    )
    new_weights = collect(slot_id, returned.reshape(slot_count, piece_rows, BS))
    return (
        layer_out.reshape(rows_here, positions, width),
        x_grad.reshape(rows_here, positions, width),
        new_weights,
        new_moments,
        new_stats,
        new_bases,
        new_vectors,
        new_vec_moments,
        grad_norm.reshape(1),
    )


def solution(mesh):
    placed = (
        P("row", "seq", None),
        P("row", "seq", None),
        P("row", "seq"),
        P("row", None),
        P(None, ("row", "seq")),
        P(),
        P(),
        P(("row", "seq"), None, None, None),
        P(("row", "seq"), None, None, None),
        P(("row", "seq"), None, None, None),
        P(),
        P(),
    )
    return jax.shard_map(
        local,
        mesh=mesh,
        in_specs=placed,
        out_specs=(
            P("row", "seq", None),
            P("row", "seq", None),
            P(None, ("row", "seq")),
            P(("row", "seq"), None, None, None),
            P(("row", "seq"), None, None, None),
            P(("row", "seq"), None, None, None),
            P(),
            P(),
            P(),
        ),
        check_vma=False,
    )
```

```python
import functools
import math

import jax
import jax.numpy as jnp
from jax import lax
from jax.experimental import pallas as pl
from jax.experimental.pallas import tpu as pltpu
from jax.sharding import PartitionSpec as P

D = 768
HEADS = 12
HD = 64
FF = 3072
LEN = 2048
BS = 256
BLOCKS = 123

BETA_MOM = 0.95
BETA_SEC = 0.95
EPSILON = 1e-08
DECAY = 0.01
VECTOR_RATE = 0.3
RATE_FACTOR = 2.0
NORM_EPS = 1e-05
NEG = -1e30
PANEL = 32
HIGHEST = lax.Precision.HIGHEST
VMEM = pltpu.VMEM
AXES = ("row", "seq")
MESH = pl.DeviceIdType.MESH


def dot_nn(a, b):
    return lax.dot_general(a, b, (((1,), (0,)), ((), ())), preferred_element_type=jnp.float32)


def dot_nt(a, b):
    return lax.dot_general(a, b, (((1,), (1,)), ((), ())), preferred_element_type=jnp.float32)


TILES = (128, 256)


def tables_of(starts, lengths, ids, offset):
    ends = jnp.stack([ids[0], ids[-1] + 1, offset])
    return jnp.concatenate([starts, lengths, ends]).astype(jnp.int32)


def split_heads(synth_ref, value_ref, f2m, v32):
    length = value_ref.shape[0]
    low_rows = lax.broadcasted_iota(jnp.int32, (2 * HD, BS), 0) < HD
    for j in range(synth_ref.shape[0]):
        tile = synth_ref[j]
        zero = jnp.zeros_like(tile)
        f2m[0, j] = jnp.where(low_rows, tile, zero)
        f2m[1, j] = jnp.where(low_rows, zero, tile)
    v32[0:length] = value_ref[...].astype(jnp.float32)
    v32[length:] = jnp.zeros((BS, 2 * HD), jnp.float32)


def each_segment(tables, positions, visit):
    segs = (tables.shape[0] - 3) // 2
    offset = tables[2 * segs + 2]

    def segment(s, carry):
        start, count = tables[s], tables[segs + s]
        low = jnp.maximum(start - offset, 0)
        high = jnp.minimum(start + count - offset, positions)

        first = low // 16 * 16

        sizes = [size for size in TILES if size < positions]
        for size, less in zip(sizes, [0, *sizes]):

            @pl.when((high - first <= size) & (high - first > less))
            def _(size=size):
                at = pl.multiple_of(jnp.minimum(first, positions - size), 16)
                visit(start, count, size, at, low, high)

        @pl.when(high - first > sizes[-1])
        def _():
            visit(start, count, positions, 0, low, high)

        return carry

    lax.fori_loop(tables[2 * segs], tables[2 * segs + 1], segment, 0)


def attn_forward_body(tables, hid_ref, synth_ref, value_ref, mixed_ref, lse_ref, f2m, v32, lbuf):
    split_heads(synth_ref, value_ref, f2m, v32)
    lane = lax.broadcasted_iota(jnp.int32, (1, BS), 1)

    def visit(start, count, size, at, low, high):
        rows = pl.ds(at, size)
        hid = hid_ref[rows, :]
        used = (count + BS - 1) // BS

        def scores(j, tops):
            keep = lane < count - j * BS
            out = []
            for h in range(2):
                part = jnp.where(keep, dot_nn(hid, f2m[h, j]), NEG)
                lbuf[h, j, 0:size] = part
                out.append(jnp.maximum(tops[h], jnp.maximum(part[:, :128], part[:, 128:])))
            return tuple(out)

        none = jnp.full((size, 128), NEG, jnp.float32)
        tops = lax.fori_loop(0, used, scores, (none, none))
        tops = [jnp.max(top, axis=1, keepdims=True) for top in tops]

        def weigh(j, carried):
            value = v32[pl.ds(start + j * BS, BS), :].astype(jnp.bfloat16)
            out = []
            for h in range(2):
                total, mix = carried[h]
                part = jnp.exp(lbuf[h, j, 0:size] - tops[h])
                total = total + part[:, :128] + part[:, 128:]
                mix = mix + dot_nn(part.astype(jnp.bfloat16), value)
                out.append((total, mix))
            return tuple(out)

        blank = jnp.zeros((size, 128), jnp.float32)
        pair = lax.fori_loop(0, used, weigh, ((blank, blank), (blank, blank)))
        sums = [jnp.sum(total, axis=1, keepdims=True) for total, _ in pair]
        left = lax.broadcasted_iota(jnp.int32, (size, 2 * HD), 1) < HD
        mix = jnp.where(left, pair[0][1], pair[1][1]) / jnp.where(left, sums[0], sums[1])
        log = jnp.where(left, tops[0] + jnp.log(sums[0]), tops[1] + jnp.log(sums[1]))
        row = lax.broadcasted_iota(jnp.int32, (size, 1), 0) + at
        here = (row >= low) & (row < high)
        mixed_ref[rows, :] = jnp.where(here, mix, mixed_ref[rows, :])
        lse_ref[rows, :] = jnp.where(here, log, lse_ref[rows, :])

    each_segment(tables, hid_ref.shape[0], visit)


def attn_specs(positions, length):
    blocks, per = length // BS, BS // (2 * HD)
    return (
        pl.BlockSpec((positions, 2 * HD), lambda p, t: (0, p)),
        pl.BlockSpec((blocks, 2 * HD, BS), lambda p, t: (p // per, p % per, 0)),
        pl.BlockSpec((length, 2 * HD), lambda p, t: (0, p)),
    )


def attn_forward(tables, hidden, synth, values):
    positions, width = hidden.shape
    length = values.shape[0]
    blocks = length // BS
    tok, f2, val = attn_specs(positions, length)
    return pl.pallas_call(
        attn_forward_body,
        name="attn_forward",
        out_shape=(jax.ShapeDtypeStruct((positions, width), jnp.float32),) * 2,
        grid_spec=pltpu.PrefetchScalarGridSpec(
            num_scalar_prefetch=1,
            grid=(width // (2 * HD),),
            in_specs=[tok, f2, val],
            out_specs=[tok] * 2,
            scratch_shapes=[
                pltpu.VMEM((2, blocks, 2 * HD, BS), jnp.bfloat16),
                pltpu.VMEM((length + BS, 2 * HD), jnp.float32),
                pltpu.VMEM((2, blocks, positions, BS), jnp.float32),
            ],
        ),
        compiler_params=pltpu.CompilerParams(vmem_limit_bytes=60 << 20, dimension_semantics=("arbitrary",)),
        cost_estimate=pl.CostEstimate(flops=4 * positions * length * width * 2, bytes_accessed=12 << 20, transcendentals=positions * length * 12),
    )(tables, hidden, synth, values)


def attn_backward_body(tables, hid_ref, synth_ref, value_ref, dmix_ref, mixed_ref, lse_ref,
                       dsynth_ref, dhid_ref, dvalue_ref, f2m, v32, dv32, dmm, dacc, df2):
    length = value_ref.shape[0]
    split_heads(synth_ref, value_ref, f2m, v32)
    dv32[...] = jnp.zeros_like(dv32)
    df2[...] = jnp.zeros_like(df2)
    lane = lax.broadcasted_iota(jnp.int32, (1, BS), 1)

    def visit(start, count, size, at, low, high):
        rows = pl.ds(at, size)
        left = lax.broadcasted_iota(jnp.int32, (size, 2 * HD), 1) < HD
        row = lax.broadcasted_iota(jnp.int32, (size, 1), 0) + at
        here = (row >= low) & (row < high)
        hid = hid_ref[rows, :]
        hid_t = hid.astype(jnp.float32).T.astype(jnp.bfloat16)
        dmix32 = dmix_ref[rows, :].astype(jnp.float32)
        dmix_t = dmix32.T.astype(jnp.bfloat16)
        dot_pair = dmix32 * mixed_ref[rows, :]
        nil = jnp.zeros_like(dmix32)
        deltas = (
            jnp.sum(jnp.where(left, dot_pair, nil), axis=1, keepdims=True),
            jnp.sum(jnp.where(left, nil, dot_pair), axis=1, keepdims=True),
        )
        dmm[0, 0:size] = jnp.where(left, dmix32, nil).astype(jnp.bfloat16)
        dmm[1, 0:size] = jnp.where(left, nil, dmix32).astype(jnp.bfloat16)
        logs = lse_ref[rows, :]
        lse = [jnp.where(here, logs[:, h * HD:h * HD + 1], -NEG) for h in range(2)]
        dacc[0:size] = jnp.zeros((size, 2 * HD), jnp.float32)

        def block(j, carry):
            keep = lane < count - j * BS
            value = v32[pl.ds(start + j * BS, BS), :].astype(jnp.bfloat16)
            parts = []
            total = None
            for h in range(2):
                synth = f2m[h, j]
                prob = jnp.where(keep, jnp.exp(dot_nn(hid, synth) - lse[h]), 0.0)
                dprob = dot_nt(dmm[h, 0:size], value)
                dlog = (prob * (dprob - deltas[h])).astype(jnp.bfloat16)
                head = slice(h * HD, (h + 1) * HD)
                df2[j, head, :] += dot_nn(hid_t[head], dlog)
                back = dot_nt(dlog, synth)
                total = back if total is None else total + back
                parts.append(dot_nn(dmix_t[head], prob.astype(jnp.bfloat16)))
            dacc[0:size] += total
            dv32[pl.ds(start + j * BS, BS), :] += jnp.concatenate(parts, axis=0).T
            return carry

        lax.fori_loop(0, (count + BS - 1) // BS, block, 0)
        dhid_ref[rows, :] = jnp.where(here, dacc[0:size], dhid_ref[rows, :].astype(jnp.float32)).astype(jnp.bfloat16)

    each_segment(tables, hid_ref.shape[0], visit)
    dvalue_ref[...] = dv32[0:length].astype(jnp.bfloat16)
    dsynth_ref[...] = df2[...].astype(jnp.bfloat16)


def attn_backward(tables, hidden, synth, values, dmix, mixed, lse):
    positions, width = hidden.shape
    length = values.shape[0]
    blocks = length // BS
    tok, f2, val = attn_specs(positions, length)
    return pl.pallas_call(
        attn_backward_body,
        name="attn_backward",
        out_shape=(
            jax.ShapeDtypeStruct((width // BS * blocks, BS, BS), jnp.bfloat16),
            jax.ShapeDtypeStruct((positions, width), jnp.bfloat16),
            jax.ShapeDtypeStruct((length, width), jnp.bfloat16),
        ),
        grid_spec=pltpu.PrefetchScalarGridSpec(
            num_scalar_prefetch=1,
            grid=(width // (2 * HD),),
            in_specs=[tok, f2, val, tok, tok, tok],
            out_specs=[f2, tok, val],
            scratch_shapes=[
                pltpu.VMEM((2, blocks, 2 * HD, BS), jnp.bfloat16),
                pltpu.VMEM((length + BS, 2 * HD), jnp.float32),
                pltpu.VMEM((length + BS, 2 * HD), jnp.float32),
                pltpu.VMEM((2, positions, 2 * HD), jnp.bfloat16),
                pltpu.VMEM((positions, 2 * HD), jnp.float32),
                pltpu.VMEM((blocks, 2 * HD, BS), jnp.float32),
            ],
        ),
        compiler_params=pltpu.CompilerParams(vmem_limit_bytes=60 << 20, dimension_semantics=("arbitrary",)),
        cost_estimate=pl.CostEstimate(flops=10 * positions * length * width * 2, bytes_accessed=24 << 20, transcendentals=positions * length * 12),
    )(tables, hidden, synth, values, dmix, mixed, lse)


def exact(a, b, da=1, db=0):
    return lax.dot_general(a, b, (((da,), (db,)), ((), ())), precision=HIGHEST, preferred_element_type=jnp.float32)

def parts_of(values):
    first = values.astype(jnp.bfloat16)
    rest = values - first.astype(jnp.float32)
    second = rest.astype(jnp.bfloat16)
    return first, second, (rest - second.astype(jnp.float32)).astype(jnp.bfloat16)


LEFT_PARTS, RIGHT_PARTS = (0, 0, 1, 0, 1, 2), (0, 1, 0, 2, 1, 0)


def exact_thin(left, right, axis):
    lefts, rights = parts_of(left), parts_of(right)
    return lax.dot_general(
        jnp.concatenate([lefts[k] for k in LEFT_PARTS], axis=axis),
        jnp.concatenate([rights[k] for k in RIGHT_PARTS], axis=0),
        (((axis,), (0,)), ((), ())),
        preferred_element_type=jnp.float32,
    )


def soap_update_body(ints, floats, got_ref, one_ref, two_ref, three_ref, moment_ref, stat_ref, basis_ref,
                     new_master_ref, new_moment_ref, new_stat_ref, wide_ref, grad_ref, master_ref, sems):
    devices, slots, part = got_ref.shape[0], got_ref.shape[1], got_ref.shape[2]
    sources, at = [], 0
    for ref in (one_ref, two_ref, three_ref):
        sources.append((ref, at, at + ref.shape[0]))
        at += ref.shape[0]

    def master_copy(k, source):
        return pltpu.make_async_copy(source, master_ref.at[k], sems.at[k])

    for k in range(slots):
        block = ints[slots + k]
        for ref, low, high in sources:

            @pl.when((block >= low) & (block < high))
            def _():
                master_copy(k, ref.at[block - low]).start()

    scale, mom_fix, sec_fix = floats[0], floats[1], floats[2]

    per = max(1, 8 // part)

    def join(d, carry):
        rows = pl.ds(pl.multiple_of(d * (per * part), per * part), per * part)
        for k in range(slots):
            pieces = [got_ref[d * per + i, k].astype(jnp.float32) for i in range(per)]
            grad_ref[k, rows, :] = pieces[0] if per == 1 else jnp.concatenate(pieces, axis=0)
        return carry

    lax.fori_loop(0, devices // per, join, 0)
    for k in range(slots):
        master_copy(k, one_ref.at[0]).wait()

    def prepare(k, carry):
        used = ints[k] > 0
        grad = jnp.where(used, grad_ref[k] * scale, 0.0)
        left, right = basis_ref[k, 0], basis_ref[k, 1]
        old_left, old_right = stat_ref[k, 0], stat_ref[k, 1]
        left_stat = BETA_SEC * old_left + (1 - BETA_SEC) * exact(grad, grad, 1, 1)
        right_stat = BETA_SEC * old_right + (1 - BETA_SEC) * exact(grad, grad, 0, 0)
        new_stat_ref[k, 0] = jnp.where(used, left_stat, old_left)
        new_stat_ref[k, 1] = jnp.where(used, right_stat, old_right)
        left_t = left.T
        for side, (turn, stat) in enumerate(((left_t, left_stat), (right.T, right_stat))):
            cross = exact(turn, stat)
            wide_ref[2 * k + side, :, 0:BS] = exact(cross, cross, 1, 1)
            wide_ref[2 * k + side, :, BS:] = cross
        momentum = BETA_MOM * moment_ref[k, 0] + (1 - BETA_MOM) * grad
        turned_grad = exact(exact(left_t, grad), right)
        turned_mom = exact(exact(left_t, momentum), right)
        old_second = moment_ref[k, 1]
        second = BETA_SEC * old_second + (1 - BETA_SEC) * turned_grad * turned_grad
        step = turned_mom / mom_fix / (jnp.sqrt(second / sec_fix) + EPSILON)
        update = exact(exact(left, step), right, 1, 1)
        master = master_ref[k].astype(jnp.float32)
        new_master_ref[k] = (master - floats[3 + k] * (update + DECAY * master)).astype(jnp.bfloat16)
        new_moment_ref[k, 0] = jnp.where(used, momentum, moment_ref[k, 0])
        new_moment_ref[k, 1] = jnp.where(used, second, old_second)
        return carry

    lax.fori_loop(0, slots, prepare, 0)


def soap_update(ints, floats, got, one, two, three, moments, stats, bases):
    slots = got.shape[1]
    whole = pl.BlockSpec(memory_space=VMEM)
    scalar = pl.BlockSpec(memory_space=pltpu.SMEM)
    anywhere = pl.BlockSpec(memory_space=pl.ANY)
    pair = jax.ShapeDtypeStruct(moments.shape, jnp.float32)
    return pl.pallas_call(
        soap_update_body,
        name="soap_update",
        out_shape=(
            jax.ShapeDtypeStruct((slots, BS, BS), jnp.bfloat16),
            pair,
            pair,
            jax.ShapeDtypeStruct((2 * slots, BS, 2 * BS), jnp.float32),
        ),
        in_specs=[scalar, scalar, whole, anywhere, anywhere, anywhere] + [whole] * 3,
        out_specs=[whole] * 4,
        scratch_shapes=[
            VMEM((slots, BS, BS), jnp.float32),
            VMEM((slots, BS, BS), jnp.bfloat16),
            pltpu.SemaphoreType.DMA((slots,)),
        ],
        compiler_params=pltpu.CompilerParams(vmem_limit_bytes=60 << 20),
        cost_estimate=pl.CostEstimate(flops=slots * 12 * 6 * 2 * BS ** 3, bytes_accessed=slots * 14 * 4 * BS * BS, transcendentals=slots * BS * BS),
    )(ints, floats, got, one, two, three, moments, stats, bases)


def soap_bases_body(ints, given_ref, basis_ref, new_basis_ref, wide):
    slots = basis_ref.shape[0]
    count = 2 * slots
    wide[...] = given_ref[...]
    group = 128 // PANEL
    groups = count // group
    row = lax.broadcasted_iota(jnp.int32, (PANEL, 128), 0)
    lane = lax.broadcasted_iota(jnp.int32, (PANEL, 128), 1)
    unit = jnp.where(row == lane % PANEL, 1.0, 0.0)
    spot = lane // PANEL * PANEL
    for p in range(BS // PANEL):
        low = p * PANEL
        rows = slice(low, low + PANEL)
        schur, inverse, pivots = [], [], []
        for q in range(groups):
            schur.append(jnp.concatenate([wide[q * group + i, rows, low:low + PANEL] for i in range(group)], axis=1))
            inverse.append(unit)
            pivots.append(unit)

        for k in range(PANEL):
            below = row > k
            for q in range(groups):
                a, b = schur[q], inverse[q]
                column = jnp.take_along_axis(a, spot + k, axis=1)
                pivot = jnp.take_along_axis(jnp.broadcast_to(a[k:k + 1], (8, 128)), spot[:8] + k, axis=1)[0:1]
                factor = jnp.where(below, column * (1.0 / pivot), 0.0)
                schur[q] = a - factor * a[k:k + 1]
                inverse[q] = b - factor * b[k:k + 1]
                pivots[q] = jnp.where(row == k, pivot, pivots[q])
        for q in range(groups):
            whole = inverse[q] * lax.rsqrt(pivots[q])
            for i in range(group):
                m = q * group + i
                near = low // 128 * 128
                limit = near + 128
                part = exact_thin(whole[:, i * PANEL:(i + 1) * PANEL], wide[m, rows, near:], 1)
                wide[m, rows, near:] = part
                if low + PANEL < limit:
                    wide[m, low + PANEL:limit, near:] -= exact_thin(
                        part[:, low + PANEL - near:limit - near], part, 0
                    )
                elif limit < BS:
                    above = wide[m, near:limit, limit:]
                    wide[m, limit:, limit:] -= exact(above[:, :BS - limit], above, 0, 0)

    def finish(k, carry):
        used = ints[k] > 0
        for side in range(2):
            new_basis_ref[k, side] = jnp.where(used, wide[2 * k + side, :, BS:].T, basis_ref[k, side])
        return carry

    lax.fori_loop(0, slots, finish, 0)


def soap_bases(ints, wide, bases):
    slots = bases.shape[0]
    whole = pl.BlockSpec(memory_space=VMEM)
    return pl.pallas_call(
        soap_bases_body,
        name="soap_bases",
        out_shape=jax.ShapeDtypeStruct(bases.shape, jnp.float32),
        in_specs=[pl.BlockSpec(memory_space=pltpu.SMEM), whole, whole],
        out_specs=whole,
        scratch_shapes=[VMEM(wide.shape, jnp.float32)],
        compiler_params=pltpu.CompilerParams(vmem_limit_bytes=60 << 20),
        cost_estimate=pl.CostEstimate(flops=slots * 4 * 6 * 2 * BS ** 3, bytes_accessed=slots * 8 * 4 * BS * BS, transcendentals=slots * BS * BS),
    )(ints, wide, bases)


def spread_pieces_body(orders, weight_ref, *refs):
    *out_refs, lay = refs
    for i in range(lay.shape[1]):
        lay[:, i, :] = weight_ref[:, i * BS:(i + 1) * BS]
    for out_ref, order in zip(out_refs, orders):
        at = 0
        for low, high in order:
            out_ref[at:at + high - low] = lay[low:high].astype(jnp.bfloat16)
            at += high - low


def spread_pieces(weights, orders):
    count, rows = weights.shape[0], weights.shape[1] // BS
    sizes = [sum(high - low for low, high in order) for order in orders]
    whole = pl.BlockSpec(memory_space=VMEM)
    return pl.pallas_call(
        functools.partial(spread_pieces_body, orders),
        name="spread_pieces",
        out_shape=[jax.ShapeDtypeStruct((size, rows, BS), jnp.bfloat16) for size in sizes],
        in_specs=[whole],
        out_specs=[whole] * len(sizes),
        scratch_shapes=[VMEM((count, rows, BS), jnp.float32)],
        compiler_params=pltpu.CompilerParams(vmem_limit_bytes=60 << 20),
    )(weights)


def collect_body(slot_id, piece_ref, out_ref):
    rows = piece_ref.shape[1]

    def place(m, carry):
        piece = piece_ref[slot_id[m]].astype(jnp.float32)
        for i in range(rows):
            out_ref[pl.ds(m, 1), i * BS:(i + 1) * BS] = piece[i:i + 1]
        return carry

    lax.fori_loop(0, out_ref.shape[0], place, 0)


def collect(slot_id, pieces):
    count, rows = slot_id.shape[0], pieces.shape[1]
    whole = pl.BlockSpec(memory_space=VMEM)
    return pl.pallas_call(
        collect_body,
        name="collect",
        out_shape=jax.ShapeDtypeStruct((count, rows * BS), jnp.float32),
        in_specs=[pl.BlockSpec(memory_space=pltpu.SMEM), whole],
        out_specs=whole,
        compiler_params=pltpu.CompilerParams(vmem_limit_bytes=60 << 20),
    )(slot_id, pieces)


def partners(bits):
    row, seq = lax.axis_index("row"), lax.axis_index("seq")
    core, flags, peers = row % 2, [], []
    for k in range(bits):
        flag = row // 2 ** (k + 1) % 2
        flags.append(flag)
        peers.append((row + (1 - 2 * flag) * 2 ** (k + 1), seq))
    return core, (row + 1 - 2 * core, seq), flags, peers


def greet(devices):
    barrier = pltpu.get_barrier_semaphore()
    for device in devices:
        pl.semaphore_signal(barrier, inc=1, device_id=device, device_id_type=MESH)
    pl.semaphore_wait(barrier, len(devices))


def in_turns(works):
    live = []
    works = list(works)
    while works or live:
        if works:
            live.append(works.pop(0))
        live = [work for work in reversed(live) if next(work, None) is not None][::-1]


def group_bounds(count, groups):
    return [(count * k // groups, count * (k + 1) // groups) for k in range(groups)]


def reduce_rows_body(bits, seqs, groups, given, *refs):
    in_refs, summed_ref, (out_ref, mine, near, *rest) = refs[:given], refs[given], refs[given + 1:]
    far = rest[:bits]
    spread, arrived, own_summed, got_summed, keep_sems, send, recv = rest[bits:]
    count, extra = mine.shape[0], own_summed.shape[0]
    part = out_ref.shape[1]
    core, sibling, flags, peers = partners(bits)
    row, seq = lax.axis_index("row"), lax.axis_index("seq")
    beside = [(row, (seq + k) % seqs) for k in range(1, seqs)]
    greet([sibling, *peers, *beside])
    used = [0]

    def copy(source, target, device):
        at = used[0]
        used[0] += 1
        return pltpu.make_async_remote_copy(
            src_ref=source, dst_ref=target, send_sem=send.at[at], recv_sem=recv.at[at],
            device_id=device, device_id_type=MESH,
        )

    some = slice(None)
    every = (some,) * bits
    bounds = group_bounds(count, groups)
    starts, kept = [[] for _ in bounds], [[] for _ in bounds]
    at = local = 0
    for ref in in_refs:
        for g, (low, high) in enumerate(bounds):
            begin, end = max(low, at), min(high, at + ref.shape[0])
            if begin < end:
                span, to = pl.ds(begin - at, end - begin), pl.ds(begin, end - begin)
                starts[g].append(copy(ref.at[(span, *every, 1 - core)], near.at[to], sibling))
                kept[g].append(pltpu.make_async_copy(ref.at[(span, *every, core)], mine.at[to], keep_sems.at[local]))
                local += 1
        at += ref.shape[0]
    for g in range(groups):
        for move in starts[g] + kept[g]:
            move.start()
    extras = [copy(summed_ref.at[:, device[1]], got_summed.at[k], device) for k, device in enumerate(beside)]
    own_extra = pltpu.make_async_copy(summed_ref.at[:, seq], own_summed, keep_sems.at[local])
    for move in (*extras, own_extra):
        move.start()

    def work(g):
        low, high = bounds[g]
        span = pl.ds(low, high - low)
        order = list(range(bits)) if g % 2 == 0 else list(range(bits - 1, -1, -1))
        place = [some] * bits
        for move in starts[g] + kept[g]:
            move.wait()

        def first(n, carry):
            total = mine[n].astype(jnp.float32) + near[n].astype(jnp.float32)
            mine[n] = total.astype(jnp.bfloat16)
            return carry

        lax.fori_loop(low, high, first, 0)
        for step, bit in enumerate(order):
            spot = bits - 1 - bit
            theirs = list(place)
            theirs[spot] = 1 - flags[bit]
            place[spot] = flags[bit]
            move = copy(mine.at[(span, *theirs)], far[step].at[span], peers[bit])
            move.start()
            yield True
            move.wait()
            last = step == bits - 1
            where = tuple(place)

            def add(n, carry, step=step, where=where, last=last):
                total = mine[(n, *where)].astype(jnp.float32) + far[step][n].astype(jnp.float32)
                if last:
                    for s in range(seqs):
                        spread[s, n] = total[s * part:(s + 1) * part].astype(jnp.bfloat16)
                else:
                    mine[(n, *where)] = total.astype(jnp.bfloat16)
                return carry

            lax.fori_loop(low, high, add, 0)
        final = [
            copy(spread.at[device[1], span], arrived.at[k, span], device) for k, device in enumerate(beside)
        ]
        for move in final:
            move.start()
        yield True
        for move in final:
            move.wait()

        def finish(n, carry):
            total = spread[seq, n].astype(jnp.float32)
            for k in range(seqs - 1):
                total = total + arrived[k, n].astype(jnp.float32)
            out_ref[n] = total
            return carry

        lax.fori_loop(low, high, finish, 0)

    in_turns([work(g) for g in range(groups)])
    for move in (*extras, own_extra):
        move.wait()

    def add_extra(n, carry):
        total = own_summed[n].astype(jnp.float32)
        for k in range(seqs - 1):
            total = total + got_summed[k, n].astype(jnp.float32)
        out_ref[count + n] = total
        return carry

    lax.fori_loop(0, extra, add_extra, 0)


def reduce_rows(terms, summed, rows, seqs, groups, collective):
    count = sum(term.shape[0] for term in terms)
    bits = (rows // 2).bit_length() - 1
    slab = BS // rows
    part = slab // seqs
    twos = (2,) * bits
    low = jnp.bfloat16
    most = len(terms) + groups + 1
    sems = groups * (bits + seqs - 1) + most + seqs
    extra = summed.shape[0]
    return pl.pallas_call(
        functools.partial(reduce_rows_body, bits, seqs, groups, len(terms)),
        name="reduce_rows",
        out_shape=jax.ShapeDtypeStruct((count + extra, part, BS), jnp.float32),
        in_specs=[pl.BlockSpec(memory_space=pl.ANY)] * (len(terms) + 1),
        out_specs=pl.BlockSpec(memory_space=VMEM),
        scratch_shapes=[
            VMEM((count, *twos, slab, BS), low),
            VMEM((count, *twos, slab, BS), low),
            *[VMEM((count, *twos[k + 1:], slab, BS), low) for k in range(bits)],
            VMEM((seqs, count, part, BS), low),
            VMEM((seqs - 1, count, part, BS), low),
            VMEM((extra, part, BS), low),
            VMEM((seqs - 1, extra, part, BS), low),
            pltpu.SemaphoreType.DMA((most,)),
            pltpu.SemaphoreType.DMA((sems,)),
            pltpu.SemaphoreType.DMA((sems,)),
        ],
        compiler_params=pltpu.CompilerParams(
            collective_id=collective, has_side_effects=True, vmem_limit_bytes=60 << 20
        ),
        cost_estimate=pl.CostEstimate(flops=count * BS * BS, bytes_accessed=4 * count * BS * BS, transcendentals=0),
    )(*[term.reshape(-1, *twos, 2, slab, BS) for term in terms], summed.reshape(-1, seqs, part, BS))


def exchange_body(seqs, sources, spot_of, late_ref, got_ref, square_ref, vector_ref, out, mine, send, recv):
    devices, own = got_ref.shape[0], got_ref.shape[1]
    part = late_ref.shape[1]
    me = lax.axis_index("row") * seqs + lax.axis_index("seq")
    barrier = pltpu.get_barrier_semaphore()

    def peer(k):
        to = (me + k) % devices
        return to, (to // seqs, to % seqs)

    def hello(k, carry):
        pl.semaphore_signal(barrier, inc=1, device_id=peer(k)[1], device_id_type=MESH)
        return carry

    lax.fori_loop(1, devices, hello, 0)

    def place(d, carry):
        for s in range(own):
            out[d, s] = late_ref[spot_of[d * own + s]].astype(jnp.bfloat16)
        return carry

    lax.fori_loop(0, devices, place, 0)

    def add(ref, total):
        def step(m, total):
            value = ref[m].astype(jnp.float32)
            return total + value * value

        return lax.fori_loop(0, ref.shape[0], step, total)

    total = add(late_ref, jnp.zeros((part, BS), jnp.float32))
    mine[...] = jnp.sum(total[:, :128] + total[:, 128:], axis=0, keepdims=True)
    pl.semaphore_wait(barrier, devices - 1)

    def move(source, target, kind, k, device):
        return pltpu.make_async_remote_copy(
            src_ref=source, dst_ref=target, send_sem=send.at[kind, k], recv_sem=recv.at[kind, k],
            device_id=device, device_id_type=MESH,
        )

    def moves(k):
        to, device = peer(k)
        return (
            move(out.at[to], got_ref.at[me], 0, k, device),
            move(mine, square_ref.at[me], 1, k, device),
        )

    def launch(k, carry):
        for one in moves(k):
            one.start()
        return carry

    lax.fori_loop(1, devices, launch, 0)

    @pl.when(me < sources[0])
    def _():
        def tell(k, carry):
            move(late_ref.at[sources[1]], vector_ref.at[me], 2, k, peer(k)[1]).start()
            return carry

        lax.fori_loop(1, devices, tell, 0)
        vector_ref[me] = late_ref[sources[1]]

    got_ref[me] = out[me]
    square_ref[me] = mine[...]

    def finish(k, carry):
        for one in moves(k):
            one.wait()
        return carry

    lax.fori_loop(1, devices, finish, 0)

    @pl.when(me < sources[0])
    def _():
        def told(k, carry):
            move(late_ref.at[sources[1]], vector_ref.at[me], 2, k, peer(k)[1]).wait_send()
            return carry

        lax.fori_loop(1, devices, told, 0)

    for d in range(sources[0]):
        @pl.when(me != d)
        def _():
            k = (me - d + devices) % devices
            move(late_ref.at[sources[1]], vector_ref.at[d], 2, k, peer(k)[1]).wait_recv()


def exchange(spot_of, late, rows, seqs, vector_spot, vector_rows, collective):
    devices = rows * seqs
    part = late.shape[1]
    own = spot_of.shape[0] // devices
    told = -(-vector_rows // part)
    whole = pl.BlockSpec(memory_space=VMEM)
    return pl.pallas_call(
        functools.partial(exchange_body, seqs, (told, vector_spot)),
        name="exchange",
        out_shape=(
            jax.ShapeDtypeStruct((devices, own, part, BS), jnp.bfloat16),
            jax.ShapeDtypeStruct((devices, 1, 128), jnp.float32),
            jax.ShapeDtypeStruct((told, part, BS), jnp.float32),
        ),
        in_specs=[pl.BlockSpec(memory_space=pltpu.SMEM), whole],
        out_specs=[whole] * 3,
        scratch_shapes=[
            VMEM((devices, own, part, BS), jnp.bfloat16),
            VMEM((1, 128), jnp.float32),
            pltpu.SemaphoreType.DMA((3, devices)),
            pltpu.SemaphoreType.DMA((3, devices)),
        ],
        compiler_params=pltpu.CompilerParams(
            collective_id=collective, has_side_effects=True, vmem_limit_bytes=60 << 20
        ),
    )(spot_of, late)


def gather_rows_body(bits, seqs, groups, ahead, parts, pace, given, *refs):
    piece_refs, token_ref = refs[:given], refs[given]
    full_refs, row_ref = refs[given + 1:2 * given + 1], refs[2 * given + 1]
    near, send, recv, chain_send, chain_recv, own_sem = refs[2 * given + 2:]
    core, sibling, flags, peers = partners(bits)
    row, seq = lax.axis_index("row"), lax.axis_index("seq")
    greet([sibling, *peers, *[(row, (seq + k) % seqs) for k in range(1, seqs)]])
    used = [0]

    def copy(source, target, device):
        at = used[0]
        used[0] += 1
        return pltpu.make_async_remote_copy(
            src_ref=source, dst_ref=target, send_sem=send.at[at], recv_sem=recv.at[at],
            device_id=device, device_id_type=MESH,
        )

    def hop(source, here, sems_out, sems_in, to_right, step):
        spot = seq - step if to_right else seq + step
        side = 0 if to_right else 1
        return pltpu.make_async_remote_copy(
            src_ref=source if step == 0 else here(spot), dst_ref=here(spot), send_sem=sems_out(side, step),
            recv_sem=sems_in(spot), device_id=(row, seq + (1 if to_right else -1)), device_id_type=MESH,
        )

    def ends(to_right, step):
        there = seq - step >= 0 if to_right else seq + step < seqs
        onward = seq + 1 < seqs if to_right else seq - 1 >= 0
        return there, onward

    def chain(line, step, finish=False):
        for to_right in (True, False):
            there, onward = ends(to_right, step)
            if step > 0 and not finish:

                @pl.when(there)
                def _():
                    hop(*line, to_right, step).wait_recv()

            @pl.when(there & onward)
            def _():
                move = hop(*line, to_right, step)
                if finish:
                    move.wait_send()
                else:
                    move.start()

    lines = []
    for g, (ref, low, high, to, _) in enumerate(groups):
        span, near_span = pl.ds(low, high - low), pl.ds(to, high - low)
        lines.append((
            piece_refs[ref].at[span],
            lambda spot, near_span=near_span: near.at[spot, near_span],
            lambda side, step, g=g: chain_send.at[g, side, step],
            lambda spot, g=g: chain_recv.at[g, spot],
        ))
    share = token_ref.shape[0] // parts

    def token_line(k):
        rows, at = pl.ds(k * share, share), len(groups) + k
        return (
            token_ref.at[rows],
            lambda spot: row_ref.at[spot, rows],
            lambda side, step: chain_send.at[at, side, step],
            lambda spot: chain_recv.at[at, spot],
        )

    token_lines = [token_line(k) for k in range(parts)]
    for line in lines:
        chain(line, 0)
    keep_tokens = pltpu.make_async_copy(token_ref, row_ref.at[seq], own_sem)
    keep_tokens.start()
    sent = []

    def work(g):
        ref, low, high, to, backwards = groups[g]
        full_ref = full_refs[ref]
        span = pl.ds(low, high - low)
        order = list(range(bits - 1, -1, -1)) if backwards else list(range(bits))
        for step in range(1, seqs):
            chain(lines[g], step)
            yield True

        def join(n, carry):
            pieces = [
                jnp.where(seq == s, piece_refs[ref][low + n], near[s, to + n]).astype(jnp.float32)
                for s in range(seqs)
            ]
            slab = jnp.concatenate(pieces, axis=0)
            full_ref[(low + n, *flags[::-1], core)] = slab.astype(jnp.bfloat16)
            return carry

        lax.fori_loop(0, high - low, join, 0)
        coming = [[] for _ in order]

        def pass_on(place, level):
            spot = full_ref.at[(span, *place[::-1], core)]
            for later in range(level + 1, bits):
                bit = order[later]
                move = copy(spot, spot, peers[bit])
                move.start()
                there = list(place)
                there[bit] = 1 - flags[bit]
                coming[later].append((tuple(there), move))
                sent.append(move)
            move = copy(spot, spot, sibling)
            move.start()
            across.append(move)

        pass_on(tuple(flags), -1)
        for level in range(bits):
            yield True
            for place, move in coming[level]:
                move.wait_recv()
                pass_on(place, level)

    across = []

    works = [work(g) for g in range(len(groups))]
    hops = [(line, step) for step in range(seqs) for line in token_lines]
    for turn in range(bits + seqs):
        for one in works:
            next(one, None)
        if turn >= ahead:
            for line, step in hops[:parts if turn == ahead else pace]:
                chain(line, step)
                hops = hops[1:]
    for line, step in hops:
        chain(line, step)
    for move in sent:
        move.wait_send()
    for move in across:
        move.wait()
    keep_tokens.wait()
    for line in [*lines, *token_lines]:
        for step in range(seqs):
            chain(line, step, True)


def gather_rows(pieces, tokens, rows, seqs, cuts, collective, ahead=2, parts=1, pace=1):
    part = pieces[0].shape[1]
    bits = (rows // 2).bit_length() - 1
    slab = BS // rows
    twos = (2,) * bits
    low = jnp.bfloat16
    whole = pl.BlockSpec(memory_space=VMEM)
    groups, at = [], 0
    for ref, piece in enumerate(pieces):
        for begin, end in group_bounds(piece.shape[0], cuts[ref]):
            groups.append((ref, begin, end, at, len(groups) % 2 == 1))
            at += end - begin
    sems = len(groups) * (2 * 2 ** bits - 1)
    *full, token_row = pl.pallas_call(
        functools.partial(gather_rows_body, bits, seqs, groups, ahead, parts, pace, len(pieces)),
        name="gather_rows",
        out_shape=(
            *[jax.ShapeDtypeStruct((piece.shape[0], *twos, 2, slab, BS), low) for piece in pieces],
            jax.ShapeDtypeStruct((seqs, *tokens.shape), low),
        ),
        in_specs=[whole] * (len(pieces) + 1),
        out_specs=[whole] * (len(pieces) + 1),
        scratch_shapes=[
            VMEM((seqs, at, part, BS), low),
            pltpu.SemaphoreType.DMA((sems,)),
            pltpu.SemaphoreType.DMA((sems,)),
            pltpu.SemaphoreType.DMA((len(groups) + parts, 2, seqs)),
            pltpu.SemaphoreType.DMA((len(groups) + parts, seqs)),
            pltpu.SemaphoreType.DMA,
        ],
        compiler_params=pltpu.CompilerParams(
            collective_id=collective, has_side_effects=True, vmem_limit_bytes=60 << 20
        ),
        cost_estimate=pl.CostEstimate(flops=0, bytes_accessed=4 * at * BS * BS, transcendentals=0),
    )(*pieces, tokens)
    return [one.reshape(-1, BS, BS) for one in full], token_row.reshape(-1, tokens.shape[1])


def normalize(values):
    centered = values - jnp.mean(values, axis=-1, keepdims=True)
    inverse = lax.rsqrt(jnp.mean(centered * centered, axis=-1, keepdims=True) + NORM_EPS)
    return centered * inverse, inverse


def column(k):
    return slice(k * BS, (k + 1) * BS)


def gate(values):
    return 1.0 / (1.0 + jnp.exp(-values))


def enter_body(spots, token_ref, row_ref, weight_ref, vector_ref, hid_ref, pre_ref, own_t_ref, value_ref, row_t_ref):
    first_at, value_at = spots
    wide = vector_ref.shape[1] // BS
    gain, shift, bias = vector_ref[0:1], vector_ref[1:2], vector_ref[4:5]

    def project(inputs, at, j):
        total = dot_nn(inputs[:, column(0)], weight_ref[at + j])
        for i in range(1, wide):
            total = total + dot_nn(inputs[:, column(i)], weight_ref[at + i * wide + j])
        return total

    def own(c, carry):
        rows = pl.ds(pl.multiple_of(c * BS, BS), BS)
        normed = normalize(token_ref[rows, :].astype(jnp.float32))[0] * gain + shift
        inputs = normed.astype(jnp.bfloat16)
        own_t_ref[:, rows] = normed.T.astype(jnp.bfloat16)
        for j in range(wide):
            pre = project(inputs, first_at, j) + bias[:, column(j)]
            pre_ref[rows, column(j)] = pre
            hid_ref[rows, column(j)] = (pre * gate(pre)).astype(jnp.bfloat16)
        return carry

    lax.fori_loop(0, token_ref.shape[0] // BS, own, 0)

    def whole_row(c, carry):
        rows = pl.ds(pl.multiple_of(c * BS, BS), BS)
        normed = normalize(row_ref[rows, :].astype(jnp.float32))[0] * gain + shift
        inputs = normed.astype(jnp.bfloat16)
        row_t_ref[:, rows] = normed.T.astype(jnp.bfloat16)
        for j in range(wide):
            value_ref[rows, column(j)] = project(inputs, value_at, j).astype(jnp.bfloat16)
        return carry

    lax.fori_loop(0, row_ref.shape[0] // BS, whole_row, 0)


def enter(tokens, token_row, weights, vectors, spots):
    positions, width = tokens.shape
    length = token_row.shape[0]
    whole = pl.BlockSpec(memory_space=VMEM)
    low = jnp.bfloat16
    return pl.pallas_call(
        functools.partial(enter_body, spots),
        name="enter",
        out_shape=(
            jax.ShapeDtypeStruct((positions, width), low),
            jax.ShapeDtypeStruct((positions, width), jnp.float32),
            jax.ShapeDtypeStruct((width, positions), low),
            jax.ShapeDtypeStruct((length, width), low),
            jax.ShapeDtypeStruct((width, length), low),
        ),
        in_specs=[whole] * 4,
        out_specs=[whole] * 5,
        compiler_params=pltpu.CompilerParams(vmem_limit_bytes=60 << 20),
        cost_estimate=pl.CostEstimate(flops=2 * (positions + length) * width * width, bytes_accessed=24 << 20, transcendentals=positions * width),
    )(tokens, token_row, weights, vectors)


def middle_body(cut, token_ref, cotangent_ref, mixed_ref, output_ref, up_a, up_b, up_c, down_ref, vector_ref,
                out_ref, terms_ref, apart_ref, dmix_ref, dmiddle_ref, sums_ref, bias_ref,
                middle, normed_in, normed_t, back_t, total, back, made, made_output, sems, output_sem):
    f, last = pl.program_id(0), pl.num_programs(0) - 1
    ups = (up_a, up_b, up_c)
    wide = len(ups)
    first_up, steps = wide * wide, bias_ref.shape[0]
    slot = f % 2

    def spot(base, step):
        return apart_ref.at[base - cut + step] if base >= cut else terms_ref.at[base + step]

    @pl.when(f == 0)
    def _():
        mixed = mixed_ref[...].astype(jnp.bfloat16)
        for j in range(wide):
            part = token_ref[:, column(j)].astype(jnp.float32)
            for i in range(wide):
                part = part + dot_nn(mixed[:, column(i)], output_ref[i * wide + j])
            middle[:, column(j)] = part
        hat, _ = normalize(middle[...])
        inputs = hat * vector_ref[2:3] + vector_ref[3:4]
        normed_in[...] = inputs.astype(jnp.bfloat16)
        normed_t[...] = inputs.T.astype(jnp.bfloat16)
        total[...] = middle[...]
        back[...] = jnp.zeros_like(back)

    def copies(at, step):
        out = []
        for i in range(wide):
            out.append(pltpu.make_async_copy(made.at[at, i], spot(first_up + i * steps, step), sems.at[at, i]))
        for j in range(wide):
            out.append(pltpu.make_async_copy(made.at[at, wide + j], spot(first_up + wide * steps, step * wide + j), sems.at[at, wide + j]))
        return out

    @pl.when(f >= 2)
    def _():
        for move in copies(slot, f - 2):
            move.wait()

    inputs = normed_in[...]
    pre = vector_ref[pl.ds(5 + f // wide, 1), pl.ds(pl.multiple_of(f % wide * BS, BS), BS)]
    for i in range(wide):
        pre = pre + dot_nn(inputs[:, column(i)], ups[i][0])
    share = gate(pre)
    hidden = pre * share
    low_hidden = hidden.astype(jnp.bfloat16)
    hidden_t = hidden.T.astype(jnp.bfloat16)
    dhidden = None
    for j in range(wide):
        total[:, column(j)] += dot_nn(low_hidden, down_ref[j])
        made[slot, wide + j] = dot_nn(hidden_t, cotangent_ref[:, column(j)]).astype(jnp.bfloat16)
        part = dot_nt(cotangent_ref[:, column(j)], down_ref[j])
        dhidden = part if dhidden is None else dhidden + part
    dhidden = dhidden.astype(jnp.bfloat16).astype(jnp.float32)
    dpre = (dhidden * (share * (1.0 + pre * (1.0 - share)))).astype(jnp.bfloat16)
    bias_ref[pl.ds(f, 1), :] = jnp.sum(dpre.astype(jnp.float32), axis=0, keepdims=True)
    for i in range(wide):
        made[slot, i] = dot_nn(normed_t[column(i), :], dpre).astype(jnp.bfloat16)
        back[:, column(i)] += dot_nt(dpre, ups[i][0])
    for move in copies(slot, f):
        move.start()

    @pl.when(f == last)
    def _():
        out_ref[...] = total[...].astype(jnp.bfloat16)
        hat, inverse = normalize(middle[...])
        dnormed = back[...]
        sums_ref[...] = jnp.zeros_like(sums_ref)
        sums_ref[0:1] = jnp.sum(dnormed * hat, axis=0, keepdims=True)
        sums_ref[1:2] = jnp.sum(dnormed, axis=0, keepdims=True)
        scaled = dnormed * vector_ref[2:3]
        dmiddle = cotangent_ref[...].astype(jnp.float32) + inverse * (
            scaled
            - jnp.mean(scaled, axis=-1, keepdims=True)
            - hat * jnp.mean(scaled * hat, axis=-1, keepdims=True)
        )
        dmiddle_ref[...] = dmiddle
        low = dmiddle.astype(jnp.bfloat16)
        back_t[...] = mixed_ref[...].T.astype(jnp.bfloat16)
        for i in range(wide):
            part = None
            for j in range(wide):
                made_output[i * wide + j] = dot_nn(back_t[column(i), :], low[:, column(j)]).astype(jnp.bfloat16)
                term = dot_nt(low[:, column(j)], output_ref[i * wide + j])
                part = term if part is None else part + term
            dmix_ref[:, column(i)] = part.astype(jnp.bfloat16)
        move = pltpu.make_async_copy(made_output, terms_ref.at[0:wide * wide], output_sem)
        move.start()
        for one in copies(1 - slot, f - 1):
            one.wait()
        for one in copies(slot, f):
            one.wait()
        move.wait()


def middle_stage(tokens, cotangent, mixed, weights, down_weights, vectors, apart):
    positions, width = tokens.shape
    wide = width // BS
    steps = down_weights.shape[0] // wide
    cut = wide * wide + (wide - apart) * steps
    low = jnp.bfloat16
    tok = pl.BlockSpec((positions, width), lambda f: (0, 0))

    def up(i):
        return pl.BlockSpec((1, BS, BS), lambda f: (wide * wide + i * steps + f, 0, 0))

    return pl.pallas_call(
        functools.partial(middle_body, cut),
        name="middle_stage",
        out_shape=(
            jax.ShapeDtypeStruct((positions, width), low),
            jax.ShapeDtypeStruct((cut, BS, BS), low),
            jax.ShapeDtypeStruct((wide * wide + 2 * wide * steps - cut, BS, BS), low),
            jax.ShapeDtypeStruct((positions, width), low),
            jax.ShapeDtypeStruct((positions, width), jnp.float32),
            jax.ShapeDtypeStruct((8, width), jnp.float32),
            jax.ShapeDtypeStruct((steps, BS), jnp.float32),
        ),
        grid=(steps,),
        in_specs=[
            tok,
            tok,
            tok,
            pl.BlockSpec((wide * wide, BS, BS), lambda f: (0, 0, 0)),
            up(0),
            up(1),
            up(2),
            pl.BlockSpec((wide, BS, BS), lambda f: (f, 0, 0)),
            pl.BlockSpec(vectors.shape, lambda f: (0, 0)),
        ],
        out_specs=[
            tok,
            pl.BlockSpec(memory_space=pl.ANY),
            pl.BlockSpec(memory_space=pl.ANY),
            tok,
            tok,
            pl.BlockSpec((8, width), lambda f: (0, 0)),
            pl.BlockSpec((steps, BS), lambda f: (0, 0)),
        ],
        scratch_shapes=[
            VMEM((positions, width), jnp.float32),
            VMEM((positions, width), low),
            VMEM((width, positions), low),
            VMEM((width, positions), low),
            VMEM((positions, width), jnp.float32),
            VMEM((positions, width), jnp.float32),
            VMEM((2, 2 * wide, BS, BS), low),
            VMEM((wide * wide, BS, BS), low),
            pltpu.SemaphoreType.DMA((2, 2 * wide)),
            pltpu.SemaphoreType.DMA,
        ],
        compiler_params=pltpu.CompilerParams(vmem_limit_bytes=60 << 20, dimension_semantics=("arbitrary",)),
        cost_estimate=pl.CostEstimate(flops=36 * positions * width * width, bytes_accessed=40 << 20, transcendentals=positions * width * 4),
    )(tokens, cotangent, mixed, weights, weights, weights, weights, down_weights, vectors)


def leave_body(spots, dhid_ref, pre_ref, own_t_ref, token_ref, row_ref, row_t_ref, dvalue_ref, weight_ref, vector_ref, sums_ref, bias_ref,
               dfirst_ref, dweight_ref, block_ref, back_ref, dpre_all, rows32):
    first_at, value_at = spots
    positions, width = dhid_ref.shape
    wide = width // BS
    sums = [jnp.zeros((1, width), jnp.float32) for _ in range(3)]

    def unproject(grads, at, i):
        total = None
        for j in range(wide):
            part = dot_nt(grads[:, column(j)], weight_ref[at + i * wide + j])
            total = part if total is None else total + part
        return total

    def own(c, sums):
        rows = pl.ds(pl.multiple_of(c * BS, BS), BS)
        pre = pre_ref[rows, :]
        share = gate(pre)
        dpre = (dhid_ref[rows, :].astype(jnp.float32) * (share * (1.0 + pre * (1.0 - share)))).astype(jnp.bfloat16)
        dpre_all[rows, :] = dpre
        hat, _ = normalize(token_ref[rows, :].astype(jnp.float32))
        back = jnp.concatenate([unproject(dpre, first_at, i) for i in range(wide)], axis=1)
        back_ref[rows, :] = back
        return (
            sums[0] + jnp.sum(back * hat, axis=0, keepdims=True),
            sums[1] + jnp.sum(back, axis=0, keepdims=True),
            sums[2] + jnp.sum(dpre.astype(jnp.float32), axis=0, keepdims=True),
        )

    sums = lax.fori_loop(0, positions // BS, own, tuple(sums))

    def whole_row(c, sums):
        rows = pl.ds(pl.multiple_of(c * BS, BS), BS)
        dvalue = dvalue_ref[rows, :]
        hat, _ = normalize(row_ref[rows, :].astype(jnp.float32))
        back = jnp.concatenate([unproject(dvalue, value_at, i) for i in range(wide)], axis=1)
        return (
            sums[0] + jnp.sum(back * hat, axis=0, keepdims=True),
            sums[1] + jnp.sum(back, axis=0, keepdims=True),
            sums[2],
        )

    sums = lax.fori_loop(0, row_ref.shape[0] // BS, whole_row, sums)
    for i in range(wide):
        for j in range(wide):
            dfirst_ref[i * wide + j] = dot_nn(own_t_ref[column(i), :], dpre_all[:, column(j)]).astype(jnp.bfloat16)
            dweight_ref[i * wide + j] = dot_nn(row_t_ref[column(i), :], dvalue_ref[:, column(j)]).astype(jnp.bfloat16)
    rows32[...] = jnp.zeros_like(rows32)
    lines = (sums[0], sums[1], sums_ref[0:1], sums_ref[1:2], sums[2])
    for r, line in enumerate(lines):
        for i in range(wide):
            rows32[r * wide + i:r * wide + i + 1, :] = line[:, column(i)]
    at = len(lines) * wide
    rows32[at:at + bias_ref.shape[0], :] = bias_ref[...]
    block_ref[0] = jnp.zeros_like(block_ref[0])
    block_ref[0, 0:rows32.shape[0], :] = rows32[...].astype(jnp.bfloat16)


def leave(dhid, pre, own_t, tokens, token_row, row_t, dvalue, weights, vectors, sums, bias, spots):
    positions, width = dhid.shape
    wide = width // BS
    whole = pl.BlockSpec(memory_space=VMEM)
    low = jnp.bfloat16
    tall = -(-(5 * wide + bias.shape[0]) // 16) * 16
    return pl.pallas_call(
        functools.partial(leave_body, spots),
        name="leave",
        out_shape=(
            jax.ShapeDtypeStruct((wide * wide, BS, BS), low),
            jax.ShapeDtypeStruct((wide * wide, BS, BS), low),
            jax.ShapeDtypeStruct((1, BS, BS), low),
            jax.ShapeDtypeStruct((positions, width), jnp.float32),
        ),
        in_specs=[whole] * 11,
        out_specs=[whole] * 4,
        scratch_shapes=[VMEM((positions, width), low), VMEM((tall, BS), jnp.float32)],
        compiler_params=pltpu.CompilerParams(vmem_limit_bytes=60 << 20),
        cost_estimate=pl.CostEstimate(flops=4 * (positions + token_row.shape[0]) * width * width, bytes_accessed=24 << 20, transcendentals=positions * width),
    )(dhid, pre, own_t, tokens, token_row, row_t, dvalue, weights, vectors, sums, bias)


def finish_body(value_at, dvalue_ref, first_ref, dmiddle_ref, token_ref, weight_ref, vector_ref, out_ref):
    wide = vector_ref.shape[1] // BS

    def chunk(c, carry):
        rows = pl.ds(pl.multiple_of(c * BS, BS), BS)
        dvalue = dvalue_ref[rows, :]
        parts = []
        for i in range(wide):
            total = first_ref[rows, column(i)]
            for j in range(wide):
                total = total + dot_nt(dvalue[:, column(j)], weight_ref[value_at + i * wide + j])
            parts.append(total)
        scaled = jnp.concatenate(parts, axis=1) * vector_ref[0:1]
        hat, inverse = normalize(token_ref[rows, :].astype(jnp.float32))
        out_ref[rows, :] = dmiddle_ref[rows, :] + inverse * (
            scaled
            - jnp.mean(scaled, axis=-1, keepdims=True)
            - hat * jnp.mean(scaled * hat, axis=-1, keepdims=True)
        )
        return carry

    lax.fori_loop(0, token_ref.shape[0] // BS, chunk, 0)


def finish_inputs(dvalue, from_first, dmiddle, tokens, weights, vectors, value_at):
    whole = pl.BlockSpec(memory_space=VMEM)
    positions, width = tokens.shape
    return pl.pallas_call(
        functools.partial(finish_body, value_at),
        name="finish_inputs",
        out_shape=jax.ShapeDtypeStruct((positions, width), jnp.float32),
        in_specs=[whole] * 6,
        out_specs=whole,
        compiler_params=pltpu.CompilerParams(vmem_limit_bytes=60 << 20),
        cost_estimate=pl.CostEstimate(flops=2 * positions * width * width, bytes_accessed=12 << 20, transcendentals=0),
    )(dvalue, from_first, dmiddle, tokens, weights, vectors)


def block_bounds():
    model_blocks = D // BS
    first_end = model_blocks * model_blocks
    synth_end = first_end + model_blocks * (LEN // BS)
    value_end = synth_end + first_end
    output_end = value_end + first_end
    expand_end = output_end + model_blocks * (FF // BS)
    return (first_end, synth_end, value_end, output_end, expand_end)


def block_scales():
    first_end, synth_end, value_end, output_end, expand_end = block_bounds()
    spots = jnp.arange(BLOCKS)
    scales = jnp.where(
        spots < first_end,
        D ** (-0.5),
        jnp.where(
            spots < synth_end,
            3.0 * HD ** (-0.5),
            jnp.where(
                spots < value_end,
                D ** (-0.5),
                jnp.where(
                    spots < output_end,
                    4.0 * D ** (-0.5),
                    jnp.where(spots < expand_end, D ** (-0.5), FF ** (-0.5)),
                ),
            ),
        ),
    )
    return scales.astype(jnp.float32)


def slot_table(owners, own_most, slot_total):
    block_count = owners.shape[0]
    block_index = jnp.arange(block_count, dtype=jnp.int32)
    same_owner = owners[:, None] == owners[None, :]
    earlier = block_index[None, :] < block_index[:, None]
    rank_within = jnp.sum(jnp.where(same_owner & earlier, 1, 0), axis=1).astype(jnp.int32)
    slot_id = owners * own_most + rank_within
    slot_hit = slot_id[:, None] == jnp.arange(slot_total, dtype=jnp.int32)[None, :]
    used = jnp.any(slot_hit, axis=0)
    block_of = jnp.sum(jnp.where(slot_hit, block_index[:, None], 0), axis=0)
    return (slot_id, used, block_of)


def vector_adam(vectors, vec_moments, grad_rows, mom_fix, sec_fix):
    first_moment = BETA_MOM * vec_moments[0] + (1 - BETA_MOM) * grad_rows
    second = BETA_SEC * vec_moments[1] + (1 - BETA_SEC) * grad_rows * grad_rows
    step_rows = first_moment / mom_fix / (jnp.sqrt(second / sec_fix) + EPSILON)
    return (vectors - VECTOR_RATE * step_rows, jnp.stack([first_moment, second]))


def local(
    tokens,
    cotangent,
    seg_ids,
    seg_lengths,
    weights,
    vectors,
    vec_moments,
    moments,
    stats,
    bases,
    owners,
    step_count,
):
    rows_here, positions, width = tokens.shape
    owner_count = lax.axis_size("row") * lax.axis_size("seq")
    own_most = moments.shape[0]
    slot_count = owner_count * own_most
    block_count = weights.shape[0]
    piece_rows = weights.shape[1] // BS
    first_end, synth_end, value_end, _, expand_end = block_bounds()
    synth_count = synth_end - first_end
    tokens = tokens.reshape(positions, width)
    pieces_one, pieces_two, pieces_three = spread_pieces(
        weights,
        (
            ((first_end, synth_end), (0, first_end), (synth_end, value_end)),
            ((value_end, expand_end),),
            ((expand_end, block_count),),
        ),
    )
    spots = (synth_count, synth_end)
    rows_total, seqs_total = lax.axis_size("row"), lax.axis_size("seq")
    (gathered_one, gathered_two), token_row = gather_rows(
        [pieces_one, pieces_two], tokens, rows_total, seqs_total, (2, 2), 3
    )
    gathered_one, pieces_three = lax.optimization_barrier((gathered_one, pieces_three))
    gathered_three = lax.all_gather(pieces_three, AXES, axis=1, tiled=True)

    slot_range = jnp.arange(seg_lengths.shape[1], dtype=jnp.int32)
    before = slot_range[None, :] < slot_range[:, None]
    starts = jnp.sum(jnp.where(before, seg_lengths[0][None, :], 0), axis=1)
    offset = lax.axis_index("seq") * positions
    tables = tables_of(starts, seg_lengths[0], seg_ids[0], offset)

    hidden, first_pre, own_t, values, row_t = enter(tokens, token_row, gathered_one, vectors, spots)
    mixed, log_total = attn_forward(tables, hidden, gathered_one, values)
    layer_out, terms_two, early_terms, back_mixed, back_middle, norm_sums, grad_ffn_bias = middle_stage(
        tokens, cotangent.reshape(positions, width), mixed, gathered_two, gathered_three, vectors, 2
    )
    early_part = lax.psum_scatter(early_terms, "row", scatter_dimension=1, tiled=True)
    synth_grad, back_hidden, value_terms = attn_backward(
        tables, hidden, gathered_one, values, back_mixed, mixed, log_total
    )
    grad_first, grad_value, vector_block, back_from_first = leave(
        back_hidden,
        first_pre,
        own_t,
        tokens,
        token_row,
        row_t,
        value_terms,
        gathered_one,
        vectors,
        norm_sums,
        grad_ffn_bias,
        spots,
    )
    late_terms = [grad_first, grad_value, vector_block, synth_grad, terms_two]
    vector_rows = vectors.shape[0] * vectors.shape[1] // BS
    sums = reduce_rows(late_terms, early_part, rows_total, seqs_total, 6, 1)
    slot_id, used, block_of = slot_table(owners, own_most, slot_count)
    device_index = lax.axis_index(AXES)
    mine_used = lax.dynamic_slice_in_dim(used, device_index * own_most, own_most)
    mine_block = lax.dynamic_slice_in_dim(block_of, device_index * own_most, own_most)
    vector_spot = 2 * first_end
    spot_of = jnp.where(
        block_of < first_end,
        block_of,
        jnp.where(
            block_of < synth_end,
            block_of + first_end + 1,
            jnp.where(block_of < value_end, block_of - synth_end + first_end, block_of + 1),
        ),
    )
    got, square_parts, vector_parts = exchange(
        spot_of, sums, rows_total, seqs_total, vector_spot, vector_rows, 2
    )
    got, value_late = lax.optimization_barrier((got, value_terms))
    value_sums = lax.psum_scatter(value_late, "seq", scatter_dimension=0, tiled=True)
    x_grad = finish_inputs(
        value_sums, back_from_first, back_middle, tokens, gathered_one, vectors, synth_end
    )
    vector_total = vector_parts.reshape(-1, BS)[:vector_rows].reshape(vectors.shape)
    grad_norm = jnp.sqrt(jnp.sum(square_parts))
    clip_max = math.sqrt(block_count * BS * BS + vectors.shape[0] * vectors.shape[1])
    scale = jnp.minimum(1.0, clip_max / grad_norm)
    step_value = step_count[0].astype(jnp.float32)
    mom_fix = 1.0 - jnp.power(BETA_MOM, step_value)
    sec_fix = 1.0 - jnp.power(BETA_SEC, step_value)
    new_vectors, new_vec_moments = vector_adam(
        vectors, vec_moments, vector_total * scale, mom_fix, sec_fix
    )
    rate_table = RATE_FACTOR * block_scales()
    slot_rates = jnp.sum(
        jnp.where(
            mine_block[:, None] == jnp.arange(block_count, dtype=jnp.int32)[None, :],
            rate_table[None, :],
            0.0,
        ),
        axis=1,
    )
    floats = jnp.concatenate([jnp.stack([scale, mom_fix, sec_fix]), slot_rates])
    mine_spot = jnp.where(
        mine_block < first_end,
        mine_block + synth_count,
        jnp.where(mine_block < synth_end, mine_block - first_end, mine_block),
    )
    ints = jnp.concatenate([mine_used.astype(jnp.int32), mine_spot])
    new_master, new_moments, new_stats, wide = soap_update(
        ints, floats, got, gathered_one, gathered_two, gathered_three, moments, stats, bases
    )
    new_bases = soap_bases(ints, wide, bases)
    returned = lax.all_to_all(
        new_master.reshape(1, own_most, BS, BS), AXES, split_axis=2, concat_axis=0, tiled=True
    )
    new_weights = collect(slot_id, returned.reshape(slot_count, piece_rows, BS))
    return (
        layer_out.reshape(rows_here, positions, width),
        x_grad.reshape(rows_here, positions, width),
        new_weights,
        new_moments,
        new_stats,
        new_bases,
        new_vectors,
        new_vec_moments,
        grad_norm.reshape(1),
    )


def solution(mesh):
    placed = (
        P("row", "seq", None),
        P("row", "seq", None),
        P("row", "seq"),
        P("row", None),
        P(None, ("row", "seq")),
        P(),
        P(),
        P(("row", "seq"), None, None, None),
        P(("row", "seq"), None, None, None),
        P(("row", "seq"), None, None, None),
        P(),
        P(),
    )
    return jax.shard_map(
        local,
        mesh=mesh,
        in_specs=placed,
        out_specs=(
            P("row", "seq", None),
            P("row", "seq", None),
            P(None, ("row", "seq")),
            P(("row", "seq"), None, None, None),
            P(("row", "seq"), None, None, None),
            P(("row", "seq"), None, None, None),
            P(),
            P(),
            P(),
        ),
        check_vma=False,
    )
```

```python
import functools
import math

import jax
import jax.numpy as jnp
from jax import lax
from jax.experimental import pallas as pl
from jax.experimental.pallas import tpu as pltpu
from jax.sharding import PartitionSpec as P

D = 768
HEADS = 12
HD = 64
FF = 3072
LEN = 2048
BS = 256
BLOCKS = 123

BETA_MOM = 0.95
BETA_SEC = 0.95
EPSILON = 1e-08
DECAY = 0.01
VECTOR_RATE = 0.3
RATE_FACTOR = 2.0
NORM_EPS = 1e-05
NEG = -1e30
PANEL = 32
HIGHEST = lax.Precision.HIGHEST
VMEM = pltpu.VMEM
AXES = ("row", "seq")
MESH = pl.DeviceIdType.MESH


def dot_nn(a, b):
    return lax.dot_general(a, b, (((1,), (0,)), ((), ())), preferred_element_type=jnp.float32)


def dot_nt(a, b):
    return lax.dot_general(a, b, (((1,), (1,)), ((), ())), preferred_element_type=jnp.float32)


TILES = (128, 256)


def tables_of(starts, lengths, ids, offset):
    ends = jnp.stack([ids[0], ids[-1] + 1, offset])
    return jnp.concatenate([starts, lengths, ends]).astype(jnp.int32)


def split_heads(synth_ref, value_ref, f2m, v32):
    length = value_ref.shape[0]
    low_rows = lax.broadcasted_iota(jnp.int32, (2 * HD, BS), 0) < HD
    for j in range(synth_ref.shape[0]):
        tile = synth_ref[j]
        zero = jnp.zeros_like(tile)
        f2m[0, j] = jnp.where(low_rows, tile, zero)
        f2m[1, j] = jnp.where(low_rows, zero, tile)
    v32[0:length] = value_ref[...].astype(jnp.float32)
    v32[length:] = jnp.zeros((BS, 2 * HD), jnp.float32)


def each_segment(tables, positions, visit):
    segs = (tables.shape[0] - 3) // 2
    offset = tables[2 * segs + 2]

    def segment(s, carry):
        start, count = tables[s], tables[segs + s]
        low = jnp.maximum(start - offset, 0)
        high = jnp.minimum(start + count - offset, positions)

        first = low // 16 * 16

        sizes = [size for size in TILES if size < positions]
        for size, less in zip(sizes, [0, *sizes]):

            @pl.when((high - first <= size) & (high - first > less))
            def _(size=size):
                at = pl.multiple_of(jnp.minimum(first, positions - size), 16)
                visit(start, count, size, at, low, high)

        @pl.when(high - first > sizes[-1])
        def _():
            visit(start, count, positions, 0, low, high)

        return carry

    lax.fori_loop(tables[2 * segs], tables[2 * segs + 1], segment, 0)


def attn_forward_body(tables, hid_ref, synth_ref, value_ref, mixed_ref, lse_ref, f2m, v32, lbuf):
    split_heads(synth_ref, value_ref, f2m, v32)
    lane = lax.broadcasted_iota(jnp.int32, (1, BS), 1)

    def visit(start, count, size, at, low, high):
        rows = pl.ds(at, size)
        hid = hid_ref[rows, :]
        used = (count + BS - 1) // BS

        def scores(j, tops):
            keep = lane < count - j * BS
            out = []
            for h in range(2):
                part = jnp.where(keep, dot_nn(hid, f2m[h, j]), NEG)
                lbuf[h, j, 0:size] = part
                out.append(jnp.maximum(tops[h], jnp.maximum(part[:, :128], part[:, 128:])))
            return tuple(out)

        none = jnp.full((size, 128), NEG, jnp.float32)
        tops = lax.fori_loop(0, used, scores, (none, none))
        tops = [jnp.max(top, axis=1, keepdims=True) for top in tops]

        def weigh(j, carried):
            value = v32[pl.ds(start + j * BS, BS), :].astype(jnp.bfloat16)
            out = []
            for h in range(2):
                total, mix = carried[h]
                part = jnp.exp(lbuf[h, j, 0:size] - tops[h])
                total = total + part[:, :128] + part[:, 128:]
                mix = mix + dot_nn(part.astype(jnp.bfloat16), value)
                out.append((total, mix))
            return tuple(out)

        blank = jnp.zeros((size, 128), jnp.float32)
        pair = lax.fori_loop(0, used, weigh, ((blank, blank), (blank, blank)))
        sums = [jnp.sum(total, axis=1, keepdims=True) for total, _ in pair]
        left = lax.broadcasted_iota(jnp.int32, (size, 2 * HD), 1) < HD
        mix = jnp.where(left, pair[0][1], pair[1][1]) / jnp.where(left, sums[0], sums[1])
        log = jnp.where(left, tops[0] + jnp.log(sums[0]), tops[1] + jnp.log(sums[1]))
        row = lax.broadcasted_iota(jnp.int32, (size, 1), 0) + at
        here = (row >= low) & (row < high)
        mixed_ref[rows, :] = jnp.where(here, mix, mixed_ref[rows, :])
        lse_ref[rows, :] = jnp.where(here, log, lse_ref[rows, :])

    each_segment(tables, hid_ref.shape[0], visit)


def attn_specs(positions, length):
    blocks, per = length // BS, BS // (2 * HD)
    return (
        pl.BlockSpec((positions, 2 * HD), lambda p, t: (0, p)),
        pl.BlockSpec((blocks, 2 * HD, BS), lambda p, t: (p // per, p % per, 0)),
        pl.BlockSpec((length, 2 * HD), lambda p, t: (0, p)),
    )


def attn_forward(tables, hidden, synth, values):
    positions, width = hidden.shape
    length = values.shape[0]
    blocks = length // BS
    tok, f2, val = attn_specs(positions, length)
    return pl.pallas_call(
        attn_forward_body,
        name="attn_forward",
        out_shape=(jax.ShapeDtypeStruct((positions, width), jnp.float32),) * 2,
        grid_spec=pltpu.PrefetchScalarGridSpec(
            num_scalar_prefetch=1,
            grid=(width // (2 * HD),),
            in_specs=[tok, f2, val],
            out_specs=[tok] * 2,
            scratch_shapes=[
                pltpu.VMEM((2, blocks, 2 * HD, BS), jnp.bfloat16),
                pltpu.VMEM((length + BS, 2 * HD), jnp.float32),
                pltpu.VMEM((2, blocks, positions, BS), jnp.float32),
            ],
        ),
        compiler_params=pltpu.CompilerParams(vmem_limit_bytes=60 << 20, dimension_semantics=("arbitrary",)),
        cost_estimate=pl.CostEstimate(flops=4 * positions * length * width * 2, bytes_accessed=12 << 20, transcendentals=positions * length * 12),
    )(tables, hidden, synth, values)


def attn_backward_body(tables, hid_ref, synth_ref, value_ref, dmix_ref, mixed_ref, lse_ref,
                       dsynth_ref, dhid_ref, dvalue_ref, f2m, v32, dv32, dmm, dacc, df2):
    length = value_ref.shape[0]
    split_heads(synth_ref, value_ref, f2m, v32)
    dv32[...] = jnp.zeros_like(dv32)
    df2[...] = jnp.zeros_like(df2)
    lane = lax.broadcasted_iota(jnp.int32, (1, BS), 1)

    def visit(start, count, size, at, low, high):
        rows = pl.ds(at, size)
        left = lax.broadcasted_iota(jnp.int32, (size, 2 * HD), 1) < HD
        row = lax.broadcasted_iota(jnp.int32, (size, 1), 0) + at
        here = (row >= low) & (row < high)
        hid = hid_ref[rows, :]
        hid_t = hid.astype(jnp.float32).T.astype(jnp.bfloat16)
        dmix32 = dmix_ref[rows, :].astype(jnp.float32)
        dmix_t = dmix32.T.astype(jnp.bfloat16)
        dot_pair = dmix32 * mixed_ref[rows, :]
        nil = jnp.zeros_like(dmix32)
        deltas = (
            jnp.sum(jnp.where(left, dot_pair, nil), axis=1, keepdims=True),
            jnp.sum(jnp.where(left, nil, dot_pair), axis=1, keepdims=True),
        )
        dmm[0, 0:size] = jnp.where(left, dmix32, nil).astype(jnp.bfloat16)
        dmm[1, 0:size] = jnp.where(left, nil, dmix32).astype(jnp.bfloat16)
        logs = lse_ref[rows, :]
        lse = [jnp.where(here, logs[:, h * HD:h * HD + 1], -NEG) for h in range(2)]
        dacc[0:size] = jnp.zeros((size, 2 * HD), jnp.float32)

        def block(j, carry):
            keep = lane < count - j * BS
            value = v32[pl.ds(start + j * BS, BS), :].astype(jnp.bfloat16)
            parts = []
            total = None
            for h in range(2):
                synth = f2m[h, j]
                prob = jnp.where(keep, jnp.exp(dot_nn(hid, synth) - lse[h]), 0.0)
                dprob = dot_nt(dmm[h, 0:size], value)
                dlog = (prob * (dprob - deltas[h])).astype(jnp.bfloat16)
                head = slice(h * HD, (h + 1) * HD)
                df2[j, head, :] += dot_nn(hid_t[head], dlog)
                back = dot_nt(dlog, synth)
                total = back if total is None else total + back
                parts.append(dot_nn(dmix_t[head], prob.astype(jnp.bfloat16)))
            dacc[0:size] += total
            dv32[pl.ds(start + j * BS, BS), :] += jnp.concatenate(parts, axis=0).T
            return carry

        lax.fori_loop(0, (count + BS - 1) // BS, block, 0)
        dhid_ref[rows, :] = jnp.where(here, dacc[0:size], dhid_ref[rows, :].astype(jnp.float32)).astype(jnp.bfloat16)

    each_segment(tables, hid_ref.shape[0], visit)
    dvalue_ref[...] = dv32[0:length].astype(jnp.bfloat16)
    dsynth_ref[...] = df2[...].astype(jnp.bfloat16)


def attn_backward(tables, hidden, synth, values, dmix, mixed, lse):
    positions, width = hidden.shape
    length = values.shape[0]
    blocks = length // BS
    tok, f2, val = attn_specs(positions, length)
    return pl.pallas_call(
        attn_backward_body,
        name="attn_backward",
        out_shape=(
            jax.ShapeDtypeStruct((width // BS * blocks, BS, BS), jnp.bfloat16),
            jax.ShapeDtypeStruct((positions, width), jnp.bfloat16),
            jax.ShapeDtypeStruct((length, width), jnp.bfloat16),
        ),
        grid_spec=pltpu.PrefetchScalarGridSpec(
            num_scalar_prefetch=1,
            grid=(width // (2 * HD),),
            in_specs=[tok, f2, val, tok, tok, tok],
            out_specs=[f2, tok, val],
            scratch_shapes=[
                pltpu.VMEM((2, blocks, 2 * HD, BS), jnp.bfloat16),
                pltpu.VMEM((length + BS, 2 * HD), jnp.float32),
                pltpu.VMEM((length + BS, 2 * HD), jnp.float32),
                pltpu.VMEM((2, positions, 2 * HD), jnp.bfloat16),
                pltpu.VMEM((positions, 2 * HD), jnp.float32),
                pltpu.VMEM((blocks, 2 * HD, BS), jnp.float32),
            ],
        ),
        compiler_params=pltpu.CompilerParams(vmem_limit_bytes=60 << 20, dimension_semantics=("arbitrary",)),
        cost_estimate=pl.CostEstimate(flops=10 * positions * length * width * 2, bytes_accessed=24 << 20, transcendentals=positions * length * 12),
    )(tables, hidden, synth, values, dmix, mixed, lse)


def exact(a, b, da=1, db=0):
    return lax.dot_general(a, b, (((da,), (db,)), ((), ())), precision=HIGHEST, preferred_element_type=jnp.float32)

def parts_of(values):
    first = values.astype(jnp.bfloat16)
    rest = values - first.astype(jnp.float32)
    second = rest.astype(jnp.bfloat16)
    return first, second, (rest - second.astype(jnp.float32)).astype(jnp.bfloat16)


LEFT_PARTS, RIGHT_PARTS = (0, 0, 1, 0, 1, 2), (0, 1, 0, 2, 1, 0)


def exact_thin(left, right, axis):
    lefts, rights = parts_of(left), parts_of(right)
    return lax.dot_general(
        jnp.concatenate([lefts[k] for k in LEFT_PARTS], axis=axis),
        jnp.concatenate([rights[k] for k in RIGHT_PARTS], axis=0),
        (((axis,), (0,)), ((), ())),
        preferred_element_type=jnp.float32,
    )


def soap_update_body(ints, floats, got_ref, one_ref, two_ref, three_ref, moment_ref, stat_ref, basis_ref,
                     new_master_ref, new_moment_ref, new_stat_ref, wide_ref, grad_ref, master_ref, sems):
    devices, slots, part = got_ref.shape[0], got_ref.shape[1], got_ref.shape[2]
    sources, at = [], 0
    for ref in (one_ref, two_ref, three_ref):
        sources.append((ref, at, at + ref.shape[0]))
        at += ref.shape[0]

    def master_copy(k, source):
        return pltpu.make_async_copy(source, master_ref.at[k], sems.at[k])

    for k in range(slots):
        block = ints[slots + k]
        for ref, low, high in sources:

            @pl.when((block >= low) & (block < high))
            def _():
                master_copy(k, ref.at[block - low]).start()

    scale, mom_fix, sec_fix = floats[0], floats[1], floats[2]

    per = max(1, 8 // part)

    def join(d, carry):
        rows = pl.ds(pl.multiple_of(d * (per * part), per * part), per * part)
        for k in range(slots):
            pieces = [got_ref[d * per + i, k].astype(jnp.float32) for i in range(per)]
            grad_ref[k, rows, :] = pieces[0] if per == 1 else jnp.concatenate(pieces, axis=0)
        return carry

    lax.fori_loop(0, devices // per, join, 0)
    for k in range(slots):
        master_copy(k, one_ref.at[0]).wait()

    def prepare(k, carry):
        used = ints[k] > 0
        grad = jnp.where(used, grad_ref[k] * scale, 0.0)
        left, right = basis_ref[k, 0], basis_ref[k, 1]
        old_left, old_right = stat_ref[k, 0], stat_ref[k, 1]
        left_stat = BETA_SEC * old_left + (1 - BETA_SEC) * exact(grad, grad, 1, 1)
        right_stat = BETA_SEC * old_right + (1 - BETA_SEC) * exact(grad, grad, 0, 0)
        new_stat_ref[k, 0] = jnp.where(used, left_stat, old_left)
        new_stat_ref[k, 1] = jnp.where(used, right_stat, old_right)
        left_t = left.T
        for side, (turn, stat) in enumerate(((left_t, left_stat), (right.T, right_stat))):
            cross = exact(turn, stat)
            wide_ref[2 * k + side, :, 0:BS] = exact(cross, cross, 1, 1)
            wide_ref[2 * k + side, :, BS:] = cross
        momentum = BETA_MOM * moment_ref[k, 0] + (1 - BETA_MOM) * grad
        turned_grad = exact(exact(left_t, grad), right)
        turned_mom = exact(exact(left_t, momentum), right)
        old_second = moment_ref[k, 1]
        second = BETA_SEC * old_second + (1 - BETA_SEC) * turned_grad * turned_grad
        step = turned_mom / mom_fix / (jnp.sqrt(second / sec_fix) + EPSILON)
        update = exact(exact(left, step), right, 1, 1)
        master = master_ref[k].astype(jnp.float32)
        new_master_ref[k] = (master - floats[3 + k] * (update + DECAY * master)).astype(jnp.bfloat16)
        new_moment_ref[k, 0] = jnp.where(used, momentum, moment_ref[k, 0])
        new_moment_ref[k, 1] = jnp.where(used, second, old_second)
        return carry

    lax.fori_loop(0, slots, prepare, 0)


def soap_update(ints, floats, got, one, two, three, moments, stats, bases):
    slots = got.shape[1]
    whole = pl.BlockSpec(memory_space=VMEM)
    scalar = pl.BlockSpec(memory_space=pltpu.SMEM)
    anywhere = pl.BlockSpec(memory_space=pl.ANY)
    pair = jax.ShapeDtypeStruct(moments.shape, jnp.float32)
    return pl.pallas_call(
        soap_update_body,
        name="soap_update",
        out_shape=(
            jax.ShapeDtypeStruct((slots, BS, BS), jnp.bfloat16),
            pair,
            pair,
            jax.ShapeDtypeStruct((2 * slots, BS, 2 * BS), jnp.float32),
        ),
        in_specs=[scalar, scalar, whole, anywhere, anywhere, anywhere] + [whole] * 3,
        out_specs=[whole] * 4,
        scratch_shapes=[
            VMEM((slots, BS, BS), jnp.float32),
            VMEM((slots, BS, BS), jnp.bfloat16),
            pltpu.SemaphoreType.DMA((slots,)),
        ],
        compiler_params=pltpu.CompilerParams(vmem_limit_bytes=60 << 20),
        cost_estimate=pl.CostEstimate(flops=slots * 12 * 6 * 2 * BS ** 3, bytes_accessed=slots * 14 * 4 * BS * BS, transcendentals=slots * BS * BS),
    )(ints, floats, got, one, two, three, moments, stats, bases)


def soap_bases_body(ints, given_ref, basis_ref, new_basis_ref, wide):
    slots = basis_ref.shape[0]
    count = 2 * slots
    wide[...] = given_ref[...]
    group = 128 // PANEL
    groups = count // group
    row = lax.broadcasted_iota(jnp.int32, (PANEL, 128), 0)
    lane = lax.broadcasted_iota(jnp.int32, (PANEL, 128), 1)
    unit = jnp.where(row == lane % PANEL, 1.0, 0.0)
    spot = lane // PANEL * PANEL
    for p in range(BS // PANEL):
        low = p * PANEL
        rows = slice(low, low + PANEL)
        schur, inverse, pivots = [], [], []
        for q in range(groups):
            schur.append(jnp.concatenate([wide[q * group + i, rows, low:low + PANEL] for i in range(group)], axis=1))
            inverse.append(unit)
            pivots.append(unit)

        for k in range(0, PANEL, 2):
            for q in range(groups):
                a, b = schur[q], inverse[q]
                first = jnp.take_along_axis(a, spot + k, axis=1)
                second = jnp.take_along_axis(a, spot + k + 1, axis=1)
                pivot, cross, corner = first[k:k + 1], second[k:k + 1], second[k + 1:k + 2]
                scale = 1.0 / pivot
                ratio = first[k + 1:k + 2] * scale
                next_pivot = corner - ratio * cross
                head = jnp.where(row > k, first * scale, 0.0)
                tail = jnp.where(row > k + 1, (second - head * cross) * (1.0 / next_pivot), 0.0)
                a_next = a[k + 1:k + 2] - ratio * a[k:k + 1]
                b_next = b[k + 1:k + 2] - ratio * b[k:k + 1]
                schur[q] = a - head * a[k:k + 1] - tail * a_next
                inverse[q] = b - head * b[k:k + 1] - tail * b_next
                pivots[q] = jnp.where(row == k, pivot, jnp.where(row == k + 1, next_pivot, pivots[q]))
        for q in range(groups):
            whole = inverse[q] * lax.rsqrt(pivots[q])
            for i in range(group):
                m = q * group + i
                near = low // 128 * 128
                limit = near + 128
                part = exact_thin(whole[:, i * PANEL:(i + 1) * PANEL], wide[m, rows, near:], 1)
                wide[m, rows, near:] = part
                if low + PANEL < limit:
                    wide[m, low + PANEL:limit, near:] -= exact_thin(
                        part[:, low + PANEL - near:limit - near], part, 0
                    )
                elif limit < BS:
                    above = wide[m, near:limit, limit:]
                    wide[m, limit:, limit:] -= exact(above[:, :BS - limit], above, 0, 0)

    def finish(k, carry):
        used = ints[k] > 0
        for side in range(2):
            new_basis_ref[k, side] = jnp.where(used, wide[2 * k + side, :, BS:].T, basis_ref[k, side])
        return carry

    lax.fori_loop(0, slots, finish, 0)


def soap_bases(ints, wide, bases):
    slots = bases.shape[0]
    whole = pl.BlockSpec(memory_space=VMEM)
    return pl.pallas_call(
        soap_bases_body,
        name="soap_bases",
        out_shape=jax.ShapeDtypeStruct(bases.shape, jnp.float32),
        in_specs=[pl.BlockSpec(memory_space=pltpu.SMEM), whole, whole],
        out_specs=whole,
        scratch_shapes=[VMEM(wide.shape, jnp.float32)],
        compiler_params=pltpu.CompilerParams(vmem_limit_bytes=60 << 20),
        cost_estimate=pl.CostEstimate(flops=slots * 4 * 6 * 2 * BS ** 3, bytes_accessed=slots * 8 * 4 * BS * BS, transcendentals=slots * BS * BS),
    )(ints, wide, bases)


def spread_pieces_body(orders, weight_ref, *refs):
    *out_refs, lay = refs
    for i in range(lay.shape[1]):
        lay[:, i, :] = weight_ref[:, i * BS:(i + 1) * BS]
    for out_ref, order in zip(out_refs, orders):
        at = 0
        for low, high in order:
            out_ref[at:at + high - low] = lay[low:high].astype(jnp.bfloat16)
            at += high - low


def spread_pieces(weights, orders):
    count, rows = weights.shape[0], weights.shape[1] // BS
    sizes = [sum(high - low for low, high in order) for order in orders]
    whole = pl.BlockSpec(memory_space=VMEM)
    return pl.pallas_call(
        functools.partial(spread_pieces_body, orders),
        name="spread_pieces",
        out_shape=[jax.ShapeDtypeStruct((size, rows, BS), jnp.bfloat16) for size in sizes],
        in_specs=[whole],
        out_specs=[whole] * len(sizes),
        scratch_shapes=[VMEM((count, rows, BS), jnp.float32)],
        compiler_params=pltpu.CompilerParams(vmem_limit_bytes=60 << 20),
    )(weights)


def collect_body(slot_id, piece_ref, out_ref):
    rows = piece_ref.shape[1]

    def place(m, carry):
        piece = piece_ref[slot_id[m]].astype(jnp.float32)
        for i in range(rows):
            out_ref[pl.ds(m, 1), i * BS:(i + 1) * BS] = piece[i:i + 1]
        return carry

    lax.fori_loop(0, out_ref.shape[0], place, 0)


def collect(slot_id, pieces):
    count, rows = slot_id.shape[0], pieces.shape[1]
    whole = pl.BlockSpec(memory_space=VMEM)
    return pl.pallas_call(
        collect_body,
        name="collect",
        out_shape=jax.ShapeDtypeStruct((count, rows * BS), jnp.float32),
        in_specs=[pl.BlockSpec(memory_space=pltpu.SMEM), whole],
        out_specs=whole,
        compiler_params=pltpu.CompilerParams(vmem_limit_bytes=60 << 20),
    )(slot_id, pieces)


def partners(bits):
    row, seq = lax.axis_index("row"), lax.axis_index("seq")
    core, flags, peers = row % 2, [], []
    for k in range(bits):
        flag = row // 2 ** (k + 1) % 2
        flags.append(flag)
        peers.append((row + (1 - 2 * flag) * 2 ** (k + 1), seq))
    return core, (row + 1 - 2 * core, seq), flags, peers


def greet(devices):
    barrier = pltpu.get_barrier_semaphore()
    for device in devices:
        pl.semaphore_signal(barrier, inc=1, device_id=device, device_id_type=MESH)
    pl.semaphore_wait(barrier, len(devices))


def in_turns(works):
    live = []
    works = list(works)
    while works or live:
        if works:
            live.append(works.pop(0))
        live = [work for work in reversed(live) if next(work, None) is not None][::-1]


def group_bounds(count, groups):
    return [(count * k // groups, count * (k + 1) // groups) for k in range(groups)]


def reduce_rows_body(bits, seqs, groups, given, *refs):
    in_refs, summed_ref, (out_ref, mine, near, *rest) = refs[:given], refs[given], refs[given + 1:]
    far = rest[:bits]
    spread, arrived, own_summed, got_summed, keep_sems, send, recv = rest[bits:]
    count, extra = mine.shape[0], own_summed.shape[0]
    part = out_ref.shape[1]
    core, sibling, flags, peers = partners(bits)
    row, seq = lax.axis_index("row"), lax.axis_index("seq")
    beside = [(row, (seq + k) % seqs) for k in range(1, seqs)]
    greet([sibling, *peers, *beside])
    used = [0]

    def copy(source, target, device):
        at = used[0]
        used[0] += 1
        return pltpu.make_async_remote_copy(
            src_ref=source, dst_ref=target, send_sem=send.at[at], recv_sem=recv.at[at],
            device_id=device, device_id_type=MESH,
        )

    some = slice(None)
    every = (some,) * bits
    bounds = group_bounds(count, groups)
    starts, kept = [[] for _ in bounds], [[] for _ in bounds]
    at = local = 0
    for ref in in_refs:
        for g, (low, high) in enumerate(bounds):
            begin, end = max(low, at), min(high, at + ref.shape[0])
            if begin < end:
                span, to = pl.ds(begin - at, end - begin), pl.ds(begin, end - begin)
                starts[g].append(copy(ref.at[(span, *every, 1 - core)], near.at[to], sibling))
                kept[g].append(pltpu.make_async_copy(ref.at[(span, *every, core)], mine.at[to], keep_sems.at[local]))
                local += 1
        at += ref.shape[0]
    for g in range(groups):
        for move in starts[g] + kept[g]:
            move.start()
    extras = [copy(summed_ref.at[:, device[1]], got_summed.at[k], device) for k, device in enumerate(beside)]
    own_extra = pltpu.make_async_copy(summed_ref.at[:, seq], own_summed, keep_sems.at[local])
    for move in (*extras, own_extra):
        move.start()

    def work(g):
        low, high = bounds[g]
        span = pl.ds(low, high - low)
        order = list(range(bits)) if g % 2 == 0 else list(range(bits - 1, -1, -1))
        place = [some] * bits
        for move in starts[g] + kept[g]:
            move.wait()

        def first(n, carry):
            total = mine[n].astype(jnp.float32) + near[n].astype(jnp.float32)
            mine[n] = total.astype(jnp.bfloat16)
            return carry

        lax.fori_loop(low, high, first, 0)
        for step, bit in enumerate(order):
            spot = bits - 1 - bit
            theirs = list(place)
            theirs[spot] = 1 - flags[bit]
            place[spot] = flags[bit]
            move = copy(mine.at[(span, *theirs)], far[step].at[span], peers[bit])
            move.start()
            yield True
            move.wait()
            last = step == bits - 1
            where = tuple(place)

            def add(n, carry, step=step, where=where, last=last):
                total = mine[(n, *where)].astype(jnp.float32) + far[step][n].astype(jnp.float32)
                if last:
                    for s in range(seqs):
                        spread[s, n] = total[s * part:(s + 1) * part].astype(jnp.bfloat16)
                else:
                    mine[(n, *where)] = total.astype(jnp.bfloat16)
                return carry

            lax.fori_loop(low, high, add, 0)
        final = [
            copy(spread.at[device[1], span], arrived.at[k, span], device) for k, device in enumerate(beside)
        ]
        for move in final:
            move.start()
        yield True
        for move in final:
            move.wait()

        def finish(n, carry):
            total = spread[seq, n].astype(jnp.float32)
            for k in range(seqs - 1):
                total = total + arrived[k, n].astype(jnp.float32)
            out_ref[n] = total
            return carry

        lax.fori_loop(low, high, finish, 0)

    in_turns([work(g) for g in range(groups)])
    for move in (*extras, own_extra):
        move.wait()

    def add_extra(n, carry):
        total = own_summed[n].astype(jnp.float32)
        for k in range(seqs - 1):
            total = total + got_summed[k, n].astype(jnp.float32)
        out_ref[count + n] = total
        return carry

    lax.fori_loop(0, extra, add_extra, 0)


def reduce_rows(terms, summed, rows, seqs, groups, collective):
    count = sum(term.shape[0] for term in terms)
    bits = (rows // 2).bit_length() - 1
    slab = BS // rows
    part = slab // seqs
    twos = (2,) * bits
    low = jnp.bfloat16
    most = len(terms) + groups + 1
    sems = groups * (bits + seqs - 1) + most + seqs
    extra = summed.shape[0]
    return pl.pallas_call(
        functools.partial(reduce_rows_body, bits, seqs, groups, len(terms)),
        name="reduce_rows",
        out_shape=jax.ShapeDtypeStruct((count + extra, part, BS), jnp.float32),
        in_specs=[pl.BlockSpec(memory_space=pl.ANY)] * (len(terms) + 1),
        out_specs=pl.BlockSpec(memory_space=VMEM),
        scratch_shapes=[
            VMEM((count, *twos, slab, BS), low),
            VMEM((count, *twos, slab, BS), low),
            *[VMEM((count, *twos[k + 1:], slab, BS), low) for k in range(bits)],
            VMEM((seqs, count, part, BS), low),
            VMEM((seqs - 1, count, part, BS), low),
            VMEM((extra, part, BS), low),
            VMEM((seqs - 1, extra, part, BS), low),
            pltpu.SemaphoreType.DMA((most,)),
            pltpu.SemaphoreType.DMA((sems,)),
            pltpu.SemaphoreType.DMA((sems,)),
        ],
        compiler_params=pltpu.CompilerParams(
            collective_id=collective, has_side_effects=True, vmem_limit_bytes=60 << 20
        ),
        cost_estimate=pl.CostEstimate(flops=count * BS * BS, bytes_accessed=4 * count * BS * BS, transcendentals=0),
    )(*[term.reshape(-1, *twos, 2, slab, BS) for term in terms], summed.reshape(-1, seqs, part, BS))


def exchange_body(seqs, sources, spot_of, late_ref, got_ref, square_ref, vector_ref, out, mine, send, recv):
    devices, own = got_ref.shape[0], got_ref.shape[1]
    part = late_ref.shape[1]
    me = lax.axis_index("row") * seqs + lax.axis_index("seq")
    barrier = pltpu.get_barrier_semaphore()

    def peer(k):
        to = (me + k) % devices
        return to, (to // seqs, to % seqs)

    def hello(k, carry):
        pl.semaphore_signal(barrier, inc=1, device_id=peer(k)[1], device_id_type=MESH)
        return carry

    lax.fori_loop(1, devices, hello, 0)

    def place(d, carry):
        for s in range(own):
            out[d, s] = late_ref[spot_of[d * own + s]].astype(jnp.bfloat16)
        return carry

    lax.fori_loop(0, devices, place, 0)

    def add(ref, total):
        def step(m, total):
            value = ref[m].astype(jnp.float32)
            return total + value * value

        return lax.fori_loop(0, ref.shape[0], step, total)

    total = add(late_ref, jnp.zeros((part, BS), jnp.float32))
    mine[...] = jnp.sum(total[:, :128] + total[:, 128:], axis=0, keepdims=True)
    pl.semaphore_wait(barrier, devices - 1)

    def move(source, target, kind, k, device):
        return pltpu.make_async_remote_copy(
            src_ref=source, dst_ref=target, send_sem=send.at[kind, k], recv_sem=recv.at[kind, k],
            device_id=device, device_id_type=MESH,
        )

    def moves(k):
        to, device = peer(k)
        return (
            move(out.at[to], got_ref.at[me], 0, k, device),
            move(mine, square_ref.at[me], 1, k, device),
        )

    def launch(k, carry):
        for one in moves(k):
            one.start()
        return carry

    lax.fori_loop(1, devices, launch, 0)

    @pl.when(me < sources[0])
    def _():
        def tell(k, carry):
            move(late_ref.at[sources[1]], vector_ref.at[me], 2, k, peer(k)[1]).start()
            return carry

        lax.fori_loop(1, devices, tell, 0)
        vector_ref[me] = late_ref[sources[1]]

    got_ref[me] = out[me]
    square_ref[me] = mine[...]

    def finish(k, carry):
        for one in moves(k):
            one.wait()
        return carry

    lax.fori_loop(1, devices, finish, 0)

    @pl.when(me < sources[0])
    def _():
        def told(k, carry):
            move(late_ref.at[sources[1]], vector_ref.at[me], 2, k, peer(k)[1]).wait_send()
            return carry

        lax.fori_loop(1, devices, told, 0)

    for d in range(sources[0]):
        @pl.when(me != d)
        def _():
            k = (me - d + devices) % devices
            move(late_ref.at[sources[1]], vector_ref.at[d], 2, k, peer(k)[1]).wait_recv()


def exchange(spot_of, late, rows, seqs, vector_spot, vector_rows, collective):
    devices = rows * seqs
    part = late.shape[1]
    own = spot_of.shape[0] // devices
    told = -(-vector_rows // part)
    whole = pl.BlockSpec(memory_space=VMEM)
    return pl.pallas_call(
        functools.partial(exchange_body, seqs, (told, vector_spot)),
        name="exchange",
        out_shape=(
            jax.ShapeDtypeStruct((devices, own, part, BS), jnp.bfloat16),
            jax.ShapeDtypeStruct((devices, 1, 128), jnp.float32),
            jax.ShapeDtypeStruct((told, part, BS), jnp.float32),
        ),
        in_specs=[pl.BlockSpec(memory_space=pltpu.SMEM), whole],
        out_specs=[whole] * 3,
        scratch_shapes=[
            VMEM((devices, own, part, BS), jnp.bfloat16),
            VMEM((1, 128), jnp.float32),
            pltpu.SemaphoreType.DMA((3, devices)),
            pltpu.SemaphoreType.DMA((3, devices)),
        ],
        compiler_params=pltpu.CompilerParams(
            collective_id=collective, has_side_effects=True, vmem_limit_bytes=60 << 20
        ),
    )(spot_of, late)


def gather_rows_body(bits, seqs, groups, ahead, parts, pace, given, *refs):
    piece_refs, token_ref = refs[:given], refs[given]
    full_refs, row_ref = refs[given + 1:2 * given + 1], refs[2 * given + 1]
    near, send, recv, chain_send, chain_recv, own_sem = refs[2 * given + 2:]
    core, sibling, flags, peers = partners(bits)
    row, seq = lax.axis_index("row"), lax.axis_index("seq")
    greet([sibling, *peers, *[(row, (seq + k) % seqs) for k in range(1, seqs)]])
    used = [0]

    def copy(source, target, device):
        at = used[0]
        used[0] += 1
        return pltpu.make_async_remote_copy(
            src_ref=source, dst_ref=target, send_sem=send.at[at], recv_sem=recv.at[at],
            device_id=device, device_id_type=MESH,
        )

    def hop(source, here, sems_out, sems_in, to_right, step):
        spot = seq - step if to_right else seq + step
        side = 0 if to_right else 1
        return pltpu.make_async_remote_copy(
            src_ref=source if step == 0 else here(spot), dst_ref=here(spot), send_sem=sems_out(side, step),
            recv_sem=sems_in(spot), device_id=(row, seq + (1 if to_right else -1)), device_id_type=MESH,
        )

    def ends(to_right, step):
        there = seq - step >= 0 if to_right else seq + step < seqs
        onward = seq + 1 < seqs if to_right else seq - 1 >= 0
        return there, onward

    def chain(line, step, finish=False):
        for to_right in (True, False):
            there, onward = ends(to_right, step)
            if step > 0 and not finish:

                @pl.when(there)
                def _():
                    hop(*line, to_right, step).wait_recv()

            @pl.when(there & onward)
            def _():
                move = hop(*line, to_right, step)
                if finish:
                    move.wait_send()
                else:
                    move.start()

    lines = []
    for g, (ref, low, high, to, _) in enumerate(groups):
        span, near_span = pl.ds(low, high - low), pl.ds(to, high - low)
        lines.append((
            piece_refs[ref].at[span],
            lambda spot, near_span=near_span: near.at[spot, near_span],
            lambda side, step, g=g: chain_send.at[g, side, step],
            lambda spot, g=g: chain_recv.at[g, spot],
        ))
    share = token_ref.shape[0] // parts

    def token_line(k):
        rows, at = pl.ds(k * share, share), len(groups) + k
        return (
            token_ref.at[rows],
            lambda spot: row_ref.at[spot, rows],
            lambda side, step: chain_send.at[at, side, step],
            lambda spot: chain_recv.at[at, spot],
        )

    token_lines = [token_line(k) for k in range(parts)]
    for line in lines:
        chain(line, 0)
    keep_tokens = pltpu.make_async_copy(token_ref, row_ref.at[seq], own_sem)
    keep_tokens.start()
    sent = []

    def work(g):
        ref, low, high, to, backwards = groups[g]
        full_ref = full_refs[ref]
        span = pl.ds(low, high - low)
        order = list(range(bits - 1, -1, -1)) if backwards else list(range(bits))
        for step in range(1, seqs):
            chain(lines[g], step)
            yield True

        def join(n, carry):
            pieces = [
                jnp.where(seq == s, piece_refs[ref][low + n], near[s, to + n]).astype(jnp.float32)
                for s in range(seqs)
            ]
            slab = jnp.concatenate(pieces, axis=0)
            full_ref[(low + n, *flags[::-1], core)] = slab.astype(jnp.bfloat16)
            return carry

        lax.fori_loop(0, high - low, join, 0)
        coming = [[] for _ in order]

        def pass_on(place, level):
            spot = full_ref.at[(span, *place[::-1], core)]
            for later in range(level + 1, bits):
                bit = order[later]
                move = copy(spot, spot, peers[bit])
                move.start()
                there = list(place)
                there[bit] = 1 - flags[bit]
                coming[later].append((tuple(there), move))
                sent.append(move)
            move = copy(spot, spot, sibling)
            move.start()
            across.append(move)

        pass_on(tuple(flags), -1)
        for level in range(bits):
            yield True
            for place, move in coming[level]:
                move.wait_recv()
                pass_on(place, level)

    across = []

    works = [work(g) for g in range(len(groups))]
    hops = [(line, step) for step in range(seqs) for line in token_lines]
    for turn in range(bits + seqs):
        for one in works:
            next(one, None)
        if turn >= ahead:
            for line, step in hops[:parts if turn == ahead else pace]:
                chain(line, step)
                hops = hops[1:]
    for line, step in hops:
        chain(line, step)
    for move in sent:
        move.wait_send()
    for move in across:
        move.wait()
    keep_tokens.wait()
    for line in [*lines, *token_lines]:
        for step in range(seqs):
            chain(line, step, True)


def gather_rows(pieces, tokens, rows, seqs, cuts, collective, ahead=2, parts=1, pace=1):
    part = pieces[0].shape[1]
    bits = (rows // 2).bit_length() - 1
    slab = BS // rows
    twos = (2,) * bits
    low = jnp.bfloat16
    whole = pl.BlockSpec(memory_space=VMEM)
    groups, at = [], 0
    for ref, piece in enumerate(pieces):
        for begin, end in group_bounds(piece.shape[0], cuts[ref]):
            groups.append((ref, begin, end, at, len(groups) % 2 == 1))
            at += end - begin
    sems = len(groups) * (2 * 2 ** bits - 1)
    *full, token_row = pl.pallas_call(
        functools.partial(gather_rows_body, bits, seqs, groups, ahead, parts, pace, len(pieces)),
        name="gather_rows",
        out_shape=(
            *[jax.ShapeDtypeStruct((piece.shape[0], *twos, 2, slab, BS), low) for piece in pieces],
            jax.ShapeDtypeStruct((seqs, *tokens.shape), low),
        ),
        in_specs=[whole] * (len(pieces) + 1),
        out_specs=[whole] * (len(pieces) + 1),
        scratch_shapes=[
            VMEM((seqs, at, part, BS), low),
            pltpu.SemaphoreType.DMA((sems,)),
            pltpu.SemaphoreType.DMA((sems,)),
            pltpu.SemaphoreType.DMA((len(groups) + parts, 2, seqs)),
            pltpu.SemaphoreType.DMA((len(groups) + parts, seqs)),
            pltpu.SemaphoreType.DMA,
        ],
        compiler_params=pltpu.CompilerParams(
            collective_id=collective, has_side_effects=True, vmem_limit_bytes=60 << 20
        ),
        cost_estimate=pl.CostEstimate(flops=0, bytes_accessed=4 * at * BS * BS, transcendentals=0),
    )(*pieces, tokens)
    return [one.reshape(-1, BS, BS) for one in full], token_row.reshape(-1, tokens.shape[1])


def normalize(values):
    centered = values - jnp.mean(values, axis=-1, keepdims=True)
    inverse = lax.rsqrt(jnp.mean(centered * centered, axis=-1, keepdims=True) + NORM_EPS)
    return centered * inverse, inverse


def column(k):
    return slice(k * BS, (k + 1) * BS)


def gate(values):
    return 1.0 / (1.0 + jnp.exp(-values))


def enter_body(spots, token_ref, row_ref, weight_ref, vector_ref, hid_ref, pre_ref, own_t_ref, value_ref, row_t_ref):
    first_at, value_at = spots
    wide = vector_ref.shape[1] // BS
    gain, shift, bias = vector_ref[0:1], vector_ref[1:2], vector_ref[4:5]

    def project(inputs, at, j):
        total = dot_nn(inputs[:, column(0)], weight_ref[at + j])
        for i in range(1, wide):
            total = total + dot_nn(inputs[:, column(i)], weight_ref[at + i * wide + j])
        return total

    def own(c, carry):
        rows = pl.ds(pl.multiple_of(c * BS, BS), BS)
        normed = normalize(token_ref[rows, :].astype(jnp.float32))[0] * gain + shift
        inputs = normed.astype(jnp.bfloat16)
        own_t_ref[:, rows] = normed.T.astype(jnp.bfloat16)
        for j in range(wide):
            pre = project(inputs, first_at, j) + bias[:, column(j)]
            pre_ref[rows, column(j)] = pre
            hid_ref[rows, column(j)] = (pre * gate(pre)).astype(jnp.bfloat16)
        return carry

    lax.fori_loop(0, token_ref.shape[0] // BS, own, 0)

    def whole_row(c, carry):
        rows = pl.ds(pl.multiple_of(c * BS, BS), BS)
        normed = normalize(row_ref[rows, :].astype(jnp.float32))[0] * gain + shift
        inputs = normed.astype(jnp.bfloat16)
        row_t_ref[:, rows] = normed.T.astype(jnp.bfloat16)
        for j in range(wide):
            value_ref[rows, column(j)] = project(inputs, value_at, j).astype(jnp.bfloat16)
        return carry

    lax.fori_loop(0, row_ref.shape[0] // BS, whole_row, 0)


def enter(tokens, token_row, weights, vectors, spots):
    positions, width = tokens.shape
    length = token_row.shape[0]
    whole = pl.BlockSpec(memory_space=VMEM)
    low = jnp.bfloat16
    return pl.pallas_call(
        functools.partial(enter_body, spots),
        name="enter",
        out_shape=(
            jax.ShapeDtypeStruct((positions, width), low),
            jax.ShapeDtypeStruct((positions, width), jnp.float32),
            jax.ShapeDtypeStruct((width, positions), low),
            jax.ShapeDtypeStruct((length, width), low),
            jax.ShapeDtypeStruct((width, length), low),
        ),
        in_specs=[whole] * 4,
        out_specs=[whole] * 5,
        compiler_params=pltpu.CompilerParams(vmem_limit_bytes=60 << 20),
        cost_estimate=pl.CostEstimate(flops=2 * (positions + length) * width * width, bytes_accessed=24 << 20, transcendentals=positions * width),
    )(tokens, token_row, weights, vectors)


def middle_body(cut, token_ref, cotangent_ref, mixed_ref, output_ref, up_a, up_b, up_c, down_ref, vector_ref,
                out_ref, terms_ref, apart_ref, dmix_ref, dmiddle_ref, sums_ref, bias_ref,
                middle, normed_in, normed_t, back_t, total, back, made, made_output, sems, output_sem):
    f, last = pl.program_id(0), pl.num_programs(0) - 1
    ups = (up_a, up_b, up_c)
    wide = len(ups)
    first_up, steps = wide * wide, bias_ref.shape[0]
    slot = f % 2

    def spot(base, step):
        return apart_ref.at[base - cut + step] if base >= cut else terms_ref.at[base + step]

    @pl.when(f == 0)
    def _():
        mixed = mixed_ref[...].astype(jnp.bfloat16)
        for j in range(wide):
            part = token_ref[:, column(j)].astype(jnp.float32)
            for i in range(wide):
                part = part + dot_nn(mixed[:, column(i)], output_ref[i * wide + j])
            middle[:, column(j)] = part
        hat, _ = normalize(middle[...])
        inputs = hat * vector_ref[2:3] + vector_ref[3:4]
        normed_in[...] = inputs.astype(jnp.bfloat16)
        normed_t[...] = inputs.T.astype(jnp.bfloat16)
        total[...] = middle[...]
        back[...] = jnp.zeros_like(back)

    def copies(at, step):
        out = []
        for i in range(wide):
            out.append(pltpu.make_async_copy(made.at[at, i], spot(first_up + i * steps, step), sems.at[at, i]))
        for j in range(wide):
            out.append(pltpu.make_async_copy(made.at[at, wide + j], spot(first_up + wide * steps, step * wide + j), sems.at[at, wide + j]))
        return out

    @pl.when(f >= 2)
    def _():
        for move in copies(slot, f - 2):
            move.wait()

    inputs = normed_in[...]
    pre = vector_ref[pl.ds(5 + f // wide, 1), pl.ds(pl.multiple_of(f % wide * BS, BS), BS)]
    for i in range(wide):
        pre = pre + dot_nn(inputs[:, column(i)], ups[i][0])
    share = gate(pre)
    hidden = pre * share
    low_hidden = hidden.astype(jnp.bfloat16)
    hidden_t = hidden.T.astype(jnp.bfloat16)
    dhidden = None
    for j in range(wide):
        total[:, column(j)] += dot_nn(low_hidden, down_ref[j])
        made[slot, wide + j] = dot_nn(hidden_t, cotangent_ref[:, column(j)]).astype(jnp.bfloat16)
        part = dot_nt(cotangent_ref[:, column(j)], down_ref[j])
        dhidden = part if dhidden is None else dhidden + part
    dhidden = dhidden.astype(jnp.bfloat16).astype(jnp.float32)
    dpre = (dhidden * (share * (1.0 + pre * (1.0 - share)))).astype(jnp.bfloat16)
    bias_ref[pl.ds(f, 1), :] = jnp.sum(dpre.astype(jnp.float32), axis=0, keepdims=True)
    for i in range(wide):
        made[slot, i] = dot_nn(normed_t[column(i), :], dpre).astype(jnp.bfloat16)
        back[:, column(i)] += dot_nt(dpre, ups[i][0])
    for move in copies(slot, f):
        move.start()

    @pl.when(f == last)
    def _():
        out_ref[...] = total[...].astype(jnp.bfloat16)
        hat, inverse = normalize(middle[...])
        dnormed = back[...]
        sums_ref[...] = jnp.zeros_like(sums_ref)
        sums_ref[0:1] = jnp.sum(dnormed * hat, axis=0, keepdims=True)
        sums_ref[1:2] = jnp.sum(dnormed, axis=0, keepdims=True)
        scaled = dnormed * vector_ref[2:3]
        dmiddle = cotangent_ref[...].astype(jnp.float32) + inverse * (
            scaled
            - jnp.mean(scaled, axis=-1, keepdims=True)
            - hat * jnp.mean(scaled * hat, axis=-1, keepdims=True)
        )
        dmiddle_ref[...] = dmiddle
        low = dmiddle.astype(jnp.bfloat16)
        back_t[...] = mixed_ref[...].T.astype(jnp.bfloat16)
        for i in range(wide):
            part = None
            for j in range(wide):
                made_output[i * wide + j] = dot_nn(back_t[column(i), :], low[:, column(j)]).astype(jnp.bfloat16)
                term = dot_nt(low[:, column(j)], output_ref[i * wide + j])
                part = term if part is None else part + term
            dmix_ref[:, column(i)] = part.astype(jnp.bfloat16)
        move = pltpu.make_async_copy(made_output, terms_ref.at[0:wide * wide], output_sem)
        move.start()
        for one in copies(1 - slot, f - 1):
            one.wait()
        for one in copies(slot, f):
            one.wait()
        move.wait()


def middle_stage(tokens, cotangent, mixed, weights, down_weights, vectors, apart):
    positions, width = tokens.shape
    wide = width // BS
    steps = down_weights.shape[0] // wide
    cut = wide * wide + (wide - apart) * steps
    low = jnp.bfloat16
    tok = pl.BlockSpec((positions, width), lambda f: (0, 0))

    def up(i):
        return pl.BlockSpec((1, BS, BS), lambda f: (wide * wide + i * steps + f, 0, 0))

    return pl.pallas_call(
        functools.partial(middle_body, cut),
        name="middle_stage",
        out_shape=(
            jax.ShapeDtypeStruct((positions, width), low),
            jax.ShapeDtypeStruct((cut, BS, BS), low),
            jax.ShapeDtypeStruct((wide * wide + 2 * wide * steps - cut, BS, BS), low),
            jax.ShapeDtypeStruct((positions, width), low),
            jax.ShapeDtypeStruct((positions, width), jnp.float32),
            jax.ShapeDtypeStruct((8, width), jnp.float32),
            jax.ShapeDtypeStruct((steps, BS), jnp.float32),
        ),
        grid=(steps,),
        in_specs=[
            tok,
            tok,
            tok,
            pl.BlockSpec((wide * wide, BS, BS), lambda f: (0, 0, 0)),
            up(0),
            up(1),
            up(2),
            pl.BlockSpec((wide, BS, BS), lambda f: (f, 0, 0)),
            pl.BlockSpec(vectors.shape, lambda f: (0, 0)),
        ],
        out_specs=[
            tok,
            pl.BlockSpec(memory_space=pl.ANY),
            pl.BlockSpec(memory_space=pl.ANY),
            tok,
            tok,
            pl.BlockSpec((8, width), lambda f: (0, 0)),
            pl.BlockSpec((steps, BS), lambda f: (0, 0)),
        ],
        scratch_shapes=[
            VMEM((positions, width), jnp.float32),
            VMEM((positions, width), low),
            VMEM((width, positions), low),
            VMEM((width, positions), low),
            VMEM((positions, width), jnp.float32),
            VMEM((positions, width), jnp.float32),
            VMEM((2, 2 * wide, BS, BS), low),
            VMEM((wide * wide, BS, BS), low),
            pltpu.SemaphoreType.DMA((2, 2 * wide)),
            pltpu.SemaphoreType.DMA,
        ],
        compiler_params=pltpu.CompilerParams(vmem_limit_bytes=60 << 20, dimension_semantics=("arbitrary",)),
        cost_estimate=pl.CostEstimate(flops=36 * positions * width * width, bytes_accessed=40 << 20, transcendentals=positions * width * 4),
    )(tokens, cotangent, mixed, weights, weights, weights, weights, down_weights, vectors)


def leave_body(spots, dhid_ref, pre_ref, own_t_ref, token_ref, row_ref, row_t_ref, dvalue_ref, weight_ref, vector_ref, sums_ref, bias_ref,
               dfirst_ref, dweight_ref, block_ref, back_ref, dpre_all, rows32):
    first_at, value_at = spots
    positions, width = dhid_ref.shape
    wide = width // BS
    sums = [jnp.zeros((1, width), jnp.float32) for _ in range(3)]

    def unproject(grads, at, i):
        total = None
        for j in range(wide):
            part = dot_nt(grads[:, column(j)], weight_ref[at + i * wide + j])
            total = part if total is None else total + part
        return total

    def own(c, sums):
        rows = pl.ds(pl.multiple_of(c * BS, BS), BS)
        pre = pre_ref[rows, :]
        share = gate(pre)
        dpre = (dhid_ref[rows, :].astype(jnp.float32) * (share * (1.0 + pre * (1.0 - share)))).astype(jnp.bfloat16)
        dpre_all[rows, :] = dpre
        hat, _ = normalize(token_ref[rows, :].astype(jnp.float32))
        back = jnp.concatenate([unproject(dpre, first_at, i) for i in range(wide)], axis=1)
        back_ref[rows, :] = back
        return (
            sums[0] + jnp.sum(back * hat, axis=0, keepdims=True),
            sums[1] + jnp.sum(back, axis=0, keepdims=True),
            sums[2] + jnp.sum(dpre.astype(jnp.float32), axis=0, keepdims=True),
        )

    sums = lax.fori_loop(0, positions // BS, own, tuple(sums))

    def whole_row(c, sums):
        rows = pl.ds(pl.multiple_of(c * BS, BS), BS)
        dvalue = dvalue_ref[rows, :]
        hat, _ = normalize(row_ref[rows, :].astype(jnp.float32))
        back = jnp.concatenate([unproject(dvalue, value_at, i) for i in range(wide)], axis=1)
        return (
            sums[0] + jnp.sum(back * hat, axis=0, keepdims=True),
            sums[1] + jnp.sum(back, axis=0, keepdims=True),
            sums[2],
        )

    sums = lax.fori_loop(0, row_ref.shape[0] // BS, whole_row, sums)
    for i in range(wide):
        for j in range(wide):
            dfirst_ref[i * wide + j] = dot_nn(own_t_ref[column(i), :], dpre_all[:, column(j)]).astype(jnp.bfloat16)
            dweight_ref[i * wide + j] = dot_nn(row_t_ref[column(i), :], dvalue_ref[:, column(j)]).astype(jnp.bfloat16)
    rows32[...] = jnp.zeros_like(rows32)
    lines = (sums[0], sums[1], sums_ref[0:1], sums_ref[1:2], sums[2])
    for r, line in enumerate(lines):
        for i in range(wide):
            rows32[r * wide + i:r * wide + i + 1, :] = line[:, column(i)]
    at = len(lines) * wide
    rows32[at:at + bias_ref.shape[0], :] = bias_ref[...]
    block_ref[0] = jnp.zeros_like(block_ref[0])
    block_ref[0, 0:rows32.shape[0], :] = rows32[...].astype(jnp.bfloat16)


def leave(dhid, pre, own_t, tokens, token_row, row_t, dvalue, weights, vectors, sums, bias, spots):
    positions, width = dhid.shape
    wide = width // BS
    whole = pl.BlockSpec(memory_space=VMEM)
    low = jnp.bfloat16
    tall = -(-(5 * wide + bias.shape[0]) // 16) * 16
    return pl.pallas_call(
        functools.partial(leave_body, spots),
        name="leave",
        out_shape=(
            jax.ShapeDtypeStruct((wide * wide, BS, BS), low),
            jax.ShapeDtypeStruct((wide * wide, BS, BS), low),
            jax.ShapeDtypeStruct((1, BS, BS), low),
            jax.ShapeDtypeStruct((positions, width), jnp.float32),
        ),
        in_specs=[whole] * 11,
        out_specs=[whole] * 4,
        scratch_shapes=[VMEM((positions, width), low), VMEM((tall, BS), jnp.float32)],
        compiler_params=pltpu.CompilerParams(vmem_limit_bytes=60 << 20),
        cost_estimate=pl.CostEstimate(flops=4 * (positions + token_row.shape[0]) * width * width, bytes_accessed=24 << 20, transcendentals=positions * width),
    )(dhid, pre, own_t, tokens, token_row, row_t, dvalue, weights, vectors, sums, bias)


def finish_body(value_at, dvalue_ref, first_ref, dmiddle_ref, token_ref, weight_ref, vector_ref, out_ref):
    wide = vector_ref.shape[1] // BS

    def chunk(c, carry):
        rows = pl.ds(pl.multiple_of(c * BS, BS), BS)
        dvalue = dvalue_ref[rows, :]
        parts = []
        for i in range(wide):
            total = first_ref[rows, column(i)]
            for j in range(wide):
                total = total + dot_nt(dvalue[:, column(j)], weight_ref[value_at + i * wide + j])
            parts.append(total)
        scaled = jnp.concatenate(parts, axis=1) * vector_ref[0:1]
        hat, inverse = normalize(token_ref[rows, :].astype(jnp.float32))
        out_ref[rows, :] = dmiddle_ref[rows, :] + inverse * (
            scaled
            - jnp.mean(scaled, axis=-1, keepdims=True)
            - hat * jnp.mean(scaled * hat, axis=-1, keepdims=True)
        )
        return carry

    lax.fori_loop(0, token_ref.shape[0] // BS, chunk, 0)


def finish_inputs(dvalue, from_first, dmiddle, tokens, weights, vectors, value_at):
    whole = pl.BlockSpec(memory_space=VMEM)
    positions, width = tokens.shape
    return pl.pallas_call(
        functools.partial(finish_body, value_at),
        name="finish_inputs",
        out_shape=jax.ShapeDtypeStruct((positions, width), jnp.float32),
        in_specs=[whole] * 6,
        out_specs=whole,
        compiler_params=pltpu.CompilerParams(vmem_limit_bytes=60 << 20),
        cost_estimate=pl.CostEstimate(flops=2 * positions * width * width, bytes_accessed=12 << 20, transcendentals=0),
    )(dvalue, from_first, dmiddle, tokens, weights, vectors)


def block_bounds():
    model_blocks = D // BS
    first_end = model_blocks * model_blocks
    synth_end = first_end + model_blocks * (LEN // BS)
    value_end = synth_end + first_end
    output_end = value_end + first_end
    expand_end = output_end + model_blocks * (FF // BS)
    return (first_end, synth_end, value_end, output_end, expand_end)


def block_scales():
    first_end, synth_end, value_end, output_end, expand_end = block_bounds()
    spots = jnp.arange(BLOCKS)
    scales = jnp.where(
        spots < first_end,
        D ** (-0.5),
        jnp.where(
            spots < synth_end,
            3.0 * HD ** (-0.5),
            jnp.where(
                spots < value_end,
                D ** (-0.5),
                jnp.where(
                    spots < output_end,
                    4.0 * D ** (-0.5),
                    jnp.where(spots < expand_end, D ** (-0.5), FF ** (-0.5)),
                ),
            ),
        ),
    )
    return scales.astype(jnp.float32)


def slot_table(owners, own_most, slot_total):
    block_count = owners.shape[0]
    block_index = jnp.arange(block_count, dtype=jnp.int32)
    same_owner = owners[:, None] == owners[None, :]
    earlier = block_index[None, :] < block_index[:, None]
    rank_within = jnp.sum(jnp.where(same_owner & earlier, 1, 0), axis=1).astype(jnp.int32)
    slot_id = owners * own_most + rank_within
    slot_hit = slot_id[:, None] == jnp.arange(slot_total, dtype=jnp.int32)[None, :]
    used = jnp.any(slot_hit, axis=0)
    block_of = jnp.sum(jnp.where(slot_hit, block_index[:, None], 0), axis=0)
    return (slot_id, used, block_of)


def vector_adam(vectors, vec_moments, grad_rows, mom_fix, sec_fix):
    first_moment = BETA_MOM * vec_moments[0] + (1 - BETA_MOM) * grad_rows
    second = BETA_SEC * vec_moments[1] + (1 - BETA_SEC) * grad_rows * grad_rows
    step_rows = first_moment / mom_fix / (jnp.sqrt(second / sec_fix) + EPSILON)
    return (vectors - VECTOR_RATE * step_rows, jnp.stack([first_moment, second]))


def local(
    tokens,
    cotangent,
    seg_ids,
    seg_lengths,
    weights,
    vectors,
    vec_moments,
    moments,
    stats,
    bases,
    owners,
    step_count,
):
    rows_here, positions, width = tokens.shape
    owner_count = lax.axis_size("row") * lax.axis_size("seq")
    own_most = moments.shape[0]
    slot_count = owner_count * own_most
    block_count = weights.shape[0]
    piece_rows = weights.shape[1] // BS
    first_end, synth_end, value_end, _, expand_end = block_bounds()
    synth_count = synth_end - first_end
    tokens = tokens.reshape(positions, width)
    pieces_one, pieces_two, pieces_three = spread_pieces(
        weights,
        (
            ((first_end, synth_end), (0, first_end), (synth_end, value_end)),
            ((value_end, expand_end),),
            ((expand_end, block_count),),
        ),
    )
    spots = (synth_count, synth_end)
    rows_total, seqs_total = lax.axis_size("row"), lax.axis_size("seq")
    (gathered_one, gathered_two), token_row = gather_rows(
        [pieces_one, pieces_two], tokens, rows_total, seqs_total, (2, 2), 3
    )
    gathered_one, pieces_three = lax.optimization_barrier((gathered_one, pieces_three))
    gathered_three = lax.all_gather(pieces_three, AXES, axis=1, tiled=True)

    slot_range = jnp.arange(seg_lengths.shape[1], dtype=jnp.int32)
    before = slot_range[None, :] < slot_range[:, None]
    starts = jnp.sum(jnp.where(before, seg_lengths[0][None, :], 0), axis=1)
    offset = lax.axis_index("seq") * positions
    tables = tables_of(starts, seg_lengths[0], seg_ids[0], offset)

    hidden, first_pre, own_t, values, row_t = enter(tokens, token_row, gathered_one, vectors, spots)
    mixed, log_total = attn_forward(tables, hidden, gathered_one, values)
    layer_out, terms_two, early_terms, back_mixed, back_middle, norm_sums, grad_ffn_bias = middle_stage(
        tokens, cotangent.reshape(positions, width), mixed, gathered_two, gathered_three, vectors, 2
    )
    early_part = lax.psum_scatter(early_terms, "row", scatter_dimension=1, tiled=True)
    synth_grad, back_hidden, value_terms = attn_backward(
        tables, hidden, gathered_one, values, back_mixed, mixed, log_total
    )
    grad_first, grad_value, vector_block, back_from_first = leave(
        back_hidden,
        first_pre,
        own_t,
        tokens,
        token_row,
        row_t,
        value_terms,
        gathered_one,
        vectors,
        norm_sums,
        grad_ffn_bias,
        spots,
    )
    late_terms = [grad_first, grad_value, vector_block, synth_grad, terms_two]
    vector_rows = vectors.shape[0] * vectors.shape[1] // BS
    sums = reduce_rows(late_terms, early_part, rows_total, seqs_total, 6, 1)
    slot_id, used, block_of = slot_table(owners, own_most, slot_count)
    device_index = lax.axis_index(AXES)
    mine_used = lax.dynamic_slice_in_dim(used, device_index * own_most, own_most)
    mine_block = lax.dynamic_slice_in_dim(block_of, device_index * own_most, own_most)
    vector_spot = 2 * first_end
    spot_of = jnp.where(
        block_of < first_end,
        block_of,
        jnp.where(
            block_of < synth_end,
            block_of + first_end + 1,
            jnp.where(block_of < value_end, block_of - synth_end + first_end, block_of + 1),
        ),
    )
    got, square_parts, vector_parts = exchange(
        spot_of, sums, rows_total, seqs_total, vector_spot, vector_rows, 2
    )
    got, value_late = lax.optimization_barrier((got, value_terms))
    value_sums = lax.psum_scatter(value_late, "seq", scatter_dimension=0, tiled=True)
    x_grad = finish_inputs(
        value_sums, back_from_first, back_middle, tokens, gathered_one, vectors, synth_end
    )
    vector_total = vector_parts.reshape(-1, BS)[:vector_rows].reshape(vectors.shape)
    grad_norm = jnp.sqrt(jnp.sum(square_parts))
    clip_max = math.sqrt(block_count * BS * BS + vectors.shape[0] * vectors.shape[1])
    scale = jnp.minimum(1.0, clip_max / grad_norm)
    step_value = step_count[0].astype(jnp.float32)
    mom_fix = 1.0 - jnp.power(BETA_MOM, step_value)
    sec_fix = 1.0 - jnp.power(BETA_SEC, step_value)
    new_vectors, new_vec_moments = vector_adam(
        vectors, vec_moments, vector_total * scale, mom_fix, sec_fix
    )
    rate_table = RATE_FACTOR * block_scales()
    slot_rates = jnp.sum(
        jnp.where(
            mine_block[:, None] == jnp.arange(block_count, dtype=jnp.int32)[None, :],
            rate_table[None, :],
            0.0,
        ),
        axis=1,
    )
    floats = jnp.concatenate([jnp.stack([scale, mom_fix, sec_fix]), slot_rates])
    mine_spot = jnp.where(
        mine_block < first_end,
        mine_block + synth_count,
        jnp.where(mine_block < synth_end, mine_block - first_end, mine_block),
    )
    ints = jnp.concatenate([mine_used.astype(jnp.int32), mine_spot])
    new_master, new_moments, new_stats, wide = soap_update(
        ints, floats, got, gathered_one, gathered_two, gathered_three, moments, stats, bases
    )
    new_bases = soap_bases(ints, wide, bases)
    returned = lax.all_to_all(
        new_master.reshape(1, own_most, BS, BS), AXES, split_axis=2, concat_axis=0, tiled=True
    )
    new_weights = collect(slot_id, returned.reshape(slot_count, piece_rows, BS))
    return (
        layer_out.reshape(rows_here, positions, width),
        x_grad.reshape(rows_here, positions, width),
        new_weights,
        new_moments,
        new_stats,
        new_bases,
        new_vectors,
        new_vec_moments,
        grad_norm.reshape(1),
    )


def solution(mesh):
    placed = (
        P("row", "seq", None),
        P("row", "seq", None),
        P("row", "seq"),
        P("row", None),
        P(None, ("row", "seq")),
        P(),
        P(),
        P(("row", "seq"), None, None, None),
        P(("row", "seq"), None, None, None),
        P(("row", "seq"), None, None, None),
        P(),
        P(),
    )
    return jax.shard_map(
        local,
        mesh=mesh,
        in_specs=placed,
        out_specs=(
            P("row", "seq", None),
            P("row", "seq", None),
            P(None, ("row", "seq")),
            P(("row", "seq"), None, None, None),
            P(("row", "seq"), None, None, None),
            P(("row", "seq"), None, None, None),
            P(),
            P(),
            P(),
        ),
        check_vma=False,
    )
```

```python
import functools
import math

import jax
import jax.numpy as jnp
from jax import lax
from jax.experimental import pallas as pl
from jax.experimental.pallas import tpu as pltpu
from jax.sharding import PartitionSpec as P

D = 768
HEADS = 12
HD = 64
FF = 3072
LEN = 2048
BS = 256
BLOCKS = 123

BETA_MOM = 0.95
BETA_SEC = 0.95
EPSILON = 1e-08
DECAY = 0.01
VECTOR_RATE = 0.3
RATE_FACTOR = 2.0
NORM_EPS = 1e-05
NEG = -1e30
PANEL = 32
HIGHEST = lax.Precision.HIGHEST
VMEM = pltpu.VMEM
AXES = ("row", "seq")
MESH = pl.DeviceIdType.MESH


def dot_nn(a, b):
    return lax.dot_general(a, b, (((1,), (0,)), ((), ())), preferred_element_type=jnp.float32)


def dot_nt(a, b):
    return lax.dot_general(a, b, (((1,), (1,)), ((), ())), preferred_element_type=jnp.float32)


TILES = (128, 256)


def tables_of(starts, lengths, ids, offset):
    ends = jnp.stack([ids[0], ids[-1] + 1, offset])
    return jnp.concatenate([starts, lengths, ends]).astype(jnp.int32)


def split_heads(synth_ref, value_ref, f2m, v32):
    length = value_ref.shape[0]
    low_rows = lax.broadcasted_iota(jnp.int32, (2 * HD, BS), 0) < HD
    for j in range(synth_ref.shape[0]):
        tile = synth_ref[j]
        zero = jnp.zeros_like(tile)
        f2m[0, j] = jnp.where(low_rows, tile, zero)
        f2m[1, j] = jnp.where(low_rows, zero, tile)
    v32[0:length] = value_ref[...].astype(jnp.float32)
    v32[length:] = jnp.zeros((BS, 2 * HD), jnp.float32)


def each_segment(tables, positions, visit):
    segs = (tables.shape[0] - 3) // 2
    offset = tables[2 * segs + 2]

    def segment(s, carry):
        start, count = tables[s], tables[segs + s]
        low = jnp.maximum(start - offset, 0)
        high = jnp.minimum(start + count - offset, positions)

        first = low // 16 * 16

        sizes = [size for size in TILES if size < positions]
        for size, less in zip(sizes, [0, *sizes]):

            @pl.when((high - first <= size) & (high - first > less))
            def _(size=size):
                at = pl.multiple_of(jnp.minimum(first, positions - size), 16)
                visit(start, count, size, at, low, high)

        @pl.when(high - first > sizes[-1])
        def _():
            visit(start, count, positions, 0, low, high)

        return carry

    lax.fori_loop(tables[2 * segs], tables[2 * segs + 1], segment, 0)


def attn_forward_body(tables, hid_ref, synth_ref, value_ref, mixed_ref, lse_ref, f2m, v32, lbuf):
    split_heads(synth_ref, value_ref, f2m, v32)
    lane = lax.broadcasted_iota(jnp.int32, (1, BS), 1)

    def visit(start, count, size, at, low, high):
        rows = pl.ds(at, size)
        hid = hid_ref[rows, :]
        used = (count + BS - 1) // BS

        def scores(j, tops):
            keep = lane < count - j * BS
            out = []
            for h in range(2):
                part = jnp.where(keep, dot_nn(hid, f2m[h, j]), NEG)
                lbuf[h, j, 0:size] = part
                out.append(jnp.maximum(tops[h], jnp.maximum(part[:, :128], part[:, 128:])))
            return tuple(out)

        none = jnp.full((size, 128), NEG, jnp.float32)
        tops = lax.fori_loop(0, used, scores, (none, none))
        tops = [jnp.max(top, axis=1, keepdims=True) for top in tops]

        def weigh(j, carried):
            value = v32[pl.ds(start + j * BS, BS), :].astype(jnp.bfloat16)
            out = []
            for h in range(2):
                total, mix = carried[h]
                part = jnp.exp(lbuf[h, j, 0:size] - tops[h])
                total = total + part[:, :128] + part[:, 128:]
                mix = mix + dot_nn(part.astype(jnp.bfloat16), value)
                out.append((total, mix))
            return tuple(out)

        blank = jnp.zeros((size, 128), jnp.float32)
        pair = lax.fori_loop(0, used, weigh, ((blank, blank), (blank, blank)))
        sums = [jnp.sum(total, axis=1, keepdims=True) for total, _ in pair]
        left = lax.broadcasted_iota(jnp.int32, (size, 2 * HD), 1) < HD
        mix = jnp.where(left, pair[0][1], pair[1][1]) / jnp.where(left, sums[0], sums[1])
        log = jnp.where(left, tops[0] + jnp.log(sums[0]), tops[1] + jnp.log(sums[1]))
        row = lax.broadcasted_iota(jnp.int32, (size, 1), 0) + at
        here = (row >= low) & (row < high)
        mixed_ref[rows, :] = jnp.where(here, mix, mixed_ref[rows, :])
        lse_ref[rows, :] = jnp.where(here, log, lse_ref[rows, :])

    each_segment(tables, hid_ref.shape[0], visit)


def attn_specs(positions, length):
    blocks, per = length // BS, BS // (2 * HD)
    return (
        pl.BlockSpec((positions, 2 * HD), lambda p, t: (0, p)),
        pl.BlockSpec((blocks, 2 * HD, BS), lambda p, t: (p // per, p % per, 0)),
        pl.BlockSpec((length, 2 * HD), lambda p, t: (0, p)),
    )


def attn_forward(tables, hidden, synth, values):
    positions, width = hidden.shape
    length = values.shape[0]
    blocks = length // BS
    tok, f2, val = attn_specs(positions, length)
    return pl.pallas_call(
        attn_forward_body,
        name="attn_forward",
        out_shape=(jax.ShapeDtypeStruct((positions, width), jnp.float32),) * 2,
        grid_spec=pltpu.PrefetchScalarGridSpec(
            num_scalar_prefetch=1,
            grid=(width // (2 * HD),),
            in_specs=[tok, f2, val],
            out_specs=[tok] * 2,
            scratch_shapes=[
                pltpu.VMEM((2, blocks, 2 * HD, BS), jnp.bfloat16),
                pltpu.VMEM((length + BS, 2 * HD), jnp.float32),
                pltpu.VMEM((2, blocks, positions, BS), jnp.float32),
            ],
        ),
        compiler_params=pltpu.CompilerParams(vmem_limit_bytes=60 << 20, dimension_semantics=("arbitrary",)),
        cost_estimate=pl.CostEstimate(flops=4 * positions * length * width * 2, bytes_accessed=12 << 20, transcendentals=positions * length * 12),
    )(tables, hidden, synth, values)


def attn_backward_body(tables, hid_ref, synth_ref, value_ref, dmix_ref, mixed_ref, lse_ref,
                       dsynth_ref, dhid_ref, dvalue_ref, f2m, v32, dv32, dmm, dacc, df2):
    length = value_ref.shape[0]
    split_heads(synth_ref, value_ref, f2m, v32)
    dv32[...] = jnp.zeros_like(dv32)
    df2[...] = jnp.zeros_like(df2)
    lane = lax.broadcasted_iota(jnp.int32, (1, BS), 1)

    def visit(start, count, size, at, low, high):
        rows = pl.ds(at, size)
        left = lax.broadcasted_iota(jnp.int32, (size, 2 * HD), 1) < HD
        row = lax.broadcasted_iota(jnp.int32, (size, 1), 0) + at
        here = (row >= low) & (row < high)
        hid = hid_ref[rows, :]
        hid_t = hid.astype(jnp.float32).T.astype(jnp.bfloat16)
        dmix32 = dmix_ref[rows, :].astype(jnp.float32)
        dmix_t = dmix32.T.astype(jnp.bfloat16)
        dot_pair = dmix32 * mixed_ref[rows, :]
        nil = jnp.zeros_like(dmix32)
        deltas = (
            jnp.sum(jnp.where(left, dot_pair, nil), axis=1, keepdims=True),
            jnp.sum(jnp.where(left, nil, dot_pair), axis=1, keepdims=True),
        )
        dmm[0, 0:size] = jnp.where(left, dmix32, nil).astype(jnp.bfloat16)
        dmm[1, 0:size] = jnp.where(left, nil, dmix32).astype(jnp.bfloat16)
        logs = lse_ref[rows, :]
        lse = [jnp.where(here, logs[:, h * HD:h * HD + 1], -NEG) for h in range(2)]
        dacc[0:size] = jnp.zeros((size, 2 * HD), jnp.float32)

        def block(j, carry):
            keep = lane < count - j * BS
            value = v32[pl.ds(start + j * BS, BS), :].astype(jnp.bfloat16)
            parts = []
            total = None
            for h in range(2):
                synth = f2m[h, j]
                prob = jnp.where(keep, jnp.exp(dot_nn(hid, synth) - lse[h]), 0.0)
                dprob = dot_nt(dmm[h, 0:size], value)
                dlog = (prob * (dprob - deltas[h])).astype(jnp.bfloat16)
                head = slice(h * HD, (h + 1) * HD)
                df2[j, head, :] += dot_nn(hid_t[head], dlog)
                back = dot_nt(dlog, synth)
                total = back if total is None else total + back
                parts.append(dot_nn(dmix_t[head], prob.astype(jnp.bfloat16)))
            dacc[0:size] += total
            dv32[pl.ds(start + j * BS, BS), :] += jnp.concatenate(parts, axis=0).T
            return carry

        lax.fori_loop(0, (count + BS - 1) // BS, block, 0)
        dhid_ref[rows, :] = jnp.where(here, dacc[0:size], dhid_ref[rows, :].astype(jnp.float32)).astype(jnp.bfloat16)

    each_segment(tables, hid_ref.shape[0], visit)
    dvalue_ref[...] = dv32[0:length].astype(jnp.bfloat16)
    dsynth_ref[...] = df2[...].astype(jnp.bfloat16)


def attn_backward(tables, hidden, synth, values, dmix, mixed, lse):
    positions, width = hidden.shape
    length = values.shape[0]
    blocks = length // BS
    tok, f2, val = attn_specs(positions, length)
    return pl.pallas_call(
        attn_backward_body,
        name="attn_backward",
        out_shape=(
            jax.ShapeDtypeStruct((width // BS * blocks, BS, BS), jnp.bfloat16),
            jax.ShapeDtypeStruct((positions, width), jnp.bfloat16),
            jax.ShapeDtypeStruct((length, width), jnp.bfloat16),
        ),
        grid_spec=pltpu.PrefetchScalarGridSpec(
            num_scalar_prefetch=1,
            grid=(width // (2 * HD),),
            in_specs=[tok, f2, val, tok, tok, tok],
            out_specs=[f2, tok, val],
            scratch_shapes=[
                pltpu.VMEM((2, blocks, 2 * HD, BS), jnp.bfloat16),
                pltpu.VMEM((length + BS, 2 * HD), jnp.float32),
                pltpu.VMEM((length + BS, 2 * HD), jnp.float32),
                pltpu.VMEM((2, positions, 2 * HD), jnp.bfloat16),
                pltpu.VMEM((positions, 2 * HD), jnp.float32),
                pltpu.VMEM((blocks, 2 * HD, BS), jnp.float32),
            ],
        ),
        compiler_params=pltpu.CompilerParams(vmem_limit_bytes=60 << 20, dimension_semantics=("arbitrary",)),
        cost_estimate=pl.CostEstimate(flops=10 * positions * length * width * 2, bytes_accessed=24 << 20, transcendentals=positions * length * 12),
    )(tables, hidden, synth, values, dmix, mixed, lse)


def exact(a, b, da=1, db=0):
    return lax.dot_general(a, b, (((da,), (db,)), ((), ())), precision=HIGHEST, preferred_element_type=jnp.float32)

def parts_of(values):
    first = values.astype(jnp.bfloat16)
    rest = values - first.astype(jnp.float32)
    second = rest.astype(jnp.bfloat16)
    return first, second, (rest - second.astype(jnp.float32)).astype(jnp.bfloat16)


LEFT_PARTS, RIGHT_PARTS = (0, 0, 1, 0, 1, 2), (0, 1, 0, 2, 1, 0)


def exact_thin(left, right, axis):
    lefts, rights = parts_of(left), parts_of(right)
    return lax.dot_general(
        jnp.concatenate([lefts[k] for k in LEFT_PARTS], axis=axis),
        jnp.concatenate([rights[k] for k in RIGHT_PARTS], axis=0),
        (((axis,), (0,)), ((), ())),
        preferred_element_type=jnp.float32,
    )


def soap_update_body(ints, floats, got_ref, one_ref, two_ref, three_ref, moment_ref, stat_ref, basis_ref,
                     new_master_ref, new_moment_ref, new_stat_ref, wide_ref, grad_ref, master_ref, sems):
    devices, slots, part = got_ref.shape[0], got_ref.shape[1], got_ref.shape[2]
    sources, at = [], 0
    for ref in (one_ref, two_ref, three_ref):
        sources.append((ref, at, at + ref.shape[0]))
        at += ref.shape[0]

    def master_copy(k, source):
        return pltpu.make_async_copy(source, master_ref.at[k], sems.at[k])

    for k in range(slots):
        block = ints[slots + k]
        for ref, low, high in sources:

            @pl.when((block >= low) & (block < high))
            def _():
                master_copy(k, ref.at[block - low]).start()

    scale, mom_fix, sec_fix = floats[0], floats[1], floats[2]

    per = max(1, 8 // part)

    def join(d, carry):
        rows = pl.ds(pl.multiple_of(d * (per * part), per * part), per * part)
        for k in range(slots):
            pieces = [got_ref[d * per + i, k].astype(jnp.float32) for i in range(per)]
            grad_ref[k, rows, :] = pieces[0] if per == 1 else jnp.concatenate(pieces, axis=0)
        return carry

    lax.fori_loop(0, devices // per, join, 0)
    for k in range(slots):
        master_copy(k, one_ref.at[0]).wait()

    def prepare(k, carry):
        used = ints[k] > 0
        grad = jnp.where(used, grad_ref[k] * scale, 0.0)
        left, right = basis_ref[k, 0], basis_ref[k, 1]
        old_left, old_right = stat_ref[k, 0], stat_ref[k, 1]
        left_stat = BETA_SEC * old_left + (1 - BETA_SEC) * exact(grad, grad, 1, 1)
        right_stat = BETA_SEC * old_right + (1 - BETA_SEC) * exact(grad, grad, 0, 0)
        new_stat_ref[k, 0] = jnp.where(used, left_stat, old_left)
        new_stat_ref[k, 1] = jnp.where(used, right_stat, old_right)
        left_t = left.T
        for side, (turn, stat) in enumerate(((left_t, left_stat), (right.T, right_stat))):
            cross = exact(turn, stat)
            wide_ref[2 * k + side, :, 0:BS] = exact(cross, cross, 1, 1)
            wide_ref[2 * k + side, :, BS:] = cross
        momentum = BETA_MOM * moment_ref[k, 0] + (1 - BETA_MOM) * grad
        turned_grad = exact(exact(left_t, grad), right)
        turned_mom = exact(exact(left_t, momentum), right)
        old_second = moment_ref[k, 1]
        second = BETA_SEC * old_second + (1 - BETA_SEC) * turned_grad * turned_grad
        step = turned_mom / mom_fix / (jnp.sqrt(second / sec_fix) + EPSILON)
        update = exact(exact(left, step), right, 1, 1)
        master = master_ref[k].astype(jnp.float32)
        new_master_ref[k] = (master - floats[3 + k] * (update + DECAY * master)).astype(jnp.bfloat16)
        new_moment_ref[k, 0] = jnp.where(used, momentum, moment_ref[k, 0])
        new_moment_ref[k, 1] = jnp.where(used, second, old_second)
        return carry

    lax.fori_loop(0, slots, prepare, 0)


def soap_update(ints, floats, got, one, two, three, moments, stats, bases):
    slots = got.shape[1]
    whole = pl.BlockSpec(memory_space=VMEM)
    scalar = pl.BlockSpec(memory_space=pltpu.SMEM)
    anywhere = pl.BlockSpec(memory_space=pl.ANY)
    pair = jax.ShapeDtypeStruct(moments.shape, jnp.float32)
    return pl.pallas_call(
        soap_update_body,
        name="soap_update",
        out_shape=(
            jax.ShapeDtypeStruct((slots, BS, BS), jnp.bfloat16),
            pair,
            pair,
            jax.ShapeDtypeStruct((2 * slots, BS, 2 * BS), jnp.float32),
        ),
        in_specs=[scalar, scalar, whole, anywhere, anywhere, anywhere] + [whole] * 3,
        out_specs=[whole] * 4,
        scratch_shapes=[
            VMEM((slots, BS, BS), jnp.float32),
            VMEM((slots, BS, BS), jnp.bfloat16),
            pltpu.SemaphoreType.DMA((slots,)),
        ],
        compiler_params=pltpu.CompilerParams(vmem_limit_bytes=60 << 20),
        cost_estimate=pl.CostEstimate(flops=slots * 12 * 6 * 2 * BS ** 3, bytes_accessed=slots * 14 * 4 * BS * BS, transcendentals=slots * BS * BS),
    )(ints, floats, got, one, two, three, moments, stats, bases)


def soap_bases_body(ints, given_ref, basis_ref, new_basis_ref, wide):
    slots = basis_ref.shape[0]
    count = 2 * slots
    wide[...] = given_ref[...]
    group = 128 // PANEL
    groups = count // group
    row = lax.broadcasted_iota(jnp.int32, (PANEL, 128), 0)
    lane = lax.broadcasted_iota(jnp.int32, (PANEL, 128), 1)
    unit = jnp.where(row == lane % PANEL, 1.0, 0.0)
    spot = lane // PANEL * PANEL
    for p in range(BS // PANEL):
        low = p * PANEL
        rows = slice(low, low + PANEL)
        schur, inverse, pivots = [], [], []
        for q in range(groups):
            schur.append(jnp.concatenate([wide[q * group + i, rows, low:low + PANEL] for i in range(group)], axis=1))
            inverse.append(unit)
            pivots.append(unit)

        for k in range(0, PANEL, 8):
            for q in range(groups):
                columns = [jnp.take_along_axis(schur[q], spot + (k + i), axis=1) for i in range(8)]
                for i in range(8):
                    at = k + i
                    pivot = columns[i][at:at + 1]
                    head = jnp.where(row > at, columns[i] * (1.0 / pivot), 0.0)
                    for j in range(i + 1, 8):
                        columns[j] = columns[j] - head * columns[j][at:at + 1]
                    schur[q] = schur[q] - head * schur[q][at:at + 1]
                    inverse[q] = inverse[q] - head * inverse[q][at:at + 1]
                    pivots[q] = jnp.where(row == at, pivot, pivots[q])
        for q in range(groups):
            whole = inverse[q] * lax.rsqrt(pivots[q])
            for i in range(group):
                m = q * group + i
                near = low // 128 * 128
                limit = near + 128
                part = exact_thin(whole[:, i * PANEL:(i + 1) * PANEL], wide[m, rows, near:], 1)
                wide[m, rows, near:] = part
                if low + PANEL < limit:
                    wide[m, low + PANEL:limit, near:] -= exact_thin(
                        part[:, low + PANEL - near:limit - near], part, 0
                    )
                elif limit < BS:
                    above = wide[m, near:limit, limit:]
                    wide[m, limit:, limit:] -= exact(above[:, :BS - limit], above, 0, 0)

    def finish(k, carry):
        used = ints[k] > 0
        for side in range(2):
            new_basis_ref[k, side] = jnp.where(used, wide[2 * k + side, :, BS:].T, basis_ref[k, side])
        return carry

    lax.fori_loop(0, slots, finish, 0)


def soap_bases(ints, wide, bases):
    slots = bases.shape[0]
    whole = pl.BlockSpec(memory_space=VMEM)
    return pl.pallas_call(
        soap_bases_body,
        name="soap_bases",
        out_shape=jax.ShapeDtypeStruct(bases.shape, jnp.float32),
        in_specs=[pl.BlockSpec(memory_space=pltpu.SMEM), whole, whole],
        out_specs=whole,
        scratch_shapes=[VMEM(wide.shape, jnp.float32)],
        compiler_params=pltpu.CompilerParams(vmem_limit_bytes=60 << 20),
        cost_estimate=pl.CostEstimate(flops=slots * 4 * 6 * 2 * BS ** 3, bytes_accessed=slots * 8 * 4 * BS * BS, transcendentals=slots * BS * BS),
    )(ints, wide, bases)


def spread_pieces_body(orders, weight_ref, *refs):
    *out_refs, lay = refs
    for i in range(lay.shape[1]):
        lay[:, i, :] = weight_ref[:, i * BS:(i + 1) * BS]
    for out_ref, order in zip(out_refs, orders):
        at = 0
        for low, high in order:
            out_ref[at:at + high - low] = lay[low:high].astype(jnp.bfloat16)
            at += high - low


def spread_pieces(weights, orders):
    count, rows = weights.shape[0], weights.shape[1] // BS
    sizes = [sum(high - low for low, high in order) for order in orders]
    whole = pl.BlockSpec(memory_space=VMEM)
    return pl.pallas_call(
        functools.partial(spread_pieces_body, orders),
        name="spread_pieces",
        out_shape=[jax.ShapeDtypeStruct((size, rows, BS), jnp.bfloat16) for size in sizes],
        in_specs=[whole],
        out_specs=[whole] * len(sizes),
        scratch_shapes=[VMEM((count, rows, BS), jnp.float32)],
        compiler_params=pltpu.CompilerParams(vmem_limit_bytes=60 << 20),
    )(weights)


def collect_body(slot_id, piece_ref, out_ref):
    rows = piece_ref.shape[1]

    def place(m, carry):
        piece = piece_ref[slot_id[m]].astype(jnp.float32)
        for i in range(rows):
            out_ref[pl.ds(m, 1), i * BS:(i + 1) * BS] = piece[i:i + 1]
        return carry

    lax.fori_loop(0, out_ref.shape[0], place, 0)


def collect(slot_id, pieces):
    count, rows = slot_id.shape[0], pieces.shape[1]
    whole = pl.BlockSpec(memory_space=VMEM)
    return pl.pallas_call(
        collect_body,
        name="collect",
        out_shape=jax.ShapeDtypeStruct((count, rows * BS), jnp.float32),
        in_specs=[pl.BlockSpec(memory_space=pltpu.SMEM), whole],
        out_specs=whole,
        compiler_params=pltpu.CompilerParams(vmem_limit_bytes=60 << 20),
    )(slot_id, pieces)


def partners(bits):
    row, seq = lax.axis_index("row"), lax.axis_index("seq")
    core, flags, peers = row % 2, [], []
    for k in range(bits):
        flag = row // 2 ** (k + 1) % 2
        flags.append(flag)
        peers.append((row + (1 - 2 * flag) * 2 ** (k + 1), seq))
    return core, (row + 1 - 2 * core, seq), flags, peers


def greet(devices):
    barrier = pltpu.get_barrier_semaphore()
    for device in devices:
        pl.semaphore_signal(barrier, inc=1, device_id=device, device_id_type=MESH)
    pl.semaphore_wait(barrier, len(devices))


def in_turns(works):
    live = []
    works = list(works)
    while works or live:
        if works:
            live.append(works.pop(0))
        live = [work for work in reversed(live) if next(work, None) is not None][::-1]


def group_bounds(count, groups):
    return [(count * k // groups, count * (k + 1) // groups) for k in range(groups)]


def reduce_rows_body(bits, seqs, groups, given, *refs):
    in_refs, summed_ref, (out_ref, mine, near, *rest) = refs[:given], refs[given], refs[given + 1:]
    far = rest[:bits]
    spread, arrived, own_summed, got_summed, keep_sems, send, recv = rest[bits:]
    count, extra = mine.shape[0], own_summed.shape[0]
    part = out_ref.shape[1]
    core, sibling, flags, peers = partners(bits)
    row, seq = lax.axis_index("row"), lax.axis_index("seq")
    beside = [(row, (seq + k) % seqs) for k in range(1, seqs)]
    greet([sibling, *peers, *beside])
    used = [0]

    def copy(source, target, device):
        at = used[0]
        used[0] += 1
        return pltpu.make_async_remote_copy(
            src_ref=source, dst_ref=target, send_sem=send.at[at], recv_sem=recv.at[at],
            device_id=device, device_id_type=MESH,
        )

    some = slice(None)
    every = (some,) * bits
    bounds = group_bounds(count, groups)
    starts, kept = [[] for _ in bounds], [[] for _ in bounds]
    at = local = 0
    for ref in in_refs:
        for g, (low, high) in enumerate(bounds):
            begin, end = max(low, at), min(high, at + ref.shape[0])
            if begin < end:
                span, to = pl.ds(begin - at, end - begin), pl.ds(begin, end - begin)
                starts[g].append(copy(ref.at[(span, *every, 1 - core)], near.at[to], sibling))
                kept[g].append(pltpu.make_async_copy(ref.at[(span, *every, core)], mine.at[to], keep_sems.at[local]))
                local += 1
        at += ref.shape[0]
    for g in range(groups):
        for move in starts[g] + kept[g]:
            move.start()
    extras = [copy(summed_ref.at[:, device[1]], got_summed.at[k], device) for k, device in enumerate(beside)]
    own_extra = pltpu.make_async_copy(summed_ref.at[:, seq], own_summed, keep_sems.at[local])
    for move in (*extras, own_extra):
        move.start()

    def work(g):
        low, high = bounds[g]
        span = pl.ds(low, high - low)
        order = list(range(bits)) if g % 2 == 0 else list(range(bits - 1, -1, -1))
        place = [some] * bits
        for move in starts[g] + kept[g]:
            move.wait()

        def first(n, carry):
            total = mine[n].astype(jnp.float32) + near[n].astype(jnp.float32)
            mine[n] = total.astype(jnp.bfloat16)
            return carry

        lax.fori_loop(low, high, first, 0)
        for step, bit in enumerate(order):
            spot = bits - 1 - bit
            theirs = list(place)
            theirs[spot] = 1 - flags[bit]
            place[spot] = flags[bit]
            move = copy(mine.at[(span, *theirs)], far[step].at[span], peers[bit])
            move.start()
            yield True
            move.wait()
            last = step == bits - 1
            where = tuple(place)

            def add(n, carry, step=step, where=where, last=last):
                total = mine[(n, *where)].astype(jnp.float32) + far[step][n].astype(jnp.float32)
                if last:
                    for s in range(seqs):
                        spread[s, n] = total[s * part:(s + 1) * part].astype(jnp.bfloat16)
                else:
                    mine[(n, *where)] = total.astype(jnp.bfloat16)
                return carry

            lax.fori_loop(low, high, add, 0)
        final = [
            copy(spread.at[device[1], span], arrived.at[k, span], device) for k, device in enumerate(beside)
        ]
        for move in final:
            move.start()
        yield True
        for move in final:
            move.wait()

        def finish(n, carry):
            total = spread[seq, n].astype(jnp.float32)
            for k in range(seqs - 1):
                total = total + arrived[k, n].astype(jnp.float32)
            out_ref[n] = total
            return carry

        lax.fori_loop(low, high, finish, 0)

    in_turns([work(g) for g in range(groups)])
    for move in (*extras, own_extra):
        move.wait()

    def add_extra(n, carry):
        total = own_summed[n].astype(jnp.float32)
        for k in range(seqs - 1):
            total = total + got_summed[k, n].astype(jnp.float32)
        out_ref[count + n] = total
        return carry

    lax.fori_loop(0, extra, add_extra, 0)


def reduce_rows(terms, summed, rows, seqs, groups, collective):
    count = sum(term.shape[0] for term in terms)
    bits = (rows // 2).bit_length() - 1
    slab = BS // rows
    part = slab // seqs
    twos = (2,) * bits
    low = jnp.bfloat16
    most = len(terms) + groups + 1
    sems = groups * (bits + seqs - 1) + most + seqs
    extra = summed.shape[0]
    return pl.pallas_call(
        functools.partial(reduce_rows_body, bits, seqs, groups, len(terms)),
        name="reduce_rows",
        out_shape=jax.ShapeDtypeStruct((count + extra, part, BS), jnp.float32),
        in_specs=[pl.BlockSpec(memory_space=pl.ANY)] * (len(terms) + 1),
        out_specs=pl.BlockSpec(memory_space=VMEM),
        scratch_shapes=[
            VMEM((count, *twos, slab, BS), low),
            VMEM((count, *twos, slab, BS), low),
            *[VMEM((count, *twos[k + 1:], slab, BS), low) for k in range(bits)],
            VMEM((seqs, count, part, BS), low),
            VMEM((seqs - 1, count, part, BS), low),
            VMEM((extra, part, BS), low),
            VMEM((seqs - 1, extra, part, BS), low),
            pltpu.SemaphoreType.DMA((most,)),
            pltpu.SemaphoreType.DMA((sems,)),
            pltpu.SemaphoreType.DMA((sems,)),
        ],
        compiler_params=pltpu.CompilerParams(
            collective_id=collective, has_side_effects=True, vmem_limit_bytes=60 << 20
        ),
        cost_estimate=pl.CostEstimate(flops=count * BS * BS, bytes_accessed=4 * count * BS * BS, transcendentals=0),
    )(*[term.reshape(-1, *twos, 2, slab, BS) for term in terms], summed.reshape(-1, seqs, part, BS))


def exchange_body(seqs, sources, spot_of, late_ref, got_ref, square_ref, vector_ref, out, mine, send, recv):
    devices, own = got_ref.shape[0], got_ref.shape[1]
    part = late_ref.shape[1]
    me = lax.axis_index("row") * seqs + lax.axis_index("seq")
    barrier = pltpu.get_barrier_semaphore()

    def peer(k):
        to = (me + k) % devices
        return to, (to // seqs, to % seqs)

    def hello(k, carry):
        pl.semaphore_signal(barrier, inc=1, device_id=peer(k)[1], device_id_type=MESH)
        return carry

    lax.fori_loop(1, devices, hello, 0)

    def place(d, carry):
        for s in range(own):
            out[d, s] = late_ref[spot_of[d * own + s]].astype(jnp.bfloat16)
        return carry

    lax.fori_loop(0, devices, place, 0)

    pl.semaphore_wait(barrier, devices - 1)

    def move(source, target, kind, k, device):
        return pltpu.make_async_remote_copy(
            src_ref=source, dst_ref=target, send_sem=send.at[kind, k], recv_sem=recv.at[kind, k],
            device_id=device, device_id_type=MESH,
        )

    def moves(k):
        to, device = peer(k)
        return (
            move(out.at[to], got_ref.at[me], 0, k, device),
            move(mine, square_ref.at[me], 1, k, device),
        )

    def launch(kind):
        def start(k, carry):
            moves(k)[kind].start()
            return carry

        return start

    lax.fori_loop(1, devices, launch(0), 0)

    def add(ref, total):
        def step(m, total):
            value = ref[m].astype(jnp.float32)
            return total + value * value

        return lax.fori_loop(0, ref.shape[0], step, total)

    total = add(late_ref, jnp.zeros((part, BS), jnp.float32))
    mine[...] = jnp.sum(total[:, :128] + total[:, 128:], axis=0, keepdims=True)
    lax.fori_loop(1, devices, launch(1), 0)

    @pl.when(me < sources[0])
    def _():
        def tell(k, carry):
            move(late_ref.at[sources[1]], vector_ref.at[me], 2, k, peer(k)[1]).start()
            return carry

        lax.fori_loop(1, devices, tell, 0)
        vector_ref[me] = late_ref[sources[1]]

    got_ref[me] = out[me]
    square_ref[me] = mine[...]

    def finish(k, carry):
        for one in moves(k):
            one.wait()
        return carry

    lax.fori_loop(1, devices, finish, 0)

    @pl.when(me < sources[0])
    def _():
        def told(k, carry):
            move(late_ref.at[sources[1]], vector_ref.at[me], 2, k, peer(k)[1]).wait_send()
            return carry

        lax.fori_loop(1, devices, told, 0)

    for d in range(sources[0]):
        @pl.when(me != d)
        def _():
            k = (me - d + devices) % devices
            move(late_ref.at[sources[1]], vector_ref.at[d], 2, k, peer(k)[1]).wait_recv()


def exchange(spot_of, late, rows, seqs, vector_spot, vector_rows, collective):
    devices = rows * seqs
    part = late.shape[1]
    own = spot_of.shape[0] // devices
    told = -(-vector_rows // part)
    whole = pl.BlockSpec(memory_space=VMEM)
    return pl.pallas_call(
        functools.partial(exchange_body, seqs, (told, vector_spot)),
        name="exchange",
        out_shape=(
            jax.ShapeDtypeStruct((devices, own, part, BS), jnp.bfloat16),
            jax.ShapeDtypeStruct((devices, 1, 128), jnp.float32),
            jax.ShapeDtypeStruct((told, part, BS), jnp.float32),
        ),
        in_specs=[pl.BlockSpec(memory_space=pltpu.SMEM), whole],
        out_specs=[whole] * 3,
        scratch_shapes=[
            VMEM((devices, own, part, BS), jnp.bfloat16),
            VMEM((1, 128), jnp.float32),
            pltpu.SemaphoreType.DMA((3, devices)),
            pltpu.SemaphoreType.DMA((3, devices)),
        ],
        compiler_params=pltpu.CompilerParams(
            collective_id=collective, has_side_effects=True, vmem_limit_bytes=60 << 20
        ),
    )(spot_of, late)


def gather_rows_body(bits, seqs, groups, ahead, parts, pace, given, *refs):
    piece_refs, token_ref = refs[:given], refs[given]
    full_refs, row_ref = refs[given + 1:2 * given + 1], refs[2 * given + 1]
    near, send, recv, chain_send, chain_recv, own_sem = refs[2 * given + 2:]
    core, sibling, flags, peers = partners(bits)
    row, seq = lax.axis_index("row"), lax.axis_index("seq")
    greet([sibling, *peers, *[(row, (seq + k) % seqs) for k in range(1, seqs)]])
    used = [0]

    def copy(source, target, device):
        at = used[0]
        used[0] += 1
        return pltpu.make_async_remote_copy(
            src_ref=source, dst_ref=target, send_sem=send.at[at], recv_sem=recv.at[at],
            device_id=device, device_id_type=MESH,
        )

    def hop(source, here, sems_out, sems_in, to_right, step):
        spot = seq - step if to_right else seq + step
        side = 0 if to_right else 1
        return pltpu.make_async_remote_copy(
            src_ref=source if step == 0 else here(spot), dst_ref=here(spot), send_sem=sems_out(side, step),
            recv_sem=sems_in(spot), device_id=(row, seq + (1 if to_right else -1)), device_id_type=MESH,
        )

    def ends(to_right, step):
        there = seq - step >= 0 if to_right else seq + step < seqs
        onward = seq + 1 < seqs if to_right else seq - 1 >= 0
        return there, onward

    def chain(line, step, finish=False):
        for to_right in (True, False):
            there, onward = ends(to_right, step)
            if step > 0 and not finish:

                @pl.when(there)
                def _():
                    hop(*line, to_right, step).wait_recv()

            @pl.when(there & onward)
            def _():
                move = hop(*line, to_right, step)
                if finish:
                    move.wait_send()
                else:
                    move.start()

    lines = []
    for g, (ref, low, high, to, _) in enumerate(groups):
        span, near_span = pl.ds(low, high - low), pl.ds(to, high - low)
        lines.append((
            piece_refs[ref].at[span],
            lambda spot, near_span=near_span: near.at[spot, near_span],
            lambda side, step, g=g: chain_send.at[g, side, step],
            lambda spot, g=g: chain_recv.at[g, spot],
        ))
    share = token_ref.shape[0] // parts

    def token_line(k):
        rows, at = pl.ds(k * share, share), len(groups) + k
        return (
            token_ref.at[rows],
            lambda spot: row_ref.at[spot, rows],
            lambda side, step: chain_send.at[at, side, step],
            lambda spot: chain_recv.at[at, spot],
        )

    token_lines = [token_line(k) for k in range(parts)]
    for line in lines:
        chain(line, 0)
    keep_tokens = pltpu.make_async_copy(token_ref, row_ref.at[seq], own_sem)
    keep_tokens.start()
    sent = []

    def work(g):
        ref, low, high, to, backwards = groups[g]
        full_ref = full_refs[ref]
        span = pl.ds(low, high - low)
        order = list(range(bits - 1, -1, -1)) if backwards else list(range(bits))
        for step in range(1, seqs):
            chain(lines[g], step)
            yield True

        def join(n, carry):
            pieces = [
                jnp.where(seq == s, piece_refs[ref][low + n], near[s, to + n]).astype(jnp.float32)
                for s in range(seqs)
            ]
            slab = jnp.concatenate(pieces, axis=0)
            full_ref[(low + n, *flags[::-1], core)] = slab.astype(jnp.bfloat16)
            return carry

        lax.fori_loop(0, high - low, join, 0)
        coming = [[] for _ in order]

        def pass_on(place, level):
            spot = full_ref.at[(span, *place[::-1], core)]
            for later in range(level + 1, bits):
                bit = order[later]
                move = copy(spot, spot, peers[bit])
                move.start()
                there = list(place)
                there[bit] = 1 - flags[bit]
                coming[later].append((tuple(there), move))
                sent.append(move)
            move = copy(spot, spot, sibling)
            move.start()
            across.append(move)

        pass_on(tuple(flags), -1)
        for level in range(bits):
            yield True
            for place, move in coming[level]:
                move.wait_recv()
                pass_on(place, level)

    across = []

    works = [work(g) for g in range(len(groups))]
    hops = [(line, step) for step in range(seqs) for line in token_lines]
    for turn in range(bits + seqs):
        for one in works:
            next(one, None)
        if turn >= ahead:
            for line, step in hops[:parts if turn == ahead else pace]:
                chain(line, step)
                hops = hops[1:]
    for line, step in hops:
        chain(line, step)
    for move in sent:
        move.wait_send()
    for move in across:
        move.wait()
    keep_tokens.wait()
    for line in [*lines, *token_lines]:
        for step in range(seqs):
            chain(line, step, True)


def gather_rows(pieces, tokens, rows, seqs, cuts, collective, ahead=2, parts=1, pace=1):
    part = pieces[0].shape[1]
    bits = (rows // 2).bit_length() - 1
    slab = BS // rows
    twos = (2,) * bits
    low = jnp.bfloat16
    whole = pl.BlockSpec(memory_space=VMEM)
    groups, at = [], 0
    for ref, piece in enumerate(pieces):
        for begin, end in group_bounds(piece.shape[0], cuts[ref]):
            groups.append((ref, begin, end, at, len(groups) % 2 == 1))
            at += end - begin
    sems = len(groups) * (2 * 2 ** bits - 1)
    *full, token_row = pl.pallas_call(
        functools.partial(gather_rows_body, bits, seqs, groups, ahead, parts, pace, len(pieces)),
        name="gather_rows",
        out_shape=(
            *[jax.ShapeDtypeStruct((piece.shape[0], *twos, 2, slab, BS), low) for piece in pieces],
            jax.ShapeDtypeStruct((seqs, *tokens.shape), low),
        ),
        in_specs=[whole] * (len(pieces) + 1),
        out_specs=[whole] * (len(pieces) + 1),
        scratch_shapes=[
            VMEM((seqs, at, part, BS), low),
            pltpu.SemaphoreType.DMA((sems,)),
            pltpu.SemaphoreType.DMA((sems,)),
            pltpu.SemaphoreType.DMA((len(groups) + parts, 2, seqs)),
            pltpu.SemaphoreType.DMA((len(groups) + parts, seqs)),
            pltpu.SemaphoreType.DMA,
        ],
        compiler_params=pltpu.CompilerParams(
            collective_id=collective, has_side_effects=True, vmem_limit_bytes=60 << 20
        ),
        cost_estimate=pl.CostEstimate(flops=0, bytes_accessed=4 * at * BS * BS, transcendentals=0),
    )(*pieces, tokens)
    return [one.reshape(-1, BS, BS) for one in full], token_row.reshape(-1, tokens.shape[1])


def normalize(values):
    centered = values - jnp.mean(values, axis=-1, keepdims=True)
    inverse = lax.rsqrt(jnp.mean(centered * centered, axis=-1, keepdims=True) + NORM_EPS)
    return centered * inverse, inverse


def column(k):
    return slice(k * BS, (k + 1) * BS)


def gate(values):
    return 1.0 / (1.0 + jnp.exp(-values))


def enter_body(spots, token_ref, row_ref, weight_ref, vector_ref, hid_ref, pre_ref, own_t_ref, value_ref, row_t_ref):
    first_at, value_at = spots
    wide = vector_ref.shape[1] // BS
    gain, shift, bias = vector_ref[0:1], vector_ref[1:2], vector_ref[4:5]

    def project(inputs, at, j):
        total = dot_nn(inputs[:, column(0)], weight_ref[at + j])
        for i in range(1, wide):
            total = total + dot_nn(inputs[:, column(i)], weight_ref[at + i * wide + j])
        return total

    def own(c, carry):
        rows = pl.ds(pl.multiple_of(c * BS, BS), BS)
        normed = normalize(token_ref[rows, :].astype(jnp.float32))[0] * gain + shift
        inputs = normed.astype(jnp.bfloat16)
        own_t_ref[:, rows] = normed.T.astype(jnp.bfloat16)
        for j in range(wide):
            pre = project(inputs, first_at, j) + bias[:, column(j)]
            pre_ref[rows, column(j)] = pre
            hid_ref[rows, column(j)] = (pre * gate(pre)).astype(jnp.bfloat16)
        return carry

    lax.fori_loop(0, token_ref.shape[0] // BS, own, 0)

    def whole_row(c, carry):
        rows = pl.ds(pl.multiple_of(c * BS, BS), BS)
        normed = normalize(row_ref[rows, :].astype(jnp.float32))[0] * gain + shift
        inputs = normed.astype(jnp.bfloat16)
        row_t_ref[:, rows] = normed.T.astype(jnp.bfloat16)
        for j in range(wide):
            value_ref[rows, column(j)] = project(inputs, value_at, j).astype(jnp.bfloat16)
        return carry

    lax.fori_loop(0, row_ref.shape[0] // BS, whole_row, 0)


def enter(tokens, token_row, weights, vectors, spots):
    positions, width = tokens.shape
    length = token_row.shape[0]
    whole = pl.BlockSpec(memory_space=VMEM)
    low = jnp.bfloat16
    return pl.pallas_call(
        functools.partial(enter_body, spots),
        name="enter",
        out_shape=(
            jax.ShapeDtypeStruct((positions, width), low),
            jax.ShapeDtypeStruct((positions, width), jnp.float32),
            jax.ShapeDtypeStruct((width, positions), low),
            jax.ShapeDtypeStruct((length, width), low),
            jax.ShapeDtypeStruct((width, length), low),
        ),
        in_specs=[whole] * 4,
        out_specs=[whole] * 5,
        compiler_params=pltpu.CompilerParams(vmem_limit_bytes=60 << 20),
        cost_estimate=pl.CostEstimate(flops=2 * (positions + length) * width * width, bytes_accessed=24 << 20, transcendentals=positions * width),
    )(tokens, token_row, weights, vectors)


def middle_body(cut, token_ref, cotangent_ref, mixed_ref, output_ref, up_a, up_b, up_c, down_ref, vector_ref,
                out_ref, terms_ref, apart_ref, dmix_ref, dmiddle_ref, sums_ref, bias_ref,
                middle, normed_in, normed_t, back_t, total, back, made, made_output, sems, output_sem):
    f, last = pl.program_id(0), pl.num_programs(0) - 1
    ups = (up_a, up_b, up_c)
    wide = len(ups)
    first_up, steps = wide * wide, bias_ref.shape[0]
    slot = f % 2

    def spot(base, step):
        return apart_ref.at[base - cut + step] if base >= cut else terms_ref.at[base + step]

    @pl.when(f == 0)
    def _():
        mixed = mixed_ref[...].astype(jnp.bfloat16)
        for j in range(wide):
            part = token_ref[:, column(j)].astype(jnp.float32)
            for i in range(wide):
                part = part + dot_nn(mixed[:, column(i)], output_ref[i * wide + j])
            middle[:, column(j)] = part
        hat, _ = normalize(middle[...])
        inputs = hat * vector_ref[2:3] + vector_ref[3:4]
        normed_in[...] = inputs.astype(jnp.bfloat16)
        normed_t[...] = inputs.T.astype(jnp.bfloat16)
        total[...] = middle[...]
        back[...] = jnp.zeros_like(back)

    def copies(at, step):
        out = []
        for i in range(wide):
            out.append(pltpu.make_async_copy(made.at[at, i], spot(first_up + i * steps, step), sems.at[at, i]))
        for j in range(wide):
            out.append(pltpu.make_async_copy(made.at[at, wide + j], spot(first_up + wide * steps, step * wide + j), sems.at[at, wide + j]))
        return out

    @pl.when(f >= 2)
    def _():
        for move in copies(slot, f - 2):
            move.wait()

    inputs = normed_in[...]
    pre = vector_ref[pl.ds(5 + f // wide, 1), pl.ds(pl.multiple_of(f % wide * BS, BS), BS)]
    for i in range(wide):
        pre = pre + dot_nn(inputs[:, column(i)], ups[i][0])
    share = gate(pre)
    hidden = pre * share
    low_hidden = hidden.astype(jnp.bfloat16)
    hidden_t = hidden.T.astype(jnp.bfloat16)
    dhidden = None
    for j in range(wide):
        total[:, column(j)] += dot_nn(low_hidden, down_ref[j])
        made[slot, wide + j] = dot_nn(hidden_t, cotangent_ref[:, column(j)]).astype(jnp.bfloat16)
        part = dot_nt(cotangent_ref[:, column(j)], down_ref[j])
        dhidden = part if dhidden is None else dhidden + part
    dhidden = dhidden.astype(jnp.bfloat16).astype(jnp.float32)
    dpre = (dhidden * (share * (1.0 + pre * (1.0 - share)))).astype(jnp.bfloat16)
    bias_ref[pl.ds(f, 1), :] = jnp.sum(dpre.astype(jnp.float32), axis=0, keepdims=True)
    for i in range(wide):
        made[slot, i] = dot_nn(normed_t[column(i), :], dpre).astype(jnp.bfloat16)
        back[:, column(i)] += dot_nt(dpre, ups[i][0])
    for move in copies(slot, f):
        move.start()

    @pl.when(f == last)
    def _():
        out_ref[...] = total[...].astype(jnp.bfloat16)
        hat, inverse = normalize(middle[...])
        dnormed = back[...]
        sums_ref[...] = jnp.zeros_like(sums_ref)
        sums_ref[0:1] = jnp.sum(dnormed * hat, axis=0, keepdims=True)
        sums_ref[1:2] = jnp.sum(dnormed, axis=0, keepdims=True)
        scaled = dnormed * vector_ref[2:3]
        dmiddle = cotangent_ref[...].astype(jnp.float32) + inverse * (
            scaled
            - jnp.mean(scaled, axis=-1, keepdims=True)
            - hat * jnp.mean(scaled * hat, axis=-1, keepdims=True)
        )
        dmiddle_ref[...] = dmiddle
        low = dmiddle.astype(jnp.bfloat16)
        back_t[...] = mixed_ref[...].T.astype(jnp.bfloat16)
        for i in range(wide):
            part = None
            for j in range(wide):
                made_output[i * wide + j] = dot_nn(back_t[column(i), :], low[:, column(j)]).astype(jnp.bfloat16)
                term = dot_nt(low[:, column(j)], output_ref[i * wide + j])
                part = term if part is None else part + term
            dmix_ref[:, column(i)] = part.astype(jnp.bfloat16)
        move = pltpu.make_async_copy(made_output, terms_ref.at[0:wide * wide], output_sem)
        move.start()
        for one in copies(1 - slot, f - 1):
            one.wait()
        for one in copies(slot, f):
            one.wait()
        move.wait()


def middle_stage(tokens, cotangent, mixed, weights, down_weights, vectors, apart):
    positions, width = tokens.shape
    wide = width // BS
    steps = down_weights.shape[0] // wide
    cut = wide * wide + (wide - apart) * steps
    low = jnp.bfloat16
    tok = pl.BlockSpec((positions, width), lambda f: (0, 0))

    def up(i):
        return pl.BlockSpec((1, BS, BS), lambda f: (wide * wide + i * steps + f, 0, 0))

    return pl.pallas_call(
        functools.partial(middle_body, cut),
        name="middle_stage",
        out_shape=(
            jax.ShapeDtypeStruct((positions, width), low),
            jax.ShapeDtypeStruct((cut, BS, BS), low),
            jax.ShapeDtypeStruct((wide * wide + 2 * wide * steps - cut, BS, BS), low),
            jax.ShapeDtypeStruct((positions, width), low),
            jax.ShapeDtypeStruct((positions, width), jnp.float32),
            jax.ShapeDtypeStruct((8, width), jnp.float32),
            jax.ShapeDtypeStruct((steps, BS), jnp.float32),
        ),
        grid=(steps,),
        in_specs=[
            tok,
            tok,
            tok,
            pl.BlockSpec((wide * wide, BS, BS), lambda f: (0, 0, 0)),
            up(0),
            up(1),
            up(2),
            pl.BlockSpec((wide, BS, BS), lambda f: (f, 0, 0)),
            pl.BlockSpec(vectors.shape, lambda f: (0, 0)),
        ],
        out_specs=[
            tok,
            pl.BlockSpec(memory_space=pl.ANY),
            pl.BlockSpec(memory_space=pl.ANY),
            tok,
            tok,
            pl.BlockSpec((8, width), lambda f: (0, 0)),
            pl.BlockSpec((steps, BS), lambda f: (0, 0)),
        ],
        scratch_shapes=[
            VMEM((positions, width), jnp.float32),
            VMEM((positions, width), low),
            VMEM((width, positions), low),
            VMEM((width, positions), low),
            VMEM((positions, width), jnp.float32),
            VMEM((positions, width), jnp.float32),
            VMEM((2, 2 * wide, BS, BS), low),
            VMEM((wide * wide, BS, BS), low),
            pltpu.SemaphoreType.DMA((2, 2 * wide)),
            pltpu.SemaphoreType.DMA,
        ],
        compiler_params=pltpu.CompilerParams(vmem_limit_bytes=60 << 20, dimension_semantics=("arbitrary",)),
        cost_estimate=pl.CostEstimate(flops=36 * positions * width * width, bytes_accessed=40 << 20, transcendentals=positions * width * 4),
    )(tokens, cotangent, mixed, weights, weights, weights, weights, down_weights, vectors)


def leave_body(spots, dhid_ref, pre_ref, own_t_ref, token_ref, row_ref, row_t_ref, dvalue_ref, weight_ref, vector_ref, sums_ref, bias_ref,
               dfirst_ref, dweight_ref, block_ref, back_ref, dpre_all, rows32):
    first_at, value_at = spots
    positions, width = dhid_ref.shape
    wide = width // BS
    sums = [jnp.zeros((1, width), jnp.float32) for _ in range(3)]

    def unproject(grads, at, i):
        total = None
        for j in range(wide):
            part = dot_nt(grads[:, column(j)], weight_ref[at + i * wide + j])
            total = part if total is None else total + part
        return total

    def own(c, sums):
        rows = pl.ds(pl.multiple_of(c * BS, BS), BS)
        pre = pre_ref[rows, :]
        share = gate(pre)
        dpre = (dhid_ref[rows, :].astype(jnp.float32) * (share * (1.0 + pre * (1.0 - share)))).astype(jnp.bfloat16)
        dpre_all[rows, :] = dpre
        hat, _ = normalize(token_ref[rows, :].astype(jnp.float32))
        back = jnp.concatenate([unproject(dpre, first_at, i) for i in range(wide)], axis=1)
        back_ref[rows, :] = back
        return (
            sums[0] + jnp.sum(back * hat, axis=0, keepdims=True),
            sums[1] + jnp.sum(back, axis=0, keepdims=True),
            sums[2] + jnp.sum(dpre.astype(jnp.float32), axis=0, keepdims=True),
        )

    sums = lax.fori_loop(0, positions // BS, own, tuple(sums))

    def whole_row(c, sums):
        rows = pl.ds(pl.multiple_of(c * BS, BS), BS)
        dvalue = dvalue_ref[rows, :]
        hat, _ = normalize(row_ref[rows, :].astype(jnp.float32))
        back = jnp.concatenate([unproject(dvalue, value_at, i) for i in range(wide)], axis=1)
        return (
            sums[0] + jnp.sum(back * hat, axis=0, keepdims=True),
            sums[1] + jnp.sum(back, axis=0, keepdims=True),
            sums[2],
        )

    sums = lax.fori_loop(0, row_ref.shape[0] // BS, whole_row, sums)
    for i in range(wide):
        for j in range(wide):
            dfirst_ref[i * wide + j] = dot_nn(own_t_ref[column(i), :], dpre_all[:, column(j)]).astype(jnp.bfloat16)
            dweight_ref[i * wide + j] = dot_nn(row_t_ref[column(i), :], dvalue_ref[:, column(j)]).astype(jnp.bfloat16)
    rows32[...] = jnp.zeros_like(rows32)
    lines = (sums[0], sums[1], sums_ref[0:1], sums_ref[1:2], sums[2])
    for r, line in enumerate(lines):
        for i in range(wide):
            rows32[r * wide + i:r * wide + i + 1, :] = line[:, column(i)]
    at = len(lines) * wide
    rows32[at:at + bias_ref.shape[0], :] = bias_ref[...]
    block_ref[0] = jnp.zeros_like(block_ref[0])
    block_ref[0, 0:rows32.shape[0], :] = rows32[...].astype(jnp.bfloat16)


def leave(dhid, pre, own_t, tokens, token_row, row_t, dvalue, weights, vectors, sums, bias, spots):
    positions, width = dhid.shape
    wide = width // BS
    whole = pl.BlockSpec(memory_space=VMEM)
    low = jnp.bfloat16
    tall = -(-(5 * wide + bias.shape[0]) // 16) * 16
    return pl.pallas_call(
        functools.partial(leave_body, spots),
        name="leave",
        out_shape=(
            jax.ShapeDtypeStruct((wide * wide, BS, BS), low),
            jax.ShapeDtypeStruct((wide * wide, BS, BS), low),
            jax.ShapeDtypeStruct((1, BS, BS), low),
            jax.ShapeDtypeStruct((positions, width), jnp.float32),
        ),
        in_specs=[whole] * 11,
        out_specs=[whole] * 4,
        scratch_shapes=[VMEM((positions, width), low), VMEM((tall, BS), jnp.float32)],
        compiler_params=pltpu.CompilerParams(vmem_limit_bytes=60 << 20),
        cost_estimate=pl.CostEstimate(flops=4 * (positions + token_row.shape[0]) * width * width, bytes_accessed=24 << 20, transcendentals=positions * width),
    )(dhid, pre, own_t, tokens, token_row, row_t, dvalue, weights, vectors, sums, bias)


def finish_body(value_at, dvalue_ref, first_ref, dmiddle_ref, token_ref, weight_ref, vector_ref, out_ref):
    wide = vector_ref.shape[1] // BS

    def chunk(c, carry):
        rows = pl.ds(pl.multiple_of(c * BS, BS), BS)
        dvalue = dvalue_ref[rows, :]
        parts = []
        for i in range(wide):
            total = first_ref[rows, column(i)]
            for j in range(wide):
                total = total + dot_nt(dvalue[:, column(j)], weight_ref[value_at + i * wide + j])
            parts.append(total)
        scaled = jnp.concatenate(parts, axis=1) * vector_ref[0:1]
        hat, inverse = normalize(token_ref[rows, :].astype(jnp.float32))
        out_ref[rows, :] = dmiddle_ref[rows, :] + inverse * (
            scaled
            - jnp.mean(scaled, axis=-1, keepdims=True)
            - hat * jnp.mean(scaled * hat, axis=-1, keepdims=True)
        )
        return carry

    lax.fori_loop(0, token_ref.shape[0] // BS, chunk, 0)


def finish_inputs(dvalue, from_first, dmiddle, tokens, weights, vectors, value_at):
    whole = pl.BlockSpec(memory_space=VMEM)
    positions, width = tokens.shape
    return pl.pallas_call(
        functools.partial(finish_body, value_at),
        name="finish_inputs",
        out_shape=jax.ShapeDtypeStruct((positions, width), jnp.float32),
        in_specs=[whole] * 6,
        out_specs=whole,
        compiler_params=pltpu.CompilerParams(vmem_limit_bytes=60 << 20),
        cost_estimate=pl.CostEstimate(flops=2 * positions * width * width, bytes_accessed=12 << 20, transcendentals=0),
    )(dvalue, from_first, dmiddle, tokens, weights, vectors)


def block_bounds():
    model_blocks = D // BS
    first_end = model_blocks * model_blocks
    synth_end = first_end + model_blocks * (LEN // BS)
    value_end = synth_end + first_end
    output_end = value_end + first_end
    expand_end = output_end + model_blocks * (FF // BS)
    return (first_end, synth_end, value_end, output_end, expand_end)


def block_scales():
    first_end, synth_end, value_end, output_end, expand_end = block_bounds()
    spots = jnp.arange(BLOCKS)
    scales = jnp.where(
        spots < first_end,
        D ** (-0.5),
        jnp.where(
            spots < synth_end,
            3.0 * HD ** (-0.5),
            jnp.where(
                spots < value_end,
                D ** (-0.5),
                jnp.where(
                    spots < output_end,
                    4.0 * D ** (-0.5),
                    jnp.where(spots < expand_end, D ** (-0.5), FF ** (-0.5)),
                ),
            ),
        ),
    )
    return scales.astype(jnp.float32)


def slot_table(owners, own_most, slot_total):
    block_count = owners.shape[0]
    block_index = jnp.arange(block_count, dtype=jnp.int32)
    same_owner = owners[:, None] == owners[None, :]
    earlier = block_index[None, :] < block_index[:, None]
    rank_within = jnp.sum(jnp.where(same_owner & earlier, 1, 0), axis=1).astype(jnp.int32)
    slot_id = owners * own_most + rank_within
    slot_hit = slot_id[:, None] == jnp.arange(slot_total, dtype=jnp.int32)[None, :]
    used = jnp.any(slot_hit, axis=0)
    block_of = jnp.sum(jnp.where(slot_hit, block_index[:, None], 0), axis=0)
    return (slot_id, used, block_of)


def vector_adam(vectors, vec_moments, grad_rows, mom_fix, sec_fix):
    first_moment = BETA_MOM * vec_moments[0] + (1 - BETA_MOM) * grad_rows
    second = BETA_SEC * vec_moments[1] + (1 - BETA_SEC) * grad_rows * grad_rows
    step_rows = first_moment / mom_fix / (jnp.sqrt(second / sec_fix) + EPSILON)
    return (vectors - VECTOR_RATE * step_rows, jnp.stack([first_moment, second]))


def local(
    tokens,
    cotangent,
    seg_ids,
    seg_lengths,
    weights,
    vectors,
    vec_moments,
    moments,
    stats,
    bases,
    owners,
    step_count,
):
    rows_here, positions, width = tokens.shape
    owner_count = lax.axis_size("row") * lax.axis_size("seq")
    own_most = moments.shape[0]
    slot_count = owner_count * own_most
    block_count = weights.shape[0]
    piece_rows = weights.shape[1] // BS
    first_end, synth_end, value_end, _, expand_end = block_bounds()
    synth_count = synth_end - first_end
    tokens = tokens.reshape(positions, width)
    pieces_one, pieces_two, pieces_three = spread_pieces(
        weights,
        (
            ((first_end, synth_end), (0, first_end), (synth_end, value_end)),
            ((value_end, expand_end),),
            ((expand_end, block_count),),
        ),
    )
    spots = (synth_count, synth_end)
    rows_total, seqs_total = lax.axis_size("row"), lax.axis_size("seq")
    (gathered_one, gathered_two), token_row = gather_rows(
        [pieces_one, pieces_two], tokens, rows_total, seqs_total, (2, 2), 3
    )
    gathered_one, pieces_three = lax.optimization_barrier((gathered_one, pieces_three))
    gathered_three = lax.all_gather(pieces_three, AXES, axis=1, tiled=True)

    slot_range = jnp.arange(seg_lengths.shape[1], dtype=jnp.int32)
    before = slot_range[None, :] < slot_range[:, None]
    starts = jnp.sum(jnp.where(before, seg_lengths[0][None, :], 0), axis=1)
    offset = lax.axis_index("seq") * positions
    tables = tables_of(starts, seg_lengths[0], seg_ids[0], offset)

    hidden, first_pre, own_t, values, row_t = enter(tokens, token_row, gathered_one, vectors, spots)
    mixed, log_total = attn_forward(tables, hidden, gathered_one, values)
    layer_out, terms_two, early_terms, back_mixed, back_middle, norm_sums, grad_ffn_bias = middle_stage(
        tokens, cotangent.reshape(positions, width), mixed, gathered_two, gathered_three, vectors, 2
    )
    early_part = lax.psum_scatter(early_terms, "row", scatter_dimension=1, tiled=True)
    synth_grad, back_hidden, value_terms = attn_backward(
        tables, hidden, gathered_one, values, back_mixed, mixed, log_total
    )
    grad_first, grad_value, vector_block, back_from_first = leave(
        back_hidden,
        first_pre,
        own_t,
        tokens,
        token_row,
        row_t,
        value_terms,
        gathered_one,
        vectors,
        norm_sums,
        grad_ffn_bias,
        spots,
    )
    late_terms = [grad_first, grad_value, vector_block, synth_grad, terms_two]
    vector_rows = vectors.shape[0] * vectors.shape[1] // BS
    sums = reduce_rows(late_terms, early_part, rows_total, seqs_total, 6, 1)
    slot_id, used, block_of = slot_table(owners, own_most, slot_count)
    device_index = lax.axis_index(AXES)
    mine_used = lax.dynamic_slice_in_dim(used, device_index * own_most, own_most)
    mine_block = lax.dynamic_slice_in_dim(block_of, device_index * own_most, own_most)
    vector_spot = 2 * first_end
    spot_of = jnp.where(
        block_of < first_end,
        block_of,
        jnp.where(
            block_of < synth_end,
            block_of + first_end + 1,
            jnp.where(block_of < value_end, block_of - synth_end + first_end, block_of + 1),
        ),
    )
    got, square_parts, vector_parts = exchange(
        spot_of, sums, rows_total, seqs_total, vector_spot, vector_rows, 2
    )
    got, value_late = lax.optimization_barrier((got, value_terms))
    value_sums = lax.psum_scatter(value_late, "seq", scatter_dimension=0, tiled=True)
    x_grad = finish_inputs(
        value_sums, back_from_first, back_middle, tokens, gathered_one, vectors, synth_end
    )
    vector_total = vector_parts.reshape(-1, BS)[:vector_rows].reshape(vectors.shape)
    grad_norm = jnp.sqrt(jnp.sum(square_parts))
    clip_max = math.sqrt(block_count * BS * BS + vectors.shape[0] * vectors.shape[1])
    scale = jnp.minimum(1.0, clip_max / grad_norm)
    step_value = step_count[0].astype(jnp.float32)
    mom_fix = 1.0 - jnp.power(BETA_MOM, step_value)
    sec_fix = 1.0 - jnp.power(BETA_SEC, step_value)
    new_vectors, new_vec_moments = vector_adam(
        vectors, vec_moments, vector_total * scale, mom_fix, sec_fix
    )
    rate_table = RATE_FACTOR * block_scales()
    slot_rates = jnp.sum(
        jnp.where(
            mine_block[:, None] == jnp.arange(block_count, dtype=jnp.int32)[None, :],
            rate_table[None, :],
            0.0,
        ),
        axis=1,
    )
    floats = jnp.concatenate([jnp.stack([scale, mom_fix, sec_fix]), slot_rates])
    mine_spot = jnp.where(
        mine_block < first_end,
        mine_block + synth_count,
        jnp.where(mine_block < synth_end, mine_block - first_end, mine_block),
    )
    ints = jnp.concatenate([mine_used.astype(jnp.int32), mine_spot])
    new_master, new_moments, new_stats, wide = soap_update(
        ints, floats, got, gathered_one, gathered_two, gathered_three, moments, stats, bases
    )
    new_bases = soap_bases(ints, wide, bases)
    returned = lax.all_to_all(
        new_master.reshape(1, own_most, BS, BS), AXES, split_axis=2, concat_axis=0, tiled=True
    )
    new_weights = collect(slot_id, returned.reshape(slot_count, piece_rows, BS))
    return (
        layer_out.reshape(rows_here, positions, width),
        x_grad.reshape(rows_here, positions, width),
        new_weights,
        new_moments,
        new_stats,
        new_bases,
        new_vectors,
        new_vec_moments,
        grad_norm.reshape(1),
    )


def solution(mesh):
    placed = (
        P("row", "seq", None),
        P("row", "seq", None),
        P("row", "seq"),
        P("row", None),
        P(None, ("row", "seq")),
        P(),
        P(),
        P(("row", "seq"), None, None, None),
        P(("row", "seq"), None, None, None),
        P(("row", "seq"), None, None, None),
        P(),
        P(),
    )
    return jax.shard_map(
        local,
        mesh=mesh,
        in_specs=placed,
        out_specs=(
            P("row", "seq", None),
            P("row", "seq", None),
            P(None, ("row", "seq")),
            P(("row", "seq"), None, None, None),
            P(("row", "seq"), None, None, None),
            P(("row", "seq"), None, None, None),
            P(),
            P(),
            P(),
        ),
        check_vma=False,
    )
```
